32 devices in a mesh: rows: 8 (over z, y), heads: 4 (over x, core).
Axes of the slice: x: 2, y: 2, z: 4, core: 2. Of those that a mesh axis runs over, the one named last changes fastest.
Arguments:
- patches: bfloat16 [8192, 1152], P(('rows', 'heads')), may hold values from -6 to 6
- time_table: bfloat16 [1024, 1152], P('rows', 'heads'), may hold values from -6 to 6
- class_table: bfloat16 [1024, 1152], P('rows', 'heads'), may hold values from -6 to 6
- w_ada: bfloat16 [1152, 6912], P('heads', 'rows'), may hold values from -0.1875 to 0.1875
- b_ada: bfloat16 [6912], replicated, may hold values from -3 to 3
- w_qkv: bfloat16 [1152, 3456], P('rows', 'heads'), may hold values from -0.1875 to 0.1875
- b_qv: bfloat16 [16, 144], P('heads'), may hold values from -0.59765625 to 0.59765625
- w_out: bfloat16 [1152, 1152], P('rows', 'heads'), may hold values from -1 to 1
- b_out: bfloat16 [1152], replicated, may hold values from -3 to 3
- w_fc1: bfloat16 [1152, 4608], P('rows', 'heads'), may hold values from -0.1875 to 0.1875
- b_fc1: bfloat16 [4608], P('heads'), may hold values from -3 to 3
- w_fc2: bfloat16 [1152, 4608], P('rows', 'heads'), may hold values from -0.09375 to 0.09375
- b_fc2: bfloat16 [1152], replicated, may hold values from -3 to 3
- image_lengths: int32 [8, 4], P('rows'), may hold values from 0 to 1024, as said below
- segment_ids: int32 [8, 1024], P('rows'), may hold values from 0 to 3, as said below
- bucket_ids: int32 [8, 4], P('rows'), may hold values from 0 to 1023
- class_labels: int32 [8, 4], P('rows'), may hold values from 0 to 1023
- cotangent: bfloat16 [8192, 1152], P(('rows', 'heads')), may hold values from -6 to 6
Outputs:
- block_out: bfloat16 [8192, 1152], P(('rows', 'heads'))
- grad_patches: float32 [8192, 1152], P(('rows', 'heads'))
- grad_time_table: float32 [1024, 1152], P('rows', 'heads')
- grad_class_table: float32 [1024, 1152], P('rows', 'heads')
- grad_w_ada: float32 [1152, 6912], P('heads', 'rows')
- grad_b_ada: float32 [6912], P('rows')
- grad_w_qkv: float32 [1152, 3456], P('rows', 'heads')
- grad_b_qv: float32 [16, 144], P('heads')
- grad_w_out: float32 [1152, 1152], P('rows', 'heads')
- grad_b_out: float32 [1152], P('rows')
- grad_w_fc1: float32 [1152, 4608], P('rows', 'heads')
- grad_b_fc1: float32 [4608], P('heads')
- grad_w_fc2: float32 [1152, 4608], P('rows', 'heads')
- grad_b_fc2: float32 [1152], P('rows')
The draws below stay inside these ranges and needn't reach their ends.
Inputs may be any that keep to these rules, and one draw needn't show every extreme that they name: `image_lengths`: each packed row holds either one image of 1024 patches in slot 0, its other slots of length 0, or 4 images of 256 patches; both kinds occur in every draw. `segment_ids`: the slot of each patch's image, consistent with image_lengths: patches are in slot order, slot k covering the patches after the first k slots' lengths.
All inputs are finite; a program needn't handle non-finite values.
Results may differ from the reference program's by a relative error of at most 0.019.
The reference program's roundings to bfloat16 on the way count: a program that leaves them out, or rounds other values in their place, can miss the bound.
Values may be sent and summed in bfloat16 or wider, within the bound.
A program may use at most 192 MiB of HBM per device.

```python
import math
import jax
import jax.numpy as jnp
from jax import lax

D = 1152
HEADS = 16
HD = 72
FF = 4608
BUCKETS = 1024
CLASSES = 1024
SEQ = 1024
SLOTS = 4
SEQS = 8
TOKENS = 8192


def packing_kind(key):
    kinds = jax.random.randint(jax.random.fold_in(key, 11), (SEQS,), 0, 2).astype(jnp.int32)
    return kinds.at[0].set(1).at[1].set(0)


def draw_image_lengths(key, part):
    kinds = packing_kind(key)
    small = jnp.full((SEQS, SLOTS), SEQ // SLOTS, jnp.int32)
    whole = jnp.zeros((SEQS, SLOTS), jnp.int32).at[:, 0].set(SEQ)
    return jnp.where(kinds[:, None] == 1, whole, small).astype(jnp.int32)


def draw_segment_ids(key, part):
    kinds = packing_kind(key)
    places = jnp.arange(SEQ, dtype=jnp.int32) // (SEQ // SLOTS)
    return jnp.where(kinds[:, None] == 1, jnp.zeros((SEQS, SEQ), jnp.int32), places[None, :]).astype(jnp.int32)


def plant(drawn, key, low, largest):
    extent = drawn.shape
    place = [jax.random.randint(jax.random.fold_in(key, axis), (), 0, extent[axis]) for axis in range(len(extent))]
    drawn = drawn.at[tuple(place)].set(low)
    longest = extent.index(max(extent))
    place[longest] = (place[longest] + 1) % extent[longest]
    return drawn.at[tuple(place)].set(largest)


def shard_levels(key, shape, cuts, least, top_value):
    def one(axis_at, shards_of):
        heights = jax.random.uniform(jax.random.fold_in(jax.random.fold_in(key, 6), axis_at), (shards_of,), jnp.float32, least / len(cuts), top_value / len(cuts))
        return jnp.repeat(jnp.exp(heights), shape[axis_at] // shards_of).reshape((-1,) + (1,) * (len(shape) - axis_at - 1))

    factor_of = one(*cuts[0])
    for cut in cuts[1:]:
        factor_of = factor_of * one(*cut)
    return factor_of


def scatter_about(key, dims, deviation, limit, shards=(), kind=jnp.bfloat16):
    drawn = deviation * jax.random.normal(key, dims, jnp.float32)
    if shards:
        drawn = drawn * shard_levels(key, dims, shards, -0.22, 0.18)
    return jnp.clip(drawn, -limit, limit).astype(kind)


def setup_inputs(seed: int = 0) -> dict:
    arg_keys = jax.random.split(jax.random.key(seed), 19)
    patches = scatter_about(arg_keys[0], (TOKENS, D), 1.0, 6.0, ((0, 32),))
    time_table = scatter_about(arg_keys[1], (BUCKETS, D), 1.0, 6.0, ((0, 8), (1, 4)))
    class_table = scatter_about(arg_keys[2], (CLASSES, D), 1.0, 6.0, ((0, 8), (1, 4)))
    w_ada = scatter_about(arg_keys[3], (D, 6 * D), D ** -0.5, 0.1875, ((0, 4), (1, 8)))
    b_ada = scatter_about(arg_keys[4], (6 * D,), 0.5, 3.0)
    w_qkv = scatter_about(arg_keys[5], (D, 3 * D), D ** -0.5, 0.1875, ((0, 8), (1, 4)))
    b_qv = scatter_about(arg_keys[6], (HEADS, 2 * HD), 0.1, 0.59765625, ((0, 4),))
    w_out = scatter_about(arg_keys[7], (D, D), (D // 32) ** -0.5, 1.0, ((0, 8), (1, 4)))
    b_out = scatter_about(arg_keys[8], (D,), 0.5, 3.0)
    w_fc1 = scatter_about(arg_keys[9], (D, FF), D ** -0.5, 0.1875, ((0, 8), (1, 4)))
    b_fc1 = scatter_about(arg_keys[10], (FF,), 0.5, 3.0, ((0, 4),))
    w_fc2 = scatter_about(arg_keys[11], (D, FF), FF ** -0.5, 0.09375, ((0, 8), (1, 4)))
    b_fc2 = scatter_about(arg_keys[12], (D,), 0.5, 3.0)
    image_lengths = draw_image_lengths(jax.random.fold_in(arg_keys[18], 71), 0)
    segment_ids = draw_segment_ids(jax.random.fold_in(arg_keys[18], 71), 0)
    bucket_ids = plant(jax.random.randint(arg_keys[15], (SEQS, SLOTS), 0, BUCKETS), jax.random.fold_in(arg_keys[15], 1), 0, BUCKETS - 1).astype(jnp.int32)
    class_labels = plant(jax.random.randint(arg_keys[16], (SEQS, SLOTS), 0, CLASSES), jax.random.fold_in(arg_keys[16], 1), 0, CLASSES - 1).astype(jnp.int32)
    cotangent = scatter_about(arg_keys[17], (TOKENS, D), 1.0, 6.0, ((0, 32),))
    return dict(patches=patches, time_table=time_table, class_table=class_table, w_ada=w_ada, b_ada=b_ada, w_qkv=w_qkv, b_qv=b_qv, w_out=w_out, b_out=b_out, w_fc1=w_fc1, b_fc1=b_fc1, w_fc2=w_fc2, b_fc2=b_fc2, image_lengths=image_lengths, segment_ids=segment_ids, bucket_ids=bucket_ids, class_labels=class_labels, cotangent=cotangent)


@jax.custom_vjp
def low(v):
    return lax.optimization_barrier(v.astype(jnp.bfloat16)).astype(jnp.float32)

@jax.custom_vjp
def low_back(v):
    return v

def low_keep(v):
    return (low(v), None)

def low_pass(kept, grad):
    return (grad,)

def back_keep(v):
    return (v, None)

def back_low(kept, grad):
    return (low(grad),)
low.defvjp(low_keep, low_pass)
low_back.defvjp(back_keep, back_low)
HIGH = lax.Precision.HIGHEST
EPSILON = 1e-06
MASKED = -1e+30
TANH_COEFF = 0.7978845608028654

def layer_norm(values):
    average = lax.optimization_barrier(jnp.mean(values, axis=-1, keepdims=True))
    centred = values - average
    variance = lax.optimization_barrier(jnp.mean(centred * centred, axis=-1, keepdims=True))
    return centred * lax.rsqrt(variance + EPSILON)

def gelu_tanh(values):
    return 0.5 * values * (1.0 + jnp.tanh(TANH_COEFF * (values + 0.044715 * values * values * values)))

def silu_plain(values):
    return values / (1.0 + jnp.exp(-values))

def image_index(lengths):
    slot_ends = jnp.cumsum(lengths, axis=-1)
    places = jnp.arange(SEQ, dtype=jnp.int32)
    return lax.optimization_barrier(jnp.sum((places[:, None] >= slot_ends[..., None, :]).astype(jnp.int32), axis=-1))

def block_forward(weights, patches, modulation, lengths, segments):
    w_qkv, b_qkv, w_out, b_out, w_fc1, b_fc1, w_fc2, b_fc2 = weights
    seq_batch = patches.shape[0]
    choose = (segments[:, :, None] == jnp.arange(SLOTS, dtype=jnp.int32)).astype(jnp.float32)
    token_mods = jnp.einsum('bsk,bkm->bsm', choose, modulation, precision=HIGH)
    shift_attn, scale_attn, gate_attn, shift_mlp, scale_mlp, gate_mlp = jnp.split(token_mods, 6, axis=-1)
    hidden_one = low(layer_norm(patches) * (1.0 + scale_attn) + shift_attn)
    projected = jnp.einsum('bsd,de->bse', hidden_one, w_qkv, precision=HIGH).reshape(seq_batch, SEQ, HEADS, 3, HD) + b_qkv
    projected = low(low_back(projected))
    query_rows = projected[:, :, :, 0]
    key_rows = projected[:, :, :, 1]
    value_rows = projected[:, :, :, 2]
    image_ids = image_index(lengths)
    allowed = image_ids[:, :, None] == image_ids[:, None, :]
    scores = jnp.einsum('bqhd,bkhd->bhqk', query_rows, key_rows, precision=HIGH) * (1.0 / math.sqrt(HD))
    scores = low_back(scores)
    scores = jnp.where(allowed[:, None], scores, MASKED)
    row_peak = lax.optimization_barrier(jnp.max(scores, axis=-1, keepdims=True))
    raised = jnp.exp(scores - row_peak)
    soft_probs = raised / lax.optimization_barrier(jnp.sum(raised, axis=-1, keepdims=True))
    mixed = jnp.einsum('bhqk,bkhd->bqhd', low(soft_probs), value_rows, precision=HIGH).reshape(seq_batch, SEQ, D)
    mixed = low(low_back(mixed))
    attn_out = low_back(jnp.einsum('bsi,oi->bso', mixed, w_out, precision=HIGH) + b_out)
    after_attn = patches + gate_attn * attn_out
    hidden_two = low(layer_norm(after_attn) * (1.0 + scale_mlp) + shift_mlp)
    inner = low_back(jnp.einsum('bsd,df->bsf', hidden_two, w_fc1, precision=HIGH) + b_fc1)
    active = low(gelu_tanh(inner))
    ffn_out = low_back(jnp.einsum('bsf,of->bso', active, w_fc2, precision=HIGH) + b_fc2)
    return after_attn + gate_mlp * ffn_out

def forward(values, image_lengths, segment_ids, bucket_ids, class_labels):
    patches, time_table, class_table, w_ada, b_ada, w_qkv, b_qv, w_out, b_out, w_fc1, b_fc1, w_fc2, b_fc2 = values
    condition = time_table[bucket_ids] + class_table[class_labels]
    lowered = low(silu_plain(condition))
    modulation = low_back(jnp.einsum('ksd,dm->ksm', lowered, w_ada, precision=HIGH) + b_ada)
    b_qkv = jnp.stack([b_qv[:, :HD], jnp.zeros_like(b_qv[:, :HD]), b_qv[:, HD:]], axis=1)
    per_block = math.gcd(SEQS, max(1, 4096 // SEQ))
    blocks = SEQS // per_block
    weights = (w_qkv, b_qkv, w_out, b_out, w_fc1, b_fc1, w_fc2, b_fc2)
    checked = jax.checkpoint(block_forward)
    stacked = (patches.reshape(blocks, per_block, SEQ, D), modulation.reshape(blocks, per_block, SLOTS, 6 * D), image_lengths.reshape(blocks, per_block, SLOTS), segment_ids.reshape(blocks, per_block, SEQ))
    results = lax.map(lambda pieces: checked(weights, pieces[0], pieces[1], pieces[2], pieces[3]), stacked)
    return results.reshape(TOKENS, D)

def reference(patches, time_table, class_table, w_ada, b_ada, w_qkv, b_qv, w_out, b_out, w_fc1, b_fc1, w_fc2, b_fc2, image_lengths, segment_ids, bucket_ids, class_labels, cotangent):
    floats = tuple((item.astype(jnp.float32) for item in (patches, time_table, class_table, w_ada, b_ada, w_qkv, b_qv, w_out, b_out, w_fc1, b_fc1, w_fc2, b_fc2)))

    def closed(values):
        return forward(values, image_lengths, segment_ids, bucket_ids, class_labels)
    result, pullback = jax.vjp(closed, floats)
    grads = pullback(cotangent.astype(jnp.float32))[0]
    return (result.astype(jnp.bfloat16), grads[0], grads[1], grads[2], grads[3], grads[4], grads[5], grads[6], grads[7], grads[8], grads[9], grads[10], grads[11], grads[12])
```

```python
import math

import jax
import jax.numpy as jnp
from jax import lax
from jax.sharding import PartitionSpec as P

EPSILON = 1e-06
MASKED = -1e30
HIGH = lax.Precision.HIGHEST
TANH_COEFF = 0.7978845608028654
BLOCK_LIMIT = 512


def layer_norm(values):
    average = jnp.mean(values, axis=-1, keepdims=True)
    centred = values - average
    variance = jnp.mean(centred * centred, axis=-1, keepdims=True)
    return centred * lax.rsqrt(variance + EPSILON)


def gelu_tanh(values):
    return (
        0.5 * values * (1.0 + jnp.tanh(TANH_COEFF * (values + 0.044715 * values * values * values)))
    )


def silu_plain(values):
    return values / (1.0 + jnp.exp(-values))


def modulate(values, shift_term, scale_term):
    return layer_norm(values) * (1.0 + scale_term) + shift_term


def contract_rows(left_matrix, right_matrix):
    return lax.dot_general(
        left_matrix, right_matrix, (((0,), (0,)), ((), ())), preferred_element_type=jnp.float32
    )


def contract_rows_exact(left_matrix, right_matrix):
    return lax.dot_general(
        left_matrix,
        right_matrix,
        (((0,), (0,)), ((), ())),
        precision=HIGH,
        preferred_element_type=jnp.float32,
    )


def times_transposed(left_matrix, right_matrix):
    return lax.dot_general(
        left_matrix, right_matrix, (((1,), (1,)), ((), ())), preferred_element_type=jnp.float32
    )


def gather_weights(w_qkv, w_out, w_fc1, w_fc2):
    return (
        lax.all_gather(w_qkv, "rows", axis=0, tiled=True),
        lax.all_gather(w_out, "rows", axis=0, tiled=True),
        lax.all_gather(w_fc1, "rows", axis=0, tiled=True),
        lax.all_gather(w_fc2, "rows", axis=0, tiled=True),
    )


def shards(
    patches,
    time_table,
    class_table,
    w_ada,
    b_ada,
    w_qkv,
    b_qv,
    w_out,
    b_out,
    w_fc1,
    b_fc1,
    w_fc2,
    b_fc2,
    image_lengths,
    segment_ids,
    bucket_ids,
    class_labels,
    cotangent,
):
    head_parts = lax.axis_size("heads")
    member = lax.axis_index("heads")
    tok_rows = patches.shape[0]
    model_width = patches.shape[1]
    seq_count = segment_ids.shape[0]
    seq_len = segment_ids.shape[1]
    slot_count = image_lengths.shape[1]
    image_count = seq_count * slot_count
    group_rows = tok_rows * head_parts
    head_local = b_qv.shape[0]
    head_size = b_qv.shape[1] // 2
    block_rows = min(BLOCK_LIMIT, seq_len)
    scale_factor = 1.0 / math.sqrt(head_size)
    row_parts = lax.axis_size("rows")
    table_rows = time_table.shape[0]
    ada_width = w_ada.shape[1]
    qkv_cols, out_cols, fc1_cols, fc2_cols = gather_weights(w_qkv, w_out, w_fc1, w_fc2)
    ids_all = lax.all_gather(
        jnp.concatenate([bucket_ids, class_labels], axis=1), "rows", axis=0, tiled=True
    )
    every_slot = row_parts * image_count
    table_places = lax.axis_index("rows") * table_rows + jnp.arange(table_rows, dtype=jnp.int32)
    bucket_hot = (
        ids_all[:, :slot_count].reshape(every_slot)[:, None] == table_places[None, :]
    ).astype(jnp.bfloat16)
    label_hot = (
        ids_all[:, slot_count:].reshape(every_slot)[:, None] == table_places[None, :]
    ).astype(jnp.bfloat16)
    condition = lax.psum(
        jnp.dot(bucket_hot, time_table, preferred_element_type=jnp.float32)
        + jnp.dot(label_hot, class_table, preferred_element_type=jnp.float32),
        "rows",
    )
    silu_value, silu_pull = jax.vjp(silu_plain, condition)
    silu_low = silu_value.astype(jnp.bfloat16)
    mods_part = jnp.dot(silu_low, w_ada, preferred_element_type=jnp.float32)
    mods_cols = lax.psum(mods_part, "heads").reshape(row_parts, image_count, ada_width)
    mods_own = lax.all_to_all(mods_cols, "rows", split_axis=0, concat_axis=0, tiled=True)
    mods_all = mods_own.transpose(1, 0, 2).reshape(
        image_count, row_parts * ada_width
    ) + b_ada.astype(jnp.float32)
    positions = member * tok_rows + jnp.arange(tok_rows, dtype=jnp.int32)
    own_segments = lax.dynamic_slice_in_dim(
        segment_ids.reshape(seq_count * seq_len), member * tok_rows, tok_rows
    )
    token_image = positions // seq_len * slot_count + own_segments
    token_hot = (token_image[:, None] == jnp.arange(image_count, dtype=jnp.int32)[None, :]).astype(
        jnp.float32
    )
    token_mods = [
        jnp.dot(
            token_hot,
            mods_all[:, part_index * model_width : (part_index + 1) * model_width],
            precision=HIGH,
        )
        for part_index in range(6)
    ]
    shift_attn, scale_attn, gate_attn, shift_mlp, scale_mlp, gate_mlp = token_mods
    inputs = patches.astype(jnp.float32)
    first_value, first_pull = jax.vjp(modulate, inputs, shift_attn, scale_attn)
    hidden_one = first_value.astype(jnp.bfloat16)
    rows_one = lax.all_gather(hidden_one, "heads", axis=0, tiled=True)
    zero_bias = jnp.zeros((head_local, head_size), b_qv.dtype)
    qkv_bias = (
        jnp.concatenate([b_qv[:, :head_size], zero_bias, b_qv[:, head_size:]], axis=1)
        .reshape(head_local * 3 * head_size)
        .astype(jnp.float32)
    )
    projected = (jnp.dot(rows_one, qkv_cols, preferred_element_type=jnp.float32) + qkv_bias).astype(
        jnp.bfloat16
    )
    seq_qkv = projected.reshape(seq_count, seq_len, head_local, 3, head_size)
    slot_ends = jnp.cumsum(image_lengths, axis=1)
    places = jnp.arange(seq_len, dtype=jnp.int32)
    image_of = jnp.sum((places[None, :, None] >= slot_ends[:, None, :]).astype(jnp.int32), axis=2)

    def block_scores(query_rows, key_rows, image_rows, image_cols):
        scores = (
            jnp.einsum("qhd,khd->hqk", query_rows, key_rows, preferred_element_type=jnp.float32)
            * scale_factor
        )
        return jnp.where((image_rows[:, None] == image_cols[None, :])[None], scores, MASKED)

    def attend_forward(pieces):
        seq_block, seq_image = pieces
        key_rows = seq_block[:, :, 1]
        value_rows = seq_block[:, :, 2]
        outputs = []
        totals = []
        for row_start in range(0, seq_len, block_rows):
            stop_row = row_start + block_rows
            query_rows = seq_block[row_start:stop_row, :, 0]
            scores = block_scores(query_rows, key_rows, seq_image[row_start:stop_row], seq_image)
            row_peak = jnp.max(scores, axis=2, keepdims=True)
            raised = jnp.exp(scores - row_peak)
            row_total = jnp.sum(raised, axis=2, keepdims=True)
            soft_low = (raised / row_total).astype(jnp.bfloat16)
            outputs.append(
                jnp.einsum(
                    "hqk,khd->qhd", soft_low, value_rows, preferred_element_type=jnp.float32
                ).astype(jnp.bfloat16)
            )
            totals.append((row_peak + jnp.log(row_total))[:, :, 0])
        return (jnp.concatenate(outputs, axis=0), jnp.concatenate(totals, axis=1))

    mixed, log_totals = lax.map(attend_forward, (seq_qkv, image_of))
    mixed_rows = mixed.reshape(group_rows, head_local * head_size)
    attn_out = lax.psum_scatter(
        times_transposed(
            lax.slice_in_dim(mixed_rows, 0, tok_rows * lax.axis_size("heads"), axis=0), out_cols
        ).astype(jnp.bfloat16),
        "heads",
        scatter_dimension=0,
        tiled=True,
    ).astype(jnp.float32) + b_out.astype(jnp.float32)
    after_attn = inputs + gate_attn * attn_out
    second_value, second_pull = jax.vjp(modulate, after_attn, shift_mlp, scale_mlp)
    hidden_two = second_value.astype(jnp.bfloat16)
    rows_two = lax.all_gather(hidden_two, "heads", axis=0, tiled=True)
    inner = jnp.dot(rows_two, fc1_cols, preferred_element_type=jnp.float32) + b_fc1.astype(
        jnp.float32
    )
    gelu_value, gelu_pull = jax.vjp(gelu_tanh, inner)
    active = gelu_value.astype(jnp.bfloat16)
    ffn_out = lax.psum_scatter(
        times_transposed(
            lax.slice_in_dim(active, 0, tok_rows * lax.axis_size("heads"), axis=0), fc2_cols
        ).astype(jnp.bfloat16),
        "heads",
        scatter_dimension=0,
        tiled=True,
    ).astype(jnp.float32) + b_fc2.astype(jnp.float32)
    block_out = (after_attn + gate_mlp * ffn_out).astype(jnp.bfloat16)
    upstream = cotangent.astype(jnp.float32)
    grad_ffn = (gate_mlp * upstream).astype(jnp.bfloat16)
    ffn_rows = lax.all_gather(grad_ffn, "heads", axis=0, tiled=True)
    grad_w_fc2 = contract_rows(ffn_rows, active)
    grad_b_fc2 = jnp.sum(ffn_rows, axis=0, dtype=jnp.float32)
    grad_active = jnp.dot(ffn_rows, fc2_cols, preferred_element_type=jnp.float32)
    grad_inner = gelu_pull(grad_active)[0].astype(jnp.bfloat16)
    grad_w_fc1 = contract_rows(rows_two, grad_inner)
    grad_b_fc1 = jnp.sum(grad_inner, axis=0, dtype=jnp.float32)
    grad_hidden_two = lax.psum_scatter(
        times_transposed(
            lax.slice_in_dim(grad_inner, 0, tok_rows * lax.axis_size("heads"), axis=0), fc1_cols
        ).astype(jnp.bfloat16),
        "heads",
        scatter_dimension=0,
        tiled=True,
    ).astype(jnp.float32)
    grad_after, grad_shift_mlp, grad_scale_mlp = second_pull(grad_hidden_two)
    grad_after = grad_after + upstream
    grad_gate_mlp = upstream * ffn_out
    grad_gate_attn = grad_after * attn_out
    grad_attn = (gate_attn * grad_after).astype(jnp.bfloat16)
    attn_rows_grad = lax.all_gather(grad_attn, "heads", axis=0, tiled=True)
    grad_w_out = contract_rows(attn_rows_grad, mixed_rows)
    grad_b_out = jnp.sum(attn_rows_grad, axis=0, dtype=jnp.float32)
    grad_mixed = jnp.dot(attn_rows_grad, out_cols, preferred_element_type=jnp.float32).astype(
        jnp.bfloat16
    )
    grad_seq = grad_mixed.reshape(seq_count, seq_len, head_local, head_size)

    def attend_backward(pieces):
        seq_block, seq_image, seq_grad, seq_totals = pieces
        key_rows = seq_block[:, :, 1]
        value_rows = seq_block[:, :, 2]
        grad_keys = jnp.zeros(key_rows.shape, jnp.float32)
        grad_values = jnp.zeros(value_rows.shape, jnp.float32)
        grad_queries = []
        for row_start in range(0, seq_len, block_rows):
            stop_row = row_start + block_rows
            query_rows = seq_block[row_start:stop_row, :, 0]
            grad_rows = seq_grad[row_start:stop_row]
            scores = block_scores(query_rows, key_rows, seq_image[row_start:stop_row], seq_image)
            soft_probs = jnp.exp(scores - seq_totals[:, row_start:stop_row, None])
            grad_probs = jnp.einsum(
                "qhd,khd->hqk", grad_rows, value_rows, preferred_element_type=jnp.float32
            )
            inner_sum = jnp.sum(soft_probs * grad_probs, axis=2, keepdims=True)
            grad_scores = (soft_probs * (grad_probs - inner_sum)).astype(jnp.bfloat16)
            grad_queries.append(
                jnp.einsum(
                    "hqk,khd->qhd", grad_scores, key_rows, preferred_element_type=jnp.float32
                )
                * scale_factor
            )
            grad_keys = (
                grad_keys
                + jnp.einsum(
                    "hqk,qhd->khd", grad_scores, query_rows, preferred_element_type=jnp.float32
                )
                * scale_factor
            )
            grad_values = grad_values + jnp.einsum(
                "hqk,qhd->khd",
                soft_probs.astype(jnp.bfloat16),
                grad_rows,
                preferred_element_type=jnp.float32,
            )
        stacked = jnp.stack([jnp.concatenate(grad_queries, axis=0), grad_keys, grad_values], axis=2)
        return stacked.astype(jnp.bfloat16)

    grad_qkv = lax.map(attend_backward, (seq_qkv, image_of, grad_seq, log_totals)).reshape(
        group_rows, head_local * 3 * head_size
    )
    grad_w_qkv = contract_rows(rows_one, grad_qkv)
    bias_terms = jnp.sum(grad_qkv, axis=0, dtype=jnp.float32).reshape(head_local, 3, head_size)
    grad_b_qv = jnp.concatenate([bias_terms[:, 0], bias_terms[:, 2]], axis=1)
    grad_hidden_one = lax.psum_scatter(
        times_transposed(
            lax.slice_in_dim(grad_qkv, 0, tok_rows * lax.axis_size("heads"), axis=0), qkv_cols
        ).astype(jnp.bfloat16),
        "heads",
        scatter_dimension=0,
        tiled=True,
    ).astype(jnp.float32)
    grad_inputs, grad_shift_attn, grad_scale_attn = first_pull(grad_hidden_one)
    grad_patches = grad_inputs + grad_after
    token_grads = (
        grad_shift_attn,
        grad_scale_attn,
        grad_gate_attn,
        grad_shift_mlp,
        grad_scale_mlp,
        grad_gate_mlp,
    )
    mods_grad_part = jnp.concatenate(
        [contract_rows_exact(token_hot, grad_term) for grad_term in token_grads], axis=1
    )
    grad_mods = lax.psum(mods_grad_part.astype(jnp.bfloat16), "heads")
    grad_cols = lax.all_to_all(
        grad_mods.reshape(image_count, row_parts, ada_width).transpose(1, 0, 2),
        "rows",
        split_axis=0,
        concat_axis=0,
        tiled=True,
    ).reshape(every_slot, ada_width)
    grad_w_ada = contract_rows(silu_low, grad_cols)
    grad_b_ada = jnp.sum(grad_cols, axis=0, dtype=jnp.float32)
    grad_silu = lax.psum(times_transposed(grad_cols, w_ada), "rows")
    grad_condition = silu_pull(grad_silu)[0]
    grad_time = contract_rows_exact(bucket_hot.astype(jnp.float32), grad_condition)
    grad_class = contract_rows_exact(label_hot.astype(jnp.float32), grad_condition)

    def row_reduced(partial):
        return lax.psum_scatter(
            partial.astype(jnp.bfloat16), "rows", scatter_dimension=0, tiled=True
        ).astype(jnp.float32)

    grad_w_qkv, grad_w_out, grad_w_fc1, grad_w_fc2 = (
        row_reduced(grad_w_qkv),
        row_reduced(grad_w_out),
        row_reduced(grad_w_fc1),
        row_reduced(grad_w_fc2),
    )
    bias_sizes = (grad_b_qv.size, grad_b_fc1.size, grad_b_out.size, grad_b_fc2.size)
    bias_all = lax.psum(
        jnp.concatenate([grad_b_qv.reshape(-1), grad_b_fc1, grad_b_out, grad_b_fc2]), "rows"
    )
    edges = [sum(bias_sizes[:step]) for step in range(5)]
    bias_rows = model_width // row_parts
    row_start = lax.axis_index("rows") * bias_rows
    grad_b_qv = bias_all[edges[0] : edges[1]].reshape(grad_b_qv.shape)
    grad_b_fc1 = bias_all[edges[1] : edges[2]]
    grad_b_out = lax.dynamic_slice_in_dim(bias_all[edges[2] : edges[3]], row_start, bias_rows)
    grad_b_fc2 = lax.dynamic_slice_in_dim(bias_all[edges[3] : edges[4]], row_start, bias_rows)
    return (
        block_out,
        grad_patches,
        grad_time,
        grad_class,
        grad_w_ada,
        grad_b_ada,
        grad_w_qkv,
        grad_b_qv,
        grad_w_out,
        grad_b_out,
        grad_w_fc1,
        grad_b_fc1,
        grad_w_fc2,
        grad_b_fc2,
    )


def solution(mesh):
    placed = (
        P(("rows", "heads"), None),
        P("rows", "heads"),
        P("rows", "heads"),
        P("heads", "rows"),
        P(),
        P("rows", "heads"),
        P("heads", None),
        P("rows", "heads"),
        P(),
        P("rows", "heads"),
        P("heads"),
        P("rows", "heads"),
        P(),
        P("rows", None),
        P("rows", None),
        P("rows", None),
        P("rows", None),
        P(("rows", "heads"), None),
    )
    return jax.shard_map(
        shards,
        mesh=mesh,
        in_specs=placed,
        out_specs=(
            P(("rows", "heads"), None),
            P(("rows", "heads"), None),
            P("rows", "heads"),
            P("rows", "heads"),
            P("heads", "rows"),
            P("rows"),
            P("rows", "heads"),
            P("heads", None),
            P("rows", "heads"),
            P("rows"),
            P("rows", "heads"),
            P("heads"),
            P("rows", "heads"),
            P("rows"),
        ),
        check_vma=False,
    )
```

```python
import functools
import math

import jax
import jax.numpy as jnp
from jax import lax
from jax.experimental import pallas as pl
from jax.experimental.pallas import tpu as pltpu
from jax.sharding import PartitionSpec as P

EPSILON = 1e-06
MASKED = -1e30
HIGH = lax.Precision.HIGHEST
TANH_COEFF = 0.7978845608028654
BLOCK_LIMIT = 512


def layer_norm(values):
    average = jnp.mean(values, axis=-1, keepdims=True)
    centred = values - average
    variance = jnp.mean(centred * centred, axis=-1, keepdims=True)
    return centred * lax.rsqrt(variance + EPSILON)


def gelu_tanh(values):
    return (
        0.5 * values * (1.0 + jnp.tanh(TANH_COEFF * (values + 0.044715 * values * values * values)))
    )


def silu_plain(values):
    return values / (1.0 + jnp.exp(-values))


def modulate(values, shift_term, scale_term):
    return layer_norm(values) * (1.0 + scale_term) + shift_term


def contract_rows(left_matrix, right_matrix):
    return lax.dot_general(
        left_matrix, right_matrix, (((0,), (0,)), ((), ())), preferred_element_type=jnp.float32
    )


def contract_rows_exact(left_matrix, right_matrix):
    return lax.dot_general(
        left_matrix,
        right_matrix,
        (((0,), (0,)), ((), ())),
        precision=HIGH,
        preferred_element_type=jnp.float32,
    )


def times_transposed(left_matrix, right_matrix):
    return lax.dot_general(
        left_matrix, right_matrix, (((1,), (1,)), ((), ())), preferred_element_type=jnp.float32
    )


def gather_weights(w_qkv, w_out, w_fc1, w_fc2):
    return (
        lax.all_gather(w_qkv, "rows", axis=0, tiled=True),
        lax.all_gather(w_out, "rows", axis=0, tiled=True),
        lax.all_gather(w_fc1, "rows", axis=0, tiled=True),
        lax.all_gather(w_fc2, "rows", axis=0, tiled=True),
    )


def shards_plain(
    patches,
    time_table,
    class_table,
    w_ada,
    b_ada,
    w_qkv,
    b_qv,
    w_out,
    b_out,
    w_fc1,
    b_fc1,
    w_fc2,
    b_fc2,
    image_lengths,
    segment_ids,
    bucket_ids,
    class_labels,
    cotangent,
):
    head_parts = lax.axis_size("heads")
    member = lax.axis_index("heads")
    tok_rows = patches.shape[0]
    model_width = patches.shape[1]
    seq_count = segment_ids.shape[0]
    seq_len = segment_ids.shape[1]
    slot_count = image_lengths.shape[1]
    image_count = seq_count * slot_count
    group_rows = tok_rows * head_parts
    head_local = b_qv.shape[0]
    head_size = b_qv.shape[1] // 2
    block_rows = min(BLOCK_LIMIT, seq_len)
    scale_factor = 1.0 / math.sqrt(head_size)
    row_parts = lax.axis_size("rows")
    table_rows = time_table.shape[0]
    ada_width = w_ada.shape[1]
    qkv_cols, out_cols, fc1_cols, fc2_cols = gather_weights(w_qkv, w_out, w_fc1, w_fc2)
    ids_all = lax.all_gather(
        jnp.concatenate([bucket_ids, class_labels], axis=1), "rows", axis=0, tiled=True
    )
    every_slot = row_parts * image_count
    table_places = lax.axis_index("rows") * table_rows + jnp.arange(table_rows, dtype=jnp.int32)
    bucket_hot = (
        ids_all[:, :slot_count].reshape(every_slot)[:, None] == table_places[None, :]
    ).astype(jnp.bfloat16)
    label_hot = (
        ids_all[:, slot_count:].reshape(every_slot)[:, None] == table_places[None, :]
    ).astype(jnp.bfloat16)
    condition = lax.psum(
        jnp.dot(bucket_hot, time_table, preferred_element_type=jnp.float32)
        + jnp.dot(label_hot, class_table, preferred_element_type=jnp.float32),
        "rows",
    )
    silu_value, silu_pull = jax.vjp(silu_plain, condition)
    silu_low = silu_value.astype(jnp.bfloat16)
    mods_part = jnp.dot(silu_low, w_ada, preferred_element_type=jnp.float32)
    mods_cols = lax.psum(mods_part, "heads").reshape(row_parts, image_count, ada_width)
    mods_own = lax.all_to_all(mods_cols, "rows", split_axis=0, concat_axis=0, tiled=True)
    mods_all = mods_own.transpose(1, 0, 2).reshape(
        image_count, row_parts * ada_width
    ) + b_ada.astype(jnp.float32)
    positions = member * tok_rows + jnp.arange(tok_rows, dtype=jnp.int32)
    own_segments = lax.dynamic_slice_in_dim(
        segment_ids.reshape(seq_count * seq_len), member * tok_rows, tok_rows
    )
    token_image = positions // seq_len * slot_count + own_segments
    token_hot = (token_image[:, None] == jnp.arange(image_count, dtype=jnp.int32)[None, :]).astype(
        jnp.float32
    )
    token_mods = [
        jnp.dot(
            token_hot,
            mods_all[:, part_index * model_width : (part_index + 1) * model_width],
            precision=HIGH,
        )
        for part_index in range(6)
    ]
    shift_attn, scale_attn, gate_attn, shift_mlp, scale_mlp, gate_mlp = token_mods
    inputs = patches.astype(jnp.float32)
    first_value, first_pull = jax.vjp(modulate, inputs, shift_attn, scale_attn)
    hidden_one = first_value.astype(jnp.bfloat16)
    rows_one = lax.all_gather(hidden_one, "heads", axis=0, tiled=True)
    zero_bias = jnp.zeros((head_local, head_size), b_qv.dtype)
    qkv_bias = (
        jnp.concatenate([b_qv[:, :head_size], zero_bias, b_qv[:, head_size:]], axis=1)
        .reshape(head_local * 3 * head_size)
        .astype(jnp.float32)
    )
    projected = (jnp.dot(rows_one, qkv_cols, preferred_element_type=jnp.float32) + qkv_bias).astype(
        jnp.bfloat16
    )
    seq_qkv = projected.reshape(seq_count, seq_len, head_local, 3, head_size)
    slot_ends = jnp.cumsum(image_lengths, axis=1)
    places = jnp.arange(seq_len, dtype=jnp.int32)
    image_of = jnp.sum((places[None, :, None] >= slot_ends[:, None, :]).astype(jnp.int32), axis=2)

    def block_scores(query_rows, key_rows, image_rows, image_cols):
        scores = (
            jnp.einsum("qhd,khd->hqk", query_rows, key_rows, preferred_element_type=jnp.float32)
            * scale_factor
        )
        return jnp.where((image_rows[:, None] == image_cols[None, :])[None], scores, MASKED)

    def attend_forward(pieces):
        seq_block, seq_image = pieces
        key_rows = seq_block[:, :, 1]
        value_rows = seq_block[:, :, 2]
        outputs = []
        totals = []
        for row_start in range(0, seq_len, block_rows):
            stop_row = row_start + block_rows
            query_rows = seq_block[row_start:stop_row, :, 0]
            scores = block_scores(query_rows, key_rows, seq_image[row_start:stop_row], seq_image)
            row_peak = jnp.max(scores, axis=2, keepdims=True)
            raised = jnp.exp(scores - row_peak)
            row_total = jnp.sum(raised, axis=2, keepdims=True)
            soft_low = (raised / row_total).astype(jnp.bfloat16)
            outputs.append(
                jnp.einsum(
                    "hqk,khd->qhd", soft_low, value_rows, preferred_element_type=jnp.float32
                ).astype(jnp.bfloat16)
            )
            totals.append((row_peak + jnp.log(row_total))[:, :, 0])
        return (jnp.concatenate(outputs, axis=0), jnp.concatenate(totals, axis=1))

    mixed, log_totals = lax.map(attend_forward, (seq_qkv, image_of))
    mixed_rows = mixed.reshape(group_rows, head_local * head_size)
    attn_out = lax.psum_scatter(
        times_transposed(
            lax.slice_in_dim(mixed_rows, 0, tok_rows * lax.axis_size("heads"), axis=0), out_cols
        ).astype(jnp.bfloat16),
        "heads",
        scatter_dimension=0,
        tiled=True,
    ).astype(jnp.float32) + b_out.astype(jnp.float32)
    after_attn = inputs + gate_attn * attn_out
    second_value, second_pull = jax.vjp(modulate, after_attn, shift_mlp, scale_mlp)
    hidden_two = second_value.astype(jnp.bfloat16)
    rows_two = lax.all_gather(hidden_two, "heads", axis=0, tiled=True)
    inner = jnp.dot(rows_two, fc1_cols, preferred_element_type=jnp.float32) + b_fc1.astype(
        jnp.float32
    )
    gelu_value, gelu_pull = jax.vjp(gelu_tanh, inner)
    active = gelu_value.astype(jnp.bfloat16)
    ffn_out = lax.psum_scatter(
        times_transposed(
            lax.slice_in_dim(active, 0, tok_rows * lax.axis_size("heads"), axis=0), fc2_cols
        ).astype(jnp.bfloat16),
        "heads",
        scatter_dimension=0,
        tiled=True,
    ).astype(jnp.float32) + b_fc2.astype(jnp.float32)
    block_out = (after_attn + gate_mlp * ffn_out).astype(jnp.bfloat16)
    upstream = cotangent.astype(jnp.float32)
    grad_ffn = (gate_mlp * upstream).astype(jnp.bfloat16)
    ffn_rows = lax.all_gather(grad_ffn, "heads", axis=0, tiled=True)
    grad_w_fc2 = contract_rows(ffn_rows, active)
    grad_b_fc2 = jnp.sum(ffn_rows, axis=0, dtype=jnp.float32)
    grad_active = jnp.dot(ffn_rows, fc2_cols, preferred_element_type=jnp.float32)
    grad_inner = gelu_pull(grad_active)[0].astype(jnp.bfloat16)
    grad_w_fc1 = contract_rows(rows_two, grad_inner)
    grad_b_fc1 = jnp.sum(grad_inner, axis=0, dtype=jnp.float32)
    grad_hidden_two = lax.psum_scatter(
        times_transposed(
            lax.slice_in_dim(grad_inner, 0, tok_rows * lax.axis_size("heads"), axis=0), fc1_cols
        ).astype(jnp.bfloat16),
        "heads",
        scatter_dimension=0,
        tiled=True,
    ).astype(jnp.float32)
    grad_after, grad_shift_mlp, grad_scale_mlp = second_pull(grad_hidden_two)
    grad_after = grad_after + upstream
    grad_gate_mlp = upstream * ffn_out
    grad_gate_attn = grad_after * attn_out
    grad_attn = (gate_attn * grad_after).astype(jnp.bfloat16)
    attn_rows_grad = lax.all_gather(grad_attn, "heads", axis=0, tiled=True)
    grad_w_out = contract_rows(attn_rows_grad, mixed_rows)
    grad_b_out = jnp.sum(attn_rows_grad, axis=0, dtype=jnp.float32)
    grad_mixed = jnp.dot(attn_rows_grad, out_cols, preferred_element_type=jnp.float32).astype(
        jnp.bfloat16
    )
    grad_seq = grad_mixed.reshape(seq_count, seq_len, head_local, head_size)

    def attend_backward(pieces):
        seq_block, seq_image, seq_grad, seq_totals = pieces
        key_rows = seq_block[:, :, 1]
        value_rows = seq_block[:, :, 2]
        grad_keys = jnp.zeros(key_rows.shape, jnp.float32)
        grad_values = jnp.zeros(value_rows.shape, jnp.float32)
        grad_queries = []
        for row_start in range(0, seq_len, block_rows):
            stop_row = row_start + block_rows
            query_rows = seq_block[row_start:stop_row, :, 0]
            grad_rows = seq_grad[row_start:stop_row]
            scores = block_scores(query_rows, key_rows, seq_image[row_start:stop_row], seq_image)
            soft_probs = jnp.exp(scores - seq_totals[:, row_start:stop_row, None])
            grad_probs = jnp.einsum(
                "qhd,khd->hqk", grad_rows, value_rows, preferred_element_type=jnp.float32
            )
            inner_sum = jnp.sum(soft_probs * grad_probs, axis=2, keepdims=True)
            grad_scores = (soft_probs * (grad_probs - inner_sum)).astype(jnp.bfloat16)
            grad_queries.append(
                jnp.einsum(
                    "hqk,khd->qhd", grad_scores, key_rows, preferred_element_type=jnp.float32
                )
                * scale_factor
            )
            grad_keys = (
                grad_keys
                + jnp.einsum(
                    "hqk,qhd->khd", grad_scores, query_rows, preferred_element_type=jnp.float32
                )
                * scale_factor
            )
            grad_values = grad_values + jnp.einsum(
                "hqk,qhd->khd",
                soft_probs.astype(jnp.bfloat16),
                grad_rows,
                preferred_element_type=jnp.float32,
            )
        stacked = jnp.stack([jnp.concatenate(grad_queries, axis=0), grad_keys, grad_values], axis=2)
        return stacked.astype(jnp.bfloat16)

    grad_qkv = lax.map(attend_backward, (seq_qkv, image_of, grad_seq, log_totals)).reshape(
        group_rows, head_local * 3 * head_size
    )
    grad_w_qkv = contract_rows(rows_one, grad_qkv)
    bias_terms = jnp.sum(grad_qkv, axis=0, dtype=jnp.float32).reshape(head_local, 3, head_size)
    grad_b_qv = jnp.concatenate([bias_terms[:, 0], bias_terms[:, 2]], axis=1)
    grad_hidden_one = lax.psum_scatter(
        times_transposed(
            lax.slice_in_dim(grad_qkv, 0, tok_rows * lax.axis_size("heads"), axis=0), qkv_cols
        ).astype(jnp.bfloat16),
        "heads",
        scatter_dimension=0,
        tiled=True,
    ).astype(jnp.float32)
    grad_inputs, grad_shift_attn, grad_scale_attn = first_pull(grad_hidden_one)
    grad_patches = grad_inputs + grad_after
    token_grads = (
        grad_shift_attn,
        grad_scale_attn,
        grad_gate_attn,
        grad_shift_mlp,
        grad_scale_mlp,
        grad_gate_mlp,
    )
    mods_grad_part = jnp.concatenate(
        [contract_rows_exact(token_hot, grad_term) for grad_term in token_grads], axis=1
    )
    grad_mods = lax.psum(mods_grad_part.astype(jnp.bfloat16), "heads")
    grad_cols = lax.all_to_all(
        grad_mods.reshape(image_count, row_parts, ada_width).transpose(1, 0, 2),
        "rows",
        split_axis=0,
        concat_axis=0,
        tiled=True,
    ).reshape(every_slot, ada_width)
    grad_w_ada = contract_rows(silu_low, grad_cols)
    grad_b_ada = jnp.sum(grad_cols, axis=0, dtype=jnp.float32)
    grad_silu = lax.psum(times_transposed(grad_cols, w_ada), "rows")
    grad_condition = silu_pull(grad_silu)[0]
    grad_time = contract_rows_exact(bucket_hot.astype(jnp.float32), grad_condition)
    grad_class = contract_rows_exact(label_hot.astype(jnp.float32), grad_condition)

    def row_reduced(partial):
        return lax.psum_scatter(
            partial.astype(jnp.bfloat16), "rows", scatter_dimension=0, tiled=True
        ).astype(jnp.float32)

    grad_w_qkv, grad_w_out, grad_w_fc1, grad_w_fc2 = (
        row_reduced(grad_w_qkv),
        row_reduced(grad_w_out),
        row_reduced(grad_w_fc1),
        row_reduced(grad_w_fc2),
    )
    bias_sizes = (grad_b_qv.size, grad_b_fc1.size, grad_b_out.size, grad_b_fc2.size)
    bias_all = lax.psum(
        jnp.concatenate([grad_b_qv.reshape(-1), grad_b_fc1, grad_b_out, grad_b_fc2]), "rows"
    )
    edges = [sum(bias_sizes[:step]) for step in range(5)]
    bias_rows = model_width // row_parts
    row_start = lax.axis_index("rows") * bias_rows
    grad_b_qv = bias_all[edges[0] : edges[1]].reshape(grad_b_qv.shape)
    grad_b_fc1 = bias_all[edges[1] : edges[2]]
    grad_b_out = lax.dynamic_slice_in_dim(bias_all[edges[2] : edges[3]], row_start, bias_rows)
    grad_b_fc2 = lax.dynamic_slice_in_dim(bias_all[edges[3] : edges[4]], row_start, bias_rows)
    return (
        block_out,
        grad_patches,
        grad_time,
        grad_class,
        grad_w_ada,
        grad_b_ada,
        grad_w_qkv,
        grad_b_qv,
        grad_w_out,
        grad_b_out,
        grad_w_fc1,
        grad_b_fc1,
        grad_w_fc2,
        grad_b_fc2,
    )


MESH = pl.DeviceIdType.MESH
ROW_PARTS = 8
HEAD_PARTS = 4
SLOT_ROWS = 8
VMEM_SPEC = pl.BlockSpec(memory_space=pltpu.VMEM)
ANY_SPEC = pl.BlockSpec(memory_space=pl.ANY)
DMA = pltpu.SemaphoreType.DMA
GRANT = 60 * 1024 * 1024


def places():
    row = lax.axis_index("rows")
    member = lax.axis_index("heads")
    sibling = member + 1 - 2 * lax.rem(member, 2)
    partner = lax.rem(member + 2, HEAD_PARTS)
    opposite = lax.rem(sibling + 2, HEAD_PARTS)
    return row, member, sibling, partner, opposite


def greet(row_steps, head_members):
    barrier = pltpu.get_barrier_semaphore()
    row = lax.axis_index("rows")
    for step in row_steps:
        pl.semaphore_signal(
            barrier,
            inc=1,
            device_id={"rows": lax.rem(row + step, ROW_PARTS)},
            device_id_type=MESH,
        )
    for other in head_members:
        pl.semaphore_signal(barrier, inc=1, device_id={"heads": other}, device_id_type=MESH)
    pl.semaphore_wait(barrier, len(row_steps) + len(head_members))


def to_row(source, target, send, recv, row):
    return pltpu.make_async_remote_copy(
        src_ref=source,
        dst_ref=target,
        send_sem=send,
        recv_sem=recv,
        device_id={"rows": row},
        device_id_type=MESH,
    )


def to_head(source, target, send, recv, member):
    return pltpu.make_async_remote_copy(
        src_ref=source,
        dst_ref=target,
        send_sem=send,
        recv_sem=recv,
        device_id={"heads": member},
        device_id_type=MESH,
    )


class RowGather:
    def __init__(self, shard, full, sends, recvs, local_sem, chunks):
        self.row = lax.axis_index("rows")
        self.level = self.row // 2
        self.side = lax.rem(self.row, 2)
        self.mate = self.row + 1 - 2 * self.side
        size = shard.shape[0] // chunks
        self.own = pltpu.make_async_copy(shard, full.at[self.row], local_sem)
        self.straight = []
        self.across = []
        for chunk in range(chunks):
            part = pl.ds(chunk * size, size)
            straight = []
            across = [
                to_row(
                    shard.at[part],
                    full.at[self.row, part],
                    sends.at[chunk, 3],
                    recvs.at[chunk, 3],
                    self.mate,
                )
            ]
            for step in range(1, 4):
                target = lax.rem(self.level + step, 4) * 2 + self.side
                origin = lax.rem(self.level + 4 - step, 4) * 2 + self.side
                straight.append(
                    to_row(
                        shard.at[part],
                        full.at[self.row, part],
                        sends.at[chunk, step - 1],
                        recvs.at[chunk, step - 1],
                        target,
                    )
                )
                across.append(
                    to_row(
                        full.at[origin, part],
                        full.at[origin, part],
                        sends.at[chunk, 3 + step],
                        recvs.at[chunk, 3 + step],
                        self.mate,
                    )
                )
            self.straight.append(straight)
            self.across.append(across)

    def start(self):
        self.own.start()
        for straight, across in zip(self.straight, self.across):
            for copy in straight:
                copy.start()
            across[0].start()

    def relay(self, chunk):
        for step in range(3):
            self.straight[chunk][step].wait_recv()
            self.across[chunk][1 + step].start()

    def finish(self):
        self.own.wait()
        for straight, across in zip(self.straight, self.across):
            for copy in straight:
                copy.wait_send()
            for copy in across:
                copy.wait()


class HeadGather:
    def __init__(self, block, full, sends, recvs, local_sem):
        row, member, sibling, partner, opposite = places()
        self.own = pltpu.make_async_copy(block, full.at[member], local_sem)
        self.beside = to_head(block, full.at[member], sends.at[0], recvs.at[0], sibling)
        self.across = to_head(block, full.at[member], sends.at[1], recvs.at[1], partner)
        self.onward = to_head(
            full.at[partner], full.at[partner], sends.at[2], recvs.at[2], sibling
        )

    def start(self):
        self.across.start()
        self.beside.start()
        self.own.start()

    def wait_sibling(self):
        self.beside.wait_recv()

    def wait_partner(self):
        self.across.wait_recv()
        self.onward.start()

    def wait_opposite(self):
        self.onward.wait_recv()

    def finish(self):
        self.own.wait()
        self.beside.wait_send()
        self.across.wait_send()
        self.onward.wait_send()


def front_kernel(
    ids_ref,
    time_ref,
    class_ref,
    ada_ref,
    patches_ref,
    qkv_ref,
    out_ref,
    qkv_full,
    out_full,
    patches_full,
    cond_all,
    mods_ref,
    ids_all,
    cond_part,
    cond_in,
    mods_part,
    mods_in,
    mods_sibling,
    mods_pair,
    mods_partner,
    small_send,
    small_recv,
    pair_send,
    pair_recv,
    head_send,
    head_recv,
    qkv_send,
    qkv_recv,
    out_send,
    out_recv,
    local_sems,
):
    row, member, sibling, partner, opposite = places()
    greet(range(1, ROW_PARTS), (sibling, partner))
    others = [(step, lax.rem(row + step, ROW_PARTS)) for step in range(1, ROW_PARTS)]

    def spread(stage, source_of, target):
        copies = []
        for step, other in others:
            copy = to_row(
                source_of(other),
                target.at[row],
                small_send.at[stage, step - 1],
                small_recv.at[stage, step - 1],
                other,
            )
            copy.start()
            copies.append(copy)
        return copies

    def settle(copies):
        for copy in copies:
            copy.wait()

    ids_copies = spread(0, lambda other: ids_ref, ids_all)
    gather_qkv = RowGather(qkv_ref, qkv_full, qkv_send, qkv_recv, local_sems.at[0], 3)
    gather_out = RowGather(out_ref, out_full, out_send, out_recv, local_sems.at[1], 1)
    gather_patches = HeadGather(patches_ref, patches_full, head_send, head_recv, local_sems.at[2])
    gather_qkv.start()
    gather_out.start()
    gather_patches.start()
    ids_all[row] = ids_ref[...]
    settle(ids_copies)
    table_rows = time_ref.shape[0]
    slots = ROW_PARTS * SLOT_ROWS
    table_places = row * table_rows + lax.broadcasted_iota(jnp.int32, (slots, table_rows), 1)
    bucket_hot = (
        ids_all[:, 0:SLOT_ROWS].reshape(slots, table_rows) == table_places
    ).astype(jnp.bfloat16)
    label_hot = (
        ids_all[:, SLOT_ROWS : 2 * SLOT_ROWS].reshape(slots, table_rows) == table_places
    ).astype(jnp.bfloat16)
    found = jnp.dot(bucket_hot, time_ref[...], preferred_element_type=jnp.float32) + jnp.dot(
        label_hot, class_ref[...], preferred_element_type=jnp.float32
    )
    cond_part[...] = found.reshape(cond_part.shape)
    copies = spread(1, lambda other: cond_part.at[other], cond_in)
    cond_in[row] = cond_part[row]
    settle(copies)
    condition = jnp.sum(cond_in[...], axis=0)
    cond_all[row] = condition
    cond_part[row] = condition
    copies = spread(2, lambda other: cond_part.at[row], cond_all)
    settle(copies)
    every = cond_all[...].reshape(slots, cond_all.shape[2])
    silu_low = (every / (1.0 + jnp.exp(-every))).astype(jnp.bfloat16)
    mods_part[...] = jnp.dot(
        silu_low, ada_ref[...], preferred_element_type=jnp.float32
    ).reshape(mods_part.shape)
    copies = spread(3, lambda other: mods_part.at[other], mods_in)
    mods_in[row] = mods_part[row]
    gather_qkv.relay(0)
    settle(copies)
    beside = to_head(mods_in, mods_sibling, pair_send.at[0], pair_recv.at[0], sibling)
    beside.start()
    gather_patches.wait_sibling()
    beside.wait()
    mods_pair[...] = mods_in[...] + mods_sibling[...]
    across = to_head(mods_pair, mods_partner, pair_send.at[1], pair_recv.at[1], partner)
    across.start()
    gather_patches.wait_partner()
    gather_qkv.relay(1)
    across.wait()
    mods_ref[...] = mods_pair[...] + mods_partner[...]
    gather_patches.wait_opposite()
    gather_qkv.relay(2)
    gather_out.relay(0)
    gather_patches.finish()
    gather_qkv.finish()
    gather_out.finish()


def front(ids, time_table, class_table, w_ada, patches, w_qkv, w_out):
    depth, ada_width = w_ada.shape
    shape = jax.ShapeDtypeStruct
    slotted = (ROW_PARTS, SLOT_ROWS)
    return pl.pallas_call(
        front_kernel,
        out_shape=(
            shape((ROW_PARTS,) + w_qkv.shape, jnp.bfloat16),
            shape((ROW_PARTS,) + w_out.shape, jnp.bfloat16),
            shape((HEAD_PARTS,) + patches.shape, jnp.bfloat16),
            shape(slotted + (depth,), jnp.float32),
            shape(slotted + (ada_width,), jnp.float32),
        ),
        in_specs=[VMEM_SPEC] * 7,
        out_specs=(ANY_SPEC, ANY_SPEC, ANY_SPEC, VMEM_SPEC, VMEM_SPEC),
        scratch_shapes=[
            pltpu.VMEM((ROW_PARTS,) + ids.shape, jnp.int32),
            pltpu.VMEM(slotted + (depth,), jnp.float32),
            pltpu.VMEM(slotted + (depth,), jnp.float32),
            pltpu.VMEM(slotted + (ada_width,), jnp.float32),
            pltpu.VMEM(slotted + (ada_width,), jnp.float32),
            pltpu.VMEM(slotted + (ada_width,), jnp.float32),
            pltpu.VMEM(slotted + (ada_width,), jnp.float32),
            pltpu.VMEM(slotted + (ada_width,), jnp.float32),
            DMA((4, 7)),
            DMA((4, 7)),
            DMA((2,)),
            DMA((2,)),
            DMA((3,)),
            DMA((3,)),
            DMA((3, 7)),
            DMA((3, 7)),
            DMA((1, 7)),
            DMA((1, 7)),
            DMA((3,)),
        ],
        compiler_params=pltpu.CompilerParams(
            collective_id=0, has_side_effects=True, vmem_limit_bytes=GRANT
        ),
        name="front",
    )(ids, time_table, class_table, w_ada, patches, w_qkv, w_out)


def shards_linked(
    patches,
    time_table,
    class_table,
    w_ada,
    b_ada,
    w_qkv,
    b_qv,
    w_out,
    b_out,
    w_fc1,
    b_fc1,
    w_fc2,
    b_fc2,
    image_lengths,
    segment_ids,
    bucket_ids,
    class_labels,
    cotangent,
):
    head_parts = lax.axis_size("heads")
    member = lax.axis_index("heads")
    tok_rows = patches.shape[0]
    model_width = patches.shape[1]
    seq_count = segment_ids.shape[0]
    seq_len = segment_ids.shape[1]
    slot_count = image_lengths.shape[1]
    image_count = seq_count * slot_count
    group_rows = tok_rows * head_parts
    head_local = b_qv.shape[0]
    head_size = b_qv.shape[1] // 2
    block_rows = min(BLOCK_LIMIT, seq_len)
    scale_factor = 1.0 / math.sqrt(head_size)
    row_parts = lax.axis_size("rows")
    table_rows = time_table.shape[0]
    ada_width = w_ada.shape[1]
    fc1_cols = lax.all_gather(w_fc1, "rows", axis=0, tiled=True)
    fc2_cols = lax.all_gather(w_fc2, "rows", axis=0, tiled=True)
    every_slot = row_parts * SLOT_ROWS
    slot_pad = jnp.full((SLOT_ROWS - slot_count,), -1, jnp.int32)
    ids = jnp.broadcast_to(
        jnp.concatenate([bucket_ids[0], slot_pad, class_labels[0], slot_pad])[:, None],
        (2 * SLOT_ROWS, table_rows),
    )
    qkv_full, out_full, patches_full, condition, mods = front(
        ids, time_table, class_table, w_ada, patches, w_qkv, w_out
    )
    qkv_cols = qkv_full.reshape(model_width, w_qkv.shape[1])
    out_cols = out_full.reshape(model_width, w_out.shape[1])
    condition = condition.reshape(every_slot, condition.shape[2])
    silu_value, silu_pull = jax.vjp(silu_plain, condition)
    silu_low = silu_value.astype(jnp.bfloat16)
    mods_all = mods[:, :slot_count].transpose(1, 0, 2).reshape(
        slot_count, row_parts * ada_width
    ) + b_ada.astype(jnp.float32)
    row_segments = segment_ids[0][:, None]

    def by_token(part_index, segments):
        vectors = mods_all[:, part_index * model_width : (part_index + 1) * model_width]
        chosen = vectors[slot_count - 1][None, :]
        for slot in range(slot_count - 2, -1, -1):
            chosen = jnp.where(segments == slot, vectors[slot][None, :], chosen)
        return chosen

    own_segments = lax.dynamic_slice_in_dim(segment_ids[0], member * tok_rows, tok_rows)[:, None]
    token_hot = (own_segments == jnp.arange(slot_count, dtype=jnp.int32)[None, :]).astype(
        jnp.float32
    )
    shift_attn, scale_attn, gate_attn, shift_mlp, scale_mlp, gate_mlp = (
        by_token(part_index, own_segments) for part_index in range(6)
    )
    inputs = patches.astype(jnp.float32)
    _, first_pull = jax.vjp(modulate, inputs, shift_attn, scale_attn)
    rows_one = modulate(
        patches_full.reshape(group_rows, model_width).astype(jnp.float32),
        by_token(0, row_segments),
        by_token(1, row_segments),
    ).astype(jnp.bfloat16)
    zero_bias = jnp.zeros((head_local, head_size), b_qv.dtype)
    qkv_bias = (
        jnp.concatenate([b_qv[:, :head_size], zero_bias, b_qv[:, head_size:]], axis=1)
        .reshape(head_local * 3 * head_size)
        .astype(jnp.float32)
    )
    projected = (jnp.dot(rows_one, qkv_cols, preferred_element_type=jnp.float32) + qkv_bias).astype(
        jnp.bfloat16
    )
    seq_qkv = projected.reshape(seq_count, seq_len, head_local, 3, head_size)
    slot_ends = jnp.cumsum(image_lengths, axis=1)
    places = jnp.arange(seq_len, dtype=jnp.int32)
    image_of = jnp.sum((places[None, :, None] >= slot_ends[:, None, :]).astype(jnp.int32), axis=2)

    def block_scores(query_rows, key_rows, image_rows, image_cols):
        scores = (
            jnp.einsum("qhd,khd->hqk", query_rows, key_rows, preferred_element_type=jnp.float32)
            * scale_factor
        )
        return jnp.where((image_rows[:, None] == image_cols[None, :])[None], scores, MASKED)

    def attend_forward(pieces):
        seq_block, seq_image = pieces
        key_rows = seq_block[:, :, 1]
        value_rows = seq_block[:, :, 2]
        outputs = []
        totals = []
        for row_start in range(0, seq_len, block_rows):
            stop_row = row_start + block_rows
            query_rows = seq_block[row_start:stop_row, :, 0]
            scores = block_scores(query_rows, key_rows, seq_image[row_start:stop_row], seq_image)
            row_peak = jnp.max(scores, axis=2, keepdims=True)
            raised = jnp.exp(scores - row_peak)
            row_total = jnp.sum(raised, axis=2, keepdims=True)
            soft_low = (raised / row_total).astype(jnp.bfloat16)
            outputs.append(
                jnp.einsum(
                    "hqk,khd->qhd", soft_low, value_rows, preferred_element_type=jnp.float32
                ).astype(jnp.bfloat16)
            )
            totals.append((row_peak + jnp.log(row_total))[:, :, 0])
        return (jnp.concatenate(outputs, axis=0), jnp.concatenate(totals, axis=1))

    mixed, log_totals = lax.map(attend_forward, (seq_qkv, image_of))
    mixed_rows = mixed.reshape(group_rows, head_local * head_size)
    attn_out = lax.psum_scatter(
        times_transposed(
            lax.slice_in_dim(mixed_rows, 0, tok_rows * lax.axis_size("heads"), axis=0), out_cols
        ).astype(jnp.bfloat16),
        "heads",
        scatter_dimension=0,
        tiled=True,
    ).astype(jnp.float32) + b_out.astype(jnp.float32)
    after_attn = inputs + gate_attn * attn_out
    second_value, second_pull = jax.vjp(modulate, after_attn, shift_mlp, scale_mlp)
    hidden_two = second_value.astype(jnp.bfloat16)
    rows_two = lax.all_gather(hidden_two, "heads", axis=0, tiled=True)
    inner = jnp.dot(rows_two, fc1_cols, preferred_element_type=jnp.float32) + b_fc1.astype(
        jnp.float32
    )
    gelu_value, gelu_pull = jax.vjp(gelu_tanh, inner)
    active = gelu_value.astype(jnp.bfloat16)
    ffn_out = lax.psum_scatter(
        times_transposed(
            lax.slice_in_dim(active, 0, tok_rows * lax.axis_size("heads"), axis=0), fc2_cols
        ).astype(jnp.bfloat16),
        "heads",
        scatter_dimension=0,
        tiled=True,
    ).astype(jnp.float32) + b_fc2.astype(jnp.float32)
    block_out = (after_attn + gate_mlp * ffn_out).astype(jnp.bfloat16)
    upstream = cotangent.astype(jnp.float32)
    grad_ffn = (gate_mlp * upstream).astype(jnp.bfloat16)
    ffn_rows = lax.all_gather(grad_ffn, "heads", axis=0, tiled=True)
    grad_w_fc2 = contract_rows(ffn_rows, active)
    grad_b_fc2 = jnp.sum(ffn_rows, axis=0, dtype=jnp.float32)
    grad_active = jnp.dot(ffn_rows, fc2_cols, preferred_element_type=jnp.float32)
    grad_inner = gelu_pull(grad_active)[0].astype(jnp.bfloat16)
    grad_w_fc1 = contract_rows(rows_two, grad_inner)
    grad_b_fc1 = jnp.sum(grad_inner, axis=0, dtype=jnp.float32)
    grad_hidden_two = lax.psum_scatter(
        times_transposed(
            lax.slice_in_dim(grad_inner, 0, tok_rows * lax.axis_size("heads"), axis=0), fc1_cols
        ).astype(jnp.bfloat16),
        "heads",
        scatter_dimension=0,
        tiled=True,
    ).astype(jnp.float32)
    grad_after, grad_shift_mlp, grad_scale_mlp = second_pull(grad_hidden_two)
    grad_after = grad_after + upstream
    grad_gate_mlp = upstream * ffn_out
    grad_gate_attn = grad_after * attn_out
    grad_attn = (gate_attn * grad_after).astype(jnp.bfloat16)
    attn_rows_grad = lax.all_gather(grad_attn, "heads", axis=0, tiled=True)
    grad_w_out = contract_rows(attn_rows_grad, mixed_rows)
    grad_b_out = jnp.sum(attn_rows_grad, axis=0, dtype=jnp.float32)
    grad_mixed = jnp.dot(attn_rows_grad, out_cols, preferred_element_type=jnp.float32).astype(
        jnp.bfloat16
    )
    grad_seq = grad_mixed.reshape(seq_count, seq_len, head_local, head_size)

    def attend_backward(pieces):
        seq_block, seq_image, seq_grad, seq_totals = pieces
        key_rows = seq_block[:, :, 1]
        value_rows = seq_block[:, :, 2]
        grad_keys = jnp.zeros(key_rows.shape, jnp.float32)
        grad_values = jnp.zeros(value_rows.shape, jnp.float32)
        grad_queries = []
        for row_start in range(0, seq_len, block_rows):
            stop_row = row_start + block_rows
            query_rows = seq_block[row_start:stop_row, :, 0]
            grad_rows = seq_grad[row_start:stop_row]
            scores = block_scores(query_rows, key_rows, seq_image[row_start:stop_row], seq_image)
            soft_probs = jnp.exp(scores - seq_totals[:, row_start:stop_row, None])
            grad_probs = jnp.einsum(
                "qhd,khd->hqk", grad_rows, value_rows, preferred_element_type=jnp.float32
            )
            inner_sum = jnp.sum(soft_probs * grad_probs, axis=2, keepdims=True)
            grad_scores = (soft_probs * (grad_probs - inner_sum)).astype(jnp.bfloat16)
            grad_queries.append(
                jnp.einsum(
                    "hqk,khd->qhd", grad_scores, key_rows, preferred_element_type=jnp.float32
                )
                * scale_factor
            )
            grad_keys = (
                grad_keys
                + jnp.einsum(
                    "hqk,qhd->khd", grad_scores, query_rows, preferred_element_type=jnp.float32
                )
                * scale_factor
            )
            grad_values = grad_values + jnp.einsum(
                "hqk,qhd->khd",
                soft_probs.astype(jnp.bfloat16),
                grad_rows,
                preferred_element_type=jnp.float32,
            )
        stacked = jnp.stack([jnp.concatenate(grad_queries, axis=0), grad_keys, grad_values], axis=2)
        return stacked.astype(jnp.bfloat16)

    grad_qkv = lax.map(attend_backward, (seq_qkv, image_of, grad_seq, log_totals)).reshape(
        group_rows, head_local * 3 * head_size
    )
    grad_w_qkv = contract_rows(rows_one, grad_qkv)
    bias_terms = jnp.sum(grad_qkv, axis=0, dtype=jnp.float32).reshape(head_local, 3, head_size)
    grad_b_qv = jnp.concatenate([bias_terms[:, 0], bias_terms[:, 2]], axis=1)
    grad_hidden_one = lax.psum_scatter(
        times_transposed(
            lax.slice_in_dim(grad_qkv, 0, tok_rows * lax.axis_size("heads"), axis=0), qkv_cols
        ).astype(jnp.bfloat16),
        "heads",
        scatter_dimension=0,
        tiled=True,
    ).astype(jnp.float32)
    grad_inputs, grad_shift_attn, grad_scale_attn = first_pull(grad_hidden_one)
    grad_patches = grad_inputs + grad_after
    token_grads = (
        grad_shift_attn,
        grad_scale_attn,
        grad_gate_attn,
        grad_shift_mlp,
        grad_scale_mlp,
        grad_gate_mlp,
    )
    mods_grad_part = jnp.concatenate(
        [contract_rows_exact(token_hot, grad_term) for grad_term in token_grads], axis=1
    )
    grad_mods = lax.psum(mods_grad_part.astype(jnp.bfloat16), "heads")
    grad_cols = lax.all_to_all(
        jnp.pad(
            grad_mods.reshape(slot_count, row_parts, ada_width).transpose(1, 0, 2),
            ((0, 0), (0, SLOT_ROWS - slot_count), (0, 0)),
        ),
        "rows",
        split_axis=0,
        concat_axis=0,
        tiled=True,
    ).reshape(every_slot, ada_width)
    grad_w_ada = contract_rows(silu_low, grad_cols)
    grad_b_ada = jnp.sum(grad_cols, axis=0, dtype=jnp.float32)
    grad_silu = lax.psum(times_transposed(grad_cols, w_ada), "rows")
    grad_condition = silu_pull(grad_silu)[0]
    ids_all = lax.all_gather(ids[:, 0], "rows", axis=0)
    table_places = lax.axis_index("rows") * table_rows + jnp.arange(table_rows, dtype=jnp.int32)
    bucket_hot = ids_all[:, :SLOT_ROWS].reshape(every_slot)[:, None] == table_places[None, :]
    label_hot = ids_all[:, SLOT_ROWS:].reshape(every_slot)[:, None] == table_places[None, :]
    grad_time = contract_rows_exact(bucket_hot.astype(jnp.float32), grad_condition)
    grad_class = contract_rows_exact(label_hot.astype(jnp.float32), grad_condition)

    def row_reduced(partial):
        return lax.psum_scatter(
            partial.astype(jnp.bfloat16), "rows", scatter_dimension=0, tiled=True
        ).astype(jnp.float32)

    grad_w_qkv, grad_w_out, grad_w_fc1, grad_w_fc2 = (
        row_reduced(grad_w_qkv),
        row_reduced(grad_w_out),
        row_reduced(grad_w_fc1),
        row_reduced(grad_w_fc2),
    )
    bias_sizes = (grad_b_qv.size, grad_b_fc1.size, grad_b_out.size, grad_b_fc2.size)
    bias_all = lax.psum(
        jnp.concatenate([grad_b_qv.reshape(-1), grad_b_fc1, grad_b_out, grad_b_fc2]), "rows"
    )
    edges = [sum(bias_sizes[:step]) for step in range(5)]
    bias_rows = model_width // row_parts
    row_start = lax.axis_index("rows") * bias_rows
    grad_b_qv = bias_all[edges[0] : edges[1]].reshape(grad_b_qv.shape)
    grad_b_fc1 = bias_all[edges[1] : edges[2]]
    grad_b_out = lax.dynamic_slice_in_dim(bias_all[edges[2] : edges[3]], row_start, bias_rows)
    grad_b_fc2 = lax.dynamic_slice_in_dim(bias_all[edges[3] : edges[4]], row_start, bias_rows)
    return (
        block_out,
        grad_patches,
        grad_time,
        grad_class,
        grad_w_ada,
        grad_b_ada,
        grad_w_qkv,
        grad_b_qv,
        grad_w_out,
        grad_b_out,
        grad_w_fc1,
        grad_b_fc1,
        grad_w_fc2,
        grad_b_fc2,
    )


def solution(mesh):
    placed = (
        P(("rows", "heads"), None),
        P("rows", "heads"),
        P("rows", "heads"),
        P("heads", "rows"),
        P(),
        P("rows", "heads"),
        P("heads", None),
        P("rows", "heads"),
        P(),
        P("rows", "heads"),
        P("heads"),
        P("rows", "heads"),
        P(),
        P("rows", None),
        P("rows", None),
        P("rows", None),
        P("rows", None),
        P(("rows", "heads"), None),
    )
    linked = mesh.shape["rows"] == ROW_PARTS and mesh.shape["heads"] == HEAD_PARTS
    return jax.shard_map(
        shards_linked if linked else shards_plain,
        mesh=mesh,
        in_specs=placed,
        out_specs=(
            P(("rows", "heads"), None),
            P(("rows", "heads"), None),
            P("rows", "heads"),
            P("rows", "heads"),
            P("heads", "rows"),
            P("rows"),
            P("rows", "heads"),
            P("heads", None),
            P("rows", "heads"),
            P("rows"),
            P("rows", "heads"),
            P("heads"),
            P("rows", "heads"),
            P("rows"),
        ),
        check_vma=False,
    )
```

```python
import functools
import math

import jax
import jax.numpy as jnp
from jax import lax
from jax.experimental import pallas as pl
from jax.experimental.pallas import tpu as pltpu
from jax.sharding import PartitionSpec as P

EPSILON = 1e-06
MASKED = -1e30
HIGH = lax.Precision.HIGHEST
TANH_COEFF = 0.7978845608028654
BLOCK_LIMIT = 512


def layer_norm(values):
    average = jnp.mean(values, axis=-1, keepdims=True)
    centred = values - average
    variance = jnp.mean(centred * centred, axis=-1, keepdims=True)
    return centred * lax.rsqrt(variance + EPSILON)


def gelu_tanh(values):
    return (
        0.5 * values * (1.0 + jnp.tanh(TANH_COEFF * (values + 0.044715 * values * values * values)))
    )


def silu_plain(values):
    return values / (1.0 + jnp.exp(-values))


def modulate(values, shift_term, scale_term):
    return layer_norm(values) * (1.0 + scale_term) + shift_term


def contract_rows(left_matrix, right_matrix):
    return lax.dot_general(
        left_matrix, right_matrix, (((0,), (0,)), ((), ())), preferred_element_type=jnp.float32
    )


def contract_rows_exact(left_matrix, right_matrix):
    return lax.dot_general(
        left_matrix,
        right_matrix,
        (((0,), (0,)), ((), ())),
        precision=HIGH,
        preferred_element_type=jnp.float32,
    )


def times_transposed(left_matrix, right_matrix):
    return lax.dot_general(
        left_matrix, right_matrix, (((1,), (1,)), ((), ())), preferred_element_type=jnp.float32
    )


def gather_weights(w_qkv, w_out, w_fc1, w_fc2):
    return (
        lax.all_gather(w_qkv, "rows", axis=0, tiled=True),
        lax.all_gather(w_out, "rows", axis=0, tiled=True),
        lax.all_gather(w_fc1, "rows", axis=0, tiled=True),
        lax.all_gather(w_fc2, "rows", axis=0, tiled=True),
    )


def shards_plain(
    patches,
    time_table,
    class_table,
    w_ada,
    b_ada,
    w_qkv,
    b_qv,
    w_out,
    b_out,
    w_fc1,
    b_fc1,
    w_fc2,
    b_fc2,
    image_lengths,
    segment_ids,
    bucket_ids,
    class_labels,
    cotangent,
):
    head_parts = lax.axis_size("heads")
    member = lax.axis_index("heads")
    tok_rows = patches.shape[0]
    model_width = patches.shape[1]
    seq_count = segment_ids.shape[0]
    seq_len = segment_ids.shape[1]
    slot_count = image_lengths.shape[1]
    image_count = seq_count * slot_count
    group_rows = tok_rows * head_parts
    head_local = b_qv.shape[0]
    head_size = b_qv.shape[1] // 2
    block_rows = min(BLOCK_LIMIT, seq_len)
    scale_factor = 1.0 / math.sqrt(head_size)
    row_parts = lax.axis_size("rows")
    table_rows = time_table.shape[0]
    ada_width = w_ada.shape[1]
    qkv_cols, out_cols, fc1_cols, fc2_cols = gather_weights(w_qkv, w_out, w_fc1, w_fc2)
    ids_all = lax.all_gather(
        jnp.concatenate([bucket_ids, class_labels], axis=1), "rows", axis=0, tiled=True
    )
    every_slot = row_parts * image_count
    table_places = lax.axis_index("rows") * table_rows + jnp.arange(table_rows, dtype=jnp.int32)
    bucket_hot = (
        ids_all[:, :slot_count].reshape(every_slot)[:, None] == table_places[None, :]
    ).astype(jnp.bfloat16)
    label_hot = (
        ids_all[:, slot_count:].reshape(every_slot)[:, None] == table_places[None, :]
    ).astype(jnp.bfloat16)
    condition = lax.psum(
        jnp.dot(bucket_hot, time_table, preferred_element_type=jnp.float32)
        + jnp.dot(label_hot, class_table, preferred_element_type=jnp.float32),
        "rows",
    )
    silu_value, silu_pull = jax.vjp(silu_plain, condition)
    silu_low = silu_value.astype(jnp.bfloat16)
    mods_part = jnp.dot(silu_low, w_ada, preferred_element_type=jnp.float32)
    mods_cols = lax.psum(mods_part, "heads").reshape(row_parts, image_count, ada_width)
    mods_own = lax.all_to_all(mods_cols, "rows", split_axis=0, concat_axis=0, tiled=True)
    mods_all = mods_own.transpose(1, 0, 2).reshape(
        image_count, row_parts * ada_width
    ) + b_ada.astype(jnp.float32)
    positions = member * tok_rows + jnp.arange(tok_rows, dtype=jnp.int32)
    own_segments = lax.dynamic_slice_in_dim(
        segment_ids.reshape(seq_count * seq_len), member * tok_rows, tok_rows
    )
    token_image = positions // seq_len * slot_count + own_segments
    token_hot = (token_image[:, None] == jnp.arange(image_count, dtype=jnp.int32)[None, :]).astype(
        jnp.float32
    )
    token_mods = [
        jnp.dot(
            token_hot,
            mods_all[:, part_index * model_width : (part_index + 1) * model_width],
            precision=HIGH,
        )
        for part_index in range(6)
    ]
    shift_attn, scale_attn, gate_attn, shift_mlp, scale_mlp, gate_mlp = token_mods
    inputs = patches.astype(jnp.float32)
    first_value, first_pull = jax.vjp(modulate, inputs, shift_attn, scale_attn)
    hidden_one = first_value.astype(jnp.bfloat16)
    rows_one = lax.all_gather(hidden_one, "heads", axis=0, tiled=True)
    zero_bias = jnp.zeros((head_local, head_size), b_qv.dtype)
    qkv_bias = (
        jnp.concatenate([b_qv[:, :head_size], zero_bias, b_qv[:, head_size:]], axis=1)
        .reshape(head_local * 3 * head_size)
        .astype(jnp.float32)
    )
    projected = (jnp.dot(rows_one, qkv_cols, preferred_element_type=jnp.float32) + qkv_bias).astype(
        jnp.bfloat16
    )
    seq_qkv = projected.reshape(seq_count, seq_len, head_local, 3, head_size)
    slot_ends = jnp.cumsum(image_lengths, axis=1)
    places = jnp.arange(seq_len, dtype=jnp.int32)
    image_of = jnp.sum((places[None, :, None] >= slot_ends[:, None, :]).astype(jnp.int32), axis=2)

    def block_scores(query_rows, key_rows, image_rows, image_cols):
        scores = (
            jnp.einsum("qhd,khd->hqk", query_rows, key_rows, preferred_element_type=jnp.float32)
            * scale_factor
        )
        return jnp.where((image_rows[:, None] == image_cols[None, :])[None], scores, MASKED)

    def attend_forward(pieces):
        seq_block, seq_image = pieces
        key_rows = seq_block[:, :, 1]
        value_rows = seq_block[:, :, 2]
        outputs = []
        totals = []
        for row_start in range(0, seq_len, block_rows):
            stop_row = row_start + block_rows
            query_rows = seq_block[row_start:stop_row, :, 0]
            scores = block_scores(query_rows, key_rows, seq_image[row_start:stop_row], seq_image)
            row_peak = jnp.max(scores, axis=2, keepdims=True)
            raised = jnp.exp(scores - row_peak)
            row_total = jnp.sum(raised, axis=2, keepdims=True)
            soft_low = (raised / row_total).astype(jnp.bfloat16)
            outputs.append(
                jnp.einsum(
                    "hqk,khd->qhd", soft_low, value_rows, preferred_element_type=jnp.float32
                ).astype(jnp.bfloat16)
            )
            totals.append((row_peak + jnp.log(row_total))[:, :, 0])
        return (jnp.concatenate(outputs, axis=0), jnp.concatenate(totals, axis=1))

    mixed, log_totals = lax.map(attend_forward, (seq_qkv, image_of))
    mixed_rows = mixed.reshape(group_rows, head_local * head_size)
    attn_out = lax.psum_scatter(
        times_transposed(
            lax.slice_in_dim(mixed_rows, 0, tok_rows * lax.axis_size("heads"), axis=0), out_cols
        ).astype(jnp.bfloat16),
        "heads",
        scatter_dimension=0,
        tiled=True,
    ).astype(jnp.float32) + b_out.astype(jnp.float32)
    after_attn = inputs + gate_attn * attn_out
    second_value, second_pull = jax.vjp(modulate, after_attn, shift_mlp, scale_mlp)
    hidden_two = second_value.astype(jnp.bfloat16)
    rows_two = lax.all_gather(hidden_two, "heads", axis=0, tiled=True)
    inner = jnp.dot(rows_two, fc1_cols, preferred_element_type=jnp.float32) + b_fc1.astype(
        jnp.float32
    )
    gelu_value, gelu_pull = jax.vjp(gelu_tanh, inner)
    active = gelu_value.astype(jnp.bfloat16)
    ffn_out = lax.psum_scatter(
        times_transposed(
            lax.slice_in_dim(active, 0, tok_rows * lax.axis_size("heads"), axis=0), fc2_cols
        ).astype(jnp.bfloat16),
        "heads",
        scatter_dimension=0,
        tiled=True,
    ).astype(jnp.float32) + b_fc2.astype(jnp.float32)
    block_out = (after_attn + gate_mlp * ffn_out).astype(jnp.bfloat16)
    upstream = cotangent.astype(jnp.float32)
    grad_ffn = (gate_mlp * upstream).astype(jnp.bfloat16)
    ffn_rows = lax.all_gather(grad_ffn, "heads", axis=0, tiled=True)
    grad_w_fc2 = contract_rows(ffn_rows, active)
    grad_b_fc2 = jnp.sum(ffn_rows, axis=0, dtype=jnp.float32)
    grad_active = jnp.dot(ffn_rows, fc2_cols, preferred_element_type=jnp.float32)
    grad_inner = gelu_pull(grad_active)[0].astype(jnp.bfloat16)
    grad_w_fc1 = contract_rows(rows_two, grad_inner)
    grad_b_fc1 = jnp.sum(grad_inner, axis=0, dtype=jnp.float32)
    grad_hidden_two = lax.psum_scatter(
        times_transposed(
            lax.slice_in_dim(grad_inner, 0, tok_rows * lax.axis_size("heads"), axis=0), fc1_cols
        ).astype(jnp.bfloat16),
        "heads",
        scatter_dimension=0,
        tiled=True,
    ).astype(jnp.float32)
    grad_after, grad_shift_mlp, grad_scale_mlp = second_pull(grad_hidden_two)
    grad_after = grad_after + upstream
    grad_gate_mlp = upstream * ffn_out
    grad_gate_attn = grad_after * attn_out
    grad_attn = (gate_attn * grad_after).astype(jnp.bfloat16)
    attn_rows_grad = lax.all_gather(grad_attn, "heads", axis=0, tiled=True)
    grad_w_out = contract_rows(attn_rows_grad, mixed_rows)
    grad_b_out = jnp.sum(attn_rows_grad, axis=0, dtype=jnp.float32)
    grad_mixed = jnp.dot(attn_rows_grad, out_cols, preferred_element_type=jnp.float32).astype(
        jnp.bfloat16
    )
    grad_seq = grad_mixed.reshape(seq_count, seq_len, head_local, head_size)

    def attend_backward(pieces):
        seq_block, seq_image, seq_grad, seq_totals = pieces
        key_rows = seq_block[:, :, 1]
        value_rows = seq_block[:, :, 2]
        grad_keys = jnp.zeros(key_rows.shape, jnp.float32)
        grad_values = jnp.zeros(value_rows.shape, jnp.float32)
        grad_queries = []
        for row_start in range(0, seq_len, block_rows):
            stop_row = row_start + block_rows
            query_rows = seq_block[row_start:stop_row, :, 0]
            grad_rows = seq_grad[row_start:stop_row]
            scores = block_scores(query_rows, key_rows, seq_image[row_start:stop_row], seq_image)
            soft_probs = jnp.exp(scores - seq_totals[:, row_start:stop_row, None])
            grad_probs = jnp.einsum(
                "qhd,khd->hqk", grad_rows, value_rows, preferred_element_type=jnp.float32
            )
            inner_sum = jnp.sum(soft_probs * grad_probs, axis=2, keepdims=True)
            grad_scores = (soft_probs * (grad_probs - inner_sum)).astype(jnp.bfloat16)
            grad_queries.append(
                jnp.einsum(
                    "hqk,khd->qhd", grad_scores, key_rows, preferred_element_type=jnp.float32
                )
                * scale_factor
            )
            grad_keys = (
                grad_keys
                + jnp.einsum(
                    "hqk,qhd->khd", grad_scores, query_rows, preferred_element_type=jnp.float32
                )
                * scale_factor
            )
            grad_values = grad_values + jnp.einsum(
                "hqk,qhd->khd",
                soft_probs.astype(jnp.bfloat16),
                grad_rows,
                preferred_element_type=jnp.float32,
            )
        stacked = jnp.stack([jnp.concatenate(grad_queries, axis=0), grad_keys, grad_values], axis=2)
        return stacked.astype(jnp.bfloat16)

    grad_qkv = lax.map(attend_backward, (seq_qkv, image_of, grad_seq, log_totals)).reshape(
        group_rows, head_local * 3 * head_size
    )
    grad_w_qkv = contract_rows(rows_one, grad_qkv)
    bias_terms = jnp.sum(grad_qkv, axis=0, dtype=jnp.float32).reshape(head_local, 3, head_size)
    grad_b_qv = jnp.concatenate([bias_terms[:, 0], bias_terms[:, 2]], axis=1)
    grad_hidden_one = lax.psum_scatter(
        times_transposed(
            lax.slice_in_dim(grad_qkv, 0, tok_rows * lax.axis_size("heads"), axis=0), qkv_cols
        ).astype(jnp.bfloat16),
        "heads",
        scatter_dimension=0,
        tiled=True,
    ).astype(jnp.float32)
    grad_inputs, grad_shift_attn, grad_scale_attn = first_pull(grad_hidden_one)
    grad_patches = grad_inputs + grad_after
    token_grads = (
        grad_shift_attn,
        grad_scale_attn,
        grad_gate_attn,
        grad_shift_mlp,
        grad_scale_mlp,
        grad_gate_mlp,
    )
    mods_grad_part = jnp.concatenate(
        [contract_rows_exact(token_hot, grad_term) for grad_term in token_grads], axis=1
    )
    grad_mods = lax.psum(mods_grad_part.astype(jnp.bfloat16), "heads")
    grad_cols = lax.all_to_all(
        grad_mods.reshape(image_count, row_parts, ada_width).transpose(1, 0, 2),
        "rows",
        split_axis=0,
        concat_axis=0,
        tiled=True,
    ).reshape(every_slot, ada_width)
    grad_w_ada = contract_rows(silu_low, grad_cols)
    grad_b_ada = jnp.sum(grad_cols, axis=0, dtype=jnp.float32)
    grad_silu = lax.psum(times_transposed(grad_cols, w_ada), "rows")
    grad_condition = silu_pull(grad_silu)[0]
    grad_time = contract_rows_exact(bucket_hot.astype(jnp.float32), grad_condition)
    grad_class = contract_rows_exact(label_hot.astype(jnp.float32), grad_condition)

    def row_reduced(partial):
        return lax.psum_scatter(
            partial.astype(jnp.bfloat16), "rows", scatter_dimension=0, tiled=True
        ).astype(jnp.float32)

    grad_w_qkv, grad_w_out, grad_w_fc1, grad_w_fc2 = (
        row_reduced(grad_w_qkv),
        row_reduced(grad_w_out),
        row_reduced(grad_w_fc1),
        row_reduced(grad_w_fc2),
    )
    bias_sizes = (grad_b_qv.size, grad_b_fc1.size, grad_b_out.size, grad_b_fc2.size)
    bias_all = lax.psum(
        jnp.concatenate([grad_b_qv.reshape(-1), grad_b_fc1, grad_b_out, grad_b_fc2]), "rows"
    )
    edges = [sum(bias_sizes[:step]) for step in range(5)]
    bias_rows = model_width // row_parts
    row_start = lax.axis_index("rows") * bias_rows
    grad_b_qv = bias_all[edges[0] : edges[1]].reshape(grad_b_qv.shape)
    grad_b_fc1 = bias_all[edges[1] : edges[2]]
    grad_b_out = lax.dynamic_slice_in_dim(bias_all[edges[2] : edges[3]], row_start, bias_rows)
    grad_b_fc2 = lax.dynamic_slice_in_dim(bias_all[edges[3] : edges[4]], row_start, bias_rows)
    return (
        block_out,
        grad_patches,
        grad_time,
        grad_class,
        grad_w_ada,
        grad_b_ada,
        grad_w_qkv,
        grad_b_qv,
        grad_w_out,
        grad_b_out,
        grad_w_fc1,
        grad_b_fc1,
        grad_w_fc2,
        grad_b_fc2,
    )


MESH = pl.DeviceIdType.MESH
ROW_PARTS = 8
HEAD_PARTS = 4
SLOT_ROWS = 8
VMEM_SPEC = pl.BlockSpec(memory_space=pltpu.VMEM)
ANY_SPEC = pl.BlockSpec(memory_space=pl.ANY)
DMA = pltpu.SemaphoreType.DMA
GRANT = 60 * 1024 * 1024


def places():
    row = lax.axis_index("rows")
    member = lax.axis_index("heads")
    sibling = member + 1 - 2 * lax.rem(member, 2)
    partner = lax.rem(member + 2, HEAD_PARTS)
    opposite = lax.rem(sibling + 2, HEAD_PARTS)
    return row, member, sibling, partner, opposite


def greet(row_steps, head_members):
    barrier = pltpu.get_barrier_semaphore()
    row = lax.axis_index("rows")
    for step in row_steps:
        pl.semaphore_signal(
            barrier,
            inc=1,
            device_id={"rows": lax.rem(row + step, ROW_PARTS)},
            device_id_type=MESH,
        )
    for other in head_members:
        pl.semaphore_signal(barrier, inc=1, device_id={"heads": other}, device_id_type=MESH)
    pl.semaphore_wait(barrier, len(row_steps) + len(head_members))


def to_row(source, target, send, recv, row):
    return pltpu.make_async_remote_copy(
        src_ref=source,
        dst_ref=target,
        send_sem=send,
        recv_sem=recv,
        device_id={"rows": row},
        device_id_type=MESH,
    )


def to_head(source, target, send, recv, member):
    return pltpu.make_async_remote_copy(
        src_ref=source,
        dst_ref=target,
        send_sem=send,
        recv_sem=recv,
        device_id={"heads": member},
        device_id_type=MESH,
    )


class RowGather:
    def __init__(self, shard, full, sends, recvs, local_sem, chunks):
        self.row = lax.axis_index("rows")
        self.level = self.row // 2
        self.side = lax.rem(self.row, 2)
        self.mate = self.row + 1 - 2 * self.side
        size = shard.shape[0] // chunks
        self.own = pltpu.make_async_copy(shard, full.at[self.row], local_sem)
        self.straight = []
        self.across = []
        for chunk in range(chunks):
            part = pl.ds(chunk * size, size)
            straight = []
            across = [
                to_row(
                    shard.at[part],
                    full.at[self.row, part],
                    sends.at[chunk, 3],
                    recvs.at[chunk, 3],
                    self.mate,
                )
            ]
            for step in range(1, 4):
                target = lax.rem(self.level + step, 4) * 2 + self.side
                origin = lax.rem(self.level + 4 - step, 4) * 2 + self.side
                straight.append(
                    to_row(
                        shard.at[part],
                        full.at[self.row, part],
                        sends.at[chunk, step - 1],
                        recvs.at[chunk, step - 1],
                        target,
                    )
                )
                across.append(
                    to_row(
                        full.at[origin, part],
                        full.at[origin, part],
                        sends.at[chunk, 3 + step],
                        recvs.at[chunk, 3 + step],
                        self.mate,
                    )
                )
            self.straight.append(straight)
            self.across.append(across)

    def start(self):
        self.own.start()
        for straight, across in zip(self.straight, self.across):
            for copy in straight:
                copy.start()
            across[0].start()

    def relay(self, chunk):
        for step in range(3):
            self.straight[chunk][step].wait_recv()
            self.across[chunk][1 + step].start()

    def finish(self):
        self.own.wait()
        for straight, across in zip(self.straight, self.across):
            for copy in straight:
                copy.wait_send()
            for copy in across:
                copy.wait()


class HeadGather:
    def __init__(self, block, full, sends, recvs, local_sem):
        row, member, sibling, partner, opposite = places()
        self.own = pltpu.make_async_copy(block, full.at[member], local_sem)
        self.beside = to_head(block, full.at[member], sends.at[0], recvs.at[0], sibling)
        self.across = to_head(block, full.at[member], sends.at[1], recvs.at[1], partner)
        self.onward = to_head(
            full.at[partner], full.at[partner], sends.at[2], recvs.at[2], sibling
        )

    def start(self):
        self.across.start()
        self.beside.start()
        self.own.start()

    def wait_sibling(self):
        self.beside.wait_recv()

    def wait_partner(self):
        self.across.wait_recv()
        self.onward.start()

    def wait_opposite(self):
        self.onward.wait_recv()

    def finish(self):
        self.own.wait()
        self.beside.wait_send()
        self.across.wait_send()
        self.onward.wait_send()


def front_kernel(
    ids_ref,
    time_ref,
    class_ref,
    ada_ref,
    patches_ref,
    qkv_ref,
    out_ref,
    qkv_full,
    out_full,
    patches_full,
    cond_all,
    mods_ref,
    ids_all,
    cond_part,
    cond_in,
    mods_part,
    mods_in,
    mods_sibling,
    mods_pair,
    mods_partner,
    small_send,
    small_recv,
    pair_send,
    pair_recv,
    head_send,
    head_recv,
    qkv_send,
    qkv_recv,
    out_send,
    out_recv,
    local_sems,
):
    row, member, sibling, partner, opposite = places()
    greet(range(1, ROW_PARTS), (sibling, partner))
    others = [(step, lax.rem(row + step, ROW_PARTS)) for step in range(1, ROW_PARTS)]

    def spread(stage, source_of, target):
        copies = []
        for step, other in others:
            copy = to_row(
                source_of(other),
                target.at[row],
                small_send.at[stage, step - 1],
                small_recv.at[stage, step - 1],
                other,
            )
            copy.start()
            copies.append(copy)
        return copies

    def settle(copies):
        for copy in copies:
            copy.wait()

    ids_copies = spread(0, lambda other: ids_ref, ids_all)
    gather_qkv = RowGather(qkv_ref, qkv_full, qkv_send, qkv_recv, local_sems.at[0], 3)
    gather_out = RowGather(out_ref, out_full, out_send, out_recv, local_sems.at[1], 1)
    gather_patches = HeadGather(patches_ref, patches_full, head_send, head_recv, local_sems.at[2])
    gather_qkv.start()
    gather_out.start()
    gather_patches.start()
    ids_all[row] = ids_ref[...]
    settle(ids_copies)
    table_rows = time_ref.shape[0]
    slots = ROW_PARTS * SLOT_ROWS
    table_places = row * table_rows + lax.broadcasted_iota(jnp.int32, (slots, table_rows), 1)
    bucket_hot = (
        ids_all[:, 0:SLOT_ROWS].reshape(slots, table_rows) == table_places
    ).astype(jnp.bfloat16)
    label_hot = (
        ids_all[:, SLOT_ROWS : 2 * SLOT_ROWS].reshape(slots, table_rows) == table_places
    ).astype(jnp.bfloat16)
    found = jnp.dot(bucket_hot, time_ref[...], preferred_element_type=jnp.float32) + jnp.dot(
        label_hot, class_ref[...], preferred_element_type=jnp.float32
    )
    cond_part[...] = found.reshape(cond_part.shape)
    copies = spread(1, lambda other: cond_part.at[other], cond_in)
    cond_in[row] = cond_part[row]
    settle(copies)
    condition = jnp.sum(cond_in[...], axis=0)
    cond_all[row] = condition
    cond_part[row] = condition
    copies = spread(2, lambda other: cond_part.at[row], cond_all)
    settle(copies)
    every = cond_all[...].reshape(slots, cond_all.shape[2])
    silu_low = (every / (1.0 + jnp.exp(-every))).astype(jnp.bfloat16)
    mods_part[...] = jnp.dot(
        silu_low, ada_ref[...], preferred_element_type=jnp.float32
    ).reshape(mods_part.shape)
    copies = spread(3, lambda other: mods_part.at[other], mods_in)
    mods_in[row] = mods_part[row]
    gather_qkv.relay(0)
    settle(copies)
    beside = to_head(mods_in, mods_sibling, pair_send.at[0], pair_recv.at[0], sibling)
    beside.start()
    gather_patches.wait_sibling()
    beside.wait()
    mods_pair[...] = mods_in[...] + mods_sibling[...]
    across = to_head(mods_pair, mods_partner, pair_send.at[1], pair_recv.at[1], partner)
    across.start()
    gather_patches.wait_partner()
    gather_qkv.relay(1)
    across.wait()
    mods_ref[...] = mods_pair[...] + mods_partner[...]
    gather_patches.wait_opposite()
    gather_qkv.relay(2)
    gather_out.relay(0)
    gather_patches.finish()
    gather_qkv.finish()
    gather_out.finish()


def front(ids, time_table, class_table, w_ada, patches, w_qkv, w_out):
    depth, ada_width = w_ada.shape
    shape = jax.ShapeDtypeStruct
    slotted = (ROW_PARTS, SLOT_ROWS)
    return pl.pallas_call(
        front_kernel,
        out_shape=(
            shape((ROW_PARTS,) + w_qkv.shape, jnp.bfloat16),
            shape((ROW_PARTS,) + w_out.shape, jnp.bfloat16),
            shape((HEAD_PARTS,) + patches.shape, jnp.bfloat16),
            shape(slotted + (depth,), jnp.float32),
            shape(slotted + (ada_width,), jnp.float32),
            shape((ROW_PARTS,) + ids.shape, jnp.int32),
        ),
        in_specs=[VMEM_SPEC] * 7,
        out_specs=(ANY_SPEC, ANY_SPEC, ANY_SPEC, VMEM_SPEC, VMEM_SPEC, VMEM_SPEC),
        scratch_shapes=[
            pltpu.VMEM(slotted + (depth,), jnp.float32),
            pltpu.VMEM(slotted + (depth,), jnp.float32),
            pltpu.VMEM(slotted + (ada_width,), jnp.float32),
            pltpu.VMEM(slotted + (ada_width,), jnp.float32),
            pltpu.VMEM(slotted + (ada_width,), jnp.float32),
            pltpu.VMEM(slotted + (ada_width,), jnp.float32),
            pltpu.VMEM(slotted + (ada_width,), jnp.float32),
            DMA((4, 7)),
            DMA((4, 7)),
            DMA((2,)),
            DMA((2,)),
            DMA((3,)),
            DMA((3,)),
            DMA((3, 7)),
            DMA((3, 7)),
            DMA((1, 7)),
            DMA((1, 7)),
            DMA((3,)),
        ],
        compiler_params=pltpu.CompilerParams(
            collective_id=0, has_side_effects=True, vmem_limit_bytes=GRANT
        ),
        name="front",
    )(ids, time_table, class_table, w_ada, patches, w_qkv, w_out)


class HeadReduce:
    def __init__(self, partial, beside_in, pair, across_in, sends, recvs):
        row, member, sibling, partner, opposite = places()
        self.member = member
        self.partner = partner
        self.partial = partial
        self.beside_in = beside_in
        self.pair = pair
        self.across_in = across_in
        self.first = to_head(
            partial.at[opposite], beside_in.at[1], sends.at[0], recvs.at[0], sibling
        )
        self.second = to_head(
            partial.at[sibling], beside_in.at[0], sends.at[1], recvs.at[1], sibling
        )
        self.across = to_head(pair, across_in, sends.at[2], recvs.at[2], partner)

    def start(self):
        self.first.start()
        self.second.start()

    def send_pair(self):
        self.first.wait_recv()
        self.pair[...] = (
            self.partial[self.partner].astype(jnp.float32)
            + self.beside_in[1].astype(jnp.float32)
        ).astype(jnp.bfloat16)
        self.across.start()

    def settle(self):
        self.second.wait_recv()
        self.across.wait_recv()

    def rows(self, part):
        return (
            self.partial[self.member, part].astype(jnp.float32)
            + self.beside_in[0, part].astype(jnp.float32)
            + self.across_in[part].astype(jnp.float32)
        )

    def finish(self):
        self.first.wait_send()
        self.second.wait_send()
        self.across.wait_send()


class RowReduce:
    def __init__(self, partial, mate_in, pair, straight_in, total, part, sends, recvs):
        row = lax.axis_index("rows")
        self.level = row // 2
        self.side = lax.rem(row, 2)
        mate = row + 1 - 2 * self.side
        self.partial = partial
        self.mate_in = mate_in
        self.pair = pair
        self.straight_in = straight_in
        self.total = total
        self.part = part
        self.beside = to_row(
            partial.at[:, 1 - self.side, part],
            mate_in.at[:, part],
            sends.at[0],
            recvs.at[0],
            mate,
        )
        self.straight = []
        for step in range(1, 4):
            target = lax.rem(self.level + step, 4)
            self.straight.append(
                to_row(
                    pair.at[target, part],
                    straight_in.at[step - 1, part],
                    sends.at[step],
                    recvs.at[step],
                    target * 2 + self.side,
                )
            )

    def start(self):
        self.beside.start()

    def send_pair(self):
        self.beside.wait_recv()

        def one(level, carry):
            self.pair[level, self.part] = (
                self.partial[level, self.side, self.part].astype(jnp.float32)
                + self.mate_in[level, self.part].astype(jnp.float32)
            ).astype(jnp.bfloat16)
            return carry

        lax.fori_loop(0, 4, one, 0)
        for copy in self.straight:
            copy.start()

    def finish(self):
        for copy in self.straight:
            copy.wait_recv()
        self.total[self.part] = (
            self.pair[self.level, self.part].astype(jnp.float32)
            + self.straight_in[0, self.part].astype(jnp.float32)
            + self.straight_in[1, self.part].astype(jnp.float32)
            + self.straight_in[2, self.part].astype(jnp.float32)
        )
        self.beside.wait_send()
        for copy in self.straight:
            copy.wait_send()


BACK_CHUNKS = (3, 3, 3, 1)


def back_kernel(
    hidden_ref,
    fc2_part,
    fc1_part,
    qkv_part,
    out_part,
    bias_ref,
    patches_ref,
    after_ref,
    scale_ref,
    hot_ref,
    sums_ref,
    silu_ref,
    slope_ref,
    bucket_ref,
    label_ref,
    ada_ref,
    patches_grad,
    time_grad,
    class_grad,
    ada_grad,
    ada_bias,
    fc2_grad,
    fc1_grad,
    qkv_grad,
    out_grad,
    bias_sum,
    beside_in,
    pair_rows,
    across_in,
    fc2_mate,
    fc2_pair,
    fc2_straight,
    fc1_mate,
    fc1_pair,
    fc1_straight,
    qkv_mate,
    qkv_pair,
    qkv_straight,
    out_mate,
    out_pair,
    out_straight,
    slot_sums,
    mods_own,
    mods_sibling,
    mods_pair,
    mods_partner,
    mods_low,
    mods_cols,
    bias_all,
    silu_part,
    silu_in,
    silu_all,
    small_send,
    small_recv,
    pair_send,
    pair_recv,
    head_send,
    head_recv,
    weight_send,
    weight_recv,
):
    row, member, sibling, partner, opposite = places()
    greet(range(1, ROW_PARTS), (sibling, partner))
    others = [(step, lax.rem(row + step, ROW_PARTS)) for step in range(1, ROW_PARTS)]

    def spread(stage, source_of, target):
        copies = []
        for step, other in others:
            copy = to_row(
                source_of(other),
                target.at[row],
                small_send.at[stage, step - 1],
                small_recv.at[stage, step - 1],
                other,
            )
            copy.start()
            copies.append(copy)
        return copies

    def settle(copies):
        for copy in copies:
            copy.wait()

    reduce_rows = HeadReduce(hidden_ref, beside_in, pair_rows, across_in, head_send, head_recv)
    reduce_rows.start()
    units = []
    for partial, mate, pair, straight, total, chunks in (
        (fc2_part, fc2_mate, fc2_pair, fc2_straight, fc2_grad, BACK_CHUNKS[0]),
        (fc1_part, fc1_mate, fc1_pair, fc1_straight, fc1_grad, BACK_CHUNKS[1]),
        (qkv_part, qkv_mate, qkv_pair, qkv_straight, qkv_grad, BACK_CHUNKS[2]),
        (out_part, out_mate, out_pair, out_straight, out_grad, BACK_CHUNKS[3]),
    ):
        size = total.shape[0] // chunks
        for chunk in range(chunks):
            place = len(units)
            units.append(
                RowReduce(
                    partial,
                    mate,
                    pair,
                    straight,
                    total,
                    pl.ds(chunk * size, size),
                    weight_send.at[place],
                    weight_recv.at[place],
                )
            )

    units[0].start()
    units[1].start()

    def advance(place):
        units[place].send_pair()
        if place + 2 < len(units):
            units[place + 2].start()
        if place > 0:
            units[place - 1].finish()

    reduce_rows.send_pair()
    advance(0)
    reduce_rows.settle()
    tok_rows = patches_ref.shape[0]
    model_width = patches_ref.shape[1]
    parts_count = 6
    slot_sums[...] = jnp.zeros_like(slot_sums)

    def rows_back(block, carry):
        part = pl.ds(pl.multiple_of(block * 128, 128), 128)
        grad = reduce_rows.rows(part)
        values = patches_ref[part].astype(jnp.float32)
        centred = values - jnp.mean(values, axis=1, keepdims=True)
        factor = lax.rsqrt(jnp.mean(centred * centred, axis=1, keepdims=True) + EPSILON)
        normed = centred * factor
        weighted = grad * scale_ref[part]
        patches_grad[part] = after_ref[part] + factor * (
            weighted
            - jnp.mean(weighted, axis=1, keepdims=True)
            - normed * jnp.mean(weighted * normed, axis=1, keepdims=True)
        )
        hot = hot_ref[:, part]
        slot_sums[0] += jnp.dot(hot, grad, precision=HIGH, preferred_element_type=jnp.float32)
        slot_sums[1] += jnp.dot(
            hot, grad * normed, precision=HIGH, preferred_element_type=jnp.float32
        )
        return carry

    lax.fori_loop(0, tok_rows // 128, rows_back, 0)
    ada_width = ada_ref.shape[1]
    fine = ada_width // 3
    for unit in range(3 * ROW_PARTS):
        part_index, within = divmod(unit * fine, model_width)
        source = (
            slot_sums[part_index, :, within : within + fine]
            if part_index < 2
            else sums_ref[part_index - 2, :, within : within + fine]
        )
        mods_own[unit // 3, :, unit % 3 * fine : (unit % 3 + 1) * fine] = source
    beside = to_head(mods_own, mods_sibling, pair_send.at[0], pair_recv.at[0], sibling)
    beside.start()
    advance(1)
    beside.wait()
    mods_pair[...] = mods_own[...] + mods_sibling[...]
    across = to_head(mods_pair, mods_partner, pair_send.at[1], pair_recv.at[1], partner)
    across.start()
    across.wait()
    mods_low[...] = (
        (mods_pair[...] + mods_partner[...]).astype(jnp.bfloat16).astype(jnp.float32)
    )
    copies = spread(0, lambda other: mods_low.at[other], mods_cols)
    bias_copies = spread(1, lambda other: bias_ref, bias_all)
    mods_cols[row] = mods_low[row]
    bias_all[row] = bias_ref[...]
    advance(2)
    advance(3)
    settle(copies)
    slots = ROW_PARTS * SLOT_ROWS
    cols = mods_cols[...].reshape(slots, ada_width)
    low = cols.astype(jnp.bfloat16)
    ada_grad[...] = jnp.dot(silu_ref[...], low, preferred_element_type=jnp.float32)
    ada_bias[...] = jnp.broadcast_to(jnp.sum(cols, axis=0, keepdims=True), ada_bias.shape)
    silu_part[...] = times_transposed(low, ada_ref[...]).reshape(silu_part.shape)
    copies = spread(2, lambda other: silu_part.at[other], silu_in)
    silu_in[row] = silu_part[row]
    settle(bias_copies)
    bias_sum[...] = jnp.sum(bias_all[...], axis=0)
    advance(4)
    advance(5)
    settle(copies)
    summed = jnp.sum(silu_in[...], axis=0)
    silu_all[row] = summed
    silu_part[row] = summed
    copies = spread(3, lambda other: silu_part.at[row], silu_all)
    advance(6)
    advance(7)
    settle(copies)
    grad_condition = silu_all[...].reshape(slots, silu_all.shape[2]) * slope_ref[...]
    time_grad[...] = jnp.dot(
        bucket_ref[...], grad_condition, precision=HIGH, preferred_element_type=jnp.float32
    )
    class_grad[...] = jnp.dot(
        label_ref[...], grad_condition, precision=HIGH, preferred_element_type=jnp.float32
    )
    advance(8)
    advance(9)
    units[9].finish()
    reduce_rows.finish()


def back(
    hidden,
    grad_w_fc2,
    grad_w_fc1,
    grad_w_qkv,
    grad_w_out,
    biases,
    patches,
    grad_after,
    scales,
    hot,
    sums,
    silu_columns,
    slopes,
    buckets,
    labels,
    w_ada,
):
    shape = jax.ShapeDtypeStruct
    tok_rows, model_width = patches.shape
    depth, ada_width = w_ada.shape
    table_rows = buckets.shape[0]
    weights = (grad_w_fc2, grad_w_fc1, grad_w_qkv, grad_w_out)
    totals = [shape(weight.shape[2:], jnp.float32) for weight in weights]
    landing = []
    for weight in weights:
        size = weight.shape[2:]
        landing += [
            pltpu.VMEM((4,) + size, jnp.bfloat16),
            pltpu.VMEM((4,) + size, jnp.bfloat16),
            pltpu.VMEM((3,) + size, jnp.bfloat16),
        ]
    slotted = (ROW_PARTS, SLOT_ROWS)
    wide = pltpu.VMEM(slotted + (ada_width,), jnp.float32)
    narrow = pltpu.VMEM(slotted + (depth,), jnp.float32)
    unit_count = sum(BACK_CHUNKS)
    return pl.pallas_call(
        back_kernel,
        out_shape=[
            shape((tok_rows, model_width), jnp.float32),
            shape((table_rows, depth), jnp.float32),
            shape((table_rows, depth), jnp.float32),
            shape((depth, ada_width), jnp.float32),
            shape((SLOT_ROWS, ada_width), jnp.float32),
        ]
        + totals
        + [shape(biases.shape, jnp.float32)],
        in_specs=[VMEM_SPEC] * 16,
        out_specs=[VMEM_SPEC] * 10,
        scratch_shapes=[
            pltpu.VMEM((2, tok_rows, model_width), jnp.bfloat16),
            pltpu.VMEM((tok_rows, model_width), jnp.bfloat16),
            pltpu.VMEM((tok_rows, model_width), jnp.bfloat16),
        ]
        + landing
        + [pltpu.VMEM((2, SLOT_ROWS, model_width), jnp.float32)]
        + [wide] * 6
        + [pltpu.VMEM((ROW_PARTS,) + biases.shape, jnp.float32)]
        + [narrow] * 3
        + [
            DMA((4, 7)),
            DMA((4, 7)),
            DMA((2,)),
            DMA((2,)),
            DMA((3,)),
            DMA((3,)),
            DMA((unit_count, 4)),
            DMA((unit_count, 4)),
        ],
        compiler_params=pltpu.CompilerParams(
            collective_id=1, has_side_effects=True, vmem_limit_bytes=GRANT
        ),
        name="back",
    )(
        hidden,
        *weights,
        biases,
        patches,
        grad_after,
        scales,
        hot,
        sums,
        silu_columns,
        slopes,
        buckets,
        labels,
        w_ada,
    )


def shards_linked(
    patches,
    time_table,
    class_table,
    w_ada,
    b_ada,
    w_qkv,
    b_qv,
    w_out,
    b_out,
    w_fc1,
    b_fc1,
    w_fc2,
    b_fc2,
    image_lengths,
    segment_ids,
    bucket_ids,
    class_labels,
    cotangent,
):
    head_parts = lax.axis_size("heads")
    member = lax.axis_index("heads")
    tok_rows = patches.shape[0]
    model_width = patches.shape[1]
    seq_count = segment_ids.shape[0]
    seq_len = segment_ids.shape[1]
    slot_count = image_lengths.shape[1]
    image_count = seq_count * slot_count
    group_rows = tok_rows * head_parts
    head_local = b_qv.shape[0]
    head_size = b_qv.shape[1] // 2
    block_rows = min(BLOCK_LIMIT, seq_len)
    scale_factor = 1.0 / math.sqrt(head_size)
    row_parts = lax.axis_size("rows")
    table_rows = time_table.shape[0]
    ada_width = w_ada.shape[1]
    fc1_cols = lax.all_gather(w_fc1, "rows", axis=0, tiled=True)
    fc2_cols = lax.all_gather(w_fc2, "rows", axis=0, tiled=True)
    every_slot = row_parts * SLOT_ROWS
    slot_pad = jnp.full((SLOT_ROWS - slot_count,), -1, jnp.int32)
    ids = jnp.broadcast_to(
        jnp.concatenate([bucket_ids[0], slot_pad, class_labels[0], slot_pad])[:, None],
        (2 * SLOT_ROWS, table_rows),
    )
    qkv_full, out_full, patches_full, condition, mods, ids_all = front(
        ids, time_table, class_table, w_ada, patches, w_qkv, w_out
    )
    qkv_cols = qkv_full.reshape(model_width, w_qkv.shape[1])
    out_cols = out_full.reshape(model_width, w_out.shape[1])
    condition = condition.reshape(every_slot, condition.shape[2])
    silu_value, silu_pull = jax.vjp(silu_plain, condition)
    silu_low = silu_value.astype(jnp.bfloat16)
    mods_all = mods[:, :slot_count].transpose(1, 0, 2).reshape(
        slot_count, row_parts * ada_width
    ) + b_ada.astype(jnp.float32)
    row_segments = segment_ids[0][:, None]

    def by_token(part_index, segments):
        vectors = mods_all[:, part_index * model_width : (part_index + 1) * model_width]
        chosen = vectors[slot_count - 1][None, :]
        for slot in range(slot_count - 2, -1, -1):
            chosen = jnp.where(segments == slot, vectors[slot][None, :], chosen)
        return chosen

    own_segments = lax.dynamic_slice_in_dim(segment_ids[0], member * tok_rows, tok_rows)[:, None]
    token_hot = (own_segments == jnp.arange(SLOT_ROWS, dtype=jnp.int32)[None, :]).astype(
        jnp.float32
    )
    shift_attn, scale_attn, gate_attn, shift_mlp, scale_mlp, gate_mlp = (
        by_token(part_index, own_segments) for part_index in range(6)
    )
    inputs = patches.astype(jnp.float32)
    rows_one = modulate(
        patches_full.reshape(group_rows, model_width).astype(jnp.float32),
        by_token(0, row_segments),
        by_token(1, row_segments),
    ).astype(jnp.bfloat16)
    zero_bias = jnp.zeros((head_local, head_size), b_qv.dtype)
    qkv_bias = (
        jnp.concatenate([b_qv[:, :head_size], zero_bias, b_qv[:, head_size:]], axis=1)
        .reshape(head_local * 3 * head_size)
        .astype(jnp.float32)
    )
    projected = (jnp.dot(rows_one, qkv_cols, preferred_element_type=jnp.float32) + qkv_bias).astype(
        jnp.bfloat16
    )
    seq_qkv = projected.reshape(seq_count, seq_len, head_local, 3, head_size)
    slot_ends = jnp.cumsum(image_lengths, axis=1)
    places = jnp.arange(seq_len, dtype=jnp.int32)
    image_of = jnp.sum((places[None, :, None] >= slot_ends[:, None, :]).astype(jnp.int32), axis=2)

    def block_scores(query_rows, key_rows, image_rows, image_cols):
        scores = (
            jnp.einsum("qhd,khd->hqk", query_rows, key_rows, preferred_element_type=jnp.float32)
            * scale_factor
        )
        return jnp.where((image_rows[:, None] == image_cols[None, :])[None], scores, MASKED)

    def attend_forward(pieces):
        seq_block, seq_image = pieces
        key_rows = seq_block[:, :, 1]
        value_rows = seq_block[:, :, 2]
        outputs = []
        totals = []
        for row_start in range(0, seq_len, block_rows):
            stop_row = row_start + block_rows
            query_rows = seq_block[row_start:stop_row, :, 0]
            scores = block_scores(query_rows, key_rows, seq_image[row_start:stop_row], seq_image)
            row_peak = jnp.max(scores, axis=2, keepdims=True)
            raised = jnp.exp(scores - row_peak)
            row_total = jnp.sum(raised, axis=2, keepdims=True)
            soft_low = (raised / row_total).astype(jnp.bfloat16)
            outputs.append(
                jnp.einsum(
                    "hqk,khd->qhd", soft_low, value_rows, preferred_element_type=jnp.float32
                ).astype(jnp.bfloat16)
            )
            totals.append((row_peak + jnp.log(row_total))[:, :, 0])
        return (jnp.concatenate(outputs, axis=0), jnp.concatenate(totals, axis=1))

    mixed, log_totals = lax.map(attend_forward, (seq_qkv, image_of))
    mixed_rows = mixed.reshape(group_rows, head_local * head_size)
    attn_out = lax.psum_scatter(
        times_transposed(
            lax.slice_in_dim(mixed_rows, 0, tok_rows * lax.axis_size("heads"), axis=0), out_cols
        ).astype(jnp.bfloat16),
        "heads",
        scatter_dimension=0,
        tiled=True,
    ).astype(jnp.float32) + b_out.astype(jnp.float32)
    after_attn = inputs + gate_attn * attn_out
    second_value, second_pull = jax.vjp(modulate, after_attn, shift_mlp, scale_mlp)
    hidden_two = second_value.astype(jnp.bfloat16)
    rows_two = lax.all_gather(hidden_two, "heads", axis=0, tiled=True)
    inner = jnp.dot(rows_two, fc1_cols, preferred_element_type=jnp.float32) + b_fc1.astype(
        jnp.float32
    )
    gelu_value, gelu_pull = jax.vjp(gelu_tanh, inner)
    active = gelu_value.astype(jnp.bfloat16)
    ffn_out = lax.psum_scatter(
        times_transposed(
            lax.slice_in_dim(active, 0, tok_rows * lax.axis_size("heads"), axis=0), fc2_cols
        ).astype(jnp.bfloat16),
        "heads",
        scatter_dimension=0,
        tiled=True,
    ).astype(jnp.float32) + b_fc2.astype(jnp.float32)
    block_out = (after_attn + gate_mlp * ffn_out).astype(jnp.bfloat16)
    upstream = cotangent.astype(jnp.float32)
    grad_ffn = (gate_mlp * upstream).astype(jnp.bfloat16)
    ffn_rows = lax.all_gather(grad_ffn, "heads", axis=0, tiled=True)
    grad_w_fc2 = contract_rows(ffn_rows, active)
    grad_b_fc2 = jnp.sum(ffn_rows, axis=0, dtype=jnp.float32)
    grad_active = jnp.dot(ffn_rows, fc2_cols, preferred_element_type=jnp.float32)
    grad_inner = gelu_pull(grad_active)[0].astype(jnp.bfloat16)
    grad_w_fc1 = contract_rows(rows_two, grad_inner)
    grad_b_fc1 = jnp.sum(grad_inner, axis=0, dtype=jnp.float32)
    grad_hidden_two = lax.psum_scatter(
        times_transposed(
            lax.slice_in_dim(grad_inner, 0, tok_rows * lax.axis_size("heads"), axis=0), fc1_cols
        ).astype(jnp.bfloat16),
        "heads",
        scatter_dimension=0,
        tiled=True,
    ).astype(jnp.float32)
    grad_after, grad_shift_mlp, grad_scale_mlp = second_pull(grad_hidden_two)
    grad_after = grad_after + upstream
    grad_gate_mlp = upstream * ffn_out
    grad_gate_attn = grad_after * attn_out
    grad_attn = (gate_attn * grad_after).astype(jnp.bfloat16)
    attn_rows_grad = lax.all_gather(grad_attn, "heads", axis=0, tiled=True)
    grad_w_out = contract_rows(attn_rows_grad, mixed_rows)
    grad_b_out = jnp.sum(attn_rows_grad, axis=0, dtype=jnp.float32)
    grad_mixed = jnp.dot(attn_rows_grad, out_cols, preferred_element_type=jnp.float32).astype(
        jnp.bfloat16
    )
    grad_seq = grad_mixed.reshape(seq_count, seq_len, head_local, head_size)

    def attend_backward(pieces):
        seq_block, seq_image, seq_grad, seq_totals = pieces
        key_rows = seq_block[:, :, 1]
        value_rows = seq_block[:, :, 2]
        grad_keys = jnp.zeros(key_rows.shape, jnp.float32)
        grad_values = jnp.zeros(value_rows.shape, jnp.float32)
        grad_queries = []
        for row_start in range(0, seq_len, block_rows):
            stop_row = row_start + block_rows
            query_rows = seq_block[row_start:stop_row, :, 0]
            grad_rows = seq_grad[row_start:stop_row]
            scores = block_scores(query_rows, key_rows, seq_image[row_start:stop_row], seq_image)
            soft_probs = jnp.exp(scores - seq_totals[:, row_start:stop_row, None])
            grad_probs = jnp.einsum(
                "qhd,khd->hqk", grad_rows, value_rows, preferred_element_type=jnp.float32
            )
            inner_sum = jnp.sum(soft_probs * grad_probs, axis=2, keepdims=True)
            grad_scores = (soft_probs * (grad_probs - inner_sum)).astype(jnp.bfloat16)
            grad_queries.append(
                jnp.einsum(
                    "hqk,khd->qhd", grad_scores, key_rows, preferred_element_type=jnp.float32
                )
                * scale_factor
            )
            grad_keys = (
                grad_keys
                + jnp.einsum(
                    "hqk,qhd->khd", grad_scores, query_rows, preferred_element_type=jnp.float32
                )
                * scale_factor
            )
            grad_values = grad_values + jnp.einsum(
                "hqk,qhd->khd",
                soft_probs.astype(jnp.bfloat16),
                grad_rows,
                preferred_element_type=jnp.float32,
            )
        stacked = jnp.stack([jnp.concatenate(grad_queries, axis=0), grad_keys, grad_values], axis=2)
        return stacked.astype(jnp.bfloat16)

    grad_qkv = lax.map(attend_backward, (seq_qkv, image_of, grad_seq, log_totals)).reshape(
        group_rows, head_local * 3 * head_size
    )
    grad_w_qkv = contract_rows(rows_one, grad_qkv)
    bias_terms = jnp.sum(grad_qkv, axis=0, dtype=jnp.float32).reshape(head_local, 3, head_size)
    grad_b_qv = jnp.concatenate([bias_terms[:, 0], bias_terms[:, 2]], axis=1)
    grad_hidden_one = times_transposed(grad_qkv, qkv_cols).astype(jnp.bfloat16)
    sums = jnp.stack(
        [
            contract_rows_exact(token_hot, grad_term)
            for grad_term in (grad_gate_attn, grad_shift_mlp, grad_scale_mlp, grad_gate_mlp)
        ]
    )
    all_ids = ids_all[:, :, 0]
    table_places = lax.axis_index("rows") * table_rows + jnp.arange(table_rows, dtype=jnp.int32)
    bucket_hot = table_places[:, None] == all_ids[:, :SLOT_ROWS].reshape(every_slot)[None, :]
    label_hot = table_places[:, None] == all_ids[:, SLOT_ROWS:].reshape(every_slot)[None, :]
    bias_flat = jnp.concatenate([grad_b_qv.reshape(-1), grad_b_fc1, grad_b_out, grad_b_fc2])
    bias_size = bias_flat.size
    bias_tiles = -(-bias_size // 1024) * 8
    biases = jnp.pad(bias_flat, (0, bias_tiles * 128 - bias_size)).reshape(bias_tiles, 128)

    def by_row(partial):
        return partial.astype(jnp.bfloat16).reshape(
            4, 2, partial.shape[0] // ROW_PARTS, partial.shape[1]
        )

    (
        grad_patches,
        grad_time,
        grad_class,
        grad_w_ada,
        grad_b_ada,
        grad_w_fc2,
        grad_w_fc1,
        grad_w_qkv,
        grad_w_out,
        bias_all,
    ) = back(
        grad_hidden_one.reshape(HEAD_PARTS, tok_rows, model_width),
        by_row(grad_w_fc2),
        by_row(grad_w_fc1),
        by_row(grad_w_qkv),
        by_row(grad_w_out),
        biases,
        patches,
        grad_after,
        1.0 + scale_attn,
        token_hot.T,
        sums,
        silu_low.T,
        silu_pull(jnp.ones_like(condition))[0],
        bucket_hot.astype(jnp.float32),
        label_hot.astype(jnp.float32),
        w_ada,
    )
    grad_b_ada = grad_b_ada[0]
    bias_all = bias_all.reshape(-1)
    bias_sizes = (grad_b_qv.size, grad_b_fc1.size, grad_b_out.size, grad_b_fc2.size)
    edges = [sum(bias_sizes[:step]) for step in range(5)]
    bias_rows = model_width // row_parts
    row_start = lax.axis_index("rows") * bias_rows
    grad_b_qv = bias_all[edges[0] : edges[1]].reshape(grad_b_qv.shape)
    grad_b_fc1 = bias_all[edges[1] : edges[2]]
    grad_b_out = lax.dynamic_slice_in_dim(bias_all[edges[2] : edges[3]], row_start, bias_rows)
    grad_b_fc2 = lax.dynamic_slice_in_dim(bias_all[edges[3] : edges[4]], row_start, bias_rows)
    return (
        block_out,
        grad_patches,
        grad_time,
        grad_class,
        grad_w_ada,
        grad_b_ada,
        grad_w_qkv,
        grad_b_qv,
        grad_w_out,
        grad_b_out,
        grad_w_fc1,
        grad_b_fc1,
        grad_w_fc2,
        grad_b_fc2,
    )


def solution(mesh):
    placed = (
        P(("rows", "heads"), None),
        P("rows", "heads"),
        P("rows", "heads"),
        P("heads", "rows"),
        P(),
        P("rows", "heads"),
        P("heads", None),
        P("rows", "heads"),
        P(),
        P("rows", "heads"),
        P("heads"),
        P("rows", "heads"),
        P(),
        P("rows", None),
        P("rows", None),
        P("rows", None),
        P("rows", None),
        P(("rows", "heads"), None),
    )
    linked = mesh.shape["rows"] == ROW_PARTS and mesh.shape["heads"] == HEAD_PARTS
    return jax.shard_map(
        shards_linked if linked else shards_plain,
        mesh=mesh,
        in_specs=placed,
        out_specs=(
            P(("rows", "heads"), None),
            P(("rows", "heads"), None),
            P("rows", "heads"),
            P("rows", "heads"),
            P("heads", "rows"),
            P("rows"),
            P("rows", "heads"),
            P("heads", None),
            P("rows", "heads"),
            P("rows"),
            P("rows", "heads"),
            P("heads"),
            P("rows", "heads"),
            P("rows"),
        ),
        check_vma=False,
    )
```

```python
import functools
import math

import jax
import jax.numpy as jnp
from jax import lax
from jax.experimental import pallas as pl
from jax.experimental.pallas import tpu as pltpu
from jax.sharding import PartitionSpec as P

EPSILON = 1e-06
MASKED = -1e30
HIGH = lax.Precision.HIGHEST
TANH_COEFF = 0.7978845608028654
BLOCK_LIMIT = 512


def layer_norm(values):
    average = jnp.mean(values, axis=-1, keepdims=True)
    centred = values - average
    variance = jnp.mean(centred * centred, axis=-1, keepdims=True)
    return centred * lax.rsqrt(variance + EPSILON)


def gelu_tanh(values):
    return (
        0.5 * values * (1.0 + jnp.tanh(TANH_COEFF * (values + 0.044715 * values * values * values)))
    )


def silu_plain(values):
    return values / (1.0 + jnp.exp(-values))


def modulate(values, shift_term, scale_term):
    return layer_norm(values) * (1.0 + scale_term) + shift_term


def contract_rows(left_matrix, right_matrix):
    return lax.dot_general(
        left_matrix, right_matrix, (((0,), (0,)), ((), ())), preferred_element_type=jnp.float32
    )


def contract_rows_exact(left_matrix, right_matrix):
    return lax.dot_general(
        left_matrix,
        right_matrix,
        (((0,), (0,)), ((), ())),
        precision=HIGH,
        preferred_element_type=jnp.float32,
    )


def times_transposed(left_matrix, right_matrix):
    return lax.dot_general(
        left_matrix, right_matrix, (((1,), (1,)), ((), ())), preferred_element_type=jnp.float32
    )


def gather_weights(w_qkv, w_out, w_fc1, w_fc2):
    return (
        lax.all_gather(w_qkv, "rows", axis=0, tiled=True),
        lax.all_gather(w_out, "rows", axis=0, tiled=True),
        lax.all_gather(w_fc1, "rows", axis=0, tiled=True),
        lax.all_gather(w_fc2, "rows", axis=0, tiled=True),
    )


def shards_plain(
    patches,
    time_table,
    class_table,
    w_ada,
    b_ada,
    w_qkv,
    b_qv,
    w_out,
    b_out,
    w_fc1,
    b_fc1,
    w_fc2,
    b_fc2,
    image_lengths,
    segment_ids,
    bucket_ids,
    class_labels,
    cotangent,
):
    head_parts = lax.axis_size("heads")
    member = lax.axis_index("heads")
    tok_rows = patches.shape[0]
    model_width = patches.shape[1]
    seq_count = segment_ids.shape[0]
    seq_len = segment_ids.shape[1]
    slot_count = image_lengths.shape[1]
    image_count = seq_count * slot_count
    group_rows = tok_rows * head_parts
    head_local = b_qv.shape[0]
    head_size = b_qv.shape[1] // 2
    block_rows = min(BLOCK_LIMIT, seq_len)
    scale_factor = 1.0 / math.sqrt(head_size)
    row_parts = lax.axis_size("rows")
    table_rows = time_table.shape[0]
    ada_width = w_ada.shape[1]
    qkv_cols, out_cols, fc1_cols, fc2_cols = gather_weights(w_qkv, w_out, w_fc1, w_fc2)
    ids_all = lax.all_gather(
        jnp.concatenate([bucket_ids, class_labels], axis=1), "rows", axis=0, tiled=True
    )
    every_slot = row_parts * image_count
    table_places = lax.axis_index("rows") * table_rows + jnp.arange(table_rows, dtype=jnp.int32)
    bucket_hot = (
        ids_all[:, :slot_count].reshape(every_slot)[:, None] == table_places[None, :]
    ).astype(jnp.bfloat16)
    label_hot = (
        ids_all[:, slot_count:].reshape(every_slot)[:, None] == table_places[None, :]
    ).astype(jnp.bfloat16)
    condition = lax.psum(
        jnp.dot(bucket_hot, time_table, preferred_element_type=jnp.float32)
        + jnp.dot(label_hot, class_table, preferred_element_type=jnp.float32),
        "rows",
    )
    silu_value, silu_pull = jax.vjp(silu_plain, condition)
    silu_low = silu_value.astype(jnp.bfloat16)
    mods_part = jnp.dot(silu_low, w_ada, preferred_element_type=jnp.float32)
    mods_cols = lax.psum(mods_part, "heads").reshape(row_parts, image_count, ada_width)
    mods_own = lax.all_to_all(mods_cols, "rows", split_axis=0, concat_axis=0, tiled=True)
    mods_all = mods_own.transpose(1, 0, 2).reshape(
        image_count, row_parts * ada_width
    ) + b_ada.astype(jnp.float32)
    positions = member * tok_rows + jnp.arange(tok_rows, dtype=jnp.int32)
    own_segments = lax.dynamic_slice_in_dim(
        segment_ids.reshape(seq_count * seq_len), member * tok_rows, tok_rows
    )
    token_image = positions // seq_len * slot_count + own_segments
    token_hot = (token_image[:, None] == jnp.arange(image_count, dtype=jnp.int32)[None, :]).astype(
        jnp.float32
    )
    token_mods = [
        jnp.dot(
            token_hot,
            mods_all[:, part_index * model_width : (part_index + 1) * model_width],
            precision=HIGH,
        )
        for part_index in range(6)
    ]
    shift_attn, scale_attn, gate_attn, shift_mlp, scale_mlp, gate_mlp = token_mods
    inputs = patches.astype(jnp.float32)
    first_value, first_pull = jax.vjp(modulate, inputs, shift_attn, scale_attn)
    hidden_one = first_value.astype(jnp.bfloat16)
    rows_one = lax.all_gather(hidden_one, "heads", axis=0, tiled=True)
    zero_bias = jnp.zeros((head_local, head_size), b_qv.dtype)
    qkv_bias = (
        jnp.concatenate([b_qv[:, :head_size], zero_bias, b_qv[:, head_size:]], axis=1)
        .reshape(head_local * 3 * head_size)
        .astype(jnp.float32)
    )
    projected = (jnp.dot(rows_one, qkv_cols, preferred_element_type=jnp.float32) + qkv_bias).astype(
        jnp.bfloat16
    )
    seq_qkv = projected.reshape(seq_count, seq_len, head_local, 3, head_size)
    slot_ends = jnp.cumsum(image_lengths, axis=1)
    places = jnp.arange(seq_len, dtype=jnp.int32)
    image_of = jnp.sum((places[None, :, None] >= slot_ends[:, None, :]).astype(jnp.int32), axis=2)

    def block_scores(query_rows, key_rows, image_rows, image_cols):
        scores = (
            jnp.einsum("qhd,khd->hqk", query_rows, key_rows, preferred_element_type=jnp.float32)
            * scale_factor
        )
        return jnp.where((image_rows[:, None] == image_cols[None, :])[None], scores, MASKED)

    def attend_forward(pieces):
        seq_block, seq_image = pieces
        key_rows = seq_block[:, :, 1]
        value_rows = seq_block[:, :, 2]
        outputs = []
        totals = []
        for row_start in range(0, seq_len, block_rows):
            stop_row = row_start + block_rows
            query_rows = seq_block[row_start:stop_row, :, 0]
            scores = block_scores(query_rows, key_rows, seq_image[row_start:stop_row], seq_image)
            row_peak = jnp.max(scores, axis=2, keepdims=True)
            raised = jnp.exp(scores - row_peak)
            row_total = jnp.sum(raised, axis=2, keepdims=True)
            soft_low = (raised / row_total).astype(jnp.bfloat16)
            outputs.append(
                jnp.einsum(
                    "hqk,khd->qhd", soft_low, value_rows, preferred_element_type=jnp.float32
                ).astype(jnp.bfloat16)
            )
            totals.append((row_peak + jnp.log(row_total))[:, :, 0])
        return (jnp.concatenate(outputs, axis=0), jnp.concatenate(totals, axis=1))

    mixed, log_totals = lax.map(attend_forward, (seq_qkv, image_of))
    mixed_rows = mixed.reshape(group_rows, head_local * head_size)
    attn_out = lax.psum_scatter(
        times_transposed(
            lax.slice_in_dim(mixed_rows, 0, tok_rows * lax.axis_size("heads"), axis=0), out_cols
        ).astype(jnp.bfloat16),
        "heads",
        scatter_dimension=0,
        tiled=True,
    ).astype(jnp.float32) + b_out.astype(jnp.float32)
    after_attn = inputs + gate_attn * attn_out
    second_value, second_pull = jax.vjp(modulate, after_attn, shift_mlp, scale_mlp)
    hidden_two = second_value.astype(jnp.bfloat16)
    rows_two = lax.all_gather(hidden_two, "heads", axis=0, tiled=True)
    inner = jnp.dot(rows_two, fc1_cols, preferred_element_type=jnp.float32) + b_fc1.astype(
        jnp.float32
    )
    gelu_value, gelu_pull = jax.vjp(gelu_tanh, inner)
    active = gelu_value.astype(jnp.bfloat16)
    ffn_out = lax.psum_scatter(
        times_transposed(
            lax.slice_in_dim(active, 0, tok_rows * lax.axis_size("heads"), axis=0), fc2_cols
        ).astype(jnp.bfloat16),
        "heads",
        scatter_dimension=0,
        tiled=True,
    ).astype(jnp.float32) + b_fc2.astype(jnp.float32)
    block_out = (after_attn + gate_mlp * ffn_out).astype(jnp.bfloat16)
    upstream = cotangent.astype(jnp.float32)
    grad_ffn = (gate_mlp * upstream).astype(jnp.bfloat16)
    ffn_rows = lax.all_gather(grad_ffn, "heads", axis=0, tiled=True)
    grad_w_fc2 = contract_rows(ffn_rows, active)
    grad_b_fc2 = jnp.sum(ffn_rows, axis=0, dtype=jnp.float32)
    grad_active = jnp.dot(ffn_rows, fc2_cols, preferred_element_type=jnp.float32)
    grad_inner = gelu_pull(grad_active)[0].astype(jnp.bfloat16)
    grad_w_fc1 = contract_rows(rows_two, grad_inner)
    grad_b_fc1 = jnp.sum(grad_inner, axis=0, dtype=jnp.float32)
    grad_hidden_two = lax.psum_scatter(
        times_transposed(
            lax.slice_in_dim(grad_inner, 0, tok_rows * lax.axis_size("heads"), axis=0), fc1_cols
        ).astype(jnp.bfloat16),
        "heads",
        scatter_dimension=0,
        tiled=True,
    ).astype(jnp.float32)
    grad_after, grad_shift_mlp, grad_scale_mlp = second_pull(grad_hidden_two)
    grad_after = grad_after + upstream
    grad_gate_mlp = upstream * ffn_out
    grad_gate_attn = grad_after * attn_out
    grad_attn = (gate_attn * grad_after).astype(jnp.bfloat16)
    attn_rows_grad = lax.all_gather(grad_attn, "heads", axis=0, tiled=True)
    grad_w_out = contract_rows(attn_rows_grad, mixed_rows)
    grad_b_out = jnp.sum(attn_rows_grad, axis=0, dtype=jnp.float32)
    grad_mixed = jnp.dot(attn_rows_grad, out_cols, preferred_element_type=jnp.float32).astype(
        jnp.bfloat16
    )
    grad_seq = grad_mixed.reshape(seq_count, seq_len, head_local, head_size)

    def attend_backward(pieces):
        seq_block, seq_image, seq_grad, seq_totals = pieces
        key_rows = seq_block[:, :, 1]
        value_rows = seq_block[:, :, 2]
        grad_keys = jnp.zeros(key_rows.shape, jnp.float32)
        grad_values = jnp.zeros(value_rows.shape, jnp.float32)
        grad_queries = []
        for row_start in range(0, seq_len, block_rows):
            stop_row = row_start + block_rows
            query_rows = seq_block[row_start:stop_row, :, 0]
            grad_rows = seq_grad[row_start:stop_row]
            scores = block_scores(query_rows, key_rows, seq_image[row_start:stop_row], seq_image)
            soft_probs = jnp.exp(scores - seq_totals[:, row_start:stop_row, None])
            grad_probs = jnp.einsum(
                "qhd,khd->hqk", grad_rows, value_rows, preferred_element_type=jnp.float32
            )
            inner_sum = jnp.sum(soft_probs * grad_probs, axis=2, keepdims=True)
            grad_scores = (soft_probs * (grad_probs - inner_sum)).astype(jnp.bfloat16)
            grad_queries.append(
                jnp.einsum(
                    "hqk,khd->qhd", grad_scores, key_rows, preferred_element_type=jnp.float32
                )
                * scale_factor
            )
            grad_keys = (
                grad_keys
                + jnp.einsum(
                    "hqk,qhd->khd", grad_scores, query_rows, preferred_element_type=jnp.float32
                )
                * scale_factor
            )
            grad_values = grad_values + jnp.einsum(
                "hqk,qhd->khd",
                soft_probs.astype(jnp.bfloat16),
                grad_rows,
                preferred_element_type=jnp.float32,
            )
        stacked = jnp.stack([jnp.concatenate(grad_queries, axis=0), grad_keys, grad_values], axis=2)
        return stacked.astype(jnp.bfloat16)

    grad_qkv = lax.map(attend_backward, (seq_qkv, image_of, grad_seq, log_totals)).reshape(
        group_rows, head_local * 3 * head_size
    )
    grad_w_qkv = contract_rows(rows_one, grad_qkv)
    bias_terms = jnp.sum(grad_qkv, axis=0, dtype=jnp.float32).reshape(head_local, 3, head_size)
    grad_b_qv = jnp.concatenate([bias_terms[:, 0], bias_terms[:, 2]], axis=1)
    grad_hidden_one = lax.psum_scatter(
        times_transposed(
            lax.slice_in_dim(grad_qkv, 0, tok_rows * lax.axis_size("heads"), axis=0), qkv_cols
        ).astype(jnp.bfloat16),
        "heads",
        scatter_dimension=0,
        tiled=True,
    ).astype(jnp.float32)
    grad_inputs, grad_shift_attn, grad_scale_attn = first_pull(grad_hidden_one)
    grad_patches = grad_inputs + grad_after
    token_grads = (
        grad_shift_attn,
        grad_scale_attn,
        grad_gate_attn,
        grad_shift_mlp,
        grad_scale_mlp,
        grad_gate_mlp,
    )
    mods_grad_part = jnp.concatenate(
        [contract_rows_exact(token_hot, grad_term) for grad_term in token_grads], axis=1
    )
    grad_mods = lax.psum(mods_grad_part.astype(jnp.bfloat16), "heads")
    grad_cols = lax.all_to_all(
        grad_mods.reshape(image_count, row_parts, ada_width).transpose(1, 0, 2),
        "rows",
        split_axis=0,
        concat_axis=0,
        tiled=True,
    ).reshape(every_slot, ada_width)
    grad_w_ada = contract_rows(silu_low, grad_cols)
    grad_b_ada = jnp.sum(grad_cols, axis=0, dtype=jnp.float32)
    grad_silu = lax.psum(times_transposed(grad_cols, w_ada), "rows")
    grad_condition = silu_pull(grad_silu)[0]
    grad_time = contract_rows_exact(bucket_hot.astype(jnp.float32), grad_condition)
    grad_class = contract_rows_exact(label_hot.astype(jnp.float32), grad_condition)

    def row_reduced(partial):
        return lax.psum_scatter(
            partial.astype(jnp.bfloat16), "rows", scatter_dimension=0, tiled=True
        ).astype(jnp.float32)

    grad_w_qkv, grad_w_out, grad_w_fc1, grad_w_fc2 = (
        row_reduced(grad_w_qkv),
        row_reduced(grad_w_out),
        row_reduced(grad_w_fc1),
        row_reduced(grad_w_fc2),
    )
    bias_sizes = (grad_b_qv.size, grad_b_fc1.size, grad_b_out.size, grad_b_fc2.size)
    bias_all = lax.psum(
        jnp.concatenate([grad_b_qv.reshape(-1), grad_b_fc1, grad_b_out, grad_b_fc2]), "rows"
    )
    edges = [sum(bias_sizes[:step]) for step in range(5)]
    bias_rows = model_width // row_parts
    row_start = lax.axis_index("rows") * bias_rows
    grad_b_qv = bias_all[edges[0] : edges[1]].reshape(grad_b_qv.shape)
    grad_b_fc1 = bias_all[edges[1] : edges[2]]
    grad_b_out = lax.dynamic_slice_in_dim(bias_all[edges[2] : edges[3]], row_start, bias_rows)
    grad_b_fc2 = lax.dynamic_slice_in_dim(bias_all[edges[3] : edges[4]], row_start, bias_rows)
    return (
        block_out,
        grad_patches,
        grad_time,
        grad_class,
        grad_w_ada,
        grad_b_ada,
        grad_w_qkv,
        grad_b_qv,
        grad_w_out,
        grad_b_out,
        grad_w_fc1,
        grad_b_fc1,
        grad_w_fc2,
        grad_b_fc2,
    )


MESH = pl.DeviceIdType.MESH
ROW_PARTS = 8
HEAD_PARTS = 4
SLOT_ROWS = 8
VMEM_SPEC = pl.BlockSpec(memory_space=pltpu.VMEM)
ANY_SPEC = pl.BlockSpec(memory_space=pl.ANY)
DMA = pltpu.SemaphoreType.DMA
GRANT = 60 * 1024 * 1024


def places():
    row = lax.axis_index("rows")
    member = lax.axis_index("heads")
    sibling = member + 1 - 2 * lax.rem(member, 2)
    partner = lax.rem(member + 2, HEAD_PARTS)
    opposite = lax.rem(sibling + 2, HEAD_PARTS)
    return row, member, sibling, partner, opposite


def greet(row_steps, head_members):
    barrier = pltpu.get_barrier_semaphore()
    row = lax.axis_index("rows")
    for step in row_steps:
        pl.semaphore_signal(
            barrier,
            inc=1,
            device_id={"rows": lax.rem(row + step, ROW_PARTS)},
            device_id_type=MESH,
        )
    for other in head_members:
        pl.semaphore_signal(barrier, inc=1, device_id={"heads": other}, device_id_type=MESH)
    pl.semaphore_wait(barrier, len(row_steps) + len(head_members))


def to_row(source, target, send, recv, row):
    return pltpu.make_async_remote_copy(
        src_ref=source,
        dst_ref=target,
        send_sem=send,
        recv_sem=recv,
        device_id={"rows": row},
        device_id_type=MESH,
    )


def to_head(source, target, send, recv, member):
    return pltpu.make_async_remote_copy(
        src_ref=source,
        dst_ref=target,
        send_sem=send,
        recv_sem=recv,
        device_id={"heads": member},
        device_id_type=MESH,
    )


class RowGather:
    def __init__(self, shard, full, sends, recvs, local_sem, chunks):
        self.row = lax.axis_index("rows")
        self.level = self.row // 2
        self.side = lax.rem(self.row, 2)
        self.mate = self.row + 1 - 2 * self.side
        size = shard.shape[0] // chunks
        self.own = pltpu.make_async_copy(shard, full.at[self.row], local_sem)
        self.straight = []
        self.across = []
        for chunk in range(chunks):
            part = pl.ds(chunk * size, size)
            straight = []
            across = [
                to_row(
                    shard.at[part],
                    full.at[self.row, part],
                    sends.at[chunk, 3],
                    recvs.at[chunk, 3],
                    self.mate,
                )
            ]
            for step in range(1, 4):
                target = lax.rem(self.level + step, 4) * 2 + self.side
                origin = lax.rem(self.level + 4 - step, 4) * 2 + self.side
                straight.append(
                    to_row(
                        shard.at[part],
                        full.at[self.row, part],
                        sends.at[chunk, step - 1],
                        recvs.at[chunk, step - 1],
                        target,
                    )
                )
                across.append(
                    to_row(
                        full.at[origin, part],
                        full.at[origin, part],
                        sends.at[chunk, 3 + step],
                        recvs.at[chunk, 3 + step],
                        self.mate,
                    )
                )
            self.straight.append(straight)
            self.across.append(across)

    def start(self, chunk):
        for copy in self.straight[chunk]:
            copy.start()
        self.across[chunk][0].start()

    def relay(self, chunk):
        for step in range(3):
            self.straight[chunk][step].wait_recv()
            self.across[chunk][1 + step].start()

    def finish(self):
        self.own.wait()
        for straight, across in zip(self.straight, self.across):
            for copy in straight:
                copy.wait_send()
            for copy in across:
                copy.wait()


class HeadGather:
    def __init__(self, block, full, sends, recvs, local_sem):
        row, member, sibling, partner, opposite = places()
        self.own = None
        if block is None:
            block = full.at[member]
        else:
            self.own = pltpu.make_async_copy(block, full.at[member], local_sem)
        self.beside = to_head(block, full.at[member], sends.at[0], recvs.at[0], sibling)
        self.across = to_head(block, full.at[member], sends.at[1], recvs.at[1], partner)
        self.onward = to_head(
            full.at[partner], full.at[partner], sends.at[2], recvs.at[2], sibling
        )

    def start(self):
        self.across.start()
        self.beside.start()
        if self.own is not None:
            self.own.start()

    def wait_sibling(self):
        self.beside.wait_recv()

    def wait_partner(self):
        self.across.wait_recv()
        self.onward.start()

    def wait_opposite(self):
        self.onward.wait_recv()

    def finish(self):
        if self.own is not None:
            self.own.wait()
        self.beside.wait_send()
        self.across.wait_send()
        self.onward.wait_send()


def front_kernel(
    ids_ref,
    time_ref,
    class_ref,
    ada_ref,
    patches_ref,
    cotangent_ref,
    qkv_ref,
    out_ref,
    fc1_ref,
    qkv_full,
    out_full,
    fc1_full,
    patches_full,
    cotangent_full,
    cond_all,
    mods_ref,
    ids_all,
    cond_part,
    cond_in,
    mods_part,
    mods_in,
    mods_sibling,
    mods_pair,
    mods_partner,
    small_send,
    small_recv,
    pair_send,
    pair_recv,
    head_send,
    head_recv,
    qkv_send,
    qkv_recv,
    out_send,
    out_recv,
    fc1_send,
    fc1_recv,
    local_sems,
):
    row, member, sibling, partner, opposite = places()
    greet(range(1, ROW_PARTS), (sibling, partner))
    others = [(step, lax.rem(row + step, ROW_PARTS)) for step in range(1, ROW_PARTS)]

    def spread(stage, source_of, target):
        copies = []
        for step, other in others:
            copy = to_row(
                source_of(other),
                target.at[row],
                small_send.at[stage, step - 1],
                small_recv.at[stage, step - 1],
                other,
            )
            copy.start()
            copies.append(copy)
        return copies

    def settle(copies):
        for copy in copies:
            copy.wait()

    ids_copies = spread(0, lambda other: ids_ref, ids_all)
    gather_qkv = RowGather(qkv_ref, qkv_full, qkv_send, qkv_recv, local_sems.at[0], 3)
    gather_out = RowGather(out_ref, out_full, out_send, out_recv, local_sems.at[1], 1)
    gather_fc1 = RowGather(fc1_ref, fc1_full, fc1_send, fc1_recv, local_sems.at[2], 3)
    gather_patches = HeadGather(
        patches_ref, patches_full, head_send.at[0], head_recv.at[0], local_sems.at[3]
    )
    gather_cotangent = HeadGather(
        cotangent_ref, cotangent_full, head_send.at[1], head_recv.at[1], local_sems.at[4]
    )
    gather_patches.start()
    gather_qkv.own.start()
    gather_out.own.start()
    gather_fc1.own.start()
    gather_qkv.start(0)
    ids_all[row] = ids_ref[...]
    settle(ids_copies)
    table_rows = time_ref.shape[0]
    slots = ROW_PARTS * SLOT_ROWS
    table_places = row * table_rows + lax.broadcasted_iota(jnp.int32, (slots, table_rows), 1)
    bucket_hot = (
        ids_all[:, 0:SLOT_ROWS].reshape(slots, table_rows) == table_places
    ).astype(jnp.bfloat16)
    label_hot = (
        ids_all[:, SLOT_ROWS : 2 * SLOT_ROWS].reshape(slots, table_rows) == table_places
    ).astype(jnp.bfloat16)
    found = jnp.dot(bucket_hot, time_ref[...], preferred_element_type=jnp.float32) + jnp.dot(
        label_hot, class_ref[...], preferred_element_type=jnp.float32
    )
    cond_part[...] = found.reshape(cond_part.shape)
    copies = spread(1, lambda other: cond_part.at[other], cond_in)
    gather_qkv.start(1)
    cond_in[row] = cond_part[row]
    settle(copies)
    condition = jnp.sum(cond_in[...], axis=0)
    cond_all[row] = condition
    cond_part[row] = condition
    copies = spread(2, lambda other: cond_part.at[row], cond_all)
    gather_qkv.relay(0)
    settle(copies)
    every = cond_all[...].reshape(slots, cond_all.shape[2])
    silu_low = (every / (1.0 + jnp.exp(-every))).astype(jnp.bfloat16)
    mods_part[...] = jnp.dot(
        silu_low, ada_ref[...], preferred_element_type=jnp.float32
    ).reshape(mods_part.shape)
    copies = spread(3, lambda other: mods_part.at[other], mods_in)
    gather_qkv.start(2)
    mods_in[row] = mods_part[row]
    gather_qkv.relay(1)
    settle(copies)
    gather_out.start(0)
    beside = to_head(mods_in, mods_sibling, pair_send.at[0], pair_recv.at[0], sibling)
    beside.start()
    gather_patches.wait_sibling()
    beside.wait()
    mods_pair[...] = mods_in[...] + mods_sibling[...]
    across = to_head(mods_pair, mods_partner, pair_send.at[1], pair_recv.at[1], partner)
    across.start()
    gather_patches.wait_partner()
    gather_cotangent.start()
    gather_fc1.start(0)
    gather_qkv.relay(2)
    across.wait()
    mods_ref[...] = mods_pair[...] + mods_partner[...]
    gather_patches.wait_opposite()
    gather_fc1.start(1)
    gather_out.relay(0)
    gather_fc1.start(2)
    gather_fc1.relay(0)
    gather_cotangent.wait_sibling()
    gather_cotangent.wait_partner()
    gather_fc1.relay(1)
    gather_cotangent.wait_opposite()
    gather_fc1.relay(2)
    gather_patches.finish()
    gather_cotangent.finish()
    gather_qkv.finish()
    gather_out.finish()
    gather_fc1.finish()


def front(ids, time_table, class_table, w_ada, patches, cotangent, w_qkv, w_out, w_fc1):
    depth, ada_width = w_ada.shape
    shape = jax.ShapeDtypeStruct
    slotted = (ROW_PARTS, SLOT_ROWS)
    wide = pltpu.VMEM(slotted + (ada_width,), jnp.float32)
    narrow = pltpu.VMEM(slotted + (depth,), jnp.float32)
    return pl.pallas_call(
        front_kernel,
        out_shape=(
            shape((ROW_PARTS,) + w_qkv.shape, jnp.bfloat16),
            shape((ROW_PARTS,) + w_out.shape, jnp.bfloat16),
            shape((ROW_PARTS,) + w_fc1.shape, jnp.bfloat16),
            shape((HEAD_PARTS,) + patches.shape, jnp.bfloat16),
            shape((HEAD_PARTS,) + patches.shape, jnp.bfloat16),
            shape(slotted + (depth,), jnp.float32),
            shape(slotted + (ada_width,), jnp.float32),
            shape((ROW_PARTS,) + ids.shape, jnp.int32),
        ),
        in_specs=[VMEM_SPEC] * 9,
        out_specs=[ANY_SPEC] * 5 + [VMEM_SPEC] * 3,
        scratch_shapes=[narrow] * 2
        + [wide] * 5
        + [
            DMA((4, 7)),
            DMA((4, 7)),
            DMA((2,)),
            DMA((2,)),
            DMA((2, 3)),
            DMA((2, 3)),
            DMA((3, 7)),
            DMA((3, 7)),
            DMA((1, 7)),
            DMA((1, 7)),
            DMA((3, 7)),
            DMA((3, 7)),
            DMA((5,)),
        ],
        compiler_params=pltpu.CompilerParams(
            collective_id=0, has_side_effects=True, vmem_limit_bytes=GRANT
        ),
        name="front",
    )(ids, time_table, class_table, w_ada, patches, cotangent, w_qkv, w_out, w_fc1)


class HeadReduce:
    def __init__(self, partial, beside_in, pair, across_in, sends, recvs):
        row, member, sibling, partner, opposite = places()
        self.member = member
        self.partner = partner
        self.partial = partial
        self.beside_in = beside_in
        self.pair = pair
        self.across_in = across_in
        self.first = to_head(
            partial.at[opposite], beside_in.at[1], sends.at[0], recvs.at[0], sibling
        )
        self.second = to_head(
            partial.at[sibling], beside_in.at[0], sends.at[1], recvs.at[1], sibling
        )
        self.across = to_head(pair, across_in, sends.at[2], recvs.at[2], partner)

    def start(self):
        self.first.start()
        self.second.start()

    def send_pair(self):
        self.first.wait_recv()
        self.pair[...] = (
            self.partial[self.partner].astype(jnp.float32)
            + self.beside_in[1].astype(jnp.float32)
        ).astype(jnp.bfloat16)
        self.across.start()

    def settle(self):
        self.second.wait_recv()
        self.across.wait_recv()

    def rows(self, part):
        return (
            self.partial[self.member, part].astype(jnp.float32)
            + self.beside_in[0, part].astype(jnp.float32)
            + self.across_in[part].astype(jnp.float32)
        )

    def finish(self):
        self.first.wait_send()
        self.second.wait_send()
        self.across.wait_send()


class RowReduce:
    def __init__(self, partial, chunk, buffers, total, sends, recvs):
        row = lax.axis_index("rows")
        self.level = row // 2
        self.side = lax.rem(row, 2)
        mate = row + 1 - 2 * self.side
        self.partial = partial
        self.mate_in, self.pair, self.straight_in = buffers
        self.total = total
        size = total.shape[0]
        self.part = pl.ds(chunk * size, size)
        self.beside = to_row(
            partial.at[:, 1 - self.side, self.part], self.mate_in, sends.at[0], recvs.at[0], mate
        )
        self.straight = []
        for step in range(1, 4):
            target = lax.rem(self.level + step, 4)
            self.straight.append(
                to_row(
                    self.pair.at[target],
                    self.straight_in.at[step - 1],
                    sends.at[step],
                    recvs.at[step],
                    target * 2 + self.side,
                )
            )

    def start(self):
        self.beside.start()

    def send_pair(self):
        self.beside.wait_recv()

        def one(level, carry):
            self.pair[level] = (
                self.partial[level, self.side, self.part].astype(jnp.float32)
                + self.mate_in[level].astype(jnp.float32)
            ).astype(jnp.bfloat16)
            return carry

        lax.fori_loop(0, 4, one, 0)
        for copy in self.straight:
            copy.start()

    def finish(self):
        for copy in self.straight:
            copy.wait_recv()
        self.total[...] = (
            self.pair[self.level].astype(jnp.float32)
            + self.straight_in[0].astype(jnp.float32)
            + self.straight_in[1].astype(jnp.float32)
            + self.straight_in[2].astype(jnp.float32)
        )
        self.beside.wait_send()
        for copy in self.straight:
            copy.wait_send()


class Reduces:
    def __init__(self, jobs, buffers, sends, recvs):
        self.units = [
            RowReduce(
                partial,
                chunk,
                buffers[3 * place : 3 * place + 3],
                total,
                sends.at[place],
                recvs.at[place],
            )
            for place, (partial, chunk, total) in enumerate(jobs)
        ]
        self.done = 0

    def start(self):
        for unit in self.units[:2]:
            unit.start()

    def advance(self):
        place = self.done
        self.done += 1
        self.units[place].send_pair()
        if place + 2 < len(self.units):
            self.units[place + 2].start()
        if place > 0:
            self.units[place - 1].finish()

    def finish(self):
        while self.done < len(self.units):
            self.advance()
        self.units[-1].finish()


def reduce_scratch(sizes):
    landing = []
    for rows, columns in sizes:
        landing += [
            pltpu.VMEM((4, rows, columns), jnp.bfloat16),
            pltpu.VMEM((4, rows, columns), jnp.bfloat16),
            pltpu.VMEM((3, rows, columns), jnp.bfloat16),
        ]
    return landing + [DMA((len(sizes), 4)), DMA((len(sizes), 4))]


def picked(vectors, part_index, segments, width):
    wide = jnp.broadcast_to(segments, (segments.shape[0], width))
    slot_count = vectors.shape[1]
    chosen = vectors[part_index, slot_count - 1 : slot_count]
    for slot in range(slot_count - 2, -1, -1):
        chosen = jnp.where(wide == slot, vectors[part_index, slot : slot + 1], chosen)
    return chosen


def centre_rows(values):
    centred = values - jnp.mean(values, axis=1, keepdims=True)
    factor = lax.rsqrt(jnp.mean(centred * centred, axis=1, keepdims=True) + EPSILON)
    return centred * factor, factor


def middle_kernel(
    mixed_ref,
    out_ref,
    fc1_ref,
    fc2_ref,
    cotangent_ref,
    patches_ref,
    segments_ref,
    hot_ref,
    vectors_ref,
    bias_ref,
    ffn_rows,
    hidden_rows,
    active_rows,
    inner_grad,
    ffn_part,
    after_ref,
    after_grad,
    attn_grad,
    slot_sums,
    inner_bias,
    fc2_part,
    fc1_part,
    fc2_head,
    fc2_neck,
    fc2_full,
    active_grad,
    first_part,
    second_part,
    first_beside,
    second_beside,
    first_pair,
    second_pair,
    first_across,
    second_across,
    attn_out,
    gather_send,
    gather_recv,
    reduce_send,
    reduce_recv,
    fc2_send,
    fc2_recv,
    local_sem,
    *reducing,
):
    row, member, sibling, partner, opposite = places()
    greet(range(1, ROW_PARTS), (sibling, partner))
    tok_rows, model_width = patches_ref.shape
    gather_fc2 = RowGather(fc2_ref, fc2_full, fc2_send, fc2_recv, local_sem, 3)
    gather_fc2.own.start()
    gather_fc2.start(0)
    gather_fc2.start(1)
    first = HeadReduce(
        first_part, first_beside, first_pair, first_across, reduce_send.at[0], reduce_recv.at[0]
    )
    second = HeadReduce(
        second_part,
        second_beside,
        second_pair,
        second_across,
        reduce_send.at[1],
        reduce_recv.at[1],
    )
    gather_hidden = HeadGather(None, hidden_rows, gather_send.at[0], gather_recv.at[0], None)
    gather_grad = HeadGather(None, attn_grad, gather_send.at[1], gather_recv.at[1], None)

    def project(block):
        first_part[block] = times_transposed(mixed_ref[block], out_ref[...]).astype(jnp.bfloat16)

    project(opposite)
    first.first.start()
    project(partner)
    first.send_pair()
    project(sibling)
    first.second.start()
    project(member)

    def scale_cotangent(block, carry):
        index = block // 2
        part = pl.ds(pl.multiple_of(lax.rem(block, 2) * 128, 128), 128)
        ffn_rows[index, part] = (
            picked(vectors_ref, 5, segments_ref[index, part], model_width)
            * cotangent_ref[index, part].astype(jnp.float32)
        ).astype(jnp.bfloat16)
        return carry

    lax.fori_loop(0, 2 * HEAD_PARTS, scale_cotangent, 0)
    gather_fc2.relay(0)
    gather_fc2.start(2)
    first.settle()

    def second_norm(block, carry):
        part = pl.ds(pl.multiple_of(block * 128, 128), 128)
        segments = segments_ref[member, part]
        out = first.rows(part) + bias_ref[0:1]
        after = patches_ref[part].astype(jnp.float32) + (
            picked(vectors_ref, 2, segments, model_width) * out
        )
        attn_out[part] = out
        after_ref[part] = after
        normed, _ = centre_rows(after)
        hidden_rows[member, part] = (
            normed * (1.0 + picked(vectors_ref, 4, segments, model_width))
            + picked(vectors_ref, 3, segments, model_width)
        ).astype(jnp.bfloat16)
        return carry

    lax.fori_loop(0, tok_rows // 128, second_norm, 0)
    gather_hidden.start()
    gather_fc2.relay(1)
    gather_fc2.relay(2)
    gather_fc2.finish()
    fc2 = fc2_full.reshape(fc1_ref.shape)

    def through_fc2(block, carry):
        active_grad[block] = jnp.dot(
            ffn_rows[block], fc2[...], preferred_element_type=jnp.float32
        )
        return carry

    lax.fori_loop(0, HEAD_PARTS, through_fc2, 0)
    inner_bias[...] = jnp.zeros_like(inner_bias)

    def feed(block, carry):
        inner = jnp.dot(
            hidden_rows[block], fc1_ref[...], preferred_element_type=jnp.float32
        ) + bias_ref[1:2]
        square = inner * inner
        bent = jnp.tanh(TANH_COEFF * (inner + 0.044715 * square * inner))
        half = 0.5 * (1.0 + bent)
        active_rows[block] = (inner * half).astype(jnp.bfloat16)
        slope = half + 0.5 * inner * (1.0 - bent * bent) * (
            TANH_COEFF * (1.0 + 3.0 * 0.044715 * square)
        )
        grad = (active_grad[block] * slope).astype(jnp.bfloat16)
        inner_grad[block] = grad
        inner_bias[...] += jnp.sum(
            grad.astype(jnp.float32).reshape(tok_rows // 8, 8, inner.shape[1]), axis=0
        )
        return carry

    def return_fc1(block, carry):
        second_part[block] = times_transposed(inner_grad[block], fc1_ref[...]).astype(jnp.bfloat16)
        return carry

    direction = sibling - member
    gather_hidden.wait_sibling()
    lax.fori_loop(0, 2, lambda step, carry: feed(member + step * direction, carry), 0)
    gather_hidden.wait_partner()
    gather_hidden.wait_opposite()

    def feed_far(step, carry):
        block = opposite - step * direction
        feed(block, carry)
        return return_fc1(block, carry)

    lax.fori_loop(0, 2, feed_far, 0)
    second.first.start()
    second.send_pair()
    lax.fori_loop(0, 2, lambda step, carry: return_fc1(sibling - step * direction, carry), 0)
    second.second.start()

    def forward_fc2(block, carry):
        ffn_part[block] = times_transposed(active_rows[block], fc2[...]).astype(jnp.bfloat16)
        return carry

    def weight_grad(left, right, target):
        height = HEAD_PARTS * tok_rows
        grad = contract_rows(
            left[...].reshape(height, left.shape[2]), right[...].reshape(height, right.shape[2])
        )
        target[...] = grad.astype(jnp.bfloat16).reshape(target.shape)

    weight_grad(ffn_rows, active_rows, fc2_part)
    reduces = Reduces(
        ((fc2_part, 0, fc2_head), (fc2_part, 1, fc2_neck)),
        reducing[:-2],
        reducing[-2],
        reducing[-1],
    )
    reduces.start()
    lax.fori_loop(0, HEAD_PARTS, forward_fc2, 0)
    slot_sums[...] = jnp.zeros_like(slot_sums)
    second.settle()

    def second_back(block, carry):
        part = pl.ds(pl.multiple_of(block * 128, 128), 128)
        segments = segments_ref[member, part]
        grad = second.rows(part)
        normed, factor = centre_rows(after_ref[part])
        weighted = grad * (1.0 + picked(vectors_ref, 4, segments, model_width))
        total = cotangent_ref[member, part].astype(jnp.float32) + factor * (
            weighted
            - jnp.mean(weighted, axis=1, keepdims=True)
            - normed * jnp.mean(weighted * normed, axis=1, keepdims=True)
        )
        after_grad[part] = total
        attn_grad[member, part] = (
            picked(vectors_ref, 2, segments, model_width) * total
        ).astype(jnp.bfloat16)
        hot = hot_ref[:, part]
        for index, term in enumerate((total * attn_out[part], grad, grad * normed)):
            slot_sums[index] += jnp.dot(
                hot, term, precision=HIGH, preferred_element_type=jnp.float32
            )
        return carry

    lax.fori_loop(0, tok_rows // 128, second_back, 0)
    gather_grad.start()
    weight_grad(hidden_rows, inner_grad, fc1_part)
    reduces.advance()
    gather_grad.wait_sibling()
    gather_grad.wait_partner()
    gather_grad.wait_opposite()
    reduces.finish()
    gather_hidden.finish()
    gather_grad.finish()
    first.finish()
    second.finish()


def middle(mixed, w_out, w_fc1, w_fc2, cotangent, patches, segments, hot, vectors, biases):
    shape = jax.ShapeDtypeStruct
    tok_rows, model_width = patches.shape
    hidden_width = w_fc1.shape[1]
    width_part = w_fc2.shape[0]
    rows_low = shape((HEAD_PARTS, tok_rows, model_width), jnp.bfloat16)
    wide_low = shape((HEAD_PARTS, tok_rows, hidden_width), jnp.bfloat16)
    own = shape((tok_rows, model_width), jnp.float32)
    own_low = pltpu.VMEM((tok_rows, model_width), jnp.bfloat16)
    group_low = pltpu.VMEM((HEAD_PARTS, tok_rows, model_width), jnp.bfloat16)
    pair_low = pltpu.VMEM((2, tok_rows, model_width), jnp.bfloat16)
    return pl.pallas_call(
        middle_kernel,
        out_shape=[
            rows_low,
            rows_low,
            wide_low,
            wide_low,
            rows_low,
            own,
            own,
            rows_low,
            shape((3, SLOT_ROWS, model_width), jnp.float32),
            shape((8, hidden_width), jnp.float32),
            shape((4, 2, width_part, hidden_width), jnp.bfloat16),
            shape((4, 2, width_part, hidden_width), jnp.bfloat16),
            shape((width_part // 3, hidden_width), jnp.float32),
            shape((width_part // 3, hidden_width), jnp.float32),
        ],
        in_specs=[VMEM_SPEC] * 10,
        out_specs=[VMEM_SPEC] * 14,
        scratch_shapes=[
            pltpu.VMEM((ROW_PARTS,) + w_fc2.shape, jnp.bfloat16),
            pltpu.VMEM((HEAD_PARTS, tok_rows, hidden_width), jnp.float32),
            group_low,
            group_low,
            pair_low,
            pair_low,
            own_low,
            own_low,
            own_low,
            own_low,
            pltpu.VMEM((tok_rows, model_width), jnp.float32),
            DMA((2, 3)),
            DMA((2, 3)),
            DMA((2, 3)),
            DMA((2, 3)),
            DMA((3, 7)),
            DMA((3, 7)),
            DMA(()),
        ]
        + reduce_scratch([(width_part // 3, hidden_width)] * 2),
        compiler_params=pltpu.CompilerParams(
            collective_id=2, has_side_effects=True, vmem_limit_bytes=GRANT
        ),
        name="middle",
    )(mixed, w_out, w_fc1, w_fc2, cotangent, patches, segments, hot, vectors, biases)


HEAD_LANES = 128


def attend_back_kernel(
    projected_ref,
    grad_ref,
    out_ref,
    totals_ref,
    keys_image,
    rows_image,
    fc2_part,
    fc1_part,
    qkv_grad,
    fc2_tail,
    fc1_head,
    fc1_neck,
    parts,
    mixed_grad,
    key_columns,
    grad_queries,
    grad_keys,
    grad_values,
    bias,
    packed,
    *reducing,
):
    greet(range(1, ROW_PARTS), ())
    reduces = Reduces(
        ((fc2_part, 2, fc2_tail), (fc1_part, 0, fc1_head), (fc1_part, 1, fc1_neck)),
        reducing[:-2],
        reducing[-2],
        reducing[-1],
    )
    reduces.start()
    blocks, tok_rows, width = projected_ref.shape
    head_local = totals_ref.shape[0]
    head_size = width // (3 * head_local)
    scale_factor = 1.0 / math.sqrt(head_size)
    parts[...] = jnp.zeros_like(parts)
    mixed_grad[...] = jnp.zeros_like(mixed_grad)

    def unpack(block, carry):
        rows = pl.ds(pl.multiple_of(block * tok_rows, tok_rows), tok_rows)
        packed[...] = projected_ref[block].astype(jnp.float32)
        for part in range(3 * head_local):
            parts[part, rows, 0:head_size] = packed[
                :, part * head_size : (part + 1) * head_size
            ].astype(jnp.bfloat16)
        packed[:, 0 : head_local * head_size] = jnp.dot(
            grad_ref[block], out_ref[...], preferred_element_type=jnp.float32
        )
        for head in range(head_local):
            mixed_grad[head, rows, 0:head_size] = packed[
                :, head * head_size : (head + 1) * head_size
            ].astype(jnp.bfloat16)
        return carry

    lax.fori_loop(0, blocks, unpack, 0)

    def turn(head, carry):
        key_columns[head] = parts[3 * head + 1].astype(jnp.float32).T.astype(jnp.bfloat16)
        return carry

    lax.fori_loop(0, head_local, turn, 0)
    grad_keys[...] = jnp.zeros_like(grad_keys)
    grad_values[...] = jnp.zeros_like(grad_values)
    seq_len = blocks * tok_rows

    for block in range(blocks):
        rows = pl.ds(block * tok_rows, tok_rows)
        same = jnp.broadcast_to(keys_image[...], (seq_len, tok_rows)) == jnp.broadcast_to(
            rows_image[block], (seq_len, tok_rows)
        )
        bias[...] = jnp.where(same, 0.0, MASKED)

        def one_head(head, carry):
            query = parts[3 * head, rows]
            grad = mixed_grad[head, rows]
            scores = times_transposed(parts[3 * head + 1], query) * scale_factor + bias[...]
            probs = jnp.exp(scores - totals_ref[head, block])
            grad_probs = times_transposed(parts[3 * head + 2], grad)
            inner = jnp.sum(probs * grad_probs, axis=0, keepdims=True)
            grad_scores = (probs * (grad_probs - inner)).astype(jnp.bfloat16)
            grad_values[head] += jnp.dot(
                probs.astype(jnp.bfloat16), grad, preferred_element_type=jnp.float32
            )
            grad_keys[head] += jnp.dot(grad_scores, query, preferred_element_type=jnp.float32)
            grad_queries[head, rows] = jnp.dot(
                key_columns[head], grad_scores, preferred_element_type=jnp.float32
            ).T
            return carry

        lax.fori_loop(0, head_local, one_head, 0)
        if block > 0:
            reduces.advance()

    def pack(block, carry):
        rows = pl.ds(pl.multiple_of(block * tok_rows, tok_rows), tok_rows)
        for head in range(head_local):
            for place, (grads, factor) in enumerate(
                ((grad_queries, scale_factor), (grad_keys, scale_factor), (grad_values, None))
            ):
                start = (3 * head + place) * head_size
                term = grads[head, rows, 0:head_size]
                packed[:, start : start + head_size] = term if factor is None else term * factor
        qkv_grad[block] = packed[...].astype(jnp.bfloat16)
        return carry

    lax.fori_loop(0, blocks, pack, 0)
    reduces.finish()


def attend_back(
    projected, grad, w_out, totals, keys_image, rows_image, grad_w_fc2, grad_w_fc1
):
    shape = jax.ShapeDtypeStruct
    blocks, tok_rows, width = projected.shape
    head_local = totals.shape[0]
    seq_len = blocks * tok_rows
    width_part, hidden_width = grad_w_fc2.shape[2:]
    third = (width_part // 3, hidden_width)
    wide = pltpu.VMEM((head_local, seq_len, HEAD_LANES), jnp.float32)
    return pl.pallas_call(
        attend_back_kernel,
        out_shape=[shape(projected.shape, jnp.bfloat16)] + [shape(third, jnp.float32)] * 3,
        in_specs=[VMEM_SPEC] * 8,
        out_specs=[VMEM_SPEC] * 4,
        scratch_shapes=[
            pltpu.VMEM((3 * head_local, seq_len, HEAD_LANES), jnp.bfloat16),
            pltpu.VMEM((head_local, seq_len, HEAD_LANES), jnp.bfloat16),
            pltpu.VMEM((head_local, HEAD_LANES, seq_len), jnp.bfloat16),
            wide,
            wide,
            wide,
            pltpu.VMEM((seq_len, tok_rows), jnp.float32),
            pltpu.VMEM((tok_rows, width), jnp.float32),
        ]
        + reduce_scratch([third] * 3),
        compiler_params=pltpu.CompilerParams(
            collective_id=3, has_side_effects=True, vmem_limit_bytes=GRANT
        ),
        name="attend_back",
    )(projected, grad, w_out, totals, keys_image, rows_image, grad_w_fc2, grad_w_fc1)


def back_kernel(
    hidden_ref,
    fc1_part,
    qkv_part,
    out_part,
    bias_ref,
    patches_ref,
    after_ref,
    scale_ref,
    hot_ref,
    sums_ref,
    silu_ref,
    slope_ref,
    bucket_ref,
    label_ref,
    ada_ref,
    ffn_ref,
    block_ref,
    gate_ref,
    cotangent_ref,
    ffn_bias,
    block_out,
    patches_grad,
    time_grad,
    class_grad,
    ada_grad,
    ada_bias,
    fc1_tail,
    qkv_head,
    qkv_neck,
    qkv_tail,
    out_grad,
    bias_sum,
    beside_in,
    pair_rows,
    across_in,
    ffn_beside,
    ffn_pair,
    ffn_across,
    slot_sums,
    mods_own,
    mods_sibling,
    mods_pair,
    mods_partner,
    mods_low,
    mods_cols,
    bias_all,
    silu_part,
    silu_in,
    silu_all,
    small_send,
    small_recv,
    pair_send,
    pair_recv,
    head_send,
    head_recv,
    *reducing,
):
    row, member, sibling, partner, opposite = places()
    greet(range(1, ROW_PARTS), (sibling, partner))
    others = [(step, lax.rem(row + step, ROW_PARTS)) for step in range(1, ROW_PARTS)]

    def spread(stage, source_of, target):
        copies = []
        for step, other in others:
            copy = to_row(
                source_of(other),
                target.at[row],
                small_send.at[stage, step - 1],
                small_recv.at[stage, step - 1],
                other,
            )
            copy.start()
            copies.append(copy)
        return copies

    def settle(copies):
        for copy in copies:
            copy.wait()

    reduce_rows = HeadReduce(
        hidden_ref, beside_in, pair_rows, across_in, head_send.at[0], head_recv.at[0]
    )
    reduce_ffn = HeadReduce(
        ffn_ref, ffn_beside, ffn_pair, ffn_across, head_send.at[1], head_recv.at[1]
    )
    reduce_rows.start()
    reduce_ffn.start()
    reduces = Reduces(
        (
            (fc1_part, 2, fc1_tail),
            (qkv_part, 0, qkv_head),
            (qkv_part, 1, qkv_neck),
            (qkv_part, 2, qkv_tail),
            (out_part, 0, out_grad),
        ),
        reducing[:-2],
        reducing[-2],
        reducing[-1],
    )
    reduces.start()
    reduce_rows.send_pair()
    reduce_ffn.send_pair()
    reduces.advance()
    reduce_rows.settle()
    tok_rows = patches_ref.shape[0]
    model_width = patches_ref.shape[1]
    slot_sums[...] = jnp.zeros_like(slot_sums)

    def rows_back(block, carry):
        part = pl.ds(pl.multiple_of(block * 128, 128), 128)
        grad = reduce_rows.rows(part)
        normed, factor = centre_rows(patches_ref[part].astype(jnp.float32))
        weighted = grad * scale_ref[part]
        patches_grad[part] = after_ref[part] + factor * (
            weighted
            - jnp.mean(weighted, axis=1, keepdims=True)
            - normed * jnp.mean(weighted * normed, axis=1, keepdims=True)
        )
        hot = hot_ref[:, part]
        slot_sums[0] += jnp.dot(hot, grad, precision=HIGH, preferred_element_type=jnp.float32)
        slot_sums[1] += jnp.dot(
            hot, grad * normed, precision=HIGH, preferred_element_type=jnp.float32
        )
        return carry

    lax.fori_loop(0, tok_rows // 128, rows_back, 0)
    reduce_ffn.settle()

    def rows_out(block, carry):
        part = pl.ds(pl.multiple_of(block * 128, 128), 128)
        ffn = reduce_ffn.rows(part) + ffn_bias[0:1]
        block_out[part] = (block_ref[part] + gate_ref[part] * ffn).astype(jnp.bfloat16)
        slot_sums[2] += jnp.dot(
            hot_ref[:, part],
            cotangent_ref[part].astype(jnp.float32) * ffn,
            precision=HIGH,
            preferred_element_type=jnp.float32,
        )
        return carry

    lax.fori_loop(0, tok_rows // 128, rows_out, 0)
    ada_width = ada_ref.shape[1]
    fine = ada_width // 3
    for unit in range(3 * ROW_PARTS):
        part_index, within = divmod(unit * fine, model_width)
        span = slice(within, within + fine)
        if part_index < 2:
            source = slot_sums[part_index, :, span]
        elif part_index == 5:
            source = slot_sums[2, :, span]
        else:
            source = sums_ref[part_index - 2, :, span]
        mods_own[unit // 3, :, unit % 3 * fine : (unit % 3 + 1) * fine] = source
    beside = to_head(mods_own, mods_sibling, pair_send.at[0], pair_recv.at[0], sibling)
    beside.start()
    reduces.advance()
    beside.wait()
    mods_pair[...] = mods_own[...] + mods_sibling[...]
    across = to_head(mods_pair, mods_partner, pair_send.at[1], pair_recv.at[1], partner)
    across.start()
    across.wait()
    mods_low[...] = (
        (mods_pair[...] + mods_partner[...]).astype(jnp.bfloat16).astype(jnp.float32)
    )
    copies = spread(0, lambda other: mods_low.at[other], mods_cols)
    bias_copies = spread(1, lambda other: bias_ref, bias_all)
    mods_cols[row] = mods_low[row]
    bias_all[row] = bias_ref[...]
    settle(copies)
    slots = ROW_PARTS * SLOT_ROWS
    cols = mods_cols[...].reshape(slots, ada_width)
    low = cols.astype(jnp.bfloat16)
    ada_grad[...] = jnp.dot(silu_ref[...], low, preferred_element_type=jnp.float32)
    ada_bias[...] = jnp.broadcast_to(jnp.sum(cols, axis=0, keepdims=True), ada_bias.shape)
    silu_part[...] = times_transposed(low, ada_ref[...]).reshape(silu_part.shape)
    copies = spread(2, lambda other: silu_part.at[other], silu_in)
    silu_in[row] = silu_part[row]
    settle(bias_copies)
    bias_sum[...] = jnp.sum(bias_all[...], axis=0)
    reduces.advance()
    settle(copies)
    summed = jnp.sum(silu_in[...], axis=0)
    silu_all[row] = summed
    silu_part[row] = summed
    copies = spread(3, lambda other: silu_part.at[row], silu_all)
    reduces.advance()
    settle(copies)
    grad_condition = silu_all[...].reshape(slots, silu_all.shape[2]) * slope_ref[...]
    time_grad[...] = jnp.dot(
        bucket_ref[...], grad_condition, precision=HIGH, preferred_element_type=jnp.float32
    )
    class_grad[...] = jnp.dot(
        label_ref[...], grad_condition, precision=HIGH, preferred_element_type=jnp.float32
    )
    reduces.finish()
    reduce_rows.finish()
    reduce_ffn.finish()


def back(
    hidden,
    grad_w_fc1,
    grad_w_qkv,
    grad_w_out,
    biases,
    patches,
    grad_after,
    scales,
    hot,
    sums,
    silu_columns,
    slopes,
    buckets,
    labels,
    w_ada,
    ffn,
    after,
    gates,
    cotangent,
    ffn_bias,
):
    shape = jax.ShapeDtypeStruct
    tok_rows, model_width = patches.shape
    depth, ada_width = w_ada.shape
    table_rows = buckets.shape[0]
    weights = (grad_w_fc1, grad_w_qkv, grad_w_out)
    thirds = [(weight.shape[2] // 3, weight.shape[3]) for weight in (grad_w_fc1, grad_w_qkv)]
    sizes = [thirds[0]] + [thirds[1]] * 3 + [grad_w_out.shape[2:]]
    totals = [shape(size, jnp.float32) for size in sizes]
    slotted = (ROW_PARTS, SLOT_ROWS)
    wide = pltpu.VMEM(slotted + (ada_width,), jnp.float32)
    narrow = pltpu.VMEM(slotted + (depth,), jnp.float32)
    return pl.pallas_call(
        back_kernel,
        out_shape=[
            shape((tok_rows, model_width), jnp.bfloat16),
            shape((tok_rows, model_width), jnp.float32),
            shape((table_rows, depth), jnp.float32),
            shape((table_rows, depth), jnp.float32),
            shape((depth, ada_width), jnp.float32),
            shape((SLOT_ROWS, ada_width), jnp.float32),
        ]
        + totals
        + [shape(biases.shape, jnp.float32)],
        in_specs=[VMEM_SPEC] * 20,
        out_specs=[VMEM_SPEC] * 12,
        scratch_shapes=[
            pltpu.VMEM((2, tok_rows, model_width), jnp.bfloat16),
            pltpu.VMEM((tok_rows, model_width), jnp.bfloat16),
            pltpu.VMEM((tok_rows, model_width), jnp.bfloat16),
        ]
        * 2
        + [pltpu.VMEM((3, SLOT_ROWS, model_width), jnp.float32)]
        + [wide] * 6
        + [pltpu.VMEM((ROW_PARTS,) + biases.shape, jnp.float32)]
        + [narrow] * 3
        + [
            DMA((4, 7)),
            DMA((4, 7)),
            DMA((2,)),
            DMA((2,)),
            DMA((2, 3)),
            DMA((2, 3)),
        ]
        + reduce_scratch(sizes),
        compiler_params=pltpu.CompilerParams(
            collective_id=1, has_side_effects=True, vmem_limit_bytes=GRANT
        ),
        name="back",
    )(
        hidden,
        *weights,
        biases,
        patches,
        grad_after,
        scales,
        hot,
        sums,
        silu_columns,
        slopes,
        buckets,
        labels,
        w_ada,
        ffn,
        after,
        gates,
        cotangent,
        ffn_bias,
    )


def shards_linked(
    patches,
    time_table,
    class_table,
    w_ada,
    b_ada,
    w_qkv,
    b_qv,
    w_out,
    b_out,
    w_fc1,
    b_fc1,
    w_fc2,
    b_fc2,
    image_lengths,
    segment_ids,
    bucket_ids,
    class_labels,
    cotangent,
):
    head_parts = lax.axis_size("heads")
    member = lax.axis_index("heads")
    tok_rows = patches.shape[0]
    model_width = patches.shape[1]
    seq_count = segment_ids.shape[0]
    seq_len = segment_ids.shape[1]
    slot_count = image_lengths.shape[1]
    image_count = seq_count * slot_count
    group_rows = tok_rows * head_parts
    head_local = b_qv.shape[0]
    head_size = b_qv.shape[1] // 2
    block_rows = min(BLOCK_LIMIT, seq_len)
    scale_factor = 1.0 / math.sqrt(head_size)
    row_parts = lax.axis_size("rows")
    table_rows = time_table.shape[0]
    ada_width = w_ada.shape[1]
    every_slot = row_parts * SLOT_ROWS
    slot_pad = jnp.full((SLOT_ROWS - slot_count,), -1, jnp.int32)
    ids = jnp.broadcast_to(
        jnp.concatenate([bucket_ids[0], slot_pad, class_labels[0], slot_pad])[:, None],
        (2 * SLOT_ROWS, table_rows),
    )
    (
        qkv_full,
        out_full,
        fc1_full,
        patches_full,
        cotangent_full,
        condition,
        mods,
        ids_all,
    ) = front(ids, time_table, class_table, w_ada, patches, cotangent, w_qkv, w_out, w_fc1)
    qkv_cols = qkv_full.reshape(model_width, w_qkv.shape[1])
    out_cols = out_full.reshape(model_width, w_out.shape[1])
    fc1_cols = fc1_full.reshape(model_width, w_fc1.shape[1])
    condition = condition.reshape(every_slot, condition.shape[2])
    silu_value, silu_pull = jax.vjp(silu_plain, condition)
    silu_low = silu_value.astype(jnp.bfloat16)
    mods_all = mods[:, :slot_count].transpose(1, 0, 2).reshape(
        slot_count, row_parts * ada_width
    ) + b_ada.astype(jnp.float32)
    row_segments = segment_ids[0][:, None]

    def by_token(part_index, segments):
        vectors = mods_all[:, part_index * model_width : (part_index + 1) * model_width]
        chosen = vectors[slot_count - 1][None, :]
        for slot in range(slot_count - 2, -1, -1):
            chosen = jnp.where(segments == slot, vectors[slot][None, :], chosen)
        return chosen

    own_segments = lax.dynamic_slice_in_dim(segment_ids[0], member * tok_rows, tok_rows)[:, None]
    token_hot = (own_segments == jnp.arange(SLOT_ROWS, dtype=jnp.int32)[None, :]).astype(
        jnp.float32
    )
    scale_attn = by_token(1, own_segments)
    gate_mlp = by_token(5, own_segments)
    rows_one = modulate(
        patches_full.reshape(group_rows, model_width).astype(jnp.float32),
        by_token(0, row_segments),
        by_token(1, row_segments),
    ).astype(jnp.bfloat16)
    zero_bias = jnp.zeros((head_local, head_size), b_qv.dtype)
    qkv_bias = (
        jnp.concatenate([b_qv[:, :head_size], zero_bias, b_qv[:, head_size:]], axis=1)
        .reshape(head_local * 3 * head_size)
        .astype(jnp.float32)
    )
    projected = (jnp.dot(rows_one, qkv_cols, preferred_element_type=jnp.float32) + qkv_bias).astype(
        jnp.bfloat16
    )
    seq_qkv = projected.reshape(seq_count, seq_len, head_local, 3, head_size)
    slot_ends = jnp.cumsum(image_lengths, axis=1)
    places = jnp.arange(seq_len, dtype=jnp.int32)
    image_of = jnp.sum((places[None, :, None] >= slot_ends[:, None, :]).astype(jnp.int32), axis=2)

    def block_scores(query_rows, key_rows, image_rows, image_cols):
        scores = (
            jnp.einsum("qhd,khd->hqk", query_rows, key_rows, preferred_element_type=jnp.float32)
            * scale_factor
        )
        return jnp.where((image_rows[:, None] == image_cols[None, :])[None], scores, MASKED)

    def attend_forward(pieces):
        seq_block, seq_image = pieces
        key_rows = seq_block[:, :, 1]
        value_rows = seq_block[:, :, 2]
        outputs = []
        totals = []
        for row_start in range(0, seq_len, block_rows):
            stop_row = row_start + block_rows
            query_rows = seq_block[row_start:stop_row, :, 0]
            scores = block_scores(query_rows, key_rows, seq_image[row_start:stop_row], seq_image)
            row_peak = jnp.max(scores, axis=2, keepdims=True)
            raised = jnp.exp(scores - row_peak)
            row_total = jnp.sum(raised, axis=2, keepdims=True)
            soft_low = (raised / row_total).astype(jnp.bfloat16)
            outputs.append(
                jnp.einsum(
                    "hqk,khd->qhd", soft_low, value_rows, preferred_element_type=jnp.float32
                ).astype(jnp.bfloat16)
            )
            totals.append((row_peak + jnp.log(row_total))[:, :, 0])
        return (jnp.concatenate(outputs, axis=0), jnp.concatenate(totals, axis=1))

    mixed, log_totals = lax.map(attend_forward, (seq_qkv, image_of))
    mixed_rows = mixed.reshape(group_rows, head_local * head_size)
    (
        ffn_rows,
        rows_two,
        active,
        grad_inner,
        ffn_part,
        after_attn,
        grad_after,
        attn_rows_grad,
        sums,
        inner_bias,
        grad_w_fc2,
        grad_w_fc1,
        fc2_head,
        fc2_neck,
    ) = middle(
        mixed_rows.reshape(head_parts, tok_rows, mixed_rows.shape[1]),
        out_cols,
        fc1_cols,
        w_fc2,
        cotangent_full,
        patches,
        segment_ids.reshape(head_parts, tok_rows, 1),
        token_hot.T,
        mods_all.reshape(slot_count, 6, model_width).transpose(1, 0, 2),
        jnp.stack([b_out, b_fc1]).astype(jnp.float32),
    )
    ffn_rows = ffn_rows.reshape(group_rows, model_width)
    grad_b_fc2 = jnp.sum(ffn_rows, axis=0, dtype=jnp.float32)
    grad_b_fc1 = jnp.sum(inner_bias, axis=0)
    grad_qkv, fc2_tail, fc1_head, fc1_neck = attend_back(
        projected.reshape(head_parts, tok_rows, projected.shape[1]),
        attn_rows_grad,
        out_cols,
        log_totals.reshape(head_local, head_parts, 1, tok_rows),
        image_of.reshape(seq_len, 1),
        image_of.reshape(head_parts, 1, tok_rows),
        grad_w_fc2,
        grad_w_fc1,
    )
    grad_qkv = grad_qkv.reshape(group_rows, head_local * 3 * head_size)
    attn_rows_grad = attn_rows_grad.reshape(group_rows, model_width)
    grad_w_out = contract_rows(attn_rows_grad, mixed_rows)
    grad_b_out = jnp.sum(attn_rows_grad, axis=0, dtype=jnp.float32)
    grad_w_qkv = contract_rows(rows_one, grad_qkv)
    bias_terms = jnp.sum(grad_qkv, axis=0, dtype=jnp.float32).reshape(head_local, 3, head_size)
    grad_b_qv = jnp.concatenate([bias_terms[:, 0], bias_terms[:, 2]], axis=1)
    grad_hidden_one = times_transposed(grad_qkv, qkv_cols).astype(jnp.bfloat16)
    all_ids = ids_all[:, :, 0]
    table_places = lax.axis_index("rows") * table_rows + jnp.arange(table_rows, dtype=jnp.int32)
    bucket_hot = table_places[:, None] == all_ids[:, :SLOT_ROWS].reshape(every_slot)[None, :]
    label_hot = table_places[:, None] == all_ids[:, SLOT_ROWS:].reshape(every_slot)[None, :]
    bias_flat = jnp.concatenate([grad_b_qv.reshape(-1), grad_b_fc1, grad_b_out, grad_b_fc2])
    bias_size = bias_flat.size
    bias_tiles = -(-bias_size // 1024) * 8
    biases = jnp.pad(bias_flat, (0, bias_tiles * 128 - bias_size)).reshape(bias_tiles, 128)

    def by_row(partial):
        return partial.astype(jnp.bfloat16).reshape(
            4, 2, partial.shape[0] // ROW_PARTS, partial.shape[1]
        )

    (
        block_out,
        grad_patches,
        grad_time,
        grad_class,
        grad_w_ada,
        grad_b_ada,
        fc1_tail,
        qkv_head,
        qkv_neck,
        qkv_tail,
        grad_w_out,
        bias_all,
    ) = back(
        grad_hidden_one.reshape(HEAD_PARTS, tok_rows, model_width),
        grad_w_fc1,
        by_row(grad_w_qkv),
        by_row(grad_w_out),
        biases,
        patches,
        grad_after,
        1.0 + scale_attn,
        token_hot.T,
        sums,
        silu_low.T,
        silu_pull(jnp.ones_like(condition))[0],
        bucket_hot.astype(jnp.float32),
        label_hot.astype(jnp.float32),
        w_ada,
        ffn_part,
        after_attn,
        gate_mlp,
        cotangent,
        b_fc2.astype(jnp.float32)[None, :],
    )
    grad_w_fc2 = jnp.concatenate([fc2_head, fc2_neck, fc2_tail], axis=0)
    grad_w_fc1 = jnp.concatenate([fc1_head, fc1_neck, fc1_tail], axis=0)
    grad_w_qkv = jnp.concatenate([qkv_head, qkv_neck, qkv_tail], axis=0)
    grad_b_ada = grad_b_ada[0]
    bias_all = bias_all.reshape(-1)
    bias_sizes = (grad_b_qv.size, grad_b_fc1.size, grad_b_out.size, grad_b_fc2.size)
    edges = [sum(bias_sizes[:step]) for step in range(5)]
    bias_rows = model_width // row_parts
    row_start = lax.axis_index("rows") * bias_rows
    grad_b_qv = bias_all[edges[0] : edges[1]].reshape(grad_b_qv.shape)
    grad_b_fc1 = bias_all[edges[1] : edges[2]]
    grad_b_out = lax.dynamic_slice_in_dim(bias_all[edges[2] : edges[3]], row_start, bias_rows)
    grad_b_fc2 = lax.dynamic_slice_in_dim(bias_all[edges[3] : edges[4]], row_start, bias_rows)
    return (
        block_out,
        grad_patches,
        grad_time,
        grad_class,
        grad_w_ada,
        grad_b_ada,
        grad_w_qkv,
        grad_b_qv,
        grad_w_out,
        grad_b_out,
        grad_w_fc1,
        grad_b_fc1,
        grad_w_fc2,
        grad_b_fc2,
    )


def solution(mesh):
    placed = (
        P(("rows", "heads"), None),
        P("rows", "heads"),
        P("rows", "heads"),
        P("heads", "rows"),
        P(),
        P("rows", "heads"),
        P("heads", None),
        P("rows", "heads"),
        P(),
        P("rows", "heads"),
        P("heads"),
        P("rows", "heads"),
        P(),
        P("rows", None),
        P("rows", None),
        P("rows", None),
        P("rows", None),
        P(("rows", "heads"), None),
    )
    linked = mesh.shape["rows"] == ROW_PARTS and mesh.shape["heads"] == HEAD_PARTS
    return jax.shard_map(
        shards_linked if linked else shards_plain,
        mesh=mesh,
        in_specs=placed,
        out_specs=(
            P(("rows", "heads"), None),
            P(("rows", "heads"), None),
            P("rows", "heads"),
            P("rows", "heads"),
            P("heads", "rows"),
            P("rows"),
            P("rows", "heads"),
            P("heads", None),
            P("rows", "heads"),
            P("rows"),
            P("rows", "heads"),
            P("heads"),
            P("rows", "heads"),
            P("rows"),
        ),
        check_vma=False,
    )
```

```python
import functools
import math

import jax
import jax.numpy as jnp
from jax import lax
from jax.experimental import pallas as pl
from jax.experimental.pallas import tpu as pltpu
from jax.sharding import PartitionSpec as P

EPSILON = 1e-06
MASKED = -1e30
HIGH = lax.Precision.HIGHEST
TANH_COEFF = 0.7978845608028654
BLOCK_LIMIT = 512


def layer_norm(values):
    average = jnp.mean(values, axis=-1, keepdims=True)
    centred = values - average
    variance = jnp.mean(centred * centred, axis=-1, keepdims=True)
    return centred * lax.rsqrt(variance + EPSILON)


def gelu_tanh(values):
    return (
        0.5 * values * (1.0 + jnp.tanh(TANH_COEFF * (values + 0.044715 * values * values * values)))
    )


def silu_plain(values):
    return values / (1.0 + jnp.exp(-values))


def modulate(values, shift_term, scale_term):
    return layer_norm(values) * (1.0 + scale_term) + shift_term


def contract_rows(left_matrix, right_matrix):
    return lax.dot_general(
        left_matrix, right_matrix, (((0,), (0,)), ((), ())), preferred_element_type=jnp.float32
    )


def contract_rows_exact(left_matrix, right_matrix):
    return lax.dot_general(
        left_matrix,
        right_matrix,
        (((0,), (0,)), ((), ())),
        precision=HIGH,
        preferred_element_type=jnp.float32,
    )


def times_transposed(left_matrix, right_matrix):
    return lax.dot_general(
        left_matrix, right_matrix, (((1,), (1,)), ((), ())), preferred_element_type=jnp.float32
    )


def gather_weights(w_qkv, w_out, w_fc1, w_fc2):
    return (
        lax.all_gather(w_qkv, "rows", axis=0, tiled=True),
        lax.all_gather(w_out, "rows", axis=0, tiled=True),
        lax.all_gather(w_fc1, "rows", axis=0, tiled=True),
        lax.all_gather(w_fc2, "rows", axis=0, tiled=True),
    )


def shards_plain(
    patches,
    time_table,
    class_table,
    w_ada,
    b_ada,
    w_qkv,
    b_qv,
    w_out,
    b_out,
    w_fc1,
    b_fc1,
    w_fc2,
    b_fc2,
    image_lengths,
    segment_ids,
    bucket_ids,
    class_labels,
    cotangent,
):
    head_parts = lax.axis_size("heads")
    member = lax.axis_index("heads")
    tok_rows = patches.shape[0]
    model_width = patches.shape[1]
    seq_count = segment_ids.shape[0]
    seq_len = segment_ids.shape[1]
    slot_count = image_lengths.shape[1]
    image_count = seq_count * slot_count
    group_rows = tok_rows * head_parts
    head_local = b_qv.shape[0]
    head_size = b_qv.shape[1] // 2
    block_rows = min(BLOCK_LIMIT, seq_len)
    scale_factor = 1.0 / math.sqrt(head_size)
    row_parts = lax.axis_size("rows")
    table_rows = time_table.shape[0]
    ada_width = w_ada.shape[1]
    qkv_cols, out_cols, fc1_cols, fc2_cols = gather_weights(w_qkv, w_out, w_fc1, w_fc2)
    ids_all = lax.all_gather(
        jnp.concatenate([bucket_ids, class_labels], axis=1), "rows", axis=0, tiled=True
    )
    every_slot = row_parts * image_count
    table_places = lax.axis_index("rows") * table_rows + jnp.arange(table_rows, dtype=jnp.int32)
    bucket_hot = (
        ids_all[:, :slot_count].reshape(every_slot)[:, None] == table_places[None, :]
    ).astype(jnp.bfloat16)
    label_hot = (
        ids_all[:, slot_count:].reshape(every_slot)[:, None] == table_places[None, :]
    ).astype(jnp.bfloat16)
    condition = lax.psum(
        jnp.dot(bucket_hot, time_table, preferred_element_type=jnp.float32)
        + jnp.dot(label_hot, class_table, preferred_element_type=jnp.float32),
        "rows",
    )
    silu_value, silu_pull = jax.vjp(silu_plain, condition)
    silu_low = silu_value.astype(jnp.bfloat16)
    mods_part = jnp.dot(silu_low, w_ada, preferred_element_type=jnp.float32)
    mods_cols = lax.psum(mods_part, "heads").reshape(row_parts, image_count, ada_width)
    mods_own = lax.all_to_all(mods_cols, "rows", split_axis=0, concat_axis=0, tiled=True)
    mods_all = mods_own.transpose(1, 0, 2).reshape(
        image_count, row_parts * ada_width
    ) + b_ada.astype(jnp.float32)
    positions = member * tok_rows + jnp.arange(tok_rows, dtype=jnp.int32)
    own_segments = lax.dynamic_slice_in_dim(
        segment_ids.reshape(seq_count * seq_len), member * tok_rows, tok_rows
    )
    token_image = positions // seq_len * slot_count + own_segments
    token_hot = (token_image[:, None] == jnp.arange(image_count, dtype=jnp.int32)[None, :]).astype(
        jnp.float32
    )
    token_mods = [
        jnp.dot(
            token_hot,
            mods_all[:, part_index * model_width : (part_index + 1) * model_width],
            precision=HIGH,
        )
        for part_index in range(6)
    ]
    shift_attn, scale_attn, gate_attn, shift_mlp, scale_mlp, gate_mlp = token_mods
    inputs = patches.astype(jnp.float32)
    first_value, first_pull = jax.vjp(modulate, inputs, shift_attn, scale_attn)
    hidden_one = first_value.astype(jnp.bfloat16)
    rows_one = lax.all_gather(hidden_one, "heads", axis=0, tiled=True)
    zero_bias = jnp.zeros((head_local, head_size), b_qv.dtype)
    qkv_bias = (
        jnp.concatenate([b_qv[:, :head_size], zero_bias, b_qv[:, head_size:]], axis=1)
        .reshape(head_local * 3 * head_size)
        .astype(jnp.float32)
    )
    projected = (jnp.dot(rows_one, qkv_cols, preferred_element_type=jnp.float32) + qkv_bias).astype(
        jnp.bfloat16
    )
    seq_qkv = projected.reshape(seq_count, seq_len, head_local, 3, head_size)
    slot_ends = jnp.cumsum(image_lengths, axis=1)
    places = jnp.arange(seq_len, dtype=jnp.int32)
    image_of = jnp.sum((places[None, :, None] >= slot_ends[:, None, :]).astype(jnp.int32), axis=2)

    def block_scores(query_rows, key_rows, image_rows, image_cols):
        scores = (
            jnp.einsum("qhd,khd->hqk", query_rows, key_rows, preferred_element_type=jnp.float32)
            * scale_factor
        )
        return jnp.where((image_rows[:, None] == image_cols[None, :])[None], scores, MASKED)

    def attend_forward(pieces):
        seq_block, seq_image = pieces
        key_rows = seq_block[:, :, 1]
        value_rows = seq_block[:, :, 2]
        outputs = []
        totals = []
        for row_start in range(0, seq_len, block_rows):
            stop_row = row_start + block_rows
            query_rows = seq_block[row_start:stop_row, :, 0]
            scores = block_scores(query_rows, key_rows, seq_image[row_start:stop_row], seq_image)
            row_peak = jnp.max(scores, axis=2, keepdims=True)
            raised = jnp.exp(scores - row_peak)
            row_total = jnp.sum(raised, axis=2, keepdims=True)
            soft_low = (raised / row_total).astype(jnp.bfloat16)
            outputs.append(
                jnp.einsum(
                    "hqk,khd->qhd", soft_low, value_rows, preferred_element_type=jnp.float32
                ).astype(jnp.bfloat16)
            )
            totals.append((row_peak + jnp.log(row_total))[:, :, 0])
        return (jnp.concatenate(outputs, axis=0), jnp.concatenate(totals, axis=1))

    mixed, log_totals = lax.map(attend_forward, (seq_qkv, image_of))
    mixed_rows = mixed.reshape(group_rows, head_local * head_size)
    attn_out = lax.psum_scatter(
        times_transposed(
            lax.slice_in_dim(mixed_rows, 0, tok_rows * lax.axis_size("heads"), axis=0), out_cols
        ).astype(jnp.bfloat16),
        "heads",
        scatter_dimension=0,
        tiled=True,
    ).astype(jnp.float32) + b_out.astype(jnp.float32)
    after_attn = inputs + gate_attn * attn_out
    second_value, second_pull = jax.vjp(modulate, after_attn, shift_mlp, scale_mlp)
    hidden_two = second_value.astype(jnp.bfloat16)
    rows_two = lax.all_gather(hidden_two, "heads", axis=0, tiled=True)
    inner = jnp.dot(rows_two, fc1_cols, preferred_element_type=jnp.float32) + b_fc1.astype(
        jnp.float32
    )
    gelu_value, gelu_pull = jax.vjp(gelu_tanh, inner)
    active = gelu_value.astype(jnp.bfloat16)
    ffn_out = lax.psum_scatter(
        times_transposed(
            lax.slice_in_dim(active, 0, tok_rows * lax.axis_size("heads"), axis=0), fc2_cols
        ).astype(jnp.bfloat16),
        "heads",
        scatter_dimension=0,
        tiled=True,
    ).astype(jnp.float32) + b_fc2.astype(jnp.float32)
    block_out = (after_attn + gate_mlp * ffn_out).astype(jnp.bfloat16)
    upstream = cotangent.astype(jnp.float32)
    grad_ffn = (gate_mlp * upstream).astype(jnp.bfloat16)
    ffn_rows = lax.all_gather(grad_ffn, "heads", axis=0, tiled=True)
    grad_w_fc2 = contract_rows(ffn_rows, active)
    grad_b_fc2 = jnp.sum(ffn_rows, axis=0, dtype=jnp.float32)
    grad_active = jnp.dot(ffn_rows, fc2_cols, preferred_element_type=jnp.float32)
    grad_inner = gelu_pull(grad_active)[0].astype(jnp.bfloat16)
    grad_w_fc1 = contract_rows(rows_two, grad_inner)
    grad_b_fc1 = jnp.sum(grad_inner, axis=0, dtype=jnp.float32)
    grad_hidden_two = lax.psum_scatter(
        times_transposed(
            lax.slice_in_dim(grad_inner, 0, tok_rows * lax.axis_size("heads"), axis=0), fc1_cols
        ).astype(jnp.bfloat16),
        "heads",
        scatter_dimension=0,
        tiled=True,
    ).astype(jnp.float32)
    grad_after, grad_shift_mlp, grad_scale_mlp = second_pull(grad_hidden_two)
    grad_after = grad_after + upstream
    grad_gate_mlp = upstream * ffn_out
    grad_gate_attn = grad_after * attn_out
    grad_attn = (gate_attn * grad_after).astype(jnp.bfloat16)
    attn_rows_grad = lax.all_gather(grad_attn, "heads", axis=0, tiled=True)
    grad_w_out = contract_rows(attn_rows_grad, mixed_rows)
    grad_b_out = jnp.sum(attn_rows_grad, axis=0, dtype=jnp.float32)
    grad_mixed = jnp.dot(attn_rows_grad, out_cols, preferred_element_type=jnp.float32).astype(
        jnp.bfloat16
    )
    grad_seq = grad_mixed.reshape(seq_count, seq_len, head_local, head_size)

    def attend_backward(pieces):
        seq_block, seq_image, seq_grad, seq_totals = pieces
        key_rows = seq_block[:, :, 1]
        value_rows = seq_block[:, :, 2]
        grad_keys = jnp.zeros(key_rows.shape, jnp.float32)
        grad_values = jnp.zeros(value_rows.shape, jnp.float32)
        grad_queries = []
        for row_start in range(0, seq_len, block_rows):
            stop_row = row_start + block_rows
            query_rows = seq_block[row_start:stop_row, :, 0]
            grad_rows = seq_grad[row_start:stop_row]
            scores = block_scores(query_rows, key_rows, seq_image[row_start:stop_row], seq_image)
            soft_probs = jnp.exp(scores - seq_totals[:, row_start:stop_row, None])
            grad_probs = jnp.einsum(
                "qhd,khd->hqk", grad_rows, value_rows, preferred_element_type=jnp.float32
            )
            inner_sum = jnp.sum(soft_probs * grad_probs, axis=2, keepdims=True)
            grad_scores = (soft_probs * (grad_probs - inner_sum)).astype(jnp.bfloat16)
            grad_queries.append(
                jnp.einsum(
                    "hqk,khd->qhd", grad_scores, key_rows, preferred_element_type=jnp.float32
                )
                * scale_factor
            )
            grad_keys = (
                grad_keys
                + jnp.einsum(
                    "hqk,qhd->khd", grad_scores, query_rows, preferred_element_type=jnp.float32
                )
                * scale_factor
            )
            grad_values = grad_values + jnp.einsum(
                "hqk,qhd->khd",
                soft_probs.astype(jnp.bfloat16),
                grad_rows,
                preferred_element_type=jnp.float32,
            )
        stacked = jnp.stack([jnp.concatenate(grad_queries, axis=0), grad_keys, grad_values], axis=2)
        return stacked.astype(jnp.bfloat16)

    grad_qkv = lax.map(attend_backward, (seq_qkv, image_of, grad_seq, log_totals)).reshape(
        group_rows, head_local * 3 * head_size
    )
    grad_w_qkv = contract_rows(rows_one, grad_qkv)
    bias_terms = jnp.sum(grad_qkv, axis=0, dtype=jnp.float32).reshape(head_local, 3, head_size)
    grad_b_qv = jnp.concatenate([bias_terms[:, 0], bias_terms[:, 2]], axis=1)
    grad_hidden_one = lax.psum_scatter(
        times_transposed(
            lax.slice_in_dim(grad_qkv, 0, tok_rows * lax.axis_size("heads"), axis=0), qkv_cols
        ).astype(jnp.bfloat16),
        "heads",
        scatter_dimension=0,
        tiled=True,
    ).astype(jnp.float32)
    grad_inputs, grad_shift_attn, grad_scale_attn = first_pull(grad_hidden_one)
    grad_patches = grad_inputs + grad_after
    token_grads = (
        grad_shift_attn,
        grad_scale_attn,
        grad_gate_attn,
        grad_shift_mlp,
        grad_scale_mlp,
        grad_gate_mlp,
    )
    mods_grad_part = jnp.concatenate(
        [contract_rows_exact(token_hot, grad_term) for grad_term in token_grads], axis=1
    )
    grad_mods = lax.psum(mods_grad_part.astype(jnp.bfloat16), "heads")
    grad_cols = lax.all_to_all(
        grad_mods.reshape(image_count, row_parts, ada_width).transpose(1, 0, 2),
        "rows",
        split_axis=0,
        concat_axis=0,
        tiled=True,
    ).reshape(every_slot, ada_width)
    grad_w_ada = contract_rows(silu_low, grad_cols)
    grad_b_ada = jnp.sum(grad_cols, axis=0, dtype=jnp.float32)
    grad_silu = lax.psum(times_transposed(grad_cols, w_ada), "rows")
    grad_condition = silu_pull(grad_silu)[0]
    grad_time = contract_rows_exact(bucket_hot.astype(jnp.float32), grad_condition)
    grad_class = contract_rows_exact(label_hot.astype(jnp.float32), grad_condition)

    def row_reduced(partial):
        return lax.psum_scatter(
            partial.astype(jnp.bfloat16), "rows", scatter_dimension=0, tiled=True
        ).astype(jnp.float32)

    grad_w_qkv, grad_w_out, grad_w_fc1, grad_w_fc2 = (
        row_reduced(grad_w_qkv),
        row_reduced(grad_w_out),
        row_reduced(grad_w_fc1),
        row_reduced(grad_w_fc2),
    )
    bias_sizes = (grad_b_qv.size, grad_b_fc1.size, grad_b_out.size, grad_b_fc2.size)
    bias_all = lax.psum(
        jnp.concatenate([grad_b_qv.reshape(-1), grad_b_fc1, grad_b_out, grad_b_fc2]), "rows"
    )
    edges = [sum(bias_sizes[:step]) for step in range(5)]
    bias_rows = model_width // row_parts
    row_start = lax.axis_index("rows") * bias_rows
    grad_b_qv = bias_all[edges[0] : edges[1]].reshape(grad_b_qv.shape)
    grad_b_fc1 = bias_all[edges[1] : edges[2]]
    grad_b_out = lax.dynamic_slice_in_dim(bias_all[edges[2] : edges[3]], row_start, bias_rows)
    grad_b_fc2 = lax.dynamic_slice_in_dim(bias_all[edges[3] : edges[4]], row_start, bias_rows)
    return (
        block_out,
        grad_patches,
        grad_time,
        grad_class,
        grad_w_ada,
        grad_b_ada,
        grad_w_qkv,
        grad_b_qv,
        grad_w_out,
        grad_b_out,
        grad_w_fc1,
        grad_b_fc1,
        grad_w_fc2,
        grad_b_fc2,
    )


MESH = pl.DeviceIdType.MESH
ROW_PARTS = 8
HEAD_PARTS = 4
SLOT_ROWS = 8
VMEM_SPEC = pl.BlockSpec(memory_space=pltpu.VMEM)
ANY_SPEC = pl.BlockSpec(memory_space=pl.ANY)
DMA = pltpu.SemaphoreType.DMA
GRANT = 60 * 1024 * 1024


def places():
    row = lax.axis_index("rows")
    member = lax.axis_index("heads")
    sibling = member + 1 - 2 * lax.rem(member, 2)
    partner = lax.rem(member + 2, HEAD_PARTS)
    opposite = lax.rem(sibling + 2, HEAD_PARTS)
    return row, member, sibling, partner, opposite


def greet(row_steps, head_members):
    barrier = pltpu.get_barrier_semaphore()
    row = lax.axis_index("rows")
    for step in row_steps:
        pl.semaphore_signal(
            barrier,
            inc=1,
            device_id={"rows": lax.rem(row + step, ROW_PARTS)},
            device_id_type=MESH,
        )
    for other in head_members:
        pl.semaphore_signal(barrier, inc=1, device_id={"heads": other}, device_id_type=MESH)
    pl.semaphore_wait(barrier, len(row_steps) + len(head_members))


def to_row(source, target, send, recv, row):
    return pltpu.make_async_remote_copy(
        src_ref=source,
        dst_ref=target,
        send_sem=send,
        recv_sem=recv,
        device_id={"rows": row},
        device_id_type=MESH,
    )


def to_head(source, target, send, recv, member):
    return pltpu.make_async_remote_copy(
        src_ref=source,
        dst_ref=target,
        send_sem=send,
        recv_sem=recv,
        device_id={"heads": member},
        device_id_type=MESH,
    )


class RowGather:
    def __init__(self, shard, full, sends, recvs, local_sem, chunks):
        self.row = lax.axis_index("rows")
        self.level = self.row // 2
        self.side = lax.rem(self.row, 2)
        self.mate = self.row + 1 - 2 * self.side
        size = shard.shape[0] // chunks
        self.own = pltpu.make_async_copy(shard, full.at[self.row], local_sem)
        self.straight = []
        self.across = []
        for chunk in range(chunks):
            part = pl.ds(chunk * size, size)
            straight = []
            across = [
                to_row(
                    shard.at[part],
                    full.at[self.row, part],
                    sends.at[chunk, 3],
                    recvs.at[chunk, 3],
                    self.mate,
                )
            ]
            for step in range(1, 4):
                target = lax.rem(self.level + step, 4) * 2 + self.side
                origin = lax.rem(self.level + 4 - step, 4) * 2 + self.side
                straight.append(
                    to_row(
                        shard.at[part],
                        full.at[self.row, part],
                        sends.at[chunk, step - 1],
                        recvs.at[chunk, step - 1],
                        target,
                    )
                )
                across.append(
                    to_row(
                        full.at[origin, part],
                        full.at[origin, part],
                        sends.at[chunk, 3 + step],
                        recvs.at[chunk, 3 + step],
                        self.mate,
                    )
                )
            self.straight.append(straight)
            self.across.append(across)

    def start(self, chunk):
        for copy in self.straight[chunk]:
            copy.start()
        self.across[chunk][0].start()

    def relay(self, chunk):
        for step in range(3):
            self.straight[chunk][step].wait_recv()
            self.across[chunk][1 + step].start()

    def finish(self):
        self.own.wait()
        for straight, across in zip(self.straight, self.across):
            for copy in straight:
                copy.wait_send()
            for copy in across:
                copy.wait()


class HeadGather:
    def __init__(self, block, full, sends, recvs, local_sem):
        row, member, sibling, partner, opposite = places()
        self.own = None
        if block is None:
            block = full.at[member]
        else:
            self.own = pltpu.make_async_copy(block, full.at[member], local_sem)
        self.beside = to_head(block, full.at[member], sends.at[0], recvs.at[0], sibling)
        self.across = to_head(block, full.at[member], sends.at[1], recvs.at[1], partner)
        self.onward = to_head(
            full.at[partner], full.at[partner], sends.at[2], recvs.at[2], sibling
        )

    def start(self):
        self.across.start()
        self.beside.start()
        if self.own is not None:
            self.own.start()

    def wait_sibling(self):
        self.beside.wait_recv()

    def wait_partner(self):
        self.across.wait_recv()
        self.onward.start()

    def wait_opposite(self):
        self.onward.wait_recv()

    def finish(self):
        if self.own is not None:
            self.own.wait()
        self.beside.wait_send()
        self.across.wait_send()
        self.onward.wait_send()


def front_kernel(
    ids_ref,
    time_ref,
    class_ref,
    ada_ref,
    patches_ref,
    cotangent_ref,
    qkv_ref,
    out_ref,
    fc1_ref,
    qkv_full,
    out_full,
    fc1_full,
    patches_full,
    cotangent_full,
    cond_all,
    mods_ref,
    ids_all,
    cond_part,
    cond_in,
    mods_part,
    mods_in,
    mods_sibling,
    mods_pair,
    mods_partner,
    small_send,
    small_recv,
    pair_send,
    pair_recv,
    head_send,
    head_recv,
    qkv_send,
    qkv_recv,
    out_send,
    out_recv,
    fc1_send,
    fc1_recv,
    local_sems,
):
    row, member, sibling, partner, opposite = places()
    greet(range(1, ROW_PARTS), (sibling, partner))
    others = [(step, lax.rem(row + step, ROW_PARTS)) for step in range(1, ROW_PARTS)]

    def spread(stage, source_of, target):
        copies = []
        for step, other in others:
            copy = to_row(
                source_of(other),
                target.at[row],
                small_send.at[stage, step - 1],
                small_recv.at[stage, step - 1],
                other,
            )
            copy.start()
            copies.append(copy)
        return copies

    def settle(copies):
        for copy in copies:
            copy.wait()

    ids_copies = spread(0, lambda other: ids_ref, ids_all)
    gather_qkv = RowGather(qkv_ref, qkv_full, qkv_send, qkv_recv, local_sems.at[0], 3)
    gather_out = RowGather(out_ref, out_full, out_send, out_recv, local_sems.at[1], 1)
    gather_fc1 = RowGather(fc1_ref, fc1_full, fc1_send, fc1_recv, local_sems.at[2], 3)
    gather_patches = HeadGather(
        patches_ref, patches_full, head_send.at[0], head_recv.at[0], local_sems.at[3]
    )
    gather_cotangent = HeadGather(
        cotangent_ref, cotangent_full, head_send.at[1], head_recv.at[1], local_sems.at[4]
    )
    gather_patches.start()
    gather_qkv.own.start()
    gather_out.own.start()
    gather_fc1.own.start()
    gather_qkv.start(0)
    ids_all[row] = ids_ref[...]
    settle(ids_copies)
    table_rows = time_ref.shape[0]
    slots = ROW_PARTS * SLOT_ROWS
    table_places = row * table_rows + lax.broadcasted_iota(jnp.int32, (slots, table_rows), 1)
    bucket_hot = (
        ids_all[:, 0:SLOT_ROWS].reshape(slots, table_rows) == table_places
    ).astype(jnp.bfloat16)
    label_hot = (
        ids_all[:, SLOT_ROWS : 2 * SLOT_ROWS].reshape(slots, table_rows) == table_places
    ).astype(jnp.bfloat16)
    found = jnp.dot(bucket_hot, time_ref[...], preferred_element_type=jnp.float32) + jnp.dot(
        label_hot, class_ref[...], preferred_element_type=jnp.float32
    )
    cond_part[...] = found.reshape(cond_part.shape)
    copies = spread(1, lambda other: cond_part.at[other], cond_in)
    gather_qkv.start(1)
    cond_in[row] = cond_part[row]
    settle(copies)
    condition = jnp.sum(cond_in[...], axis=0)
    cond_all[row] = condition
    cond_part[row] = condition
    copies = spread(2, lambda other: cond_part.at[row], cond_all)
    gather_qkv.relay(0)
    settle(copies)
    every = cond_all[...].reshape(slots, cond_all.shape[2])
    silu_low = (every / (1.0 + jnp.exp(-every))).astype(jnp.bfloat16)
    mods_part[...] = jnp.dot(
        silu_low, ada_ref[...], preferred_element_type=jnp.float32
    ).reshape(mods_part.shape)
    copies = spread(3, lambda other: mods_part.at[other], mods_in)
    gather_qkv.start(2)
    mods_in[row] = mods_part[row]
    gather_qkv.relay(1)
    settle(copies)
    gather_out.start(0)
    beside = to_head(mods_in, mods_sibling, pair_send.at[0], pair_recv.at[0], sibling)
    beside.start()
    gather_patches.wait_sibling()
    beside.wait()
    mods_pair[...] = mods_in[...] + mods_sibling[...]
    across = to_head(mods_pair, mods_partner, pair_send.at[1], pair_recv.at[1], partner)
    across.start()
    gather_patches.wait_partner()
    gather_cotangent.start()
    gather_fc1.start(0)
    gather_qkv.relay(2)
    across.wait()
    mods_ref[...] = mods_pair[...] + mods_partner[...]
    gather_patches.wait_opposite()
    gather_fc1.start(1)
    gather_out.relay(0)
    gather_fc1.start(2)
    gather_fc1.relay(0)
    gather_cotangent.wait_sibling()
    gather_cotangent.wait_partner()
    gather_fc1.relay(1)
    gather_cotangent.wait_opposite()
    gather_fc1.relay(2)
    gather_patches.finish()
    gather_cotangent.finish()
    gather_qkv.finish()
    gather_out.finish()
    gather_fc1.finish()


def front(ids, time_table, class_table, w_ada, patches, cotangent, w_qkv, w_out, w_fc1):
    depth, ada_width = w_ada.shape
    shape = jax.ShapeDtypeStruct
    slotted = (ROW_PARTS, SLOT_ROWS)
    wide = pltpu.VMEM(slotted + (ada_width,), jnp.float32)
    narrow = pltpu.VMEM(slotted + (depth,), jnp.float32)
    return pl.pallas_call(
        front_kernel,
        out_shape=(
            shape((ROW_PARTS,) + w_qkv.shape, jnp.bfloat16),
            shape((ROW_PARTS,) + w_out.shape, jnp.bfloat16),
            shape((ROW_PARTS,) + w_fc1.shape, jnp.bfloat16),
            shape((HEAD_PARTS,) + patches.shape, jnp.bfloat16),
            shape((HEAD_PARTS,) + patches.shape, jnp.bfloat16),
            shape(slotted + (depth,), jnp.float32),
            shape(slotted + (ada_width,), jnp.float32),
            shape((ROW_PARTS,) + ids.shape, jnp.int32),
        ),
        in_specs=[VMEM_SPEC] * 9,
        out_specs=[ANY_SPEC] * 5 + [VMEM_SPEC] * 3,
        scratch_shapes=[narrow] * 2
        + [wide] * 5
        + [
            DMA((4, 7)),
            DMA((4, 7)),
            DMA((2,)),
            DMA((2,)),
            DMA((2, 3)),
            DMA((2, 3)),
            DMA((3, 7)),
            DMA((3, 7)),
            DMA((1, 7)),
            DMA((1, 7)),
            DMA((3, 7)),
            DMA((3, 7)),
            DMA((5,)),
        ],
        compiler_params=pltpu.CompilerParams(
            collective_id=0, has_side_effects=True, vmem_limit_bytes=GRANT
        ),
        name="front",
    )(ids, time_table, class_table, w_ada, patches, cotangent, w_qkv, w_out, w_fc1)


class HeadReduce:
    def __init__(self, partial, beside_in, pair, across_in, sends, recvs):
        row, member, sibling, partner, opposite = places()
        self.member = member
        self.partner = partner
        self.partial = partial
        self.beside_in = beside_in
        self.pair = pair
        self.across_in = across_in
        self.first = to_head(
            partial.at[opposite], beside_in.at[1], sends.at[0], recvs.at[0], sibling
        )
        self.second = to_head(
            partial.at[sibling], beside_in.at[0], sends.at[1], recvs.at[1], sibling
        )
        self.across = to_head(pair, across_in, sends.at[2], recvs.at[2], partner)

    def start(self):
        self.first.start()
        self.second.start()

    def send_pair(self):
        self.first.wait_recv()
        self.pair[...] = (
            self.partial[self.partner].astype(jnp.float32)
            + self.beside_in[1].astype(jnp.float32)
        ).astype(jnp.bfloat16)
        self.across.start()

    def settle(self):
        self.second.wait_recv()
        self.across.wait_recv()

    def rows(self, part):
        return (
            self.partial[self.member, part].astype(jnp.float32)
            + self.beside_in[0, part].astype(jnp.float32)
            + self.across_in[part].astype(jnp.float32)
        )

    def finish(self):
        self.first.wait_send()
        self.second.wait_send()
        self.across.wait_send()


class RowReduce:
    def __init__(self, partial, chunk, buffers, total, sends, recvs):
        row = lax.axis_index("rows")
        self.level = row // 2
        self.side = lax.rem(row, 2)
        mate = row + 1 - 2 * self.side
        self.partial = partial
        self.mate_in, self.pair, self.straight_in = buffers
        self.total = total
        size = total.shape[0]
        self.part = pl.ds(chunk * size, size)
        self.beside = to_row(
            partial.at[:, 1 - self.side, self.part], self.mate_in, sends.at[0], recvs.at[0], mate
        )
        self.straight = []
        for step in range(1, 4):
            target = lax.rem(self.level + step, 4)
            self.straight.append(
                to_row(
                    self.pair.at[target],
                    self.straight_in.at[step - 1],
                    sends.at[step],
                    recvs.at[step],
                    target * 2 + self.side,
                )
            )

    def start(self):
        self.beside.start()

    def send_pair(self):
        self.beside.wait_recv()

        def one(level, carry):
            self.pair[level] = (
                self.partial[level, self.side, self.part].astype(jnp.float32)
                + self.mate_in[level].astype(jnp.float32)
            ).astype(jnp.bfloat16)
            return carry

        lax.fori_loop(0, 4, one, 0)
        for copy in self.straight:
            copy.start()

    def finish(self):
        for copy in self.straight:
            copy.wait_recv()
        self.total[...] = (
            self.pair[self.level].astype(jnp.float32)
            + self.straight_in[0].astype(jnp.float32)
            + self.straight_in[1].astype(jnp.float32)
            + self.straight_in[2].astype(jnp.float32)
        )
        self.beside.wait_send()
        for copy in self.straight:
            copy.wait_send()


def row_reduces(jobs, reducing):
    buffers, sends, recvs = reducing[:-2], reducing[-2], reducing[-1]
    return [
        RowReduce(
            partial,
            chunk,
            buffers[3 * place : 3 * place + 3],
            total,
            sends.at[place],
            recvs.at[place],
        )
        for place, (partial, chunk, total) in enumerate(jobs)
    ]


def reduce_scratch(sizes):
    landing = []
    for rows, columns in sizes:
        landing += [
            pltpu.VMEM((4, rows, columns), jnp.bfloat16),
            pltpu.VMEM((4, rows, columns), jnp.bfloat16),
            pltpu.VMEM((3, rows, columns), jnp.bfloat16),
        ]
    return landing + [DMA((len(sizes), 4)), DMA((len(sizes), 4))]


def picked(vectors, part_index, segments, width):
    wide = jnp.broadcast_to(segments, (segments.shape[0], width))
    slot_count = vectors.shape[1]
    chosen = vectors[part_index, slot_count - 1 : slot_count]
    for slot in range(slot_count - 2, -1, -1):
        chosen = jnp.where(wide == slot, vectors[part_index, slot : slot + 1], chosen)
    return chosen


def centre_rows(values):
    centred = values - jnp.mean(values, axis=1, keepdims=True)
    factor = lax.rsqrt(jnp.mean(centred * centred, axis=1, keepdims=True) + EPSILON)
    return centred * factor, factor


def weight_grad(left, right, target):
    blocks, tok_rows, depth = left.shape
    height = blocks * tok_rows
    flat = target.reshape(depth, target.shape[3])
    third = depth // 3

    def some(step, carry):
        columns = pl.ds(pl.multiple_of(step * third, 128), third)
        flat[columns] = contract_rows(
            left[:, :, columns].reshape(height, third),
            right[...].reshape(height, right.shape[2]),
        ).astype(jnp.bfloat16)
        return carry

    lax.fori_loop(0, 3, some, 0)


def middle_kernel(
    mixed_ref,
    out_ref,
    fc1_ref,
    fc2_ref,
    cotangent_ref,
    patches_ref,
    segments_ref,
    hot_ref,
    vectors_ref,
    bias_ref,
    ffn_rows,
    hidden_rows,
    active_rows,
    inner_grad,
    ffn_part,
    after_ref,
    after_grad,
    attn_grad,
    slot_sums,
    bias_sums,
    fc2_rest,
    fc1_part,
    fc2_head,
    fc2_neck,
    fc2_part,
    inner_bias,
    ffn_bias,
    fc2_full,
    active_grad,
    first_part,
    second_part,
    first_beside,
    second_beside,
    first_pair,
    second_pair,
    first_across,
    second_across,
    attn_out,
    gather_send,
    gather_recv,
    reduce_send,
    reduce_recv,
    fc2_send,
    fc2_recv,
    local_sem,
    *reducing,
):
    row, member, sibling, partner, opposite = places()
    greet(range(1, ROW_PARTS), (sibling, partner))
    tok_rows, model_width = patches_ref.shape
    gather_fc2 = RowGather(fc2_ref, fc2_full, fc2_send, fc2_recv, local_sem, 3)
    gather_fc2.own.start()
    gather_fc2.start(0)
    gather_fc2.start(1)
    first = HeadReduce(
        first_part, first_beside, first_pair, first_across, reduce_send.at[0], reduce_recv.at[0]
    )
    second = HeadReduce(
        second_part,
        second_beside,
        second_pair,
        second_across,
        reduce_send.at[1],
        reduce_recv.at[1],
    )
    gather_hidden = HeadGather(None, hidden_rows, gather_send.at[0], gather_recv.at[0], None)
    gather_grad = HeadGather(None, attn_grad, gather_send.at[1], gather_recv.at[1], None)

    def project(block):
        first_part[block] = times_transposed(mixed_ref[block], out_ref[...]).astype(jnp.bfloat16)

    project(opposite)
    first.first.start()
    project(partner)
    first.send_pair()
    project(sibling)
    first.second.start()
    project(member)

    def scale_cotangent(block, carry):
        index = block // 2
        part = pl.ds(pl.multiple_of(lax.rem(block, 2) * 128, 128), 128)
        grad = (
            picked(vectors_ref, 5, segments_ref[index, part], model_width)
            * cotangent_ref[index, part].astype(jnp.float32)
        ).astype(jnp.bfloat16)
        ffn_rows[index, part] = grad
        ffn_bias[...] += jnp.sum(grad.astype(jnp.float32).reshape(16, 8, model_width), axis=0)
        return carry

    ffn_bias[...] = jnp.zeros_like(ffn_bias)
    lax.fori_loop(0, 2 * HEAD_PARTS, scale_cotangent, 0)
    gather_fc2.relay(0)
    gather_fc2.start(2)
    first.settle()

    def second_norm(block, carry):
        part = pl.ds(pl.multiple_of(block * 128, 128), 128)
        segments = segments_ref[member, part]
        out = first.rows(part) + bias_ref[0:1]
        after = patches_ref[part].astype(jnp.float32) + (
            picked(vectors_ref, 2, segments, model_width) * out
        )
        attn_out[part] = out
        after_ref[part] = after
        normed, _ = centre_rows(after)
        hidden_rows[member, part] = (
            normed * (1.0 + picked(vectors_ref, 4, segments, model_width))
            + picked(vectors_ref, 3, segments, model_width)
        ).astype(jnp.bfloat16)
        return carry

    lax.fori_loop(0, tok_rows // 128, second_norm, 0)
    gather_hidden.start()
    gather_fc2.relay(1)
    gather_fc2.relay(2)
    gather_fc2.finish()
    fc2 = fc2_full.reshape(fc1_ref.shape)

    def through_fc2(block, carry):
        active_grad[block] = jnp.dot(
            ffn_rows[block], fc2[...], preferred_element_type=jnp.float32
        )
        return carry

    lax.fori_loop(0, HEAD_PARTS, through_fc2, 0)
    inner_bias[...] = jnp.zeros_like(inner_bias)

    def feed(block, carry):
        inner = jnp.dot(
            hidden_rows[block], fc1_ref[...], preferred_element_type=jnp.float32
        ) + bias_ref[1:2]
        square = inner * inner
        bent = jnp.tanh(TANH_COEFF * (inner + 0.044715 * square * inner))
        half = 0.5 * (1.0 + bent)
        active_rows[block] = (inner * half).astype(jnp.bfloat16)
        slope = half + 0.5 * inner * (1.0 - bent * bent) * (
            TANH_COEFF * (1.0 + 3.0 * 0.044715 * square)
        )
        grad = (active_grad[block] * slope).astype(jnp.bfloat16)
        inner_grad[block] = grad
        inner_bias[...] += jnp.sum(
            grad.astype(jnp.float32).reshape(tok_rows // 8, 8, inner.shape[1]), axis=0
        )
        return carry

    def return_fc1(block, carry):
        second_part[block] = times_transposed(inner_grad[block], fc1_ref[...]).astype(jnp.bfloat16)
        return carry

    direction = sibling - member
    gather_hidden.wait_sibling()
    lax.fori_loop(0, 2, lambda step, carry: feed(member + step * direction, carry), 0)
    gather_hidden.wait_partner()
    gather_hidden.wait_opposite()

    def feed_far(step, carry):
        block = opposite - step * direction
        feed(block, carry)
        return return_fc1(block, carry)

    lax.fori_loop(0, 2, feed_far, 0)
    second.first.start()
    second.send_pair()
    lax.fori_loop(0, 2, lambda step, carry: return_fc1(sibling - step * direction, carry), 0)
    second.second.start()

    def forward_fc2(block, carry):
        ffn_part[block] = times_transposed(active_rows[block], fc2[...]).astype(jnp.bfloat16)
        return carry

    weight_grad(ffn_rows, active_rows, fc2_part)
    third = fc2_rest.shape[2]
    fc2_rest[...] = fc2_part[:, :, 2 * third : 3 * third]
    reduces = row_reduces(((fc2_part, 0, fc2_head), (fc2_part, 1, fc2_neck)), reducing)
    for unit in reduces:
        unit.start()
    lax.fori_loop(0, HEAD_PARTS, forward_fc2, 0)
    slot_sums[...] = jnp.zeros_like(slot_sums)
    second.settle()

    def second_back(block, carry):
        part = pl.ds(pl.multiple_of(block * 128, 128), 128)
        segments = segments_ref[member, part]
        grad = second.rows(part)
        normed, factor = centre_rows(after_ref[part])
        weighted = grad * (1.0 + picked(vectors_ref, 4, segments, model_width))
        total = cotangent_ref[member, part].astype(jnp.float32) + factor * (
            weighted
            - jnp.mean(weighted, axis=1, keepdims=True)
            - normed * jnp.mean(weighted * normed, axis=1, keepdims=True)
        )
        after_grad[part] = total
        attn_grad[member, part] = (
            picked(vectors_ref, 2, segments, model_width) * total
        ).astype(jnp.bfloat16)
        hot = hot_ref[:, part]
        for index, term in enumerate((total * attn_out[part], grad, grad * normed)):
            slot_sums[index] += jnp.dot(
                hot, term, precision=HIGH, preferred_element_type=jnp.float32
            )
        return carry

    lax.fori_loop(0, tok_rows // 128, second_back, 0)
    gather_grad.start()
    weight_grad(hidden_rows, inner_grad, fc1_part)
    reduces[0].send_pair()
    bias_sums[...] = jnp.zeros_like(bias_sums)
    bias_sums[0:1] = jnp.sum(inner_bias[...], axis=0, keepdims=True)
    bias_sums[1:2] = jnp.sum(ffn_bias[...], axis=0, keepdims=True)
    gather_grad.wait_sibling()
    gather_grad.wait_partner()
    gather_grad.wait_opposite()
    reduces[1].send_pair()
    for unit in reduces:
        unit.finish()
    gather_hidden.finish()
    gather_grad.finish()
    first.finish()
    second.finish()


def middle(mixed, w_out, w_fc1, w_fc2, cotangent, patches, segments, hot, vectors, biases):
    shape = jax.ShapeDtypeStruct
    tok_rows, model_width = patches.shape
    hidden_width = w_fc1.shape[1]
    width_part = w_fc2.shape[0]
    rows_low = shape((HEAD_PARTS, tok_rows, model_width), jnp.bfloat16)
    wide_low = shape((HEAD_PARTS, tok_rows, hidden_width), jnp.bfloat16)
    own = shape((tok_rows, model_width), jnp.float32)
    own_low = pltpu.VMEM((tok_rows, model_width), jnp.bfloat16)
    group_low = pltpu.VMEM((HEAD_PARTS, tok_rows, model_width), jnp.bfloat16)
    pair_low = pltpu.VMEM((2, tok_rows, model_width), jnp.bfloat16)
    return pl.pallas_call(
        middle_kernel,
        out_shape=[
            rows_low,
            rows_low,
            wide_low,
            wide_low,
            rows_low,
            own,
            own,
            rows_low,
            shape((3, SLOT_ROWS, model_width), jnp.float32),
            shape((8, hidden_width), jnp.float32),
            shape((4, 2, width_part // 3, hidden_width), jnp.bfloat16),
            shape((4, 2, width_part, hidden_width), jnp.bfloat16),
            shape((width_part // 3, hidden_width), jnp.float32),
            shape((width_part // 3, hidden_width), jnp.float32),
        ],
        in_specs=[VMEM_SPEC] * 10,
        out_specs=[VMEM_SPEC] * 14,
        scratch_shapes=[
            pltpu.VMEM((4, 2, width_part, hidden_width), jnp.bfloat16),
            pltpu.VMEM((8, hidden_width), jnp.float32),
            pltpu.VMEM((8, model_width), jnp.float32),
            pltpu.VMEM((ROW_PARTS,) + w_fc2.shape, jnp.bfloat16),
            pltpu.VMEM((HEAD_PARTS, tok_rows, hidden_width), jnp.float32),
            group_low,
            group_low,
            pair_low,
            pair_low,
            own_low,
            own_low,
            own_low,
            own_low,
            pltpu.VMEM((tok_rows, model_width), jnp.float32),
            DMA((2, 3)),
            DMA((2, 3)),
            DMA((2, 3)),
            DMA((2, 3)),
            DMA((3, 7)),
            DMA((3, 7)),
            DMA(()),
        ]
        + reduce_scratch([(width_part // 3, hidden_width)] * 2),
        compiler_params=pltpu.CompilerParams(
            collective_id=2, has_side_effects=True, vmem_limit_bytes=GRANT
        ),
        name="middle",
    )(mixed, w_out, w_fc1, w_fc2, cotangent, patches, segments, hot, vectors, biases)


HEAD_LANES = 128


def rear_kernel(
    projected_ref,
    grad_ref,
    out_ref,
    totals_ref,
    keys_image,
    rows_image,
    fc2_part,
    fc1_part,
    hidden_rows,
    qkv_ref,
    mixed_ref,
    bias_ref,
    patches_ref,
    after_ref,
    vectors_ref,
    segments_ref,
    hot_ref,
    sums_ref,
    silu_ref,
    slope_ref,
    bucket_ref,
    label_ref,
    ada_ref,
    ffn_ref,
    block_ref,
    cotangent_ref,
    ffn_bias,
    block_out,
    patches_grad,
    time_grad,
    class_grad,
    ada_grad,
    ada_bias,
    fc2_tail,
    fc1_grad,
    qkv_grad,
    out_grad,
    bias_sum,
    parts,
    mixed_grad,
    key_columns,
    grad_keys,
    grad_values,
    bias,
    packed,
    packed_grad,
    hidden_part,
    qkv_part,
    out_part,
    bias_own,
    beside_in,
    pair_rows,
    across_in,
    ffn_beside,
    ffn_pair,
    ffn_across,
    slot_sums,
    mods_own,
    mods_sibling,
    mods_pair,
    mods_partner,
    mods_cols,
    bias_all,
    silu_part,
    silu_in,
    silu_all,
    small_send,
    small_recv,
    pair_send,
    pair_recv,
    head_send,
    head_recv,
    *reducing,
):
    row, member, sibling, partner, opposite = places()
    greet(range(1, ROW_PARTS), (sibling, partner))
    others = [(step, lax.rem(row + step, ROW_PARTS)) for step in range(1, ROW_PARTS)]

    def spread(stage, source_of, target):
        copies = []
        for step, other in others:
            copy = to_row(
                source_of(other),
                target.at[row],
                small_send.at[stage, step - 1],
                small_recv.at[stage, step - 1],
                other,
            )
            copy.start()
            copies.append(copy)
        return copies

    def settle(copies):
        for copy in copies:
            copy.wait()

    third = fc2_tail.shape[0]
    units = row_reduces(
        [(fc2_part, 0, fc2_tail)]
        + [(fc1_part, chunk, fc1_grad.at[pl.ds(chunk * third, third)]) for chunk in range(3)]
        + [(out_part, 0, out_grad)]
        + [(qkv_part, chunk, qkv_grad.at[pl.ds(chunk * third, third)]) for chunk in range(3)],
        reducing,
    )
    reduce_rows = HeadReduce(
        hidden_part, beside_in, pair_rows, across_in, head_send.at[0], head_recv.at[0]
    )
    reduce_ffn = HeadReduce(
        ffn_ref, ffn_beside, ffn_pair, ffn_across, head_send.at[1], head_recv.at[1]
    )
    for unit in units[:3]:
        unit.start()
    reduce_ffn.start()
    reduce_ffn.send_pair()
    blocks, tok_rows, width = projected_ref.shape
    model_width = patches_ref.shape[1]
    head_local = totals_ref.shape[0]
    head_size = width // (3 * head_local)
    scale_factor = 1.0 / math.sqrt(head_size)
    seq_len = blocks * tok_rows
    parts[...] = jnp.zeros_like(parts)
    mixed_grad[...] = jnp.zeros_like(mixed_grad)
    bias_own[...] = jnp.zeros_like(bias_own)

    def unpack(block, carry):
        rows = pl.ds(pl.multiple_of(block * tok_rows, tok_rows), tok_rows)
        packed[...] = projected_ref[block].astype(jnp.float32)
        for part in range(3 * head_local):
            parts[part, rows, 0:head_size] = packed[
                :, part * head_size : (part + 1) * head_size
            ].astype(jnp.bfloat16)
        packed[:, 0 : head_local * head_size] = jnp.dot(
            grad_ref[block], out_ref[...], preferred_element_type=jnp.float32
        )
        for head in range(head_local):
            mixed_grad[head, rows, 0:head_size] = packed[
                :, head * head_size : (head + 1) * head_size
            ].astype(jnp.bfloat16)
        bias_own[0] += jnp.sum(
            grad_ref[block].astype(jnp.float32).reshape(tok_rows // 8, 8, model_width), axis=0
        )
        return carry

    lax.fori_loop(0, blocks, unpack, 0)

    def turn(head, carry):
        key_columns[head] = parts[3 * head + 1].astype(jnp.float32).T.astype(jnp.bfloat16)
        return carry

    lax.fori_loop(0, head_local, turn, 0)
    grad_keys[...] = jnp.zeros_like(grad_keys)
    grad_values[...] = jnp.zeros_like(grad_values)
    weight_grad(grad_ref, mixed_ref, out_part)

    for block in range(blocks):
        rows = pl.ds(block * tok_rows, tok_rows)
        same = jnp.broadcast_to(keys_image[...], (seq_len, tok_rows)) == jnp.broadcast_to(
            rows_image[block], (seq_len, tok_rows)
        )
        bias[...] = jnp.where(same, 0.0, MASKED)

        def one_head(head, carry):
            query = parts[3 * head, rows]
            grad = mixed_grad[head, rows]
            scores = times_transposed(parts[3 * head + 1], query) * scale_factor + bias[...]
            probs = jnp.exp(scores - totals_ref[head, block])
            grad_probs = times_transposed(parts[3 * head + 2], grad)
            inner = jnp.sum(probs * grad_probs, axis=0, keepdims=True)
            grad_scores = (probs * (grad_probs - inner)).astype(jnp.bfloat16)
            grad_values[head] += jnp.dot(
                probs.astype(jnp.bfloat16), grad, preferred_element_type=jnp.float32
            )
            grad_keys[head] += jnp.dot(grad_scores, query, preferred_element_type=jnp.float32)
            lanes = pl.ds(pl.multiple_of(head * HEAD_LANES, HEAD_LANES), HEAD_LANES)
            hidden_part[block, :, lanes] = (
                jnp.dot(key_columns[head], grad_scores, preferred_element_type=jnp.float32).T
                * scale_factor
            ).astype(jnp.bfloat16)
            return carry

        lax.fori_loop(0, head_local, one_head, 0)
        units[block].send_pair()
        if block < 2:
            units[block + 3].start()

    def pack(block, carry):
        rows = pl.ds(pl.multiple_of(block * tok_rows, tok_rows), tok_rows)
        for head in range(head_local):
            lane = head * HEAD_LANES
            terms = (
                hidden_part[block, :, lane : lane + head_size].astype(jnp.float32),
                grad_keys[head, rows, 0:head_size] * scale_factor,
                grad_values[head, rows, 0:head_size],
            )
            for place, term in enumerate(terms):
                start = (3 * head + place) * head_size
                packed[:, start : start + head_size] = term
        low = packed[...].astype(jnp.bfloat16)
        packed_grad[block] = low
        bias_own[1, :, 0:width] += jnp.sum(
            low.astype(jnp.float32).reshape(tok_rows // 8, 8, width), axis=0
        )
        return carry

    lax.fori_loop(0, blocks, pack, 0)
    direction = sibling - member

    def project_back(block):
        hidden_part[block] = times_transposed(packed_grad[block], qkv_ref[...]).astype(
            jnp.bfloat16
        )

    def far(step, carry):
        project_back(opposite - step * direction)
        return carry

    def near(step, carry):
        project_back(sibling - step * direction)
        return carry

    lax.fori_loop(0, 2, far, 0)
    reduce_rows.first.start()
    reduce_rows.send_pair()
    lax.fori_loop(0, 2, near, 0)
    reduce_rows.second.start()
    weight_grad(hidden_rows, packed_grad, qkv_part)
    for unit in units[5:]:
        unit.start()
    bias_own[2] = jnp.zeros_like(bias_own[2])
    bias_own[2] = bias_ref[...]
    bias_own[2, 2:3] = jnp.sum(bias_own[0], axis=0, keepdims=True)
    bias_own[2, 3:4] = jnp.sum(bias_own[1], axis=0, keepdims=True)
    bias_copies = spread(1, lambda other: bias_own.at[2], bias_all)
    bias_all[row] = bias_own[2]
    units[4].send_pair()
    slot_sums[...] = jnp.zeros_like(slot_sums)
    reduce_ffn.settle()

    def rows_out(block, carry):
        part = pl.ds(pl.multiple_of(block * 128, 128), 128)
        ffn = reduce_ffn.rows(part) + ffn_bias[0:1]
        gate = picked(vectors_ref, 5, segments_ref[member, part], model_width)
        block_out[part] = (block_ref[part] + gate * ffn).astype(jnp.bfloat16)
        slot_sums[2] += jnp.dot(
            hot_ref[:, part],
            cotangent_ref[part].astype(jnp.float32) * ffn,
            precision=HIGH,
            preferred_element_type=jnp.float32,
        )
        return carry

    lax.fori_loop(0, tok_rows // 128, rows_out, 0)
    units[0].finish()
    units[1].finish()
    units[5].send_pair()
    reduce_rows.settle()

    def rows_back(block, carry):
        part = pl.ds(pl.multiple_of(block * 128, 128), 128)
        grad = reduce_rows.rows(part)
        normed, factor = centre_rows(patches_ref[part].astype(jnp.float32))
        weighted = grad * (1.0 + picked(vectors_ref, 1, segments_ref[member, part], model_width))
        patches_grad[part] = after_ref[part] + factor * (
            weighted
            - jnp.mean(weighted, axis=1, keepdims=True)
            - normed * jnp.mean(weighted * normed, axis=1, keepdims=True)
        )
        hot = hot_ref[:, part]
        slot_sums[0] += jnp.dot(hot, grad, precision=HIGH, preferred_element_type=jnp.float32)
        slot_sums[1] += jnp.dot(
            hot, grad * normed, precision=HIGH, preferred_element_type=jnp.float32
        )
        return carry

    lax.fori_loop(0, tok_rows // 128, rows_back, 0)
    ada_width = ada_ref.shape[1]
    fine = ada_width // 3
    for unit in range(3 * ROW_PARTS):
        part_index, within = divmod(unit * fine, model_width)
        span = slice(within, within + fine)
        if part_index < 2:
            source = slot_sums[part_index, :, span]
        elif part_index == 5:
            source = slot_sums[2, :, span]
        else:
            source = sums_ref[part_index - 2, :, span]
        mods_own[unit // 3, :, unit % 3 * fine : (unit % 3 + 1) * fine] = source
    beside = to_head(mods_own, mods_sibling, pair_send.at[0], pair_recv.at[0], sibling)
    beside.start()
    units[6].send_pair()
    beside.wait()
    mods_pair[...] = mods_own[...] + mods_sibling[...]
    across = to_head(mods_pair, mods_partner, pair_send.at[1], pair_recv.at[1], partner)
    across.start()
    units[2].finish()
    units[3].finish()
    settle(bias_copies)
    bias_sum[...] = jnp.sum(bias_all[...], axis=0)
    across.wait()
    mods_own[...] = (
        (mods_pair[...] + mods_partner[...]).astype(jnp.bfloat16).astype(jnp.float32)
    )
    copies = spread(0, lambda other: mods_own.at[other], mods_cols)
    mods_cols[row] = mods_own[row]
    units[7].send_pair()
    units[4].finish()
    settle(copies)
    slots = ROW_PARTS * SLOT_ROWS
    cols = mods_cols[...].reshape(slots, ada_width)
    low = cols.astype(jnp.bfloat16)
    silu_part[...] = times_transposed(low, ada_ref[...]).reshape(silu_part.shape)
    copies = spread(2, lambda other: silu_part.at[other], silu_in)
    silu_in[row] = silu_part[row]
    ada_grad[...] = jnp.dot(silu_ref[...], low, preferred_element_type=jnp.float32)
    ada_bias[...] = jnp.broadcast_to(jnp.sum(cols, axis=0, keepdims=True), ada_bias.shape)
    settle(copies)
    summed = jnp.sum(silu_in[...], axis=0)
    silu_all[row] = summed
    silu_part[row] = summed
    copies = spread(3, lambda other: silu_part.at[row], silu_all)
    units[5].finish()
    units[6].finish()
    units[7].finish()
    settle(copies)
    grad_condition = silu_all[...].reshape(slots, silu_all.shape[2]) * slope_ref[...]
    time_grad[...] = jnp.dot(
        bucket_ref[...], grad_condition, precision=HIGH, preferred_element_type=jnp.float32
    )
    class_grad[...] = jnp.dot(
        label_ref[...], grad_condition, precision=HIGH, preferred_element_type=jnp.float32
    )
    reduce_rows.finish()
    reduce_ffn.finish()


def rear(*args):
    shape = jax.ShapeDtypeStruct
    projected, w_out, totals, grad_w_fc2, w_qkv, biases, patches, buckets, w_ada = (
        args[place] for place in (0, 2, 3, 6, 9, 11, 12, 20, 22)
    )
    blocks, tok_rows, width = projected.shape
    head_local = totals.shape[0]
    seq_len = blocks * tok_rows
    model_width = patches.shape[1]
    third, hidden_width = grad_w_fc2.shape[2:]
    width_part = 3 * third
    out_width = w_out.shape[1]
    depth, ada_width = w_ada.shape
    table_rows = buckets.shape[0]
    low = jnp.bfloat16
    full = jnp.float32
    heads_wide = pltpu.VMEM((head_local, seq_len, HEAD_LANES), full)
    slotted = (ROW_PARTS, SLOT_ROWS)
    wide = pltpu.VMEM(slotted + (ada_width,), full)
    narrow = pltpu.VMEM(slotted + (depth,), full)
    sizes = (
        [(third, hidden_width)] * 4 + [(width_part, out_width)] + [(third, width)] * 3
    )
    return pl.pallas_call(
        rear_kernel,
        out_shape=[
            shape((tok_rows, model_width), low),
            shape((tok_rows, model_width), full),
            shape((table_rows, depth), full),
            shape((table_rows, depth), full),
            shape((depth, ada_width), full),
            shape((SLOT_ROWS, ada_width), full),
            shape((third, hidden_width), full),
            shape((width_part, hidden_width), full),
            shape((width_part, width), full),
            shape((width_part, out_width), full),
            shape(biases.shape, full),
        ],
        in_specs=[VMEM_SPEC] * 27,
        out_specs=[VMEM_SPEC] * 11,
        scratch_shapes=[
            pltpu.VMEM((3 * head_local, seq_len, HEAD_LANES), low),
            pltpu.VMEM((head_local, seq_len, HEAD_LANES), low),
            pltpu.VMEM((head_local, HEAD_LANES, seq_len), low),
            heads_wide,
            heads_wide,
            pltpu.VMEM((seq_len, tok_rows), full),
            pltpu.VMEM((tok_rows, width), full),
            pltpu.VMEM((blocks, tok_rows, width), low),
            pltpu.VMEM((blocks, tok_rows, model_width), low),
            pltpu.VMEM((4, 2, width_part, width), low),
            pltpu.VMEM((4, 2, width_part, out_width), low),
            pltpu.VMEM((3,) + biases.shape, full),
        ]
        + [
            pltpu.VMEM((2, tok_rows, model_width), low),
            pltpu.VMEM((tok_rows, model_width), low),
            pltpu.VMEM((tok_rows, model_width), low),
        ]
        * 2
        + [pltpu.VMEM((3, SLOT_ROWS, model_width), full)]
        + [wide] * 5
        + [pltpu.VMEM((ROW_PARTS,) + biases.shape, full)]
        + [narrow] * 3
        + [
            DMA((4, 7)),
            DMA((4, 7)),
            DMA((2,)),
            DMA((2,)),
            DMA((2, 3)),
            DMA((2, 3)),
        ]
        + reduce_scratch(sizes),
        compiler_params=pltpu.CompilerParams(
            collective_id=1, has_side_effects=True, vmem_limit_bytes=67_000_000
        ),
        name="rear",
    )(*args)


def shards_linked(
    patches,
    time_table,
    class_table,
    w_ada,
    b_ada,
    w_qkv,
    b_qv,
    w_out,
    b_out,
    w_fc1,
    b_fc1,
    w_fc2,
    b_fc2,
    image_lengths,
    segment_ids,
    bucket_ids,
    class_labels,
    cotangent,
):
    head_parts = lax.axis_size("heads")
    member = lax.axis_index("heads")
    tok_rows = patches.shape[0]
    model_width = patches.shape[1]
    seq_count = segment_ids.shape[0]
    seq_len = segment_ids.shape[1]
    slot_count = image_lengths.shape[1]
    image_count = seq_count * slot_count
    group_rows = tok_rows * head_parts
    head_local = b_qv.shape[0]
    head_size = b_qv.shape[1] // 2
    block_rows = min(BLOCK_LIMIT, seq_len)
    scale_factor = 1.0 / math.sqrt(head_size)
    row_parts = lax.axis_size("rows")
    table_rows = time_table.shape[0]
    ada_width = w_ada.shape[1]
    every_slot = row_parts * SLOT_ROWS
    slot_pad = jnp.full((SLOT_ROWS - slot_count,), -1, jnp.int32)
    ids = jnp.broadcast_to(
        jnp.concatenate([bucket_ids[0], slot_pad, class_labels[0], slot_pad])[:, None],
        (2 * SLOT_ROWS, table_rows),
    )
    (
        qkv_full,
        out_full,
        fc1_full,
        patches_full,
        cotangent_full,
        condition,
        mods,
        ids_all,
    ) = front(ids, time_table, class_table, w_ada, patches, cotangent, w_qkv, w_out, w_fc1)
    qkv_cols = qkv_full.reshape(model_width, w_qkv.shape[1])
    out_cols = out_full.reshape(model_width, w_out.shape[1])
    fc1_cols = fc1_full.reshape(model_width, w_fc1.shape[1])
    condition = condition.reshape(every_slot, condition.shape[2])
    silu_value, silu_pull = jax.vjp(silu_plain, condition)
    silu_low = silu_value.astype(jnp.bfloat16)
    mods_all = mods[:, :slot_count].transpose(1, 0, 2).reshape(
        slot_count, row_parts * ada_width
    ) + b_ada.astype(jnp.float32)
    row_segments = segment_ids[0][:, None]

    def by_token(part_index, segments):
        vectors = mods_all[:, part_index * model_width : (part_index + 1) * model_width]
        chosen = vectors[slot_count - 1][None, :]
        for slot in range(slot_count - 2, -1, -1):
            chosen = jnp.where(segments == slot, vectors[slot][None, :], chosen)
        return chosen

    own_segments = lax.dynamic_slice_in_dim(segment_ids[0], member * tok_rows, tok_rows)[:, None]
    token_hot = (own_segments == jnp.arange(SLOT_ROWS, dtype=jnp.int32)[None, :]).astype(
        jnp.float32
    )
    rows_one = modulate(
        patches_full.reshape(group_rows, model_width).astype(jnp.float32),
        by_token(0, row_segments),
        by_token(1, row_segments),
    ).astype(jnp.bfloat16)
    zero_bias = jnp.zeros((head_local, head_size), b_qv.dtype)
    qkv_bias = (
        jnp.concatenate([b_qv[:, :head_size], zero_bias, b_qv[:, head_size:]], axis=1)
        .reshape(head_local * 3 * head_size)
        .astype(jnp.float32)
    )
    projected = (jnp.dot(rows_one, qkv_cols, preferred_element_type=jnp.float32) + qkv_bias).astype(
        jnp.bfloat16
    )
    seq_qkv = projected.reshape(seq_count, seq_len, head_local, 3, head_size)
    slot_ends = jnp.cumsum(image_lengths, axis=1)
    places = jnp.arange(seq_len, dtype=jnp.int32)
    image_of = jnp.sum((places[None, :, None] >= slot_ends[:, None, :]).astype(jnp.int32), axis=2)

    def block_scores(query_rows, key_rows, image_rows, image_cols):
        scores = (
            jnp.einsum("qhd,khd->hqk", query_rows, key_rows, preferred_element_type=jnp.float32)
            * scale_factor
        )
        return jnp.where((image_rows[:, None] == image_cols[None, :])[None], scores, MASKED)

    def attend_forward(pieces):
        seq_block, seq_image = pieces
        key_rows = seq_block[:, :, 1]
        value_rows = seq_block[:, :, 2]
        outputs = []
        totals = []
        for row_start in range(0, seq_len, block_rows):
            stop_row = row_start + block_rows
            query_rows = seq_block[row_start:stop_row, :, 0]
            scores = block_scores(query_rows, key_rows, seq_image[row_start:stop_row], seq_image)
            row_peak = jnp.max(scores, axis=2, keepdims=True)
            raised = jnp.exp(scores - row_peak)
            row_total = jnp.sum(raised, axis=2, keepdims=True)
            soft_low = (raised / row_total).astype(jnp.bfloat16)
            outputs.append(
                jnp.einsum(
                    "hqk,khd->qhd", soft_low, value_rows, preferred_element_type=jnp.float32
                ).astype(jnp.bfloat16)
            )
            totals.append((row_peak + jnp.log(row_total))[:, :, 0])
        return (jnp.concatenate(outputs, axis=0), jnp.concatenate(totals, axis=1))

    mixed, log_totals = lax.map(attend_forward, (seq_qkv, image_of))
    mixed_rows = mixed.reshape(head_parts, tok_rows, head_local * head_size)
    vectors = mods_all.reshape(slot_count, 6, model_width).transpose(1, 0, 2)
    segments = segment_ids.reshape(head_parts, tok_rows, 1)
    (
        ffn_rows,
        rows_two,
        active,
        grad_inner,
        ffn_part,
        after_attn,
        grad_after,
        attn_rows_grad,
        sums,
        bias_sums,
        grad_w_fc2,
        grad_w_fc1,
        fc2_head,
        fc2_neck,
    ) = middle(
        mixed_rows,
        out_cols,
        fc1_cols,
        w_fc2,
        cotangent_full,
        patches,
        segments,
        token_hot.T,
        vectors,
        jnp.stack([b_out, b_fc1]).astype(jnp.float32),
    )
    all_ids = ids_all[:, :, 0]
    table_places = lax.axis_index("rows") * table_rows + jnp.arange(table_rows, dtype=jnp.int32)
    bucket_hot = table_places[:, None] == all_ids[:, :SLOT_ROWS].reshape(every_slot)[None, :]
    label_hot = table_places[:, None] == all_ids[:, SLOT_ROWS:].reshape(every_slot)[None, :]
    (
        block_out,
        grad_patches,
        grad_time,
        grad_class,
        grad_w_ada,
        grad_b_ada,
        fc2_tail,
        grad_w_fc1,
        grad_w_qkv,
        grad_w_out,
        bias_all,
    ) = rear(
        projected.reshape(head_parts, tok_rows, projected.shape[1]),
        attn_rows_grad,
        out_cols,
        log_totals.reshape(head_local, head_parts, 1, tok_rows),
        image_of.reshape(seq_len, 1),
        image_of.reshape(head_parts, 1, tok_rows),
        grad_w_fc2,
        grad_w_fc1,
        rows_one.reshape(head_parts, tok_rows, model_width),
        qkv_cols,
        mixed_rows,
        bias_sums,
        patches,
        grad_after,
        vectors,
        segments,
        token_hot.T,
        sums,
        silu_low.T,
        silu_pull(jnp.ones_like(condition))[0],
        bucket_hot.astype(jnp.float32),
        label_hot.astype(jnp.float32),
        w_ada,
        ffn_part,
        after_attn,
        cotangent,
        b_fc2.astype(jnp.float32)[None, :],
    )
    grad_w_fc2 = jnp.concatenate([fc2_head, fc2_neck, fc2_tail], axis=0)
    grad_b_ada = grad_b_ada[0]
    bias_rows = model_width // row_parts
    row_start = lax.axis_index("rows") * bias_rows
    grad_b_fc1 = bias_all[0]
    grad_b_fc2 = lax.dynamic_slice_in_dim(bias_all[1], row_start, bias_rows)
    grad_b_out = lax.dynamic_slice_in_dim(bias_all[2], row_start, bias_rows)
    bias_terms = bias_all[3, : head_local * 3 * head_size].reshape(head_local, 3, head_size)
    grad_b_qv = jnp.concatenate([bias_terms[:, 0], bias_terms[:, 2]], axis=1)
    return (
        block_out,
        grad_patches,
        grad_time,
        grad_class,
        grad_w_ada,
        grad_b_ada,
        grad_w_qkv,
        grad_b_qv,
        grad_w_out,
        grad_b_out,
        grad_w_fc1,
        grad_b_fc1,
        grad_w_fc2,
        grad_b_fc2,
    )


def solution(mesh):
    placed = (
        P(("rows", "heads"), None),
        P("rows", "heads"),
        P("rows", "heads"),
        P("heads", "rows"),
        P(),
        P("rows", "heads"),
        P("heads", None),
        P("rows", "heads"),
        P(),
        P("rows", "heads"),
        P("heads"),
        P("rows", "heads"),
        P(),
        P("rows", None),
        P("rows", None),
        P("rows", None),
        P("rows", None),
        P(("rows", "heads"), None),
    )
    linked = mesh.shape["rows"] == ROW_PARTS and mesh.shape["heads"] == HEAD_PARTS
    return jax.shard_map(
        shards_linked if linked else shards_plain,
        mesh=mesh,
        in_specs=placed,
        out_specs=(
            P(("rows", "heads"), None),
            P(("rows", "heads"), None),
            P("rows", "heads"),
            P("rows", "heads"),
            P("heads", "rows"),
            P("rows"),
            P("rows", "heads"),
            P("heads", None),
            P("rows", "heads"),
            P("rows"),
            P("rows", "heads"),
            P("heads"),
            P("rows", "heads"),
            P("rows"),
        ),
        check_vma=False,
    )
```

```python
import functools
import math

import jax
import jax.numpy as jnp
from jax import lax
from jax.experimental import pallas as pl
from jax.experimental.pallas import tpu as pltpu
from jax.sharding import PartitionSpec as P

EPSILON = 1e-06
MASKED = -1e30
HIGH = lax.Precision.HIGHEST
TANH_COEFF = 0.7978845608028654
BLOCK_LIMIT = 512


def layer_norm(values):
    average = jnp.mean(values, axis=-1, keepdims=True)
    centred = values - average
    variance = jnp.mean(centred * centred, axis=-1, keepdims=True)
    return centred * lax.rsqrt(variance + EPSILON)


def gelu_tanh(values):
    return (
        0.5 * values * (1.0 + jnp.tanh(TANH_COEFF * (values + 0.044715 * values * values * values)))
    )


def silu_plain(values):
    return values / (1.0 + jnp.exp(-values))


def modulate(values, shift_term, scale_term):
    return layer_norm(values) * (1.0 + scale_term) + shift_term


def contract_rows(left_matrix, right_matrix):
    return lax.dot_general(
        left_matrix, right_matrix, (((0,), (0,)), ((), ())), preferred_element_type=jnp.float32
    )


def contract_rows_exact(left_matrix, right_matrix):
    return lax.dot_general(
        left_matrix,
        right_matrix,
        (((0,), (0,)), ((), ())),
        precision=HIGH,
        preferred_element_type=jnp.float32,
    )


def times_transposed(left_matrix, right_matrix):
    return lax.dot_general(
        left_matrix, right_matrix, (((1,), (1,)), ((), ())), preferred_element_type=jnp.float32
    )


def gather_weights(w_qkv, w_out, w_fc1, w_fc2):
    return (
        lax.all_gather(w_qkv, "rows", axis=0, tiled=True),
        lax.all_gather(w_out, "rows", axis=0, tiled=True),
        lax.all_gather(w_fc1, "rows", axis=0, tiled=True),
        lax.all_gather(w_fc2, "rows", axis=0, tiled=True),
    )


def shards_plain(
    patches,
    time_table,
    class_table,
    w_ada,
    b_ada,
    w_qkv,
    b_qv,
    w_out,
    b_out,
    w_fc1,
    b_fc1,
    w_fc2,
    b_fc2,
    image_lengths,
    segment_ids,
    bucket_ids,
    class_labels,
    cotangent,
):
    head_parts = lax.axis_size("heads")
    member = lax.axis_index("heads")
    tok_rows = patches.shape[0]
    model_width = patches.shape[1]
    seq_count = segment_ids.shape[0]
    seq_len = segment_ids.shape[1]
    slot_count = image_lengths.shape[1]
    image_count = seq_count * slot_count
    group_rows = tok_rows * head_parts
    head_local = b_qv.shape[0]
    head_size = b_qv.shape[1] // 2
    block_rows = min(BLOCK_LIMIT, seq_len)
    scale_factor = 1.0 / math.sqrt(head_size)
    row_parts = lax.axis_size("rows")
    table_rows = time_table.shape[0]
    ada_width = w_ada.shape[1]
    qkv_cols, out_cols, fc1_cols, fc2_cols = gather_weights(w_qkv, w_out, w_fc1, w_fc2)
    ids_all = lax.all_gather(
        jnp.concatenate([bucket_ids, class_labels], axis=1), "rows", axis=0, tiled=True
    )
    every_slot = row_parts * image_count
    table_places = lax.axis_index("rows") * table_rows + jnp.arange(table_rows, dtype=jnp.int32)
    bucket_hot = (
        ids_all[:, :slot_count].reshape(every_slot)[:, None] == table_places[None, :]
    ).astype(jnp.bfloat16)
    label_hot = (
        ids_all[:, slot_count:].reshape(every_slot)[:, None] == table_places[None, :]
    ).astype(jnp.bfloat16)
    condition = lax.psum(
        jnp.dot(bucket_hot, time_table, preferred_element_type=jnp.float32)
        + jnp.dot(label_hot, class_table, preferred_element_type=jnp.float32),
        "rows",
    )
    silu_value, silu_pull = jax.vjp(silu_plain, condition)
    silu_low = silu_value.astype(jnp.bfloat16)
    mods_part = jnp.dot(silu_low, w_ada, preferred_element_type=jnp.float32)
    mods_cols = lax.psum(mods_part, "heads").reshape(row_parts, image_count, ada_width)
    mods_own = lax.all_to_all(mods_cols, "rows", split_axis=0, concat_axis=0, tiled=True)
    mods_all = mods_own.transpose(1, 0, 2).reshape(
        image_count, row_parts * ada_width
    ) + b_ada.astype(jnp.float32)
    positions = member * tok_rows + jnp.arange(tok_rows, dtype=jnp.int32)
    own_segments = lax.dynamic_slice_in_dim(
        segment_ids.reshape(seq_count * seq_len), member * tok_rows, tok_rows
    )
    token_image = positions // seq_len * slot_count + own_segments
    token_hot = (token_image[:, None] == jnp.arange(image_count, dtype=jnp.int32)[None, :]).astype(
        jnp.float32
    )
    token_mods = [
        jnp.dot(
            token_hot,
            mods_all[:, part_index * model_width : (part_index + 1) * model_width],
            precision=HIGH,
        )
        for part_index in range(6)
    ]
    shift_attn, scale_attn, gate_attn, shift_mlp, scale_mlp, gate_mlp = token_mods
    inputs = patches.astype(jnp.float32)
    first_value, first_pull = jax.vjp(modulate, inputs, shift_attn, scale_attn)
    hidden_one = first_value.astype(jnp.bfloat16)
    rows_one = lax.all_gather(hidden_one, "heads", axis=0, tiled=True)
    zero_bias = jnp.zeros((head_local, head_size), b_qv.dtype)
    qkv_bias = (
        jnp.concatenate([b_qv[:, :head_size], zero_bias, b_qv[:, head_size:]], axis=1)
        .reshape(head_local * 3 * head_size)
        .astype(jnp.float32)
    )
    projected = (jnp.dot(rows_one, qkv_cols, preferred_element_type=jnp.float32) + qkv_bias).astype(
        jnp.bfloat16
    )
    seq_qkv = projected.reshape(seq_count, seq_len, head_local, 3, head_size)
    slot_ends = jnp.cumsum(image_lengths, axis=1)
    places = jnp.arange(seq_len, dtype=jnp.int32)
    image_of = jnp.sum((places[None, :, None] >= slot_ends[:, None, :]).astype(jnp.int32), axis=2)

    def block_scores(query_rows, key_rows, image_rows, image_cols):
        scores = (
            jnp.einsum("qhd,khd->hqk", query_rows, key_rows, preferred_element_type=jnp.float32)
            * scale_factor
        )
        return jnp.where((image_rows[:, None] == image_cols[None, :])[None], scores, MASKED)

    def attend_forward(pieces):
        seq_block, seq_image = pieces
        key_rows = seq_block[:, :, 1]
        value_rows = seq_block[:, :, 2]
        outputs = []
        totals = []
        for row_start in range(0, seq_len, block_rows):
            stop_row = row_start + block_rows
            query_rows = seq_block[row_start:stop_row, :, 0]
            scores = block_scores(query_rows, key_rows, seq_image[row_start:stop_row], seq_image)
            row_peak = jnp.max(scores, axis=2, keepdims=True)
            raised = jnp.exp(scores - row_peak)
            row_total = jnp.sum(raised, axis=2, keepdims=True)
            soft_low = (raised / row_total).astype(jnp.bfloat16)
            outputs.append(
                jnp.einsum(
                    "hqk,khd->qhd", soft_low, value_rows, preferred_element_type=jnp.float32
                ).astype(jnp.bfloat16)
            )
            totals.append((row_peak + jnp.log(row_total))[:, :, 0])
        return (jnp.concatenate(outputs, axis=0), jnp.concatenate(totals, axis=1))

    mixed, log_totals = lax.map(attend_forward, (seq_qkv, image_of))
    mixed_rows = mixed.reshape(group_rows, head_local * head_size)
    attn_out = lax.psum_scatter(
        times_transposed(
            lax.slice_in_dim(mixed_rows, 0, tok_rows * lax.axis_size("heads"), axis=0), out_cols
        ).astype(jnp.bfloat16),
        "heads",
        scatter_dimension=0,
        tiled=True,
    ).astype(jnp.float32) + b_out.astype(jnp.float32)
    after_attn = inputs + gate_attn * attn_out
    second_value, second_pull = jax.vjp(modulate, after_attn, shift_mlp, scale_mlp)
    hidden_two = second_value.astype(jnp.bfloat16)
    rows_two = lax.all_gather(hidden_two, "heads", axis=0, tiled=True)
    inner = jnp.dot(rows_two, fc1_cols, preferred_element_type=jnp.float32) + b_fc1.astype(
        jnp.float32
    )
    gelu_value, gelu_pull = jax.vjp(gelu_tanh, inner)
    active = gelu_value.astype(jnp.bfloat16)
    ffn_out = lax.psum_scatter(
        times_transposed(
            lax.slice_in_dim(active, 0, tok_rows * lax.axis_size("heads"), axis=0), fc2_cols
        ).astype(jnp.bfloat16),
        "heads",
        scatter_dimension=0,
        tiled=True,
    ).astype(jnp.float32) + b_fc2.astype(jnp.float32)
    block_out = (after_attn + gate_mlp * ffn_out).astype(jnp.bfloat16)
    upstream = cotangent.astype(jnp.float32)
    grad_ffn = (gate_mlp * upstream).astype(jnp.bfloat16)
    ffn_rows = lax.all_gather(grad_ffn, "heads", axis=0, tiled=True)
    grad_w_fc2 = contract_rows(ffn_rows, active)
    grad_b_fc2 = jnp.sum(ffn_rows, axis=0, dtype=jnp.float32)
    grad_active = jnp.dot(ffn_rows, fc2_cols, preferred_element_type=jnp.float32)
    grad_inner = gelu_pull(grad_active)[0].astype(jnp.bfloat16)
    grad_w_fc1 = contract_rows(rows_two, grad_inner)
    grad_b_fc1 = jnp.sum(grad_inner, axis=0, dtype=jnp.float32)
    grad_hidden_two = lax.psum_scatter(
        times_transposed(
            lax.slice_in_dim(grad_inner, 0, tok_rows * lax.axis_size("heads"), axis=0), fc1_cols
        ).astype(jnp.bfloat16),
        "heads",
        scatter_dimension=0,
        tiled=True,
    ).astype(jnp.float32)
    grad_after, grad_shift_mlp, grad_scale_mlp = second_pull(grad_hidden_two)
    grad_after = grad_after + upstream
    grad_gate_mlp = upstream * ffn_out
    grad_gate_attn = grad_after * attn_out
    grad_attn = (gate_attn * grad_after).astype(jnp.bfloat16)
    attn_rows_grad = lax.all_gather(grad_attn, "heads", axis=0, tiled=True)
    grad_w_out = contract_rows(attn_rows_grad, mixed_rows)
    grad_b_out = jnp.sum(attn_rows_grad, axis=0, dtype=jnp.float32)
    grad_mixed = jnp.dot(attn_rows_grad, out_cols, preferred_element_type=jnp.float32).astype(
        jnp.bfloat16
    )
    grad_seq = grad_mixed.reshape(seq_count, seq_len, head_local, head_size)

    def attend_backward(pieces):
        seq_block, seq_image, seq_grad, seq_totals = pieces
        key_rows = seq_block[:, :, 1]
        value_rows = seq_block[:, :, 2]
        grad_keys = jnp.zeros(key_rows.shape, jnp.float32)
        grad_values = jnp.zeros(value_rows.shape, jnp.float32)
        grad_queries = []
        for row_start in range(0, seq_len, block_rows):
            stop_row = row_start + block_rows
            query_rows = seq_block[row_start:stop_row, :, 0]
            grad_rows = seq_grad[row_start:stop_row]
            scores = block_scores(query_rows, key_rows, seq_image[row_start:stop_row], seq_image)
            soft_probs = jnp.exp(scores - seq_totals[:, row_start:stop_row, None])
            grad_probs = jnp.einsum(
                "qhd,khd->hqk", grad_rows, value_rows, preferred_element_type=jnp.float32
            )
            inner_sum = jnp.sum(soft_probs * grad_probs, axis=2, keepdims=True)
            grad_scores = (soft_probs * (grad_probs - inner_sum)).astype(jnp.bfloat16)
            grad_queries.append(
                jnp.einsum(
                    "hqk,khd->qhd", grad_scores, key_rows, preferred_element_type=jnp.float32
                )
                * scale_factor
            )
            grad_keys = (
                grad_keys
                + jnp.einsum(
                    "hqk,qhd->khd", grad_scores, query_rows, preferred_element_type=jnp.float32
                )
                * scale_factor
            )
            grad_values = grad_values + jnp.einsum(
                "hqk,qhd->khd",
                soft_probs.astype(jnp.bfloat16),
                grad_rows,
                preferred_element_type=jnp.float32,
            )
        stacked = jnp.stack([jnp.concatenate(grad_queries, axis=0), grad_keys, grad_values], axis=2)
        return stacked.astype(jnp.bfloat16)

    grad_qkv = lax.map(attend_backward, (seq_qkv, image_of, grad_seq, log_totals)).reshape(
        group_rows, head_local * 3 * head_size
    )
    grad_w_qkv = contract_rows(rows_one, grad_qkv)
    bias_terms = jnp.sum(grad_qkv, axis=0, dtype=jnp.float32).reshape(head_local, 3, head_size)
    grad_b_qv = jnp.concatenate([bias_terms[:, 0], bias_terms[:, 2]], axis=1)
    grad_hidden_one = lax.psum_scatter(
        times_transposed(
            lax.slice_in_dim(grad_qkv, 0, tok_rows * lax.axis_size("heads"), axis=0), qkv_cols
        ).astype(jnp.bfloat16),
        "heads",
        scatter_dimension=0,
        tiled=True,
    ).astype(jnp.float32)
    grad_inputs, grad_shift_attn, grad_scale_attn = first_pull(grad_hidden_one)
    grad_patches = grad_inputs + grad_after
    token_grads = (
        grad_shift_attn,
        grad_scale_attn,
        grad_gate_attn,
        grad_shift_mlp,
        grad_scale_mlp,
        grad_gate_mlp,
    )
    mods_grad_part = jnp.concatenate(
        [contract_rows_exact(token_hot, grad_term) for grad_term in token_grads], axis=1
    )
    grad_mods = lax.psum(mods_grad_part.astype(jnp.bfloat16), "heads")
    grad_cols = lax.all_to_all(
        grad_mods.reshape(image_count, row_parts, ada_width).transpose(1, 0, 2),
        "rows",
        split_axis=0,
        concat_axis=0,
        tiled=True,
    ).reshape(every_slot, ada_width)
    grad_w_ada = contract_rows(silu_low, grad_cols)
    grad_b_ada = jnp.sum(grad_cols, axis=0, dtype=jnp.float32)
    grad_silu = lax.psum(times_transposed(grad_cols, w_ada), "rows")
    grad_condition = silu_pull(grad_silu)[0]
    grad_time = contract_rows_exact(bucket_hot.astype(jnp.float32), grad_condition)
    grad_class = contract_rows_exact(label_hot.astype(jnp.float32), grad_condition)

    def row_reduced(partial):
        return lax.psum_scatter(
            partial.astype(jnp.bfloat16), "rows", scatter_dimension=0, tiled=True
        ).astype(jnp.float32)

    grad_w_qkv, grad_w_out, grad_w_fc1, grad_w_fc2 = (
        row_reduced(grad_w_qkv),
        row_reduced(grad_w_out),
        row_reduced(grad_w_fc1),
        row_reduced(grad_w_fc2),
    )
    bias_sizes = (grad_b_qv.size, grad_b_fc1.size, grad_b_out.size, grad_b_fc2.size)
    bias_all = lax.psum(
        jnp.concatenate([grad_b_qv.reshape(-1), grad_b_fc1, grad_b_out, grad_b_fc2]), "rows"
    )
    edges = [sum(bias_sizes[:step]) for step in range(5)]
    bias_rows = model_width // row_parts
    row_start = lax.axis_index("rows") * bias_rows
    grad_b_qv = bias_all[edges[0] : edges[1]].reshape(grad_b_qv.shape)
    grad_b_fc1 = bias_all[edges[1] : edges[2]]
    grad_b_out = lax.dynamic_slice_in_dim(bias_all[edges[2] : edges[3]], row_start, bias_rows)
    grad_b_fc2 = lax.dynamic_slice_in_dim(bias_all[edges[3] : edges[4]], row_start, bias_rows)
    return (
        block_out,
        grad_patches,
        grad_time,
        grad_class,
        grad_w_ada,
        grad_b_ada,
        grad_w_qkv,
        grad_b_qv,
        grad_w_out,
        grad_b_out,
        grad_w_fc1,
        grad_b_fc1,
        grad_w_fc2,
        grad_b_fc2,
    )


MESH = pl.DeviceIdType.MESH
ROW_PARTS = 8
HEAD_PARTS = 4
SLOT_ROWS = 8
VMEM_SPEC = pl.BlockSpec(memory_space=pltpu.VMEM)
ANY_SPEC = pl.BlockSpec(memory_space=pl.ANY)
DMA = pltpu.SemaphoreType.DMA
GRANT = 60 * 1024 * 1024


def places():
    row = lax.axis_index("rows")
    member = lax.axis_index("heads")
    sibling = member + 1 - 2 * lax.rem(member, 2)
    partner = lax.rem(member + 2, HEAD_PARTS)
    opposite = lax.rem(sibling + 2, HEAD_PARTS)
    return row, member, sibling, partner, opposite


def greet(row_steps, head_members):
    barrier = pltpu.get_barrier_semaphore()
    row = lax.axis_index("rows")
    for step in row_steps:
        pl.semaphore_signal(
            barrier,
            inc=1,
            device_id={"rows": lax.rem(row + step, ROW_PARTS)},
            device_id_type=MESH,
        )
    for other in head_members:
        pl.semaphore_signal(barrier, inc=1, device_id={"heads": other}, device_id_type=MESH)
    pl.semaphore_wait(barrier, len(row_steps) + len(head_members))


def to_row(source, target, send, recv, row):
    return pltpu.make_async_remote_copy(
        src_ref=source,
        dst_ref=target,
        send_sem=send,
        recv_sem=recv,
        device_id={"rows": row},
        device_id_type=MESH,
    )


def to_head(source, target, send, recv, member):
    return pltpu.make_async_remote_copy(
        src_ref=source,
        dst_ref=target,
        send_sem=send,
        recv_sem=recv,
        device_id={"heads": member},
        device_id_type=MESH,
    )


class RowGather:
    def __init__(self, shard, full, sends, recvs, local_sem, chunks):
        self.row = lax.axis_index("rows")
        self.level = self.row // 2
        self.side = lax.rem(self.row, 2)
        self.mate = self.row + 1 - 2 * self.side
        size = shard.shape[0] // chunks
        self.own = pltpu.make_async_copy(shard, full.at[self.row], local_sem)
        self.straight = []
        self.across = []
        for chunk in range(chunks):
            part = pl.ds(chunk * size, size)
            straight = []
            across = [
                to_row(
                    shard.at[part],
                    full.at[self.row, part],
                    sends.at[chunk, 3],
                    recvs.at[chunk, 3],
                    self.mate,
                )
            ]
            for step in range(1, 4):
                target = lax.rem(self.level + step, 4) * 2 + self.side
                origin = lax.rem(self.level + 4 - step, 4) * 2 + self.side
                straight.append(
                    to_row(
                        shard.at[part],
                        full.at[self.row, part],
                        sends.at[chunk, step - 1],
                        recvs.at[chunk, step - 1],
                        target,
                    )
                )
                across.append(
                    to_row(
                        full.at[origin, part],
                        full.at[origin, part],
                        sends.at[chunk, 3 + step],
                        recvs.at[chunk, 3 + step],
                        self.mate,
                    )
                )
            self.straight.append(straight)
            self.across.append(across)

    def start(self, chunk):
        for copy in self.straight[chunk]:
            copy.start()
        self.across[chunk][0].start()

    def relay(self, chunk):
        for step in range(3):
            self.straight[chunk][step].wait_recv()
            self.across[chunk][1 + step].start()

    def finish(self):
        self.own.wait()
        for straight, across in zip(self.straight, self.across):
            for copy in straight:
                copy.wait_send()
            for copy in across:
                copy.wait()


class HeadGather:
    def __init__(self, block, full, sends, recvs, local_sem):
        row, member, sibling, partner, opposite = places()
        self.own = None
        if block is None:
            block = full.at[member]
        else:
            self.own = pltpu.make_async_copy(block, full.at[member], local_sem)
        self.beside = to_head(block, full.at[member], sends.at[0], recvs.at[0], sibling)
        self.across = to_head(block, full.at[member], sends.at[1], recvs.at[1], partner)
        self.onward = to_head(
            full.at[partner], full.at[partner], sends.at[2], recvs.at[2], sibling
        )

    def start(self):
        self.across.start()
        self.beside.start()
        if self.own is not None:
            self.own.start()

    def wait_sibling(self):
        self.beside.wait_recv()

    def wait_partner(self):
        self.across.wait_recv()
        self.onward.start()

    def wait_opposite(self):
        self.onward.wait_recv()

    def finish(self):
        if self.own is not None:
            self.own.wait()
        self.beside.wait_send()
        self.across.wait_send()
        self.onward.wait_send()


def front_kernel(
    ids_ref,
    time_ref,
    class_ref,
    ada_ref,
    patches_ref,
    qkv_ref,
    qkv_full,
    patches_full,
    cond_all,
    mods_ref,
    ids_all,
    cond_part,
    cond_in,
    mods_part,
    mods_in,
    mods_sibling,
    mods_pair,
    mods_partner,
    small_send,
    small_recv,
    pair_send,
    pair_recv,
    head_send,
    head_recv,
    qkv_send,
    qkv_recv,
    local_sems,
):
    row, member, sibling, partner, opposite = places()
    greet(range(1, ROW_PARTS), (sibling, partner))
    others = [(step, lax.rem(row + step, ROW_PARTS)) for step in range(1, ROW_PARTS)]

    def spread(stage, source_of, target):
        copies = []
        for step, other in others:
            copy = to_row(
                source_of(other),
                target.at[row],
                small_send.at[stage, step - 1],
                small_recv.at[stage, step - 1],
                other,
            )
            copy.start()
            copies.append(copy)
        return copies

    def settle(copies):
        for copy in copies:
            copy.wait()

    ids_copies = spread(0, lambda other: ids_ref, ids_all)
    gather_qkv = RowGather(qkv_ref, qkv_full, qkv_send, qkv_recv, local_sems.at[0], 3)
    gather_patches = HeadGather(patches_ref, patches_full, head_send, head_recv, local_sems.at[1])
    gather_patches.start()
    gather_qkv.own.start()
    gather_qkv.start(0)
    ids_all[row] = ids_ref[...]
    settle(ids_copies)
    table_rows = time_ref.shape[0]
    slots = ROW_PARTS * SLOT_ROWS
    table_places = row * table_rows + lax.broadcasted_iota(jnp.int32, (slots, table_rows), 1)
    bucket_hot = (
        ids_all[:, 0:SLOT_ROWS].reshape(slots, table_rows) == table_places
    ).astype(jnp.bfloat16)
    label_hot = (
        ids_all[:, SLOT_ROWS : 2 * SLOT_ROWS].reshape(slots, table_rows) == table_places
    ).astype(jnp.bfloat16)
    found = jnp.dot(bucket_hot, time_ref[...], preferred_element_type=jnp.float32) + jnp.dot(
        label_hot, class_ref[...], preferred_element_type=jnp.float32
    )
    cond_part[...] = found.reshape(cond_part.shape)
    copies = spread(1, lambda other: cond_part.at[other], cond_in)
    gather_qkv.start(1)
    cond_in[row] = cond_part[row]
    settle(copies)
    condition = jnp.sum(cond_in[...], axis=0)
    cond_all[row] = condition
    cond_part[row] = condition
    copies = spread(2, lambda other: cond_part.at[row], cond_all)
    gather_qkv.relay(0)
    settle(copies)
    every = cond_all[...].reshape(slots, cond_all.shape[2])
    silu_low = (every / (1.0 + jnp.exp(-every))).astype(jnp.bfloat16)
    mods_part[...] = jnp.dot(
        silu_low, ada_ref[...], preferred_element_type=jnp.float32
    ).reshape(mods_part.shape)
    copies = spread(3, lambda other: mods_part.at[other], mods_in)
    gather_qkv.start(2)
    mods_in[row] = mods_part[row]
    gather_qkv.relay(1)
    settle(copies)
    beside = to_head(mods_in, mods_sibling, pair_send.at[0], pair_recv.at[0], sibling)
    beside.start()
    gather_patches.wait_sibling()
    beside.wait()
    mods_pair[...] = mods_in[...] + mods_sibling[...]
    across = to_head(mods_pair, mods_partner, pair_send.at[1], pair_recv.at[1], partner)
    across.start()
    gather_patches.wait_partner()
    gather_qkv.relay(2)
    across.wait()
    mods_ref[...] = mods_pair[...] + mods_partner[...]
    gather_patches.wait_opposite()
    gather_patches.finish()
    gather_qkv.finish()


def front(ids, time_table, class_table, w_ada, patches, w_qkv):
    depth, ada_width = w_ada.shape
    shape = jax.ShapeDtypeStruct
    slotted = (ROW_PARTS, SLOT_ROWS)
    wide = pltpu.VMEM(slotted + (ada_width,), jnp.float32)
    narrow = pltpu.VMEM(slotted + (depth,), jnp.float32)
    return pl.pallas_call(
        front_kernel,
        out_shape=(
            shape((ROW_PARTS,) + w_qkv.shape, jnp.bfloat16),
            shape((HEAD_PARTS,) + patches.shape, jnp.bfloat16),
            shape(slotted + (depth,), jnp.float32),
            shape(slotted + (ada_width,), jnp.float32),
            shape((ROW_PARTS,) + ids.shape, jnp.int32),
        ),
        in_specs=[VMEM_SPEC] * 6,
        out_specs=[ANY_SPEC] * 2 + [VMEM_SPEC] * 3,
        scratch_shapes=[narrow] * 2
        + [wide] * 5
        + [
            DMA((4, 7)),
            DMA((4, 7)),
            DMA((2,)),
            DMA((2,)),
            DMA((3,)),
            DMA((3,)),
            DMA((3, 7)),
            DMA((3, 7)),
            DMA((2,)),
        ],
        compiler_params=pltpu.CompilerParams(
            collective_id=0, has_side_effects=True, vmem_limit_bytes=GRANT
        ),
        name="front",
    )(ids, time_table, class_table, w_ada, patches, w_qkv)


class HeadReduce:
    def __init__(self, partial, beside_in, pair, across_in, sends, recvs):
        row, member, sibling, partner, opposite = places()
        self.member = member
        self.partner = partner
        self.partial = partial
        self.beside_in = beside_in
        self.pair = pair
        self.across_in = across_in
        self.first = to_head(
            partial.at[opposite], beside_in.at[1], sends.at[0], recvs.at[0], sibling
        )
        self.second = to_head(
            partial.at[sibling], beside_in.at[0], sends.at[1], recvs.at[1], sibling
        )
        self.across = to_head(pair, across_in, sends.at[2], recvs.at[2], partner)

    def start(self):
        self.first.start()
        self.second.start()

    def send_pair(self):
        self.first.wait_recv()
        self.pair[...] = (
            self.partial[self.partner].astype(jnp.float32)
            + self.beside_in[1].astype(jnp.float32)
        ).astype(jnp.bfloat16)
        self.across.start()

    def settle(self):
        self.second.wait_recv()
        self.across.wait_recv()

    def rows(self, part):
        return (
            self.partial[self.member, part].astype(jnp.float32)
            + self.beside_in[0, part].astype(jnp.float32)
            + self.across_in[part].astype(jnp.float32)
        )

    def finish(self):
        self.first.wait_send()
        self.second.wait_send()
        self.across.wait_send()


class RowReduce:
    def __init__(self, partial, chunk, buffers, total, sends, recvs):
        row = lax.axis_index("rows")
        self.level = row // 2
        self.side = lax.rem(row, 2)
        mate = row + 1 - 2 * self.side
        self.partial = partial
        self.mate_in, self.pair, self.straight_in = buffers
        self.total = total
        size = total.shape[0]
        self.part = pl.ds(chunk * size, size)
        self.beside = to_row(
            partial.at[:, 1 - self.side, self.part], self.mate_in, sends.at[0], recvs.at[0], mate
        )
        self.straight = []
        for step in range(1, 4):
            target = lax.rem(self.level + step, 4)
            self.straight.append(
                to_row(
                    self.pair.at[target],
                    self.straight_in.at[step - 1],
                    sends.at[step],
                    recvs.at[step],
                    target * 2 + self.side,
                )
            )

    def start(self):
        self.beside.start()

    def send_pair(self):
        self.beside.wait_recv()

        def one(level, carry):
            self.pair[level] = (
                self.partial[level, self.side, self.part].astype(jnp.float32)
                + self.mate_in[level].astype(jnp.float32)
            ).astype(jnp.bfloat16)
            return carry

        lax.fori_loop(0, 4, one, 0)
        for copy in self.straight:
            copy.start()

    def finish(self):
        for copy in self.straight:
            copy.wait_recv()
        self.total[...] = (
            self.pair[self.level].astype(jnp.float32)
            + self.straight_in[0].astype(jnp.float32)
            + self.straight_in[1].astype(jnp.float32)
            + self.straight_in[2].astype(jnp.float32)
        )
        self.beside.wait_send()
        for copy in self.straight:
            copy.wait_send()


def row_reduces(jobs, reducing):
    buffers, sends, recvs = reducing[:-2], reducing[-2], reducing[-1]
    return [
        RowReduce(
            partial,
            chunk,
            buffers[3 * place : 3 * place + 3],
            total,
            sends.at[place],
            recvs.at[place],
        )
        for place, (partial, chunk, total) in enumerate(jobs)
    ]


def reduce_scratch(sizes):
    landing = []
    for rows, columns in sizes:
        landing += [
            pltpu.VMEM((4, rows, columns), jnp.bfloat16),
            pltpu.VMEM((4, rows, columns), jnp.bfloat16),
            pltpu.VMEM((3, rows, columns), jnp.bfloat16),
        ]
    return landing + [DMA((len(sizes), 4)), DMA((len(sizes), 4))]


def picked(vectors, part_index, segments, width):
    wide = jnp.broadcast_to(segments, (segments.shape[0], width))
    slot_count = vectors.shape[1]
    chosen = vectors[part_index, slot_count - 1 : slot_count]
    for slot in range(slot_count - 2, -1, -1):
        chosen = jnp.where(wide == slot, vectors[part_index, slot : slot + 1], chosen)
    return chosen


def centre_rows(values):
    centred = values - jnp.mean(values, axis=1, keepdims=True)
    factor = lax.rsqrt(jnp.mean(centred * centred, axis=1, keepdims=True) + EPSILON)
    return centred * factor, factor


def weight_grad(left, right, target):
    blocks, tok_rows, depth = left.shape
    height = blocks * tok_rows
    flat = target.reshape(depth, target.shape[3])
    third = depth // 3

    def some(step, carry):
        columns = pl.ds(pl.multiple_of(step * third, 128), third)
        flat[columns] = contract_rows(
            left[:, :, columns].reshape(height, third),
            right[...].reshape(height, right.shape[2]),
        ).astype(jnp.bfloat16)
        return carry

    lax.fori_loop(0, 3, some, 0)


def core_kernel(
    patches_full,
    qkv_ref,
    out_shard,
    fc1_shard,
    fc2_shard,
    cotangent_ref,
    patches_ref,
    segments_ref,
    keys_image,
    rows_image,
    hot_ref,
    vectors_ref,
    bias_ref,
    qkv_bias,
    normed_rows,
    parts,
    totals_out,
    mixed,
    out_w,
    active_rows,
    after_ref,
    after_grad,
    attn_grad,
    slot_sums,
    bias_sums,
    fc2_rest,
    fc1_part,
    fc2_head,
    fc2_neck,
    ffn_rows,
    hidden_rows,
    inner_grad,
    fc2_part,
    inner_bias,
    ffn_bias,
    out_full,
    fc1_full,
    fc2_full,
    active_grad,
    value_columns,
    head_mixed,
    bias,
    group_part,
    beside_in,
    pair_rows,
    across_in,
    attn_out,
    gather_send,
    gather_recv,
    reduce_send,
    reduce_recv,
    out_send,
    out_recv,
    fc1_send,
    fc1_recv,
    fc2_send,
    fc2_recv,
    local_sems,
    *reducing,
):
    row, member, sibling, partner, opposite = places()
    direction = sibling - member
    greet(range(1, ROW_PARTS), (sibling, partner))
    tok_rows, model_width = patches_ref.shape
    blocks = normed_rows.shape[0]
    seq_len = blocks * tok_rows
    width = qkv_ref.shape[1]
    head_local = totals_out.shape[0]
    head_size = width // (3 * head_local)
    scale_factor = 1.0 / math.sqrt(head_size)
    loads = [
        pltpu.make_async_copy(patches_full.at[block], normed_rows.at[block], local_sems.at[block])
        for block in range(blocks)
    ]
    for load in loads:
        load.start()
    gather_out = RowGather(out_shard, out_full, out_send, out_recv, local_sems.at[4], 1)
    gather_fc1 = RowGather(fc1_shard, fc1_full, fc1_send, fc1_recv, local_sems.at[5], 3)
    gather_fc2 = RowGather(fc2_shard, fc2_full, fc2_send, fc2_recv, local_sems.at[6], 3)
    gather_cotangent = HeadGather(
        cotangent_ref, ffn_rows, gather_send.at[2], gather_recv.at[2], local_sems.at[7]
    )
    gather_out.own.start()
    gather_out.start(0)
    gather_fc1.own.start()
    gather_fc1.start(0)
    gather_fc2.own.start()
    gather_cotangent.start()
    reduce_attn = HeadReduce(
        group_part, beside_in, pair_rows, across_in, reduce_send.at[0], reduce_recv.at[0]
    )
    reduce_hidden = HeadReduce(
        group_part, beside_in, pair_rows, across_in, reduce_send.at[1], reduce_recv.at[1]
    )
    gather_hidden = HeadGather(None, hidden_rows, gather_send.at[0], gather_recv.at[0], None)
    gather_grad = HeadGather(None, attn_grad, gather_send.at[1], gather_recv.at[1], None)
    parts[...] = jnp.zeros_like(parts)
    for load in loads:
        load.wait()

    def first_norm(step, carry):
        block = step // 2
        part = pl.ds(pl.multiple_of(lax.rem(step, 2) * 128, 128), 128)
        segments = segments_ref[block, part]
        normed, _ = centre_rows(normed_rows[block, part].astype(jnp.float32))
        normed_rows[block, part] = (
            normed * (1.0 + picked(vectors_ref, 1, segments, model_width))
            + picked(vectors_ref, 0, segments, model_width)
        ).astype(jnp.bfloat16)
        return carry

    lax.fori_loop(0, 2 * blocks, first_norm, 0)
    gather_out.relay(0)
    gather_fc1.start(1)

    def project_in(block, carry):
        rows = pl.ds(pl.multiple_of(block * tok_rows, tok_rows), tok_rows)
        active_grad[0, :, 0:width] = (
            jnp.dot(normed_rows[block], qkv_ref[...], preferred_element_type=jnp.float32)
            + qkv_bias[...]
        )
        for part in range(3 * head_local):
            parts[part, rows, 0:head_size] = active_grad[
                0, :, part * head_size : (part + 1) * head_size
            ].astype(jnp.bfloat16)
        return carry

    lax.fori_loop(0, blocks, project_in, 0)
    gather_fc1.relay(0)
    gather_fc1.start(2)

    def turn(head, carry):
        value_columns[head] = parts[3 * head + 2].astype(jnp.float32).T.astype(jnp.bfloat16)
        return carry

    lax.fori_loop(0, head_local, turn, 0)

    def attend(block):
        rows = pl.ds(pl.multiple_of(block * tok_rows, tok_rows), tok_rows)
        same = jnp.broadcast_to(keys_image[...], (seq_len, tok_rows)) == jnp.broadcast_to(
            rows_image[block], (seq_len, tok_rows)
        )
        bias[...] = jnp.where(same, 0.0, MASKED)

        def one_head(head, carry):
            scores = (
                times_transposed(parts[3 * head + 1], parts[3 * head, rows]) * scale_factor
                + bias[...]
            )
            peak = jnp.max(scores, axis=0, keepdims=True)
            raised = jnp.exp(scores - peak)
            total = jnp.sum(raised, axis=0, keepdims=True)
            totals_out[head, block] = peak + jnp.log(total)
            head_mixed[head] = jnp.dot(
                value_columns[head],
                (raised * (1.0 / total)).astype(jnp.bfloat16),
                preferred_element_type=jnp.float32,
            ).T
            return carry

        lax.fori_loop(0, head_local, one_head, 0)
        for head in range(head_local):
            active_grad[1, :, head * head_size : (head + 1) * head_size] = head_mixed[
                head, :, 0:head_size
            ]
        mixed[block] = active_grad[1, :, 0 : head_local * head_size].astype(jnp.bfloat16)

    def attend_pair(base, factor):
        def one(step, carry):
            attend(base + step * factor)
            return carry

        lax.fori_loop(0, 2, one, 0)

    def project(block):
        group_part[block] = times_transposed(mixed[block], out_w[...]).astype(jnp.bfloat16)

    attend_pair(opposite, -direction)
    gather_out.finish()
    out_w[...] = out_full[...].reshape(out_w.shape)
    project(opposite)
    reduce_attn.first.start()
    project(partner)
    reduce_attn.send_pair()
    gather_fc1.relay(1)
    gather_fc2.start(0)
    attend_pair(sibling, -direction)
    gather_fc1.relay(2)
    gather_fc2.start(1)
    project(sibling)
    reduce_attn.second.start()
    project(member)
    gather_cotangent.wait_sibling()
    gather_cotangent.wait_partner()
    gather_cotangent.wait_opposite()
    gather_cotangent.finish()

    def scale_cotangent(step, carry):
        block = step // 2
        part = pl.ds(pl.multiple_of(lax.rem(step, 2) * 128, 128), 128)
        grad = (
            picked(vectors_ref, 5, segments_ref[block, part], model_width)
            * ffn_rows[block, part].astype(jnp.float32)
        ).astype(jnp.bfloat16)
        ffn_rows[block, part] = grad
        ffn_bias[...] += jnp.sum(grad.astype(jnp.float32).reshape(16, 8, model_width), axis=0)
        return carry

    ffn_bias[...] = jnp.zeros_like(ffn_bias)
    lax.fori_loop(0, 2 * blocks, scale_cotangent, 0)
    gather_fc2.relay(0)
    gather_fc2.start(2)
    reduce_attn.settle()

    def second_norm(block, carry):
        part = pl.ds(pl.multiple_of(block * 128, 128), 128)
        segments = segments_ref[member, part]
        out = reduce_attn.rows(part) + bias_ref[0:1]
        after = patches_ref[part].astype(jnp.float32) + (
            picked(vectors_ref, 2, segments, model_width) * out
        )
        attn_out[part] = out
        after_ref[part] = after
        normed, _ = centre_rows(after)
        hidden_rows[member, part] = (
            normed * (1.0 + picked(vectors_ref, 4, segments, model_width))
            + picked(vectors_ref, 3, segments, model_width)
        ).astype(jnp.bfloat16)
        return carry

    lax.fori_loop(0, tok_rows // 128, second_norm, 0)
    gather_hidden.start()
    reduce_attn.finish()
    gather_fc2.relay(1)
    gather_fc2.relay(2)
    gather_fc1.finish()
    gather_fc2.finish()
    hidden_width = active_rows.shape[2]
    fc1 = fc1_full.reshape(model_width, hidden_width)
    fc2 = fc2_full.reshape(model_width, hidden_width)

    def through_fc2(block, carry):
        active_grad[block] = jnp.dot(
            ffn_rows[block], fc2[...], preferred_element_type=jnp.float32
        )
        return carry

    lax.fori_loop(0, HEAD_PARTS, through_fc2, 0)
    inner_bias[...] = jnp.zeros_like(inner_bias)

    def feed(block, carry):
        inner = jnp.dot(
            hidden_rows[block], fc1[...], preferred_element_type=jnp.float32
        ) + bias_ref[1:2]
        square = inner * inner
        bent = jnp.tanh(TANH_COEFF * (inner + 0.044715 * square * inner))
        half = 0.5 * (1.0 + bent)
        active_rows[block] = (inner * half).astype(jnp.bfloat16)
        slope = half + 0.5 * inner * (1.0 - bent * bent) * (
            TANH_COEFF * (1.0 + 3.0 * 0.044715 * square)
        )
        grad = (active_grad[block] * slope).astype(jnp.bfloat16)
        inner_grad[block] = grad
        inner_bias[...] += jnp.sum(
            grad.astype(jnp.float32).reshape(tok_rows // 8, 8, inner.shape[1]), axis=0
        )
        return carry

    def return_fc1(block, carry):
        group_part[block] = times_transposed(inner_grad[block], fc1[...]).astype(jnp.bfloat16)
        return carry

    gather_hidden.wait_sibling()
    lax.fori_loop(0, 2, lambda step, carry: feed(member + step * direction, carry), 0)
    gather_hidden.wait_partner()
    gather_hidden.wait_opposite()

    def feed_far(step, carry):
        block = opposite - step * direction
        feed(block, carry)
        return return_fc1(block, carry)

    lax.fori_loop(0, 2, feed_far, 0)
    reduce_hidden.first.start()
    reduce_hidden.send_pair()
    lax.fori_loop(0, 2, lambda step, carry: return_fc1(sibling - step * direction, carry), 0)
    reduce_hidden.second.start()

    def forward_fc2(block, carry):
        active_rows[block] = times_transposed(active_rows[block], fc2[...]).astype(jnp.bfloat16)
        return carry

    weight_grad(ffn_rows, active_rows, fc2_part)
    third = fc2_rest.shape[2]
    fc2_rest[...] = fc2_part[:, :, 2 * third : 3 * third]
    reduces = row_reduces(((fc2_part, 0, fc2_head), (fc2_part, 1, fc2_neck)), reducing)
    for unit in reduces:
        unit.start()
    lax.fori_loop(0, HEAD_PARTS, forward_fc2, 0)
    slot_sums[...] = jnp.zeros_like(slot_sums)
    reduce_hidden.settle()

    def second_back(block, carry):
        part = pl.ds(pl.multiple_of(block * 128, 128), 128)
        segments = segments_ref[member, part]
        grad = reduce_hidden.rows(part)
        normed, factor = centre_rows(after_ref[part])
        weighted = grad * (1.0 + picked(vectors_ref, 4, segments, model_width))
        total = cotangent_ref[part].astype(jnp.float32) + factor * (
            weighted
            - jnp.mean(weighted, axis=1, keepdims=True)
            - normed * jnp.mean(weighted * normed, axis=1, keepdims=True)
        )
        after_grad[part] = total
        attn_grad[member, part] = (
            picked(vectors_ref, 2, segments, model_width) * total
        ).astype(jnp.bfloat16)
        hot = hot_ref[:, part]
        for index, term in enumerate((total * attn_out[part], grad, grad * normed)):
            slot_sums[index] += jnp.dot(
                hot, term, precision=HIGH, preferred_element_type=jnp.float32
            )
        return carry

    lax.fori_loop(0, tok_rows // 128, second_back, 0)
    gather_grad.start()
    weight_grad(hidden_rows, inner_grad, fc1_part)
    reduces[0].send_pair()
    bias_sums[...] = jnp.zeros_like(bias_sums)
    bias_sums[0:1] = jnp.sum(inner_bias[...], axis=0, keepdims=True)
    bias_sums[1:2] = jnp.sum(ffn_bias[...], axis=0, keepdims=True)
    gather_grad.wait_sibling()
    gather_grad.wait_partner()
    gather_grad.wait_opposite()
    reduces[1].send_pair()
    for unit in reduces:
        unit.finish()
    gather_hidden.finish()
    gather_grad.finish()
    reduce_hidden.finish()


def core(head_size, *args):
    shape = jax.ShapeDtypeStruct
    patches_full, w_qkv, out_shard, fc1_shard = args[:4]
    blocks, tok_rows, model_width = patches_full.shape
    seq_len = blocks * tok_rows
    out_width = out_shard.shape[1]
    width_part, hidden_width = fc1_shard.shape
    third = width_part // 3
    head_local = out_width // head_size
    low = jnp.bfloat16
    full = jnp.float32
    rows_low = shape((blocks, tok_rows, model_width), low)
    own = shape((tok_rows, model_width), full)
    own_low = pltpu.VMEM((tok_rows, model_width), low)
    group_low = pltpu.VMEM((blocks, tok_rows, model_width), low)
    hidden_low = pltpu.VMEM((blocks, tok_rows, hidden_width), low)
    part_low = (4, 2, width_part, hidden_width)
    return pl.pallas_call(
        core_kernel,
        out_shape=[
            rows_low,
            shape((3 * head_local, seq_len, HEAD_LANES), low),
            shape((head_local, blocks, 1, tok_rows), full),
            shape((blocks, tok_rows, out_width), low),
            shape((model_width, out_width), low),
            rows_low,
            own,
            own,
            rows_low,
            shape((3, SLOT_ROWS, model_width), full),
            shape((8, hidden_width), full),
            shape((4, 2, third, hidden_width), low),
            shape(part_low, low),
            shape((third, hidden_width), full),
            shape((third, hidden_width), full),
        ],
        in_specs=[ANY_SPEC] + [VMEM_SPEC] * 13,
        out_specs=[VMEM_SPEC] * 15,
        scratch_shapes=[
            group_low,
            group_low,
            hidden_low,
            pltpu.VMEM(part_low, low),
            pltpu.VMEM((8, hidden_width), full),
            pltpu.VMEM((8, model_width), full),
            pltpu.VMEM((ROW_PARTS,) + out_shard.shape, low),
            pltpu.VMEM((ROW_PARTS,) + fc1_shard.shape, low),
            pltpu.VMEM((ROW_PARTS,) + fc1_shard.shape, low),
            pltpu.VMEM((blocks, tok_rows, hidden_width), full),
            pltpu.VMEM((head_local, HEAD_LANES, seq_len), low),
            pltpu.VMEM((head_local, tok_rows, HEAD_LANES), full),
            pltpu.VMEM((seq_len, tok_rows), full),
            group_low,
            pltpu.VMEM((2, tok_rows, model_width), low),
            own_low,
            own_low,
            pltpu.VMEM((tok_rows, model_width), full),
            DMA((3, 3)),
            DMA((3, 3)),
            DMA((2, 3)),
            DMA((2, 3)),
            DMA((1, 7)),
            DMA((1, 7)),
            DMA((3, 7)),
            DMA((3, 7)),
            DMA((3, 7)),
            DMA((3, 7)),
            DMA((8,)),
        ]
        + reduce_scratch([(third, hidden_width)] * 2),
        compiler_params=pltpu.CompilerParams(
            collective_id=2, has_side_effects=True, vmem_limit_bytes=67_000_000
        ),
        name="core",
    )(*args)


HEAD_LANES = 128


def rear_kernel(
    parts,
    grad_ref,
    out_ref,
    totals_ref,
    keys_image,
    rows_image,
    fc2_part,
    fc1_part,
    hidden_rows,
    qkv_ref,
    mixed_ref,
    bias_ref,
    patches_ref,
    after_ref,
    vectors_ref,
    segments_ref,
    hot_ref,
    sums_ref,
    silu_ref,
    slope_ref,
    bucket_ref,
    label_ref,
    ada_ref,
    ffn_ref,
    block_ref,
    cotangent_ref,
    ffn_bias,
    block_out,
    patches_grad,
    time_grad,
    class_grad,
    ada_grad,
    ada_bias,
    fc2_tail,
    fc1_grad,
    qkv_grad,
    out_grad,
    bias_sum,
    mixed_grad,
    key_columns,
    grad_keys,
    grad_values,
    bias,
    packed,
    packed_grad,
    hidden_part,
    qkv_part,
    out_part,
    bias_own,
    beside_in,
    pair_rows,
    across_in,
    ffn_beside,
    ffn_pair,
    ffn_across,
    slot_sums,
    mods_own,
    mods_sibling,
    mods_pair,
    mods_partner,
    mods_cols,
    bias_all,
    silu_part,
    silu_in,
    silu_all,
    small_send,
    small_recv,
    pair_send,
    pair_recv,
    head_send,
    head_recv,
    *reducing,
):
    row, member, sibling, partner, opposite = places()
    greet(range(1, ROW_PARTS), (sibling, partner))
    others = [(step, lax.rem(row + step, ROW_PARTS)) for step in range(1, ROW_PARTS)]

    def spread(stage, source_of, target):
        copies = []
        for step, other in others:
            copy = to_row(
                source_of(other),
                target.at[row],
                small_send.at[stage, step - 1],
                small_recv.at[stage, step - 1],
                other,
            )
            copy.start()
            copies.append(copy)
        return copies

    def settle(copies):
        for copy in copies:
            copy.wait()

    third = fc2_tail.shape[0]
    units = row_reduces(
        [(fc2_part, 0, fc2_tail)]
        + [(fc1_part, chunk, fc1_grad.at[pl.ds(chunk * third, third)]) for chunk in range(3)]
        + [(out_part, 0, out_grad)]
        + [(qkv_part, chunk, qkv_grad.at[pl.ds(chunk * third, third)]) for chunk in range(3)],
        reducing,
    )
    reduce_rows = HeadReduce(
        hidden_part, beside_in, pair_rows, across_in, head_send.at[0], head_recv.at[0]
    )
    reduce_ffn = HeadReduce(
        ffn_ref, ffn_beside, ffn_pair, ffn_across, head_send.at[1], head_recv.at[1]
    )
    for unit in units[:3]:
        unit.start()
    reduce_ffn.start()
    reduce_ffn.send_pair()
    blocks, tok_rows, model_width = grad_ref.shape
    width = qkv_ref.shape[1]
    head_local = totals_ref.shape[0]
    head_size = width // (3 * head_local)
    scale_factor = 1.0 / math.sqrt(head_size)
    seq_len = blocks * tok_rows
    mixed_grad[...] = jnp.zeros_like(mixed_grad)
    bias_own[...] = jnp.zeros_like(bias_own)

    def unpack(block, carry):
        rows = pl.ds(pl.multiple_of(block * tok_rows, tok_rows), tok_rows)
        packed[:, 0 : head_local * head_size] = jnp.dot(
            grad_ref[block], out_ref[...], preferred_element_type=jnp.float32
        )
        for head in range(head_local):
            mixed_grad[head, rows, 0:head_size] = packed[
                :, head * head_size : (head + 1) * head_size
            ].astype(jnp.bfloat16)
        bias_own[0] += jnp.sum(
            grad_ref[block].astype(jnp.float32).reshape(tok_rows // 8, 8, model_width), axis=0
        )
        return carry

    lax.fori_loop(0, blocks, unpack, 0)

    def turn(head, carry):
        key_columns[head] = parts[3 * head + 1].astype(jnp.float32).T.astype(jnp.bfloat16)
        return carry

    lax.fori_loop(0, head_local, turn, 0)
    grad_keys[...] = jnp.zeros_like(grad_keys)
    grad_values[...] = jnp.zeros_like(grad_values)
    weight_grad(grad_ref, mixed_ref, out_part)

    for block in range(blocks):
        rows = pl.ds(block * tok_rows, tok_rows)
        same = jnp.broadcast_to(keys_image[...], (seq_len, tok_rows)) == jnp.broadcast_to(
            rows_image[block], (seq_len, tok_rows)
        )
        bias[...] = jnp.where(same, 0.0, MASKED)

        def one_head(head, carry):
            query = parts[3 * head, rows]
            grad = mixed_grad[head, rows]
            scores = times_transposed(parts[3 * head + 1], query) * scale_factor + bias[...]
            probs = jnp.exp(scores - totals_ref[head, block])
            grad_probs = times_transposed(parts[3 * head + 2], grad)
            inner = jnp.sum(probs * grad_probs, axis=0, keepdims=True)
            grad_scores = (probs * (grad_probs - inner)).astype(jnp.bfloat16)
            grad_values[head] += jnp.dot(
                probs.astype(jnp.bfloat16), grad, preferred_element_type=jnp.float32
            )
            grad_keys[head] += jnp.dot(grad_scores, query, preferred_element_type=jnp.float32)
            lanes = pl.ds(pl.multiple_of(head * HEAD_LANES, HEAD_LANES), HEAD_LANES)
            hidden_part[block, :, lanes] = (
                jnp.dot(key_columns[head], grad_scores, preferred_element_type=jnp.float32).T
                * scale_factor
            ).astype(jnp.bfloat16)
            return carry

        lax.fori_loop(0, head_local, one_head, 0)
        units[block].send_pair()
        if block < 2:
            units[block + 3].start()

    def pack(block, carry):
        rows = pl.ds(pl.multiple_of(block * tok_rows, tok_rows), tok_rows)
        for head in range(head_local):
            lane = head * HEAD_LANES
            terms = (
                hidden_part[block, :, lane : lane + head_size].astype(jnp.float32),
                grad_keys[head, rows, 0:head_size] * scale_factor,
                grad_values[head, rows, 0:head_size],
            )
            for place, term in enumerate(terms):
                start = (3 * head + place) * head_size
                packed[:, start : start + head_size] = term
        low = packed[...].astype(jnp.bfloat16)
        packed_grad[block] = low
        bias_own[1, :, 0:width] += jnp.sum(
            low.astype(jnp.float32).reshape(tok_rows // 8, 8, width), axis=0
        )
        return carry

    lax.fori_loop(0, blocks, pack, 0)
    direction = sibling - member

    def project_back(block):
        hidden_part[block] = times_transposed(packed_grad[block], qkv_ref[...]).astype(
            jnp.bfloat16
        )

    def far(step, carry):
        project_back(opposite - step * direction)
        return carry

    def near(step, carry):
        project_back(sibling - step * direction)
        return carry

    lax.fori_loop(0, 2, far, 0)
    reduce_rows.first.start()
    reduce_rows.send_pair()
    lax.fori_loop(0, 2, near, 0)
    reduce_rows.second.start()
    weight_grad(hidden_rows, packed_grad, qkv_part)
    for unit in units[5:]:
        unit.start()
    bias_own[2] = jnp.zeros_like(bias_own[2])
    bias_own[2] = bias_ref[...]
    bias_own[2, 2:3] = jnp.sum(bias_own[0], axis=0, keepdims=True)
    bias_own[2, 3:4] = jnp.sum(bias_own[1], axis=0, keepdims=True)
    bias_copies = spread(1, lambda other: bias_own.at[2], bias_all)
    bias_all[row] = bias_own[2]
    units[4].send_pair()
    slot_sums[...] = jnp.zeros_like(slot_sums)
    reduce_ffn.settle()

    def rows_out(block, carry):
        part = pl.ds(pl.multiple_of(block * 128, 128), 128)
        ffn = reduce_ffn.rows(part) + ffn_bias[0:1]
        gate = picked(vectors_ref, 5, segments_ref[member, part], model_width)
        block_out[part] = (block_ref[part] + gate * ffn).astype(jnp.bfloat16)
        slot_sums[2] += jnp.dot(
            hot_ref[:, part],
            cotangent_ref[part].astype(jnp.float32) * ffn,
            precision=HIGH,
            preferred_element_type=jnp.float32,
        )
        return carry

    lax.fori_loop(0, tok_rows // 128, rows_out, 0)
    units[0].finish()
    units[1].finish()
    units[5].send_pair()
    reduce_rows.settle()

    def rows_back(block, carry):
        part = pl.ds(pl.multiple_of(block * 128, 128), 128)
        grad = reduce_rows.rows(part)
        normed, factor = centre_rows(patches_ref[part].astype(jnp.float32))
        weighted = grad * (1.0 + picked(vectors_ref, 1, segments_ref[member, part], model_width))
        patches_grad[part] = after_ref[part] + factor * (
            weighted
            - jnp.mean(weighted, axis=1, keepdims=True)
            - normed * jnp.mean(weighted * normed, axis=1, keepdims=True)
        )
        hot = hot_ref[:, part]
        slot_sums[0] += jnp.dot(hot, grad, precision=HIGH, preferred_element_type=jnp.float32)
        slot_sums[1] += jnp.dot(
            hot, grad * normed, precision=HIGH, preferred_element_type=jnp.float32
        )
        return carry

    lax.fori_loop(0, tok_rows // 128, rows_back, 0)
    ada_width = ada_ref.shape[1]
    fine = ada_width // 3
    for unit in range(3 * ROW_PARTS):
        part_index, within = divmod(unit * fine, model_width)
        span = slice(within, within + fine)
        if part_index < 2:
            source = slot_sums[part_index, :, span]
        elif part_index == 5:
            source = slot_sums[2, :, span]
        else:
            source = sums_ref[part_index - 2, :, span]
        mods_own[unit // 3, :, unit % 3 * fine : (unit % 3 + 1) * fine] = source
    beside = to_head(mods_own, mods_sibling, pair_send.at[0], pair_recv.at[0], sibling)
    beside.start()
    units[6].send_pair()
    beside.wait()
    mods_pair[...] = mods_own[...] + mods_sibling[...]
    across = to_head(mods_pair, mods_partner, pair_send.at[1], pair_recv.at[1], partner)
    across.start()
    units[2].finish()
    units[3].finish()
    settle(bias_copies)
    bias_sum[...] = jnp.sum(bias_all[...], axis=0)
    across.wait()
    mods_own[...] = (
        (mods_pair[...] + mods_partner[...]).astype(jnp.bfloat16).astype(jnp.float32)
    )
    copies = spread(0, lambda other: mods_own.at[other], mods_cols)
    mods_cols[row] = mods_own[row]
    units[7].send_pair()
    units[4].finish()
    settle(copies)
    slots = ROW_PARTS * SLOT_ROWS
    cols = mods_cols[...].reshape(slots, ada_width)
    low = cols.astype(jnp.bfloat16)
    silu_part[...] = times_transposed(low, ada_ref[...]).reshape(silu_part.shape)
    copies = spread(2, lambda other: silu_part.at[other], silu_in)
    silu_in[row] = silu_part[row]
    ada_grad[...] = jnp.dot(silu_ref[...], low, preferred_element_type=jnp.float32)
    ada_bias[...] = jnp.broadcast_to(jnp.sum(cols, axis=0, keepdims=True), ada_bias.shape)
    settle(copies)
    summed = jnp.sum(silu_in[...], axis=0)
    silu_all[row] = summed
    silu_part[row] = summed
    copies = spread(3, lambda other: silu_part.at[row], silu_all)
    units[5].finish()
    units[6].finish()
    units[7].finish()
    settle(copies)
    grad_condition = silu_all[...].reshape(slots, silu_all.shape[2]) * slope_ref[...]
    time_grad[...] = jnp.dot(
        bucket_ref[...], grad_condition, precision=HIGH, preferred_element_type=jnp.float32
    )
    class_grad[...] = jnp.dot(
        label_ref[...], grad_condition, precision=HIGH, preferred_element_type=jnp.float32
    )
    reduce_rows.finish()
    reduce_ffn.finish()


def rear(*args):
    shape = jax.ShapeDtypeStruct
    grads, w_out, totals, grad_w_fc2, w_qkv, biases, buckets, w_ada = (
        args[place] for place in (1, 2, 3, 6, 9, 11, 20, 22)
    )
    blocks, tok_rows, model_width = grads.shape
    width = w_qkv.shape[1]
    head_local = totals.shape[0]
    seq_len = blocks * tok_rows
    third, hidden_width = grad_w_fc2.shape[2:]
    width_part = 3 * third
    out_width = w_out.shape[1]
    depth, ada_width = w_ada.shape
    table_rows = buckets.shape[0]
    low = jnp.bfloat16
    full = jnp.float32
    heads_wide = pltpu.VMEM((head_local, seq_len, HEAD_LANES), full)
    slotted = (ROW_PARTS, SLOT_ROWS)
    wide = pltpu.VMEM(slotted + (ada_width,), full)
    narrow = pltpu.VMEM(slotted + (depth,), full)
    sizes = (
        [(third, hidden_width)] * 4 + [(width_part, out_width)] + [(third, width)] * 3
    )
    return pl.pallas_call(
        rear_kernel,
        out_shape=[
            shape((tok_rows, model_width), low),
            shape((tok_rows, model_width), full),
            shape((table_rows, depth), full),
            shape((table_rows, depth), full),
            shape((depth, ada_width), full),
            shape((SLOT_ROWS, ada_width), full),
            shape((third, hidden_width), full),
            shape((width_part, hidden_width), full),
            shape((width_part, width), full),
            shape((width_part, out_width), full),
            shape(biases.shape, full),
        ],
        in_specs=[VMEM_SPEC] * 27,
        out_specs=[VMEM_SPEC] * 11,
        scratch_shapes=[
            pltpu.VMEM((head_local, seq_len, HEAD_LANES), low),
            pltpu.VMEM((head_local, HEAD_LANES, seq_len), low),
            heads_wide,
            heads_wide,
            pltpu.VMEM((seq_len, tok_rows), full),
            pltpu.VMEM((tok_rows, width), full),
            pltpu.VMEM((blocks, tok_rows, width), low),
            pltpu.VMEM((blocks, tok_rows, model_width), low),
            pltpu.VMEM((4, 2, width_part, width), low),
            pltpu.VMEM((4, 2, width_part, out_width), low),
            pltpu.VMEM((3,) + biases.shape, full),
        ]
        + [
            pltpu.VMEM((2, tok_rows, model_width), low),
            pltpu.VMEM((tok_rows, model_width), low),
            pltpu.VMEM((tok_rows, model_width), low),
        ]
        * 2
        + [pltpu.VMEM((3, SLOT_ROWS, model_width), full)]
        + [wide] * 5
        + [pltpu.VMEM((ROW_PARTS,) + biases.shape, full)]
        + [narrow] * 3
        + [
            DMA((4, 7)),
            DMA((4, 7)),
            DMA((2,)),
            DMA((2,)),
            DMA((2, 3)),
            DMA((2, 3)),
        ]
        + reduce_scratch(sizes),
        compiler_params=pltpu.CompilerParams(
            collective_id=1, has_side_effects=True, vmem_limit_bytes=67_000_000
        ),
        name="rear",
    )(*args)


def shards_linked(
    patches,
    time_table,
    class_table,
    w_ada,
    b_ada,
    w_qkv,
    b_qv,
    w_out,
    b_out,
    w_fc1,
    b_fc1,
    w_fc2,
    b_fc2,
    image_lengths,
    segment_ids,
    bucket_ids,
    class_labels,
    cotangent,
):
    head_parts = lax.axis_size("heads")
    member = lax.axis_index("heads")
    tok_rows = patches.shape[0]
    model_width = patches.shape[1]
    seq_count = segment_ids.shape[0]
    seq_len = segment_ids.shape[1]
    slot_count = image_lengths.shape[1]
    image_count = seq_count * slot_count
    group_rows = tok_rows * head_parts
    head_local = b_qv.shape[0]
    head_size = b_qv.shape[1] // 2
    block_rows = min(BLOCK_LIMIT, seq_len)
    scale_factor = 1.0 / math.sqrt(head_size)
    row_parts = lax.axis_size("rows")
    table_rows = time_table.shape[0]
    ada_width = w_ada.shape[1]
    every_slot = row_parts * SLOT_ROWS
    slot_pad = jnp.full((SLOT_ROWS - slot_count,), -1, jnp.int32)
    ids = jnp.broadcast_to(
        jnp.concatenate([bucket_ids[0], slot_pad, class_labels[0], slot_pad])[:, None],
        (2 * SLOT_ROWS, table_rows),
    )
    qkv_full, patches_full, condition, mods, ids_all = front(
        ids, time_table, class_table, w_ada, patches, w_qkv
    )
    qkv_cols = qkv_full.reshape(model_width, w_qkv.shape[1])
    condition = condition.reshape(every_slot, condition.shape[2])
    silu_value, silu_pull = jax.vjp(silu_plain, condition)
    silu_low = silu_value.astype(jnp.bfloat16)
    mods_all = mods[:, :slot_count].transpose(1, 0, 2).reshape(
        slot_count, row_parts * ada_width
    ) + b_ada.astype(jnp.float32)
    own_segments = lax.dynamic_slice_in_dim(segment_ids[0], member * tok_rows, tok_rows)[:, None]
    token_hot = (own_segments == jnp.arange(SLOT_ROWS, dtype=jnp.int32)[None, :]).astype(
        jnp.float32
    )
    zero_bias = jnp.zeros((head_local, head_size), b_qv.dtype)
    qkv_bias = (
        jnp.concatenate([b_qv[:, :head_size], zero_bias, b_qv[:, head_size:]], axis=1)
        .reshape(head_local * 3 * head_size)
        .astype(jnp.float32)
    )
    slot_ends = jnp.cumsum(image_lengths, axis=1)
    places = jnp.arange(seq_len, dtype=jnp.int32)
    image_of = jnp.sum((places[None, :, None] >= slot_ends[:, None, :]).astype(jnp.int32), axis=2)

    vectors = mods_all.reshape(slot_count, 6, model_width).transpose(1, 0, 2)
    segments = segment_ids.reshape(head_parts, tok_rows, 1)
    keys_image = image_of.reshape(seq_len, 1)
    rows_image = image_of.reshape(head_parts, 1, tok_rows)
    (
        rows_one,
        parts,
        totals,
        mixed_rows,
        out_cols,
        ffn_part,
        after_attn,
        grad_after,
        attn_rows_grad,
        sums,
        bias_sums,
        grad_w_fc2,
        grad_w_fc1,
        fc2_head,
        fc2_neck,
    ) = core(
        head_size,
        patches_full,
        qkv_cols,
        w_out,
        w_fc1,
        w_fc2,
        cotangent,
        patches,
        segments,
        keys_image,
        rows_image,
        token_hot.T,
        vectors,
        jnp.stack([b_out, b_fc1]).astype(jnp.float32),
        qkv_bias[None, :],
    )
    all_ids = ids_all[:, :, 0]
    table_places = lax.axis_index("rows") * table_rows + jnp.arange(table_rows, dtype=jnp.int32)
    bucket_hot = table_places[:, None] == all_ids[:, :SLOT_ROWS].reshape(every_slot)[None, :]
    label_hot = table_places[:, None] == all_ids[:, SLOT_ROWS:].reshape(every_slot)[None, :]
    (
        block_out,
        grad_patches,
        grad_time,
        grad_class,
        grad_w_ada,
        grad_b_ada,
        fc2_tail,
        grad_w_fc1,
        grad_w_qkv,
        grad_w_out,
        bias_all,
    ) = rear(
        parts,
        attn_rows_grad,
        out_cols,
        totals,
        keys_image,
        rows_image,
        grad_w_fc2,
        grad_w_fc1,
        rows_one,
        qkv_cols,
        mixed_rows,
        bias_sums,
        patches,
        grad_after,
        vectors,
        segments,
        token_hot.T,
        sums,
        silu_low.T,
        silu_pull(jnp.ones_like(condition))[0],
        bucket_hot.astype(jnp.float32),
        label_hot.astype(jnp.float32),
        w_ada,
        ffn_part,
        after_attn,
        cotangent,
        b_fc2.astype(jnp.float32)[None, :],
    )
    grad_w_fc2 = jnp.concatenate([fc2_head, fc2_neck, fc2_tail], axis=0)
    grad_b_ada = grad_b_ada[0]
    bias_rows = model_width // row_parts
    row_start = lax.axis_index("rows") * bias_rows
    grad_b_fc1 = bias_all[0]
    grad_b_fc2 = lax.dynamic_slice_in_dim(bias_all[1], row_start, bias_rows)
    grad_b_out = lax.dynamic_slice_in_dim(bias_all[2], row_start, bias_rows)
    bias_terms = bias_all[3, : head_local * 3 * head_size].reshape(head_local, 3, head_size)
    grad_b_qv = jnp.concatenate([bias_terms[:, 0], bias_terms[:, 2]], axis=1)
    return (
        block_out,
        grad_patches,
        grad_time,
        grad_class,
        grad_w_ada,
        grad_b_ada,
        grad_w_qkv,
        grad_b_qv,
        grad_w_out,
        grad_b_out,
        grad_w_fc1,
        grad_b_fc1,
        grad_w_fc2,
        grad_b_fc2,
    )


def solution(mesh):
    placed = (
        P(("rows", "heads"), None),
        P("rows", "heads"),
        P("rows", "heads"),
        P("heads", "rows"),
        P(),
        P("rows", "heads"),
        P("heads", None),
        P("rows", "heads"),
        P(),
        P("rows", "heads"),
        P("heads"),
        P("rows", "heads"),
        P(),
        P("rows", None),
        P("rows", None),
        P("rows", None),
        P("rows", None),
        P(("rows", "heads"), None),
    )
    linked = mesh.shape["rows"] == ROW_PARTS and mesh.shape["heads"] == HEAD_PARTS
    return jax.shard_map(
        shards_linked if linked else shards_plain,
        mesh=mesh,
        in_specs=placed,
        out_specs=(
            P(("rows", "heads"), None),
            P(("rows", "heads"), None),
            P("rows", "heads"),
            P("rows", "heads"),
            P("heads", "rows"),
            P("rows"),
            P("rows", "heads"),
            P("heads", None),
            P("rows", "heads"),
            P("rows"),
            P("rows", "heads"),
            P("heads"),
            P("rows", "heads"),
            P("rows"),
        ),
        check_vma=False,
    )
```

```python
import functools
import math

import jax
import jax.numpy as jnp
from jax import lax
from jax.experimental import pallas as pl
from jax.experimental.pallas import tpu as pltpu
from jax.sharding import PartitionSpec as P

EPSILON = 1e-06
MASKED = -1e30
HIGH = lax.Precision.HIGHEST
TANH_COEFF = 0.7978845608028654
BLOCK_LIMIT = 512


def layer_norm(values):
    average = jnp.mean(values, axis=-1, keepdims=True)
    centred = values - average
    variance = jnp.mean(centred * centred, axis=-1, keepdims=True)
    return centred * lax.rsqrt(variance + EPSILON)


def gelu_tanh(values):
    return (
        0.5 * values * (1.0 + jnp.tanh(TANH_COEFF * (values + 0.044715 * values * values * values)))
    )


def silu_plain(values):
    return values / (1.0 + jnp.exp(-values))


def modulate(values, shift_term, scale_term):
    return layer_norm(values) * (1.0 + scale_term) + shift_term


def contract_rows(left_matrix, right_matrix):
    return lax.dot_general(
        left_matrix, right_matrix, (((0,), (0,)), ((), ())), preferred_element_type=jnp.float32
    )


def contract_rows_exact(left_matrix, right_matrix):
    return lax.dot_general(
        left_matrix,
        right_matrix,
        (((0,), (0,)), ((), ())),
        precision=HIGH,
        preferred_element_type=jnp.float32,
    )


def times_transposed(left_matrix, right_matrix):
    return lax.dot_general(
        left_matrix, right_matrix, (((1,), (1,)), ((), ())), preferred_element_type=jnp.float32
    )


def gather_weights(w_qkv, w_out, w_fc1, w_fc2):
    return (
        lax.all_gather(w_qkv, "rows", axis=0, tiled=True),
        lax.all_gather(w_out, "rows", axis=0, tiled=True),
        lax.all_gather(w_fc1, "rows", axis=0, tiled=True),
        lax.all_gather(w_fc2, "rows", axis=0, tiled=True),
    )


def shards_plain(
    patches,
    time_table,
    class_table,
    w_ada,
    b_ada,
    w_qkv,
    b_qv,
    w_out,
    b_out,
    w_fc1,
    b_fc1,
    w_fc2,
    b_fc2,
    image_lengths,
    segment_ids,
    bucket_ids,
    class_labels,
    cotangent,
):
    head_parts = lax.axis_size("heads")
    member = lax.axis_index("heads")
    tok_rows = patches.shape[0]
    model_width = patches.shape[1]
    seq_count = segment_ids.shape[0]
    seq_len = segment_ids.shape[1]
    slot_count = image_lengths.shape[1]
    image_count = seq_count * slot_count
    group_rows = tok_rows * head_parts
    head_local = b_qv.shape[0]
    head_size = b_qv.shape[1] // 2
    block_rows = min(BLOCK_LIMIT, seq_len)
    scale_factor = 1.0 / math.sqrt(head_size)
    row_parts = lax.axis_size("rows")
    table_rows = time_table.shape[0]
    ada_width = w_ada.shape[1]
    qkv_cols, out_cols, fc1_cols, fc2_cols = gather_weights(w_qkv, w_out, w_fc1, w_fc2)
    ids_all = lax.all_gather(
        jnp.concatenate([bucket_ids, class_labels], axis=1), "rows", axis=0, tiled=True
    )
    every_slot = row_parts * image_count
    table_places = lax.axis_index("rows") * table_rows + jnp.arange(table_rows, dtype=jnp.int32)
    bucket_hot = (
        ids_all[:, :slot_count].reshape(every_slot)[:, None] == table_places[None, :]
    ).astype(jnp.bfloat16)
    label_hot = (
        ids_all[:, slot_count:].reshape(every_slot)[:, None] == table_places[None, :]
    ).astype(jnp.bfloat16)
    condition = lax.psum(
        jnp.dot(bucket_hot, time_table, preferred_element_type=jnp.float32)
        + jnp.dot(label_hot, class_table, preferred_element_type=jnp.float32),
        "rows",
    )
    silu_value, silu_pull = jax.vjp(silu_plain, condition)
    silu_low = silu_value.astype(jnp.bfloat16)
    mods_part = jnp.dot(silu_low, w_ada, preferred_element_type=jnp.float32)
    mods_cols = lax.psum(mods_part, "heads").reshape(row_parts, image_count, ada_width)
    mods_own = lax.all_to_all(mods_cols, "rows", split_axis=0, concat_axis=0, tiled=True)
    mods_all = mods_own.transpose(1, 0, 2).reshape(
        image_count, row_parts * ada_width
    ) + b_ada.astype(jnp.float32)
    positions = member * tok_rows + jnp.arange(tok_rows, dtype=jnp.int32)
    own_segments = lax.dynamic_slice_in_dim(
        segment_ids.reshape(seq_count * seq_len), member * tok_rows, tok_rows
    )
    token_image = positions // seq_len * slot_count + own_segments
    token_hot = (token_image[:, None] == jnp.arange(image_count, dtype=jnp.int32)[None, :]).astype(
        jnp.float32
    )
    token_mods = [
        jnp.dot(
            token_hot,
            mods_all[:, part_index * model_width : (part_index + 1) * model_width],
            precision=HIGH,
        )
        for part_index in range(6)
    ]
    shift_attn, scale_attn, gate_attn, shift_mlp, scale_mlp, gate_mlp = token_mods
    inputs = patches.astype(jnp.float32)
    first_value, first_pull = jax.vjp(modulate, inputs, shift_attn, scale_attn)
    hidden_one = first_value.astype(jnp.bfloat16)
    rows_one = lax.all_gather(hidden_one, "heads", axis=0, tiled=True)
    zero_bias = jnp.zeros((head_local, head_size), b_qv.dtype)
    qkv_bias = (
        jnp.concatenate([b_qv[:, :head_size], zero_bias, b_qv[:, head_size:]], axis=1)
        .reshape(head_local * 3 * head_size)
        .astype(jnp.float32)
    )
    projected = (jnp.dot(rows_one, qkv_cols, preferred_element_type=jnp.float32) + qkv_bias).astype(
        jnp.bfloat16
    )
    seq_qkv = projected.reshape(seq_count, seq_len, head_local, 3, head_size)
    slot_ends = jnp.cumsum(image_lengths, axis=1)
    places = jnp.arange(seq_len, dtype=jnp.int32)
    image_of = jnp.sum((places[None, :, None] >= slot_ends[:, None, :]).astype(jnp.int32), axis=2)

    def block_scores(query_rows, key_rows, image_rows, image_cols):
        scores = (
            jnp.einsum("qhd,khd->hqk", query_rows, key_rows, preferred_element_type=jnp.float32)
            * scale_factor
        )
        return jnp.where((image_rows[:, None] == image_cols[None, :])[None], scores, MASKED)

    def attend_forward(pieces):
        seq_block, seq_image = pieces
        key_rows = seq_block[:, :, 1]
        value_rows = seq_block[:, :, 2]
        outputs = []
        totals = []
        for row_start in range(0, seq_len, block_rows):
            stop_row = row_start + block_rows
            query_rows = seq_block[row_start:stop_row, :, 0]
            scores = block_scores(query_rows, key_rows, seq_image[row_start:stop_row], seq_image)
            row_peak = jnp.max(scores, axis=2, keepdims=True)
            raised = jnp.exp(scores - row_peak)
            row_total = jnp.sum(raised, axis=2, keepdims=True)
            soft_low = (raised / row_total).astype(jnp.bfloat16)
            outputs.append(
                jnp.einsum(
                    "hqk,khd->qhd", soft_low, value_rows, preferred_element_type=jnp.float32
                ).astype(jnp.bfloat16)
            )
            totals.append((row_peak + jnp.log(row_total))[:, :, 0])
        return (jnp.concatenate(outputs, axis=0), jnp.concatenate(totals, axis=1))

    mixed, log_totals = lax.map(attend_forward, (seq_qkv, image_of))
    mixed_rows = mixed.reshape(group_rows, head_local * head_size)
    attn_out = lax.psum_scatter(
        times_transposed(
            lax.slice_in_dim(mixed_rows, 0, tok_rows * lax.axis_size("heads"), axis=0), out_cols
        ).astype(jnp.bfloat16),
        "heads",
        scatter_dimension=0,
        tiled=True,
    ).astype(jnp.float32) + b_out.astype(jnp.float32)
    after_attn = inputs + gate_attn * attn_out
    second_value, second_pull = jax.vjp(modulate, after_attn, shift_mlp, scale_mlp)
    hidden_two = second_value.astype(jnp.bfloat16)
    rows_two = lax.all_gather(hidden_two, "heads", axis=0, tiled=True)
    inner = jnp.dot(rows_two, fc1_cols, preferred_element_type=jnp.float32) + b_fc1.astype(
        jnp.float32
    )
    gelu_value, gelu_pull = jax.vjp(gelu_tanh, inner)
    active = gelu_value.astype(jnp.bfloat16)
    ffn_out = lax.psum_scatter(
        times_transposed(
            lax.slice_in_dim(active, 0, tok_rows * lax.axis_size("heads"), axis=0), fc2_cols
        ).astype(jnp.bfloat16),
        "heads",
        scatter_dimension=0,
        tiled=True,
    ).astype(jnp.float32) + b_fc2.astype(jnp.float32)
    block_out = (after_attn + gate_mlp * ffn_out).astype(jnp.bfloat16)
    upstream = cotangent.astype(jnp.float32)
    grad_ffn = (gate_mlp * upstream).astype(jnp.bfloat16)
    ffn_rows = lax.all_gather(grad_ffn, "heads", axis=0, tiled=True)
    grad_w_fc2 = contract_rows(ffn_rows, active)
    grad_b_fc2 = jnp.sum(ffn_rows, axis=0, dtype=jnp.float32)
    grad_active = jnp.dot(ffn_rows, fc2_cols, preferred_element_type=jnp.float32)
    grad_inner = gelu_pull(grad_active)[0].astype(jnp.bfloat16)
    grad_w_fc1 = contract_rows(rows_two, grad_inner)
    grad_b_fc1 = jnp.sum(grad_inner, axis=0, dtype=jnp.float32)
    grad_hidden_two = lax.psum_scatter(
        times_transposed(
            lax.slice_in_dim(grad_inner, 0, tok_rows * lax.axis_size("heads"), axis=0), fc1_cols
        ).astype(jnp.bfloat16),
        "heads",
        scatter_dimension=0,
        tiled=True,
    ).astype(jnp.float32)
    grad_after, grad_shift_mlp, grad_scale_mlp = second_pull(grad_hidden_two)
    grad_after = grad_after + upstream
    grad_gate_mlp = upstream * ffn_out
    grad_gate_attn = grad_after * attn_out
    grad_attn = (gate_attn * grad_after).astype(jnp.bfloat16)
    attn_rows_grad = lax.all_gather(grad_attn, "heads", axis=0, tiled=True)
    grad_w_out = contract_rows(attn_rows_grad, mixed_rows)
    grad_b_out = jnp.sum(attn_rows_grad, axis=0, dtype=jnp.float32)
    grad_mixed = jnp.dot(attn_rows_grad, out_cols, preferred_element_type=jnp.float32).astype(
        jnp.bfloat16
    )
    grad_seq = grad_mixed.reshape(seq_count, seq_len, head_local, head_size)

    def attend_backward(pieces):
        seq_block, seq_image, seq_grad, seq_totals = pieces
        key_rows = seq_block[:, :, 1]
        value_rows = seq_block[:, :, 2]
        grad_keys = jnp.zeros(key_rows.shape, jnp.float32)
        grad_values = jnp.zeros(value_rows.shape, jnp.float32)
        grad_queries = []
        for row_start in range(0, seq_len, block_rows):
            stop_row = row_start + block_rows
            query_rows = seq_block[row_start:stop_row, :, 0]
            grad_rows = seq_grad[row_start:stop_row]
            scores = block_scores(query_rows, key_rows, seq_image[row_start:stop_row], seq_image)
            soft_probs = jnp.exp(scores - seq_totals[:, row_start:stop_row, None])
            grad_probs = jnp.einsum(
                "qhd,khd->hqk", grad_rows, value_rows, preferred_element_type=jnp.float32
            )
            inner_sum = jnp.sum(soft_probs * grad_probs, axis=2, keepdims=True)
            grad_scores = (soft_probs * (grad_probs - inner_sum)).astype(jnp.bfloat16)
            grad_queries.append(
                jnp.einsum(
                    "hqk,khd->qhd", grad_scores, key_rows, preferred_element_type=jnp.float32
                )
                * scale_factor
            )
            grad_keys = (
                grad_keys
                + jnp.einsum(
                    "hqk,qhd->khd", grad_scores, query_rows, preferred_element_type=jnp.float32
                )
                * scale_factor
            )
            grad_values = grad_values + jnp.einsum(
                "hqk,qhd->khd",
                soft_probs.astype(jnp.bfloat16),
                grad_rows,
                preferred_element_type=jnp.float32,
            )
        stacked = jnp.stack([jnp.concatenate(grad_queries, axis=0), grad_keys, grad_values], axis=2)
        return stacked.astype(jnp.bfloat16)

    grad_qkv = lax.map(attend_backward, (seq_qkv, image_of, grad_seq, log_totals)).reshape(
        group_rows, head_local * 3 * head_size
    )
    grad_w_qkv = contract_rows(rows_one, grad_qkv)
    bias_terms = jnp.sum(grad_qkv, axis=0, dtype=jnp.float32).reshape(head_local, 3, head_size)
    grad_b_qv = jnp.concatenate([bias_terms[:, 0], bias_terms[:, 2]], axis=1)
    grad_hidden_one = lax.psum_scatter(
        times_transposed(
            lax.slice_in_dim(grad_qkv, 0, tok_rows * lax.axis_size("heads"), axis=0), qkv_cols
        ).astype(jnp.bfloat16),
        "heads",
        scatter_dimension=0,
        tiled=True,
    ).astype(jnp.float32)
    grad_inputs, grad_shift_attn, grad_scale_attn = first_pull(grad_hidden_one)
    grad_patches = grad_inputs + grad_after
    token_grads = (
        grad_shift_attn,
        grad_scale_attn,
        grad_gate_attn,
        grad_shift_mlp,
        grad_scale_mlp,
        grad_gate_mlp,
    )
    mods_grad_part = jnp.concatenate(
        [contract_rows_exact(token_hot, grad_term) for grad_term in token_grads], axis=1
    )
    grad_mods = lax.psum(mods_grad_part.astype(jnp.bfloat16), "heads")
    grad_cols = lax.all_to_all(
        grad_mods.reshape(image_count, row_parts, ada_width).transpose(1, 0, 2),
        "rows",
        split_axis=0,
        concat_axis=0,
        tiled=True,
    ).reshape(every_slot, ada_width)
    grad_w_ada = contract_rows(silu_low, grad_cols)
    grad_b_ada = jnp.sum(grad_cols, axis=0, dtype=jnp.float32)
    grad_silu = lax.psum(times_transposed(grad_cols, w_ada), "rows")
    grad_condition = silu_pull(grad_silu)[0]
    grad_time = contract_rows_exact(bucket_hot.astype(jnp.float32), grad_condition)
    grad_class = contract_rows_exact(label_hot.astype(jnp.float32), grad_condition)

    def row_reduced(partial):
        return lax.psum_scatter(
            partial.astype(jnp.bfloat16), "rows", scatter_dimension=0, tiled=True
        ).astype(jnp.float32)

    grad_w_qkv, grad_w_out, grad_w_fc1, grad_w_fc2 = (
        row_reduced(grad_w_qkv),
        row_reduced(grad_w_out),
        row_reduced(grad_w_fc1),
        row_reduced(grad_w_fc2),
    )
    bias_sizes = (grad_b_qv.size, grad_b_fc1.size, grad_b_out.size, grad_b_fc2.size)
    bias_all = lax.psum(
        jnp.concatenate([grad_b_qv.reshape(-1), grad_b_fc1, grad_b_out, grad_b_fc2]), "rows"
    )
    edges = [sum(bias_sizes[:step]) for step in range(5)]
    bias_rows = model_width // row_parts
    row_start = lax.axis_index("rows") * bias_rows
    grad_b_qv = bias_all[edges[0] : edges[1]].reshape(grad_b_qv.shape)
    grad_b_fc1 = bias_all[edges[1] : edges[2]]
    grad_b_out = lax.dynamic_slice_in_dim(bias_all[edges[2] : edges[3]], row_start, bias_rows)
    grad_b_fc2 = lax.dynamic_slice_in_dim(bias_all[edges[3] : edges[4]], row_start, bias_rows)
    return (
        block_out,
        grad_patches,
        grad_time,
        grad_class,
        grad_w_ada,
        grad_b_ada,
        grad_w_qkv,
        grad_b_qv,
        grad_w_out,
        grad_b_out,
        grad_w_fc1,
        grad_b_fc1,
        grad_w_fc2,
        grad_b_fc2,
    )


MESH = pl.DeviceIdType.MESH
ROW_PARTS = 8
HEAD_PARTS = 4
SLOT_ROWS = 8
VMEM_SPEC = pl.BlockSpec(memory_space=pltpu.VMEM)
ANY_SPEC = pl.BlockSpec(memory_space=pl.ANY)
DMA = pltpu.SemaphoreType.DMA
GRANT = 60 * 1024 * 1024


def places():
    row = lax.axis_index("rows")
    member = lax.axis_index("heads")
    sibling = member + 1 - 2 * lax.rem(member, 2)
    partner = lax.rem(member + 2, HEAD_PARTS)
    opposite = lax.rem(sibling + 2, HEAD_PARTS)
    return row, member, sibling, partner, opposite


def greet(row_steps, head_members):
    barrier = pltpu.get_barrier_semaphore()
    row = lax.axis_index("rows")
    for step in row_steps:
        pl.semaphore_signal(
            barrier,
            inc=1,
            device_id={"rows": lax.rem(row + step, ROW_PARTS)},
            device_id_type=MESH,
        )
    for other in head_members:
        pl.semaphore_signal(barrier, inc=1, device_id={"heads": other}, device_id_type=MESH)
    pl.semaphore_wait(barrier, len(row_steps) + len(head_members))


def to_row(source, target, send, recv, row):
    return pltpu.make_async_remote_copy(
        src_ref=source,
        dst_ref=target,
        send_sem=send,
        recv_sem=recv,
        device_id={"rows": row},
        device_id_type=MESH,
    )


def to_head(source, target, send, recv, member):
    return pltpu.make_async_remote_copy(
        src_ref=source,
        dst_ref=target,
        send_sem=send,
        recv_sem=recv,
        device_id={"heads": member},
        device_id_type=MESH,
    )


class RowGather:
    def __init__(self, shard, full, sends, recvs, local_sem, chunks):
        self.row = lax.axis_index("rows")
        self.level = self.row // 2
        self.side = lax.rem(self.row, 2)
        self.mate = self.row + 1 - 2 * self.side
        size = shard.shape[0] // chunks
        self.own = pltpu.make_async_copy(shard, full.at[self.row], local_sem)
        self.straight = []
        self.across = []
        for chunk in range(chunks):
            part = pl.ds(chunk * size, size)
            straight = []
            across = [
                to_row(
                    shard.at[part],
                    full.at[self.row, part],
                    sends.at[chunk, 3],
                    recvs.at[chunk, 3],
                    self.mate,
                )
            ]
            for step in range(1, 4):
                target = lax.rem(self.level + step, 4) * 2 + self.side
                origin = lax.rem(self.level + 4 - step, 4) * 2 + self.side
                straight.append(
                    to_row(
                        shard.at[part],
                        full.at[self.row, part],
                        sends.at[chunk, step - 1],
                        recvs.at[chunk, step - 1],
                        target,
                    )
                )
                across.append(
                    to_row(
                        full.at[origin, part],
                        full.at[origin, part],
                        sends.at[chunk, 3 + step],
                        recvs.at[chunk, 3 + step],
                        self.mate,
                    )
                )
            self.straight.append(straight)
            self.across.append(across)

    def start(self, chunk):
        for copy in self.straight[chunk]:
            copy.start()
        self.across[chunk][0].start()

    def relay(self, chunk):
        for step in range(3):
            self.straight[chunk][step].wait_recv()
            self.across[chunk][1 + step].start()

    def finish(self):
        self.own.wait()
        for straight, across in zip(self.straight, self.across):
            for copy in straight:
                copy.wait_send()
            for copy in across:
                copy.wait()


class HeadGather:
    def __init__(self, block, full, sends, recvs, local_sem):
        row, member, sibling, partner, opposite = places()
        self.own = None
        if block is None:
            block = full.at[member]
        else:
            self.own = pltpu.make_async_copy(block, full.at[member], local_sem)
        self.beside = to_head(block, full.at[member], sends.at[0], recvs.at[0], sibling)
        self.across = to_head(block, full.at[member], sends.at[1], recvs.at[1], partner)
        self.onward = to_head(
            full.at[partner], full.at[partner], sends.at[2], recvs.at[2], sibling
        )

    def start(self):
        self.across.start()
        self.beside.start()
        if self.own is not None:
            self.own.start()

    def wait_sibling(self):
        self.beside.wait_recv()

    def wait_partner(self):
        self.across.wait_recv()
        self.onward.start()

    def wait_opposite(self):
        self.onward.wait_recv()

    def finish(self):
        if self.own is not None:
            self.own.wait()
        self.beside.wait_send()
        self.across.wait_send()
        self.onward.wait_send()


def front_kernel(
    bucket_ref,
    label_ref,
    time_ref,
    class_ref,
    ada_ref,
    patches_ref,
    qkv_ref,
    qkv_full,
    patches_full,
    cond_all,
    mods_ref,
    ids_all,
    ids_own,
    cond_part,
    cond_in,
    mods_part,
    mods_in,
    mods_sibling,
    mods_pair,
    mods_partner,
    small_send,
    small_recv,
    pair_send,
    pair_recv,
    head_send,
    head_recv,
    qkv_send,
    qkv_recv,
    local_sems,
):
    row, member, sibling, partner, opposite = places()
    greet(range(1, ROW_PARTS), (sibling, partner))
    others = [(step, lax.rem(row + step, ROW_PARTS)) for step in range(1, ROW_PARTS)]

    def spread(stage, source_of, target):
        copies = []
        for step, other in others:
            copy = to_row(
                source_of(other),
                target.at[row],
                small_send.at[stage, step - 1],
                small_recv.at[stage, step - 1],
                other,
            )
            copy.start()
            copies.append(copy)
        return copies

    def settle(copies):
        for copy in copies:
            copy.wait()

    table_rows = time_ref.shape[1]
    slots = ROW_PARTS * SLOT_ROWS
    ids_own[...] = jnp.full_like(ids_own, -1)
    for start, chosen in ((0, bucket_ref), (SLOT_ROWS, label_ref)):
        for slot in range(chosen.shape[1]):
            ids_own[start + slot : start + slot + 1] = jnp.broadcast_to(
                chosen[0:1, slot : slot + 1], (1, table_rows)
            )
    ids_copies = spread(0, lambda other: ids_own, ids_all)
    gather_qkv = RowGather(qkv_ref, qkv_full, qkv_send, qkv_recv, local_sems.at[0], 3)
    gather_patches = HeadGather(patches_ref, patches_full, head_send, head_recv, local_sems.at[1])
    gather_patches.start()
    gather_qkv.own.start()
    gather_qkv.start(0)
    ids_all[row] = ids_own[...]
    settle(ids_copies)
    bucket_hot, label_hot = (hot.astype(jnp.bfloat16) for hot in table_hots(ids_all, table_rows))
    found = times_transposed(bucket_hot, time_ref[...]) + times_transposed(
        label_hot, class_ref[...]
    )
    cond_part[...] = found.reshape(cond_part.shape)
    copies = spread(1, lambda other: cond_part.at[other], cond_in)
    gather_qkv.start(1)
    cond_in[row] = cond_part[row]
    settle(copies)
    condition = jnp.sum(cond_in[...], axis=0)
    cond_all[row] = condition
    cond_part[row] = condition
    copies = spread(2, lambda other: cond_part.at[row], cond_all)
    gather_qkv.relay(0)
    settle(copies)
    every = cond_all[...].reshape(slots, cond_all.shape[2])
    silu_low = (every / (1.0 + jnp.exp(-every))).astype(jnp.bfloat16)
    mods_part[...] = jnp.dot(
        silu_low, ada_ref[...], preferred_element_type=jnp.float32
    ).reshape(mods_part.shape)
    copies = spread(3, lambda other: mods_part.at[other], mods_in)
    gather_qkv.start(2)
    mods_in[row] = mods_part[row]
    gather_qkv.relay(1)
    settle(copies)
    beside = to_head(mods_in, mods_sibling, pair_send.at[0], pair_recv.at[0], sibling)
    beside.start()
    gather_patches.wait_sibling()
    beside.wait()
    mods_pair[...] = mods_in[...] + mods_sibling[...]
    across = to_head(mods_pair, mods_partner, pair_send.at[1], pair_recv.at[1], partner)
    across.start()
    gather_patches.wait_partner()
    gather_qkv.relay(2)
    across.wait()
    mods_ref[...] = mods_pair[...] + mods_partner[...]
    gather_patches.wait_opposite()
    gather_patches.finish()
    gather_qkv.finish()


def front(bucket_ids, class_labels, time_columns, class_columns, w_ada, patches, w_qkv):
    depth, ada_width = w_ada.shape
    shape = jax.ShapeDtypeStruct
    slotted = (ROW_PARTS, SLOT_ROWS)
    wide = pltpu.VMEM(slotted + (ada_width,), jnp.float32)
    narrow = pltpu.VMEM(slotted + (depth,), jnp.float32)
    return pl.pallas_call(
        front_kernel,
        out_shape=(
            shape((ROW_PARTS,) + w_qkv.shape, jnp.bfloat16),
            shape((HEAD_PARTS,) + patches.shape, jnp.bfloat16),
            shape(slotted + (depth,), jnp.float32),
            shape(slotted + (ada_width,), jnp.float32),
            shape((ROW_PARTS, 2 * SLOT_ROWS, time_columns.shape[1]), jnp.int32),
        ),
        in_specs=[VMEM_SPEC] * 7,
        out_specs=[ANY_SPEC] * 2 + [VMEM_SPEC] * 3,
        scratch_shapes=[pltpu.VMEM((2 * SLOT_ROWS, time_columns.shape[1]), jnp.int32)]
        + [narrow] * 2
        + [wide] * 5
        + [
            DMA((4, 7)),
            DMA((4, 7)),
            DMA((2,)),
            DMA((2,)),
            DMA((3,)),
            DMA((3,)),
            DMA((3, 7)),
            DMA((3, 7)),
            DMA((2,)),
        ],
        compiler_params=pltpu.CompilerParams(
            collective_id=0, has_side_effects=True, vmem_limit_bytes=GRANT
        ),
        name="front",
    )(bucket_ids, class_labels, time_columns, class_columns, w_ada, patches, w_qkv)


class HeadReduce:
    def __init__(self, partial, beside_in, pair, across_in, sends, recvs):
        row, member, sibling, partner, opposite = places()
        self.member = member
        self.partner = partner
        self.partial = partial
        self.beside_in = beside_in
        self.pair = pair
        self.across_in = across_in
        self.first = to_head(
            partial.at[opposite], beside_in.at[1], sends.at[0], recvs.at[0], sibling
        )
        self.second = to_head(
            partial.at[sibling], beside_in.at[0], sends.at[1], recvs.at[1], sibling
        )
        self.across = to_head(pair, across_in, sends.at[2], recvs.at[2], partner)

    def start(self):
        self.first.start()
        self.second.start()

    def send_pair(self):
        self.first.wait_recv()
        self.pair[...] = (
            self.partial[self.partner].astype(jnp.float32)
            + self.beside_in[1].astype(jnp.float32)
        ).astype(jnp.bfloat16)
        self.across.start()

    def settle(self):
        self.second.wait_recv()
        self.across.wait_recv()

    def rows(self, part):
        return (
            self.partial[self.member, part].astype(jnp.float32)
            + self.beside_in[0, part].astype(jnp.float32)
            + self.across_in[part].astype(jnp.float32)
        )

    def finish(self):
        self.first.wait_send()
        self.second.wait_send()
        self.across.wait_send()


class RowReduce:
    def __init__(self, partial, chunk, buffers, total, sends, recvs):
        row = lax.axis_index("rows")
        self.level = row // 2
        self.side = lax.rem(row, 2)
        mate = row + 1 - 2 * self.side
        self.partial = partial
        self.mate_in, self.pair, self.straight_in = buffers
        self.total = total
        size = total.shape[0]
        self.part = pl.ds(chunk * size, size)
        self.beside = to_row(
            partial.at[:, 1 - self.side, self.part], self.mate_in, sends.at[0], recvs.at[0], mate
        )
        self.straight = []
        for step in range(1, 4):
            target = lax.rem(self.level + step, 4)
            self.straight.append(
                to_row(
                    self.pair.at[target],
                    self.straight_in.at[step - 1],
                    sends.at[step],
                    recvs.at[step],
                    target * 2 + self.side,
                )
            )

    def start(self):
        self.beside.start()

    def send_pair(self):
        self.beside.wait_recv()

        def one(level, carry):
            self.pair[level] = (
                self.partial[level, self.side, self.part].astype(jnp.float32)
                + self.mate_in[level].astype(jnp.float32)
            ).astype(jnp.bfloat16)
            return carry

        lax.fori_loop(0, 4, one, 0)
        for copy in self.straight:
            copy.start()

    def finish(self):
        for copy in self.straight:
            copy.wait_recv()
        self.total[...] = (
            self.pair[self.level].astype(jnp.float32)
            + self.straight_in[0].astype(jnp.float32)
            + self.straight_in[1].astype(jnp.float32)
            + self.straight_in[2].astype(jnp.float32)
        )
        self.beside.wait_send()
        for copy in self.straight:
            copy.wait_send()


def row_reduces(jobs, reducing):
    buffers, sends, recvs = reducing[:-2], reducing[-2], reducing[-1]
    return [
        RowReduce(
            partial,
            chunk,
            buffers[3 * place : 3 * place + 3],
            total,
            sends.at[place],
            recvs.at[place],
        )
        for place, (partial, chunk, total) in enumerate(jobs)
    ]


def reduce_scratch(sizes):
    landing = []
    for rows, columns in sizes:
        landing += [
            pltpu.VMEM((4, rows, columns), jnp.bfloat16),
            pltpu.VMEM((4, rows, columns), jnp.bfloat16),
            pltpu.VMEM((3, rows, columns), jnp.bfloat16),
        ]
    return landing + [DMA((len(sizes), 4)), DMA((len(sizes), 4))]


def picked(vectors, part_index, segments, width):
    wide = jnp.concatenate([segments] * (width // segments.shape[1]), axis=1)
    slot_count = vectors.shape[1]
    chosen = vectors[part_index, slot_count - 1 : slot_count]
    for slot in range(slot_count - 2, -1, -1):
        chosen = jnp.where(wide == slot, vectors[part_index, slot : slot + 1], chosen)
    return chosen


def slot_hot(segment_row, start):
    chosen = segment_row[:, pl.ds(pl.multiple_of(start, 128), 128)]
    slots = lax.broadcasted_iota(jnp.int32, (SLOT_ROWS, 128), 0)
    return (jnp.broadcast_to(chosen, slots.shape) == slots).astype(jnp.float32)


def table_hots(ids_all, table_rows):
    slots = ROW_PARTS * SLOT_ROWS
    table_places = lax.axis_index("rows") * table_rows + lax.broadcasted_iota(
        jnp.int32, (slots, table_rows), 1
    )
    return [
        ids_all[:, start : start + SLOT_ROWS].reshape(slots, table_rows) == table_places
        for start in (0, SLOT_ROWS)
    ]


def centre_rows(values):
    centred = values - jnp.mean(values, axis=1, keepdims=True)
    factor = lax.rsqrt(jnp.mean(centred * centred, axis=1, keepdims=True) + EPSILON)
    return centred * factor, factor


def weight_grad(left, right, target):
    blocks, tok_rows, depth = left.shape
    height = blocks * tok_rows
    flat = target.reshape(depth, target.shape[3])
    third = depth // 3

    def some(step, carry):
        columns = pl.ds(pl.multiple_of(step * third, 128), third)
        flat[columns] = contract_rows(
            left[:, :, columns].reshape(height, third),
            right[...].reshape(height, right.shape[2]),
        ).astype(jnp.bfloat16)
        return carry

    lax.fori_loop(0, 3, some, 0)


def core_kernel(
    patches_full,
    qkv_ref,
    out_shard,
    fc1_shard,
    fc2_shard,
    cotangent_ref,
    patches_ref,
    segment_row,
    mods_ref,
    ada_bias,
    bias_ref,
    value_bias,
    segments_ref,
    vectors_ref,
    normed_rows,
    parts,
    totals_out,
    mixed,
    out_w,
    active_rows,
    after_ref,
    after_grad,
    attn_grad,
    slot_sums,
    bias_sums,
    fc2_rest,
    fc1_part,
    fc2_head,
    fc2_neck,
    qkv_bias,
    ffn_rows,
    hidden_rows,
    inner_grad,
    fc2_part,
    inner_bias,
    ffn_bias,
    out_full,
    fc1_full,
    fc2_full,
    active_grad,
    value_columns,
    head_mixed,
    bias,
    group_part,
    beside_in,
    pair_rows,
    across_in,
    attn_out,
    gather_send,
    gather_recv,
    reduce_send,
    reduce_recv,
    out_send,
    out_recv,
    fc1_send,
    fc1_recv,
    fc2_send,
    fc2_recv,
    local_sems,
    *reducing,
):
    row, member, sibling, partner, opposite = places()
    direction = sibling - member
    greet(range(1, ROW_PARTS), (sibling, partner))
    tok_rows, model_width = patches_ref.shape
    blocks = normed_rows.shape[0]
    seq_len = blocks * tok_rows
    width = qkv_ref.shape[1]
    head_local = totals_out.shape[0]
    head_size = width // (3 * head_local)
    scale_factor = 1.0 / math.sqrt(head_size)
    loads = [
        pltpu.make_async_copy(patches_full.at[block], normed_rows.at[block], local_sems.at[block])
        for block in range(blocks)
    ]
    for load in loads:
        load.start()
    gather_out = RowGather(out_shard, out_full, out_send, out_recv, local_sems.at[4], 1)
    gather_fc1 = RowGather(fc1_shard, fc1_full, fc1_send, fc1_recv, local_sems.at[5], 3)
    gather_fc2 = RowGather(fc2_shard, fc2_full, fc2_send, fc2_recv, local_sems.at[6], 3)
    gather_cotangent = HeadGather(
        cotangent_ref, ffn_rows, gather_send.at[2], gather_recv.at[2], local_sems.at[7]
    )
    gather_out.own.start()
    gather_out.start(0)
    gather_fc1.own.start()
    gather_fc2.own.start()
    for gather in (gather_fc1, gather_fc2):
        for chunk in range(3):
            gather.start(chunk)
    gather_cotangent.start()
    reduce_attn = HeadReduce(
        group_part, beside_in, pair_rows, across_in, reduce_send.at[0], reduce_recv.at[0]
    )
    reduce_hidden = HeadReduce(
        group_part, beside_in, pair_rows, across_in, reduce_send.at[1], reduce_recv.at[1]
    )
    gather_hidden = HeadGather(None, hidden_rows, gather_send.at[0], gather_recv.at[0], None)
    gather_grad = HeadGather(None, attn_grad, gather_send.at[1], gather_recv.at[1], None)
    parts[...] = jnp.zeros_like(parts)
    segments_ref[...] = (
        jnp.broadcast_to(segment_row[...].astype(jnp.float32), (128, seq_len))
        .T.astype(jnp.int32)
    )
    slot_count = vectors_ref.shape[1]
    fine = mods_ref.shape[2] // 3
    for unit in range(3 * ROW_PARTS):
        part_index, within = divmod(unit * fine, model_width)
        span = slice(within, within + fine)
        vectors_ref[part_index, :, span] = mods_ref[
            unit // 3, 0:slot_count, unit % 3 * fine : (unit % 3 + 1) * fine
        ]
    for part_index in range(6):
        vectors_ref[part_index] += ada_bias[part_index : part_index + 1]
    qkv_bias[...] = jnp.zeros_like(qkv_bias)
    for head in range(head_local):
        for place in (0, 2):
            start = (3 * head + place) * head_size
            taken = slice(place // 2 * head_size, (place // 2 + 1) * head_size)
            qkv_bias[:, start : start + head_size] = value_bias[head : head + 1, taken]
    for load in loads:
        load.wait()

    def first_norm(step, carry):
        block = step // 2
        part = pl.ds(pl.multiple_of(lax.rem(step, 2) * 128, 128), 128)
        segments = segments_ref[pl.ds(pl.multiple_of(step * 128, 128), 128)]
        normed, _ = centre_rows(normed_rows[block, part].astype(jnp.float32))
        normed_rows[block, part] = (
            normed * (1.0 + picked(vectors_ref, 1, segments, model_width))
            + picked(vectors_ref, 0, segments, model_width)
        ).astype(jnp.bfloat16)
        return carry

    lax.fori_loop(0, 2 * blocks, first_norm, 0)
    gather_out.relay(0)

    def project_in(block, carry):
        rows = pl.ds(pl.multiple_of(block * tok_rows, tok_rows), tok_rows)
        active_grad[0, :, 0:width] = (
            jnp.dot(normed_rows[block], qkv_ref[...], preferred_element_type=jnp.float32)
            + qkv_bias[...]
        )
        for part in range(3 * head_local):
            parts[part, rows, 0:head_size] = active_grad[
                0, :, part * head_size : (part + 1) * head_size
            ].astype(jnp.bfloat16)
        return carry

    lax.fori_loop(0, blocks, project_in, 0)
    gather_fc1.relay(0)

    def turn(head, carry):
        value_columns[head] = parts[3 * head + 2].astype(jnp.float32).T.astype(jnp.bfloat16)
        return carry

    lax.fori_loop(0, head_local, turn, 0)

    def attend(block):
        rows = pl.ds(pl.multiple_of(block * tok_rows, tok_rows), tok_rows)
        keys = jnp.concatenate([segments_ref[...]] * (tok_rows // 128), axis=1)
        same = keys == jnp.broadcast_to(segment_row[:, rows], keys.shape)
        bias[...] = jnp.where(same, 0.0, MASKED)

        def one_head(head, carry):
            scores = (
                times_transposed(parts[3 * head + 1], parts[3 * head, rows]) * scale_factor
                + bias[...]
            )
            peak = jnp.max(scores, axis=0, keepdims=True)
            raised = jnp.exp(scores - peak)
            total = jnp.sum(raised, axis=0, keepdims=True)
            totals_out[head, block] = peak + jnp.log(total)
            head_mixed[head] = jnp.dot(
                value_columns[head],
                (raised * (1.0 / total)).astype(jnp.bfloat16),
                preferred_element_type=jnp.float32,
            ).T
            return carry

        lax.fori_loop(0, head_local, one_head, 0)
        for head in range(head_local):
            active_grad[1, :, head * head_size : (head + 1) * head_size] = head_mixed[
                head, :, 0:head_size
            ]
        mixed[block] = active_grad[1, :, 0 : head_local * head_size].astype(jnp.bfloat16)

    def attend_pair(base, factor):
        def one(step, carry):
            attend(base + step * factor)
            return carry

        lax.fori_loop(0, 2, one, 0)

    def project(block):
        group_part[block] = times_transposed(mixed[block], out_w[...]).astype(jnp.bfloat16)

    attend_pair(opposite, -direction)
    gather_out.finish()
    out_w[...] = out_full[...].reshape(out_w.shape)
    project(opposite)
    reduce_attn.first.start()
    project(partner)
    reduce_attn.send_pair()
    gather_fc1.relay(1)
    attend_pair(sibling, -direction)
    gather_fc1.relay(2)
    project(sibling)
    reduce_attn.second.start()
    project(member)
    gather_cotangent.wait_sibling()
    gather_cotangent.wait_partner()
    gather_cotangent.wait_opposite()
    gather_cotangent.finish()

    def scale_cotangent(step, carry):
        block = step // 2
        part = pl.ds(pl.multiple_of(lax.rem(step, 2) * 128, 128), 128)
        segments = segments_ref[pl.ds(pl.multiple_of(step * 128, 128), 128)]
        grad = (
            picked(vectors_ref, 5, segments, model_width)
            * ffn_rows[block, part].astype(jnp.float32)
        ).astype(jnp.bfloat16)
        ffn_rows[block, part] = grad
        ffn_bias[...] += jnp.sum(grad.astype(jnp.float32).reshape(16, 8, model_width), axis=0)
        return carry

    ffn_bias[...] = jnp.zeros_like(ffn_bias)
    lax.fori_loop(0, 2 * blocks, scale_cotangent, 0)
    gather_fc2.relay(0)
    reduce_attn.settle()

    def second_norm(block, carry):
        part = pl.ds(pl.multiple_of(block * 128, 128), 128)
        segments = segments_ref[
            pl.ds(pl.multiple_of(member * tok_rows + block * 128, 128), 128)
        ]
        out = reduce_attn.rows(part) + bias_ref[0:1]
        after = patches_ref[part].astype(jnp.float32) + (
            picked(vectors_ref, 2, segments, model_width) * out
        )
        attn_out[part] = out
        after_ref[part] = after
        normed, _ = centre_rows(after)
        hidden_rows[member, part] = (
            normed * (1.0 + picked(vectors_ref, 4, segments, model_width))
            + picked(vectors_ref, 3, segments, model_width)
        ).astype(jnp.bfloat16)
        return carry

    lax.fori_loop(0, tok_rows // 128, second_norm, 0)
    gather_hidden.start()
    reduce_attn.finish()
    gather_fc2.relay(1)
    gather_fc1.finish()
    hidden_width = active_rows.shape[2]
    fc1 = fc1_full.reshape(model_width, hidden_width)
    fc2 = fc2_full.reshape(model_width, hidden_width)

    inner_bias[...] = jnp.zeros_like(inner_bias)

    def feed(block, carry):
        inner = jnp.dot(
            hidden_rows[block], fc1[...], preferred_element_type=jnp.float32
        ) + bias_ref[1:2]
        square = inner * inner
        bent = jnp.tanh(TANH_COEFF * (inner + 0.044715 * square * inner))
        half = 0.5 * (1.0 + bent)
        active_rows[block] = (inner * half).astype(jnp.bfloat16)
        active_grad[block] = half + 0.5 * inner * (1.0 - bent * bent) * (
            TANH_COEFF * (1.0 + 3.0 * 0.044715 * square)
        )
        return carry

    def through_fc2(block, carry):
        grad = (
            jnp.dot(ffn_rows[block], fc2[...], preferred_element_type=jnp.float32)
            * active_grad[block]
        ).astype(jnp.bfloat16)
        inner_grad[block] = grad
        inner_bias[...] += jnp.sum(
            grad.astype(jnp.float32).reshape(tok_rows // 8, 8, hidden_width), axis=0
        )
        return carry

    def return_fc1(block, carry):
        group_part[block] = times_transposed(inner_grad[block], fc1[...]).astype(jnp.bfloat16)
        return carry

    gather_hidden.wait_sibling()
    lax.fori_loop(0, 2, lambda step, carry: feed(member + step * direction, carry), 0)
    gather_fc2.relay(2)
    gather_hidden.wait_partner()
    gather_hidden.wait_opposite()
    lax.fori_loop(0, 2, lambda step, carry: feed(opposite - step * direction, carry), 0)
    gather_fc2.finish()

    def turn_back(block, carry):
        through_fc2(block, carry)
        return return_fc1(block, carry)

    lax.fori_loop(0, 2, lambda step, carry: turn_back(opposite - step * direction, carry), 0)
    reduce_hidden.first.start()
    reduce_hidden.send_pair()
    lax.fori_loop(0, 2, lambda step, carry: turn_back(sibling - step * direction, carry), 0)
    reduce_hidden.second.start()

    def forward_fc2(block, carry):
        active_rows[block] = times_transposed(active_rows[block], fc2[...]).astype(jnp.bfloat16)
        return carry

    weight_grad(ffn_rows, active_rows, fc2_part)
    third = fc2_rest.shape[2]
    fc2_rest[...] = fc2_part[:, :, 2 * third : 3 * third]
    reduces = row_reduces(((fc2_part, 0, fc2_head), (fc2_part, 1, fc2_neck)), reducing)
    for unit in reduces:
        unit.start()
    lax.fori_loop(0, HEAD_PARTS, forward_fc2, 0)
    slot_sums[...] = jnp.zeros_like(slot_sums)
    reduce_hidden.settle()

    def second_back(block, carry):
        part = pl.ds(pl.multiple_of(block * 128, 128), 128)
        segments = segments_ref[
            pl.ds(pl.multiple_of(member * tok_rows + block * 128, 128), 128)
        ]
        grad = reduce_hidden.rows(part)
        normed, factor = centre_rows(after_ref[part])
        weighted = grad * (1.0 + picked(vectors_ref, 4, segments, model_width))
        total = cotangent_ref[part].astype(jnp.float32) + factor * (
            weighted
            - jnp.mean(weighted, axis=1, keepdims=True)
            - normed * jnp.mean(weighted * normed, axis=1, keepdims=True)
        )
        after_grad[part] = total
        attn_grad[member, part] = (
            picked(vectors_ref, 2, segments, model_width) * total
        ).astype(jnp.bfloat16)
        hot = slot_hot(segment_row, member * tok_rows + block * 128)
        for index, term in enumerate((total * attn_out[part], grad, grad * normed)):
            slot_sums[index] += jnp.dot(
                hot, term, precision=HIGH, preferred_element_type=jnp.float32
            )
        return carry

    lax.fori_loop(0, tok_rows // 128, second_back, 0)
    gather_grad.start()
    weight_grad(hidden_rows, inner_grad, fc1_part)
    reduces[0].send_pair()
    bias_sums[...] = jnp.zeros_like(bias_sums)
    bias_sums[0:1] = jnp.sum(inner_bias[...], axis=0, keepdims=True)
    bias_sums[1:2] = jnp.sum(ffn_bias[...], axis=0, keepdims=True)
    gather_grad.wait_sibling()
    gather_grad.wait_partner()
    gather_grad.wait_opposite()
    reduces[1].send_pair()
    for unit in reduces:
        unit.finish()
    gather_hidden.finish()
    gather_grad.finish()
    reduce_hidden.finish()


def core(slot_count, head_size, *args):
    shape = jax.ShapeDtypeStruct
    patches_full, w_qkv, out_shard, fc1_shard = args[:4]
    blocks, tok_rows, model_width = patches_full.shape
    seq_len = blocks * tok_rows
    out_width = out_shard.shape[1]
    width_part, hidden_width = fc1_shard.shape
    third = width_part // 3
    head_local = out_width // head_size
    low = jnp.bfloat16
    full = jnp.float32
    rows_low = shape((blocks, tok_rows, model_width), low)
    own = shape((tok_rows, model_width), full)
    own_low = pltpu.VMEM((tok_rows, model_width), low)
    group_low = pltpu.VMEM((blocks, tok_rows, model_width), low)
    hidden_low = pltpu.VMEM((blocks, tok_rows, hidden_width), low)
    part_low = (4, 2, width_part, hidden_width)
    return pl.pallas_call(
        core_kernel,
        out_shape=[
            shape((seq_len, 128), jnp.int32),
            shape((6, slot_count, model_width), full),
            rows_low,
            shape((3 * head_local, seq_len, HEAD_LANES), low),
            shape((head_local, blocks, 1, tok_rows), full),
            shape((blocks, tok_rows, out_width), low),
            shape((model_width, out_width), low),
            rows_low,
            own,
            own,
            rows_low,
            shape((3, SLOT_ROWS, model_width), full),
            shape((8, hidden_width), full),
            shape((4, 2, third, hidden_width), low),
            shape(part_low, low),
            shape((third, hidden_width), full),
            shape((third, hidden_width), full),
        ],
        in_specs=[ANY_SPEC] + [VMEM_SPEC] * 11,
        out_specs=[VMEM_SPEC] * 17,
        scratch_shapes=[
            pltpu.VMEM((1, args[1].shape[1]), full),
            group_low,
            group_low,
            hidden_low,
            pltpu.VMEM(part_low, low),
            pltpu.VMEM((8, hidden_width), full),
            pltpu.VMEM((8, model_width), full),
            pltpu.VMEM((ROW_PARTS,) + out_shard.shape, low),
            pltpu.VMEM((ROW_PARTS,) + fc1_shard.shape, low),
            pltpu.VMEM((ROW_PARTS,) + fc1_shard.shape, low),
            pltpu.VMEM((blocks, tok_rows, hidden_width), full),
            pltpu.VMEM((head_local, HEAD_LANES, seq_len), low),
            pltpu.VMEM((head_local, tok_rows, HEAD_LANES), full),
            pltpu.VMEM((seq_len, tok_rows), full),
            group_low,
            pltpu.VMEM((2, tok_rows, model_width), low),
            own_low,
            own_low,
            pltpu.VMEM((tok_rows, model_width), full),
            DMA((3, 3)),
            DMA((3, 3)),
            DMA((2, 3)),
            DMA((2, 3)),
            DMA((1, 7)),
            DMA((1, 7)),
            DMA((3, 7)),
            DMA((3, 7)),
            DMA((3, 7)),
            DMA((3, 7)),
            DMA((8,)),
        ]
        + reduce_scratch([(third, hidden_width)] * 2),
        compiler_params=pltpu.CompilerParams(
            collective_id=2, has_side_effects=True, vmem_limit_bytes=67_000_000
        ),
        name="core",
    )(*args)


HEAD_LANES = 128


def rear_kernel(
    parts,
    grad_ref,
    out_ref,
    totals_ref,
    segment_row,
    segments_ref,
    fc2_part,
    fc1_part,
    hidden_rows,
    qkv_ref,
    mixed_ref,
    bias_ref,
    patches_ref,
    after_ref,
    vectors_ref,
    sums_ref,
    condition_ref,
    ids_all,
    ada_ref,
    ffn_ref,
    block_ref,
    cotangent_ref,
    bias_rows,
    fc2_head,
    fc2_neck,
    block_out,
    patches_grad,
    time_grad,
    class_grad,
    ada_grad,
    ada_bias,
    fc2_grad,
    fc1_grad,
    qkv_grad,
    out_grad,
    bias_sum,
    mixed_grad,
    key_columns,
    grad_keys,
    grad_values,
    bias,
    packed,
    packed_grad,
    hidden_part,
    qkv_part,
    out_part,
    bias_own,
    beside_in,
    pair_rows,
    across_in,
    ffn_beside,
    ffn_pair,
    ffn_across,
    slot_sums,
    mods_own,
    mods_sibling,
    mods_pair,
    mods_partner,
    mods_low,
    mods_cols,
    bias_all,
    silu_part,
    silu_in,
    silu_all,
    small_send,
    small_recv,
    pair_send,
    pair_recv,
    head_send,
    head_recv,
    *reducing,
):
    row, member, sibling, partner, opposite = places()
    greet(range(1, ROW_PARTS), (sibling, partner))
    others = [(step, lax.rem(row + step, ROW_PARTS)) for step in range(1, ROW_PARTS)]

    def spread(stage, source_of, target):
        copies = []
        for step, other in others:
            copy = to_row(
                source_of(other),
                target.at[row],
                small_send.at[stage, step - 1],
                small_recv.at[stage, step - 1],
                other,
            )
            copy.start()
            copies.append(copy)
        return copies

    def settle(copies):
        for copy in copies:
            copy.wait()

    third = fc2_head.shape[0]
    fc2_grad[0:third] = fc2_head[...]
    fc2_grad[third : 2 * third] = fc2_neck[...]
    units = row_reduces(
        [(fc2_part, 0, fc2_grad.at[pl.ds(2 * third, third)])]
        + [(fc1_part, chunk, fc1_grad.at[pl.ds(chunk * third, third)]) for chunk in range(3)]
        + [(out_part, 0, out_grad)]
        + [(qkv_part, chunk, qkv_grad.at[pl.ds(chunk * third, third)]) for chunk in range(3)],
        reducing,
    )
    reduce_rows = HeadReduce(
        hidden_part, beside_in, pair_rows, across_in, head_send.at[0], head_recv.at[0]
    )
    reduce_ffn = HeadReduce(
        ffn_ref, ffn_beside, ffn_pair, ffn_across, head_send.at[1], head_recv.at[1]
    )
    for unit in units[:3]:
        unit.start()
    reduce_ffn.start()
    reduce_ffn.send_pair()
    blocks, tok_rows, model_width = grad_ref.shape
    width = qkv_ref.shape[1]
    head_local = totals_ref.shape[0]
    head_size = width // (3 * head_local)
    scale_factor = 1.0 / math.sqrt(head_size)
    seq_len = blocks * tok_rows
    mixed_grad[...] = jnp.zeros_like(mixed_grad)
    bias_own[...] = jnp.zeros_like(bias_own)

    def unpack(block, carry):
        rows = pl.ds(pl.multiple_of(block * tok_rows, tok_rows), tok_rows)
        packed[:, 0 : head_local * head_size] = jnp.dot(
            grad_ref[block], out_ref[...], preferred_element_type=jnp.float32
        )
        for head in range(head_local):
            mixed_grad[head, rows, 0:head_size] = packed[
                :, head * head_size : (head + 1) * head_size
            ].astype(jnp.bfloat16)
        bias_own[0] += jnp.sum(
            grad_ref[block].astype(jnp.float32).reshape(tok_rows // 8, 8, model_width), axis=0
        )
        return carry

    lax.fori_loop(0, blocks, unpack, 0)

    def turn(head, carry):
        key_columns[head] = parts[3 * head + 1].astype(jnp.float32).T.astype(jnp.bfloat16)
        return carry

    lax.fori_loop(0, head_local, turn, 0)
    grad_keys[...] = jnp.zeros_like(grad_keys)
    grad_values[...] = jnp.zeros_like(grad_values)
    weight_grad(grad_ref, mixed_ref, out_part)

    for block in range(blocks):
        rows = pl.ds(block * tok_rows, tok_rows)
        keys = jnp.concatenate([segments_ref[...]] * (tok_rows // 128), axis=1)
        same = keys == jnp.broadcast_to(segment_row[:, rows], keys.shape)
        bias[...] = jnp.where(same, 0.0, MASKED)

        def one_head(head, carry):
            query = parts[3 * head, rows]
            grad = mixed_grad[head, rows]
            scores = times_transposed(parts[3 * head + 1], query) * scale_factor + bias[...]
            probs = jnp.exp(scores - totals_ref[head, block])
            grad_probs = times_transposed(parts[3 * head + 2], grad)
            inner = jnp.sum(probs * grad_probs, axis=0, keepdims=True)
            grad_scores = (probs * (grad_probs - inner)).astype(jnp.bfloat16)
            grad_values[head] += jnp.dot(
                probs.astype(jnp.bfloat16), grad, preferred_element_type=jnp.float32
            )
            grad_keys[head] += jnp.dot(grad_scores, query, preferred_element_type=jnp.float32)
            lanes = pl.ds(pl.multiple_of(head * HEAD_LANES, HEAD_LANES), HEAD_LANES)
            hidden_part[block, :, lanes] = (
                jnp.dot(key_columns[head], grad_scores, preferred_element_type=jnp.float32).T
                * scale_factor
            ).astype(jnp.bfloat16)
            return carry

        lax.fori_loop(0, head_local, one_head, 0)
        units[block].send_pair()
        if block < 2:
            units[block + 3].start()

    def pack(block, carry):
        rows = pl.ds(pl.multiple_of(block * tok_rows, tok_rows), tok_rows)
        for head in range(head_local):
            lane = head * HEAD_LANES
            terms = (
                hidden_part[block, :, lane : lane + head_size].astype(jnp.float32),
                grad_keys[head, rows, 0:head_size] * scale_factor,
                grad_values[head, rows, 0:head_size],
            )
            for place, term in enumerate(terms):
                start = (3 * head + place) * head_size
                packed[:, start : start + head_size] = term
        low = packed[...].astype(jnp.bfloat16)
        packed_grad[block] = low
        bias_own[1, :, 0:width] += jnp.sum(
            low.astype(jnp.float32).reshape(tok_rows // 8, 8, width), axis=0
        )
        return carry

    lax.fori_loop(0, blocks, pack, 0)
    direction = sibling - member

    def project_back(block):
        hidden_part[block] = times_transposed(packed_grad[block], qkv_ref[...]).astype(
            jnp.bfloat16
        )

    def far(step, carry):
        project_back(opposite - step * direction)
        return carry

    def near(step, carry):
        project_back(sibling - step * direction)
        return carry

    lax.fori_loop(0, 2, far, 0)
    reduce_rows.first.start()
    reduce_rows.send_pair()
    lax.fori_loop(0, 2, near, 0)
    reduce_rows.second.start()
    weight_grad(hidden_rows, packed_grad, qkv_part)
    for unit in units[5:]:
        unit.start()
    bias_own[2] = jnp.zeros_like(bias_own[2])
    bias_own[2] = bias_ref[...]
    bias_own[2, 2:3] = jnp.sum(bias_own[0], axis=0, keepdims=True)
    bias_own[2, 3:4] = jnp.sum(bias_own[1], axis=0, keepdims=True)
    bias_copies = spread(1, lambda other: bias_own.at[2], bias_all)
    bias_all[row] = bias_own[2]
    units[4].send_pair()
    slot_sums[...] = jnp.zeros_like(slot_sums)
    reduce_ffn.settle()

    def rows_out(block, carry):
        part = pl.ds(pl.multiple_of(block * 128, 128), 128)
        ffn = reduce_ffn.rows(part) + bias_rows[2:3]
        place = pl.multiple_of(member * tok_rows + block * 128, 128)
        gate = picked(vectors_ref, 5, segments_ref[pl.ds(place, 128)], model_width)
        block_out[part] = (block_ref[part] + gate * ffn).astype(jnp.bfloat16)
        slot_sums[2] += jnp.dot(
            slot_hot(segment_row, place),
            cotangent_ref[part].astype(jnp.float32) * ffn,
            precision=HIGH,
            preferred_element_type=jnp.float32,
        )
        return carry

    lax.fori_loop(0, tok_rows // 128, rows_out, 0)
    units[0].finish()
    units[1].finish()
    units[5].send_pair()
    reduce_rows.settle()

    def rows_back(block, carry):
        part = pl.ds(pl.multiple_of(block * 128, 128), 128)
        grad = reduce_rows.rows(part)
        normed, factor = centre_rows(patches_ref[part].astype(jnp.float32))
        place = pl.multiple_of(member * tok_rows + block * 128, 128)
        weighted = grad * (
            1.0 + picked(vectors_ref, 1, segments_ref[pl.ds(place, 128)], model_width)
        )
        patches_grad[part] = after_ref[part] + factor * (
            weighted
            - jnp.mean(weighted, axis=1, keepdims=True)
            - normed * jnp.mean(weighted * normed, axis=1, keepdims=True)
        )
        hot = slot_hot(segment_row, place)
        slot_sums[0] += jnp.dot(hot, grad, precision=HIGH, preferred_element_type=jnp.float32)
        slot_sums[1] += jnp.dot(
            hot, grad * normed, precision=HIGH, preferred_element_type=jnp.float32
        )
        return carry

    lax.fori_loop(0, tok_rows // 128, rows_back, 0)
    ada_width = ada_ref.shape[1]
    fine = ada_width // 3
    for unit in range(3 * ROW_PARTS):
        part_index, within = divmod(unit * fine, model_width)
        span = slice(within, within + fine)
        if part_index < 2:
            source = slot_sums[part_index, :, span]
        elif part_index == 5:
            source = slot_sums[2, :, span]
        else:
            source = sums_ref[part_index - 2, :, span]
        mods_own[unit // 3, :, unit % 3 * fine : (unit % 3 + 1) * fine] = source
    beside = to_head(mods_own, mods_sibling, pair_send.at[0], pair_recv.at[0], sibling)
    beside.start()
    units[6].send_pair()
    beside.wait()
    mods_pair[...] = (mods_own[...] + mods_sibling[...]).astype(jnp.bfloat16)
    across = to_head(mods_pair, mods_partner, pair_send.at[1], pair_recv.at[1], partner)
    across.start()
    units[2].finish()
    units[3].finish()
    settle(bias_copies)
    bias_sum[...] = jnp.sum(bias_all[...], axis=0)
    across.wait()
    mods_low[...] = (
        mods_pair[...].astype(jnp.float32) + mods_partner[...].astype(jnp.float32)
    ).astype(jnp.bfloat16)
    copies = spread(0, lambda other: mods_low.at[other], mods_cols)
    mods_cols[row] = mods_low[row]
    units[7].send_pair()
    units[4].finish()
    settle(copies)
    slots = ROW_PARTS * SLOT_ROWS
    cols = mods_cols[...].astype(jnp.float32).reshape(slots, ada_width)
    low = cols.astype(jnp.bfloat16)
    condition = condition_ref[...].reshape(slots, condition_ref.shape[2])
    bent = 1.0 / (1.0 + jnp.exp(-condition))
    silu_part[...] = times_transposed(low, ada_ref[...]).reshape(silu_part.shape)
    copies = spread(2, lambda other: silu_part.at[other], silu_in)
    silu_in[row] = silu_part[row]
    ada_grad[...] = contract_rows((condition * bent).astype(jnp.bfloat16), low)
    ada_bias[...] = jnp.broadcast_to(jnp.sum(cols, axis=0, keepdims=True), ada_bias.shape)
    settle(copies)
    summed = jnp.sum(silu_in[...], axis=0)
    silu_all[row] = summed
    silu_part[row] = summed
    copies = spread(3, lambda other: silu_part.at[row], silu_all)
    units[5].finish()
    units[6].finish()
    units[7].finish()
    settle(copies)
    grad_condition = silu_all[...].reshape(slots, silu_all.shape[2]) * (
        bent * (1.0 + condition * (1.0 - bent))
    )
    for target, hot in zip((time_grad, class_grad), table_hots(ids_all, time_grad.shape[1])):
        target[...] = contract_rows_exact(grad_condition, hot.astype(jnp.float32))
    reduce_rows.finish()
    reduce_ffn.finish()


def rear(*args):
    shape = jax.ShapeDtypeStruct
    grads, w_out, totals, grad_w_fc2, w_qkv, biases, ids_all, w_ada = (
        args[place] for place in (1, 2, 3, 6, 9, 11, 17, 18)
    )
    blocks, tok_rows, model_width = grads.shape
    width = w_qkv.shape[1]
    head_local = totals.shape[0]
    seq_len = blocks * tok_rows
    third, hidden_width = grad_w_fc2.shape[2:]
    width_part = 3 * third
    out_width = w_out.shape[1]
    depth, ada_width = w_ada.shape
    table_rows = ids_all.shape[2]
    low = jnp.bfloat16
    full = jnp.float32
    heads_wide = pltpu.VMEM((head_local, seq_len, HEAD_LANES), full)
    slotted = (ROW_PARTS, SLOT_ROWS)
    wide = pltpu.VMEM(slotted + (ada_width,), full)
    wide_low = pltpu.VMEM(slotted + (ada_width,), low)
    narrow = pltpu.VMEM(slotted + (depth,), full)
    sizes = (
        [(third, hidden_width)] * 4 + [(width_part, out_width)] + [(third, width)] * 3
    )
    return pl.pallas_call(
        rear_kernel,
        out_shape=[
            shape((tok_rows, model_width), low),
            shape((tok_rows, model_width), full),
            shape((depth, table_rows), full),
            shape((depth, table_rows), full),
            shape((depth, ada_width), full),
            shape((SLOT_ROWS, ada_width), full),
            shape((width_part, hidden_width), full),
            shape((width_part, hidden_width), full),
            shape((width_part, width), full),
            shape((width_part, out_width), full),
            shape(biases.shape, full),
        ],
        in_specs=[VMEM_SPEC] * 25,
        out_specs=[VMEM_SPEC] * 11,
        scratch_shapes=[
            pltpu.VMEM((head_local, seq_len, HEAD_LANES), low),
            pltpu.VMEM((head_local, HEAD_LANES, seq_len), low),
            heads_wide,
            heads_wide,
            pltpu.VMEM((seq_len, tok_rows), full),
            pltpu.VMEM((tok_rows, width), full),
            pltpu.VMEM((blocks, tok_rows, width), low),
            pltpu.VMEM((blocks, tok_rows, model_width), low),
            pltpu.VMEM((4, 2, width_part, width), low),
            pltpu.VMEM((4, 2, width_part, out_width), low),
            pltpu.VMEM((3,) + biases.shape, full),
        ]
        + [
            pltpu.VMEM((2, tok_rows, model_width), low),
            pltpu.VMEM((tok_rows, model_width), low),
            pltpu.VMEM((tok_rows, model_width), low),
        ]
        * 2
        + [pltpu.VMEM((3, SLOT_ROWS, model_width), full)]
        + [wide] * 2
        + [wide_low] * 4
        + [pltpu.VMEM((ROW_PARTS,) + biases.shape, full)]
        + [narrow] * 3
        + [
            DMA((4, 7)),
            DMA((4, 7)),
            DMA((2,)),
            DMA((2,)),
            DMA((2, 3)),
            DMA((2, 3)),
        ]
        + reduce_scratch(sizes),
        compiler_params=pltpu.CompilerParams(
            collective_id=1, has_side_effects=True, vmem_limit_bytes=67_000_000
        ),
        name="rear",
    )(*args)


def shards_linked(
    patches,
    time_table,
    class_table,
    w_ada,
    b_ada,
    w_qkv,
    b_qv,
    w_out,
    b_out,
    w_fc1,
    b_fc1,
    w_fc2,
    b_fc2,
    image_lengths,
    segment_ids,
    bucket_ids,
    class_labels,
    cotangent,
):
    model_width = patches.shape[1]
    slot_count = image_lengths.shape[1]
    head_local = b_qv.shape[0]
    head_size = b_qv.shape[1] // 2
    qkv_full, patches_full, condition, mods, ids_all = front(
        bucket_ids, class_labels, time_table.T, class_table.T, w_ada, patches, w_qkv
    )
    qkv_cols = qkv_full.reshape(model_width, w_qkv.shape[1])
    biases = jnp.stack([b_out, b_fc1, b_fc2]).astype(jnp.float32)
    (
        segments,
        vectors,
        rows_one,
        parts,
        totals,
        mixed_rows,
        out_cols,
        ffn_part,
        after_attn,
        grad_after,
        attn_rows_grad,
        sums,
        bias_sums,
        grad_w_fc2,
        grad_w_fc1,
        fc2_head,
        fc2_neck,
    ) = core(
        slot_count,
        head_size,
        patches_full,
        qkv_cols,
        w_out,
        w_fc1,
        w_fc2,
        cotangent,
        patches,
        segment_ids,
        mods,
        b_ada.astype(jnp.float32).reshape(6, model_width),
        biases,
        b_qv.astype(jnp.float32),
    )
    (
        block_out,
        grad_patches,
        grad_time,
        grad_class,
        grad_w_ada,
        grad_b_ada,
        grad_w_fc2,
        grad_w_fc1,
        grad_w_qkv,
        grad_w_out,
        bias_all,
    ) = rear(
        parts,
        attn_rows_grad,
        out_cols,
        totals,
        segment_ids,
        segments,
        grad_w_fc2,
        grad_w_fc1,
        rows_one,
        qkv_cols,
        mixed_rows,
        bias_sums,
        patches,
        grad_after,
        vectors,
        sums,
        condition,
        ids_all,
        w_ada,
        ffn_part,
        after_attn,
        cotangent,
        biases,
        fc2_head,
        fc2_neck,
    )
    grad_time = grad_time.T
    grad_class = grad_class.T
    grad_b_ada = grad_b_ada[0]
    bias_rows = model_width // lax.axis_size("rows")
    row_start = lax.axis_index("rows") * bias_rows
    grad_b_fc1 = bias_all[0]
    grad_b_fc2 = lax.dynamic_slice_in_dim(bias_all[1], row_start, bias_rows)
    grad_b_out = lax.dynamic_slice_in_dim(bias_all[2], row_start, bias_rows)
    bias_terms = bias_all[3, : head_local * 3 * head_size].reshape(head_local, 3, head_size)
    grad_b_qv = jnp.concatenate([bias_terms[:, 0], bias_terms[:, 2]], axis=1)
    return (
        block_out,
        grad_patches,
        grad_time,
        grad_class,
        grad_w_ada,
        grad_b_ada,
        grad_w_qkv,
        grad_b_qv,
        grad_w_out,
        grad_b_out,
        grad_w_fc1,
        grad_b_fc1,
        grad_w_fc2,
        grad_b_fc2,
    )


def solution(mesh):
    placed = (
        P(("rows", "heads"), None),
        P("rows", "heads"),
        P("rows", "heads"),
        P("heads", "rows"),
        P(),
        P("rows", "heads"),
        P("heads", None),
        P("rows", "heads"),
        P(),
        P("rows", "heads"),
        P("heads"),
        P("rows", "heads"),
        P(),
        P("rows", None),
        P("rows", None),
        P("rows", None),
        P("rows", None),
        P(("rows", "heads"), None),
    )
    linked = mesh.shape["rows"] == ROW_PARTS and mesh.shape["heads"] == HEAD_PARTS
    return jax.shard_map(
        shards_linked if linked else shards_plain,
        mesh=mesh,
        in_specs=placed,
        out_specs=(
            P(("rows", "heads"), None),
            P(("rows", "heads"), None),
            P("rows", "heads"),
            P("rows", "heads"),
            P("heads", "rows"),
            P("rows"),
            P("rows", "heads"),
            P("heads", None),
            P("rows", "heads"),
            P("rows"),
            P("rows", "heads"),
            P("heads"),
            P("rows", "heads"),
            P("rows"),
        ),
        check_vma=False,
    )
```

```python
import functools
import math

import jax
import jax.numpy as jnp
from jax import lax
from jax.experimental import pallas as pl
from jax.experimental.pallas import tpu as pltpu
from jax.sharding import PartitionSpec as P

EPSILON = 1e-06
MASKED = -1e30
HIGH = lax.Precision.HIGHEST
TANH_COEFF = 0.7978845608028654
BLOCK_LIMIT = 512


def layer_norm(values):
    average = jnp.mean(values, axis=-1, keepdims=True)
    centred = values - average
    variance = jnp.mean(centred * centred, axis=-1, keepdims=True)
    return centred * lax.rsqrt(variance + EPSILON)


def gelu_tanh(values):
    return (
        0.5 * values * (1.0 + jnp.tanh(TANH_COEFF * (values + 0.044715 * values * values * values)))
    )


def silu_plain(values):
    return values / (1.0 + jnp.exp(-values))


def modulate(values, shift_term, scale_term):
    return layer_norm(values) * (1.0 + scale_term) + shift_term


def contract_rows(left_matrix, right_matrix):
    return lax.dot_general(
        left_matrix, right_matrix, (((0,), (0,)), ((), ())), preferred_element_type=jnp.float32
    )


def contract_rows_exact(left_matrix, right_matrix):
    return lax.dot_general(
        left_matrix,
        right_matrix,
        (((0,), (0,)), ((), ())),
        precision=HIGH,
        preferred_element_type=jnp.float32,
    )


def times_transposed(left_matrix, right_matrix):
    return lax.dot_general(
        left_matrix, right_matrix, (((1,), (1,)), ((), ())), preferred_element_type=jnp.float32
    )


def gather_weights(w_qkv, w_out, w_fc1, w_fc2):
    return (
        lax.all_gather(w_qkv, "rows", axis=0, tiled=True),
        lax.all_gather(w_out, "rows", axis=0, tiled=True),
        lax.all_gather(w_fc1, "rows", axis=0, tiled=True),
        lax.all_gather(w_fc2, "rows", axis=0, tiled=True),
    )


def shards_plain(
    patches,
    time_table,
    class_table,
    w_ada,
    b_ada,
    w_qkv,
    b_qv,
    w_out,
    b_out,
    w_fc1,
    b_fc1,
    w_fc2,
    b_fc2,
    image_lengths,
    segment_ids,
    bucket_ids,
    class_labels,
    cotangent,
):
    head_parts = lax.axis_size("heads")
    member = lax.axis_index("heads")
    tok_rows = patches.shape[0]
    model_width = patches.shape[1]
    seq_count = segment_ids.shape[0]
    seq_len = segment_ids.shape[1]
    slot_count = image_lengths.shape[1]
    image_count = seq_count * slot_count
    group_rows = tok_rows * head_parts
    head_local = b_qv.shape[0]
    head_size = b_qv.shape[1] // 2
    block_rows = min(BLOCK_LIMIT, seq_len)
    scale_factor = 1.0 / math.sqrt(head_size)
    row_parts = lax.axis_size("rows")
    table_rows = time_table.shape[0]
    ada_width = w_ada.shape[1]
    qkv_cols, out_cols, fc1_cols, fc2_cols = gather_weights(w_qkv, w_out, w_fc1, w_fc2)
    ids_all = lax.all_gather(
        jnp.concatenate([bucket_ids, class_labels], axis=1), "rows", axis=0, tiled=True
    )
    every_slot = row_parts * image_count
    table_places = lax.axis_index("rows") * table_rows + jnp.arange(table_rows, dtype=jnp.int32)
    bucket_hot = (
        ids_all[:, :slot_count].reshape(every_slot)[:, None] == table_places[None, :]
    ).astype(jnp.bfloat16)
    label_hot = (
        ids_all[:, slot_count:].reshape(every_slot)[:, None] == table_places[None, :]
    ).astype(jnp.bfloat16)
    condition = lax.psum(
        jnp.dot(bucket_hot, time_table, preferred_element_type=jnp.float32)
        + jnp.dot(label_hot, class_table, preferred_element_type=jnp.float32),
        "rows",
    )
    silu_value, silu_pull = jax.vjp(silu_plain, condition)
    silu_low = silu_value.astype(jnp.bfloat16)
    mods_part = jnp.dot(silu_low, w_ada, preferred_element_type=jnp.float32)
    mods_cols = lax.psum(mods_part, "heads").reshape(row_parts, image_count, ada_width)
    mods_own = lax.all_to_all(mods_cols, "rows", split_axis=0, concat_axis=0, tiled=True)
    mods_all = mods_own.transpose(1, 0, 2).reshape(
        image_count, row_parts * ada_width
    ) + b_ada.astype(jnp.float32)
    positions = member * tok_rows + jnp.arange(tok_rows, dtype=jnp.int32)
    own_segments = lax.dynamic_slice_in_dim(
        segment_ids.reshape(seq_count * seq_len), member * tok_rows, tok_rows
    )
    token_image = positions // seq_len * slot_count + own_segments
    token_hot = (token_image[:, None] == jnp.arange(image_count, dtype=jnp.int32)[None, :]).astype(
        jnp.float32
    )
    token_mods = [
        jnp.dot(
            token_hot,
            mods_all[:, part_index * model_width : (part_index + 1) * model_width],
            precision=HIGH,
        )
        for part_index in range(6)
    ]
    shift_attn, scale_attn, gate_attn, shift_mlp, scale_mlp, gate_mlp = token_mods
    inputs = patches.astype(jnp.float32)
    first_value, first_pull = jax.vjp(modulate, inputs, shift_attn, scale_attn)
    hidden_one = first_value.astype(jnp.bfloat16)
    rows_one = lax.all_gather(hidden_one, "heads", axis=0, tiled=True)
    zero_bias = jnp.zeros((head_local, head_size), b_qv.dtype)
    qkv_bias = (
        jnp.concatenate([b_qv[:, :head_size], zero_bias, b_qv[:, head_size:]], axis=1)
        .reshape(head_local * 3 * head_size)
        .astype(jnp.float32)
    )
    projected = (jnp.dot(rows_one, qkv_cols, preferred_element_type=jnp.float32) + qkv_bias).astype(
        jnp.bfloat16
    )
    seq_qkv = projected.reshape(seq_count, seq_len, head_local, 3, head_size)
    slot_ends = jnp.cumsum(image_lengths, axis=1)
    places = jnp.arange(seq_len, dtype=jnp.int32)
    image_of = jnp.sum((places[None, :, None] >= slot_ends[:, None, :]).astype(jnp.int32), axis=2)

    def block_scores(query_rows, key_rows, image_rows, image_cols):
        scores = (
            jnp.einsum("qhd,khd->hqk", query_rows, key_rows, preferred_element_type=jnp.float32)
            * scale_factor
        )
        return jnp.where((image_rows[:, None] == image_cols[None, :])[None], scores, MASKED)

    def attend_forward(pieces):
        seq_block, seq_image = pieces
        key_rows = seq_block[:, :, 1]
        value_rows = seq_block[:, :, 2]
        outputs = []
        totals = []
        for row_start in range(0, seq_len, block_rows):
            stop_row = row_start + block_rows
            query_rows = seq_block[row_start:stop_row, :, 0]
            scores = block_scores(query_rows, key_rows, seq_image[row_start:stop_row], seq_image)
            row_peak = jnp.max(scores, axis=2, keepdims=True)
            raised = jnp.exp(scores - row_peak)
            row_total = jnp.sum(raised, axis=2, keepdims=True)
            soft_low = (raised / row_total).astype(jnp.bfloat16)
            outputs.append(
                jnp.einsum(
                    "hqk,khd->qhd", soft_low, value_rows, preferred_element_type=jnp.float32
                ).astype(jnp.bfloat16)
            )
            totals.append((row_peak + jnp.log(row_total))[:, :, 0])
        return (jnp.concatenate(outputs, axis=0), jnp.concatenate(totals, axis=1))

    mixed, log_totals = lax.map(attend_forward, (seq_qkv, image_of))
    mixed_rows = mixed.reshape(group_rows, head_local * head_size)
    attn_out = lax.psum_scatter(
        times_transposed(
            lax.slice_in_dim(mixed_rows, 0, tok_rows * lax.axis_size("heads"), axis=0), out_cols
        ).astype(jnp.bfloat16),
        "heads",
        scatter_dimension=0,
        tiled=True,
    ).astype(jnp.float32) + b_out.astype(jnp.float32)
    after_attn = inputs + gate_attn * attn_out
    second_value, second_pull = jax.vjp(modulate, after_attn, shift_mlp, scale_mlp)
    hidden_two = second_value.astype(jnp.bfloat16)
    rows_two = lax.all_gather(hidden_two, "heads", axis=0, tiled=True)
    inner = jnp.dot(rows_two, fc1_cols, preferred_element_type=jnp.float32) + b_fc1.astype(
        jnp.float32
    )
    gelu_value, gelu_pull = jax.vjp(gelu_tanh, inner)
    active = gelu_value.astype(jnp.bfloat16)
    ffn_out = lax.psum_scatter(
        times_transposed(
            lax.slice_in_dim(active, 0, tok_rows * lax.axis_size("heads"), axis=0), fc2_cols
        ).astype(jnp.bfloat16),
        "heads",
        scatter_dimension=0,
        tiled=True,
    ).astype(jnp.float32) + b_fc2.astype(jnp.float32)
    block_out = (after_attn + gate_mlp * ffn_out).astype(jnp.bfloat16)
    upstream = cotangent.astype(jnp.float32)
    grad_ffn = (gate_mlp * upstream).astype(jnp.bfloat16)
    ffn_rows = lax.all_gather(grad_ffn, "heads", axis=0, tiled=True)
    grad_w_fc2 = contract_rows(ffn_rows, active)
    grad_b_fc2 = jnp.sum(ffn_rows, axis=0, dtype=jnp.float32)
    grad_active = jnp.dot(ffn_rows, fc2_cols, preferred_element_type=jnp.float32)
    grad_inner = gelu_pull(grad_active)[0].astype(jnp.bfloat16)
    grad_w_fc1 = contract_rows(rows_two, grad_inner)
    grad_b_fc1 = jnp.sum(grad_inner, axis=0, dtype=jnp.float32)
    grad_hidden_two = lax.psum_scatter(
        times_transposed(
            lax.slice_in_dim(grad_inner, 0, tok_rows * lax.axis_size("heads"), axis=0), fc1_cols
        ).astype(jnp.bfloat16),
        "heads",
        scatter_dimension=0,
        tiled=True,
    ).astype(jnp.float32)
    grad_after, grad_shift_mlp, grad_scale_mlp = second_pull(grad_hidden_two)
    grad_after = grad_after + upstream
    grad_gate_mlp = upstream * ffn_out
    grad_gate_attn = grad_after * attn_out
    grad_attn = (gate_attn * grad_after).astype(jnp.bfloat16)
    attn_rows_grad = lax.all_gather(grad_attn, "heads", axis=0, tiled=True)
    grad_w_out = contract_rows(attn_rows_grad, mixed_rows)
    grad_b_out = jnp.sum(attn_rows_grad, axis=0, dtype=jnp.float32)
    grad_mixed = jnp.dot(attn_rows_grad, out_cols, preferred_element_type=jnp.float32).astype(
        jnp.bfloat16
    )
    grad_seq = grad_mixed.reshape(seq_count, seq_len, head_local, head_size)

    def attend_backward(pieces):
        seq_block, seq_image, seq_grad, seq_totals = pieces
        key_rows = seq_block[:, :, 1]
        value_rows = seq_block[:, :, 2]
        grad_keys = jnp.zeros(key_rows.shape, jnp.float32)
        grad_values = jnp.zeros(value_rows.shape, jnp.float32)
        grad_queries = []
        for row_start in range(0, seq_len, block_rows):
            stop_row = row_start + block_rows
            query_rows = seq_block[row_start:stop_row, :, 0]
            grad_rows = seq_grad[row_start:stop_row]
            scores = block_scores(query_rows, key_rows, seq_image[row_start:stop_row], seq_image)
            soft_probs = jnp.exp(scores - seq_totals[:, row_start:stop_row, None])
            grad_probs = jnp.einsum(
                "qhd,khd->hqk", grad_rows, value_rows, preferred_element_type=jnp.float32
            )
            inner_sum = jnp.sum(soft_probs * grad_probs, axis=2, keepdims=True)
            grad_scores = (soft_probs * (grad_probs - inner_sum)).astype(jnp.bfloat16)
            grad_queries.append(
                jnp.einsum(
                    "hqk,khd->qhd", grad_scores, key_rows, preferred_element_type=jnp.float32
                )
                * scale_factor
            )
            grad_keys = (
                grad_keys
                + jnp.einsum(
                    "hqk,qhd->khd", grad_scores, query_rows, preferred_element_type=jnp.float32
                )
                * scale_factor
            )
            grad_values = grad_values + jnp.einsum(
                "hqk,qhd->khd",
                soft_probs.astype(jnp.bfloat16),
                grad_rows,
                preferred_element_type=jnp.float32,
            )
        stacked = jnp.stack([jnp.concatenate(grad_queries, axis=0), grad_keys, grad_values], axis=2)
        return stacked.astype(jnp.bfloat16)

    grad_qkv = lax.map(attend_backward, (seq_qkv, image_of, grad_seq, log_totals)).reshape(
        group_rows, head_local * 3 * head_size
    )
    grad_w_qkv = contract_rows(rows_one, grad_qkv)
    bias_terms = jnp.sum(grad_qkv, axis=0, dtype=jnp.float32).reshape(head_local, 3, head_size)
    grad_b_qv = jnp.concatenate([bias_terms[:, 0], bias_terms[:, 2]], axis=1)
    grad_hidden_one = lax.psum_scatter(
        times_transposed(
            lax.slice_in_dim(grad_qkv, 0, tok_rows * lax.axis_size("heads"), axis=0), qkv_cols
        ).astype(jnp.bfloat16),
        "heads",
        scatter_dimension=0,
        tiled=True,
    ).astype(jnp.float32)
    grad_inputs, grad_shift_attn, grad_scale_attn = first_pull(grad_hidden_one)
    grad_patches = grad_inputs + grad_after
    token_grads = (
        grad_shift_attn,
        grad_scale_attn,
        grad_gate_attn,
        grad_shift_mlp,
        grad_scale_mlp,
        grad_gate_mlp,
    )
    mods_grad_part = jnp.concatenate(
        [contract_rows_exact(token_hot, grad_term) for grad_term in token_grads], axis=1
    )
    grad_mods = lax.psum(mods_grad_part.astype(jnp.bfloat16), "heads")
    grad_cols = lax.all_to_all(
        grad_mods.reshape(image_count, row_parts, ada_width).transpose(1, 0, 2),
        "rows",
        split_axis=0,
        concat_axis=0,
        tiled=True,
    ).reshape(every_slot, ada_width)
    grad_w_ada = contract_rows(silu_low, grad_cols)
    grad_b_ada = jnp.sum(grad_cols, axis=0, dtype=jnp.float32)
    grad_silu = lax.psum(times_transposed(grad_cols, w_ada), "rows")
    grad_condition = silu_pull(grad_silu)[0]
    grad_time = contract_rows_exact(bucket_hot.astype(jnp.float32), grad_condition)
    grad_class = contract_rows_exact(label_hot.astype(jnp.float32), grad_condition)

    def row_reduced(partial):
        return lax.psum_scatter(
            partial.astype(jnp.bfloat16), "rows", scatter_dimension=0, tiled=True
        ).astype(jnp.float32)

    grad_w_qkv, grad_w_out, grad_w_fc1, grad_w_fc2 = (
        row_reduced(grad_w_qkv),
        row_reduced(grad_w_out),
        row_reduced(grad_w_fc1),
        row_reduced(grad_w_fc2),
    )
    bias_sizes = (grad_b_qv.size, grad_b_fc1.size, grad_b_out.size, grad_b_fc2.size)
    bias_all = lax.psum(
        jnp.concatenate([grad_b_qv.reshape(-1), grad_b_fc1, grad_b_out, grad_b_fc2]), "rows"
    )
    edges = [sum(bias_sizes[:step]) for step in range(5)]
    bias_rows = model_width // row_parts
    row_start = lax.axis_index("rows") * bias_rows
    grad_b_qv = bias_all[edges[0] : edges[1]].reshape(grad_b_qv.shape)
    grad_b_fc1 = bias_all[edges[1] : edges[2]]
    grad_b_out = lax.dynamic_slice_in_dim(bias_all[edges[2] : edges[3]], row_start, bias_rows)
    grad_b_fc2 = lax.dynamic_slice_in_dim(bias_all[edges[3] : edges[4]], row_start, bias_rows)
    return (
        block_out,
        grad_patches,
        grad_time,
        grad_class,
        grad_w_ada,
        grad_b_ada,
        grad_w_qkv,
        grad_b_qv,
        grad_w_out,
        grad_b_out,
        grad_w_fc1,
        grad_b_fc1,
        grad_w_fc2,
        grad_b_fc2,
    )


MESH = pl.DeviceIdType.MESH
ROW_PARTS = 8
HEAD_PARTS = 4
SLOT_ROWS = 8
VMEM_SPEC = pl.BlockSpec(memory_space=pltpu.VMEM)
ANY_SPEC = pl.BlockSpec(memory_space=pl.ANY)
DMA = pltpu.SemaphoreType.DMA
GRANT = 60 * 1024 * 1024


def places():
    row = lax.axis_index("rows")
    member = lax.axis_index("heads")
    sibling = member + 1 - 2 * lax.rem(member, 2)
    partner = lax.rem(member + 2, HEAD_PARTS)
    opposite = lax.rem(sibling + 2, HEAD_PARTS)
    return row, member, sibling, partner, opposite


def greet(row_steps, head_members):
    barrier = pltpu.get_barrier_semaphore()
    row = lax.axis_index("rows")
    for step in row_steps:
        pl.semaphore_signal(
            barrier,
            inc=1,
            device_id={"rows": lax.rem(row + step, ROW_PARTS)},
            device_id_type=MESH,
        )
    for other in head_members:
        pl.semaphore_signal(barrier, inc=1, device_id={"heads": other}, device_id_type=MESH)
    pl.semaphore_wait(barrier, len(row_steps) + len(head_members))


def to_row(source, target, send, recv, row):
    return pltpu.make_async_remote_copy(
        src_ref=source,
        dst_ref=target,
        send_sem=send,
        recv_sem=recv,
        device_id={"rows": row},
        device_id_type=MESH,
    )


def to_head(source, target, send, recv, member):
    return pltpu.make_async_remote_copy(
        src_ref=source,
        dst_ref=target,
        send_sem=send,
        recv_sem=recv,
        device_id={"heads": member},
        device_id_type=MESH,
    )


class RowGather:
    def __init__(self, shard, full, sends, recvs, local_sem, chunks):
        self.row = lax.axis_index("rows")
        self.level = self.row // 2
        self.side = lax.rem(self.row, 2)
        self.mate = self.row + 1 - 2 * self.side
        above = lax.rem(self.level + 1, 4) * 2 + self.side
        size = shard.shape[0] // chunks
        self.own = pltpu.make_async_copy(shard, full.at[self.row], local_sem)
        self.straight = []
        self.across = []
        for chunk in range(chunks):
            part = pl.ds(chunk * size, size)
            straight = []
            across = []
            for step in range(4):
                origin = lax.rem(self.level + 4 - step, 4) * 2 + self.side
                source = shard.at[part] if step == 0 else full.at[origin, part]
                target = full.at[origin, part]
                across.append(
                    to_row(
                        source,
                        target,
                        sends.at[chunk, 3 + step],
                        recvs.at[chunk, 3 + step],
                        self.mate,
                    )
                )
                if step < 3:
                    straight.append(
                        to_row(
                            source, target, sends.at[chunk, step], recvs.at[chunk, step], above
                        )
                    )
            self.straight.append(straight)
            self.across.append(across)

    def start(self, chunk):
        self.straight[chunk][0].start()
        self.across[chunk][0].start()

    def hop(self, chunk, step):
        self.straight[chunk][step].wait_recv()
        if step < 2:
            self.straight[chunk][step + 1].start()
        self.across[chunk][step + 1].start()

    def finish(self):
        self.own.wait()
        for straight, across in zip(self.straight, self.across):
            for copy in straight:
                copy.wait_send()
            for copy in across:
                copy.wait()


class HeadGather:
    def __init__(self, block, full, sends, recvs, local_sem):
        row, member, sibling, partner, opposite = places()
        self.own = None
        if block is None:
            block = full.at[member]
        else:
            self.own = pltpu.make_async_copy(block, full.at[member], local_sem)
        self.beside = to_head(block, full.at[member], sends.at[0], recvs.at[0], sibling)
        self.across = to_head(block, full.at[member], sends.at[1], recvs.at[1], partner)
        self.onward = to_head(
            full.at[partner], full.at[partner], sends.at[2], recvs.at[2], sibling
        )

    def start(self):
        self.across.start()
        self.beside.start()
        if self.own is not None:
            self.own.start()

    def wait_sibling(self):
        self.beside.wait_recv()

    def wait_partner(self):
        self.across.wait_recv()
        self.onward.start()

    def wait_opposite(self):
        self.onward.wait_recv()

    def finish(self):
        if self.own is not None:
            self.own.wait()
        self.beside.wait_send()
        self.across.wait_send()
        self.onward.wait_send()


def front_kernel(
    bucket_ref,
    label_ref,
    time_ref,
    class_ref,
    ada_ref,
    patches_ref,
    qkv_ref,
    qkv_full,
    patches_full,
    cond_all,
    mods_ref,
    ids_all,
    ids_own,
    cond_part,
    cond_in,
    mods_part,
    mods_in,
    mods_sibling,
    mods_pair,
    mods_partner,
    small_send,
    small_recv,
    pair_send,
    pair_recv,
    head_send,
    head_recv,
    qkv_send,
    qkv_recv,
    local_sems,
):
    row, member, sibling, partner, opposite = places()
    greet(range(1, ROW_PARTS), (sibling, partner))
    others = [(step, lax.rem(row + step, ROW_PARTS)) for step in range(1, ROW_PARTS)]

    def spread(stage, source_of, target):
        copies = []
        for step, other in others:
            copy = to_row(
                source_of(other),
                target.at[row],
                small_send.at[stage, step - 1],
                small_recv.at[stage, step - 1],
                other,
            )
            copy.start()
            copies.append(copy)
        return copies

    def settle(copies):
        for copy in copies:
            copy.wait()

    table_rows = time_ref.shape[1]
    slots = ROW_PARTS * SLOT_ROWS
    ids_own[...] = jnp.full_like(ids_own, -1)
    for start, chosen in ((0, bucket_ref), (SLOT_ROWS, label_ref)):
        for slot in range(chosen.shape[1]):
            ids_own[start + slot : start + slot + 1] = jnp.broadcast_to(
                chosen[0:1, slot : slot + 1], (1, table_rows)
            )
    ids_copies = spread(0, lambda other: ids_own, ids_all)
    gather_qkv = RowGather(qkv_ref, qkv_full, qkv_send, qkv_recv, local_sems.at[0], 3)
    gather_patches = HeadGather(patches_ref, patches_full, head_send, head_recv, local_sems.at[1])
    gather_patches.start()
    gather_qkv.own.start()
    gather_qkv.start(0)
    ids_all[row] = ids_own[...]
    settle(ids_copies)
    bucket_hot, label_hot = (hot.astype(jnp.bfloat16) for hot in table_hots(ids_all, table_rows))
    found = times_transposed(bucket_hot, time_ref[...]) + times_transposed(
        label_hot, class_ref[...]
    )
    cond_part[...] = found.reshape(cond_part.shape)
    copies = spread(1, lambda other: cond_part.at[other], cond_in)
    gather_qkv.start(1)
    cond_in[row] = cond_part[row]
    gather_qkv.hop(0, 0)
    settle(copies)
    condition = jnp.sum(cond_in[...], axis=0)
    cond_all[row] = condition
    cond_part[row] = condition
    copies = spread(2, lambda other: cond_part.at[row], cond_all)
    gather_qkv.start(2)
    gather_qkv.hop(1, 0)
    gather_qkv.hop(0, 1)
    settle(copies)
    every = cond_all[...].reshape(slots, cond_all.shape[2])
    silu_low = (every / (1.0 + jnp.exp(-every))).astype(jnp.bfloat16)
    mods_part[...] = jnp.dot(
        silu_low, ada_ref[...], preferred_element_type=jnp.float32
    ).reshape(mods_part.shape)
    copies = spread(3, lambda other: mods_part.at[other], mods_in)
    mods_in[row] = mods_part[row]
    gather_qkv.hop(2, 0)
    gather_qkv.hop(1, 1)
    gather_qkv.hop(0, 2)
    settle(copies)
    beside = to_head(mods_in, mods_sibling, pair_send.at[0], pair_recv.at[0], sibling)
    beside.start()
    gather_patches.wait_sibling()
    beside.wait()
    mods_pair[...] = mods_in[...] + mods_sibling[...]
    across = to_head(mods_pair, mods_partner, pair_send.at[1], pair_recv.at[1], partner)
    across.start()
    gather_patches.wait_partner()
    gather_qkv.hop(2, 1)
    gather_qkv.hop(1, 2)
    across.wait()
    mods_ref[...] = mods_pair[...] + mods_partner[...]
    gather_qkv.hop(2, 2)
    gather_patches.wait_opposite()
    gather_patches.finish()
    gather_qkv.finish()


def front(bucket_ids, class_labels, time_columns, class_columns, w_ada, patches, w_qkv):
    depth, ada_width = w_ada.shape
    shape = jax.ShapeDtypeStruct
    slotted = (ROW_PARTS, SLOT_ROWS)
    wide = pltpu.VMEM(slotted + (ada_width,), jnp.float32)
    narrow = pltpu.VMEM(slotted + (depth,), jnp.float32)
    return pl.pallas_call(
        front_kernel,
        out_shape=(
            shape((ROW_PARTS,) + w_qkv.shape, jnp.bfloat16),
            shape((HEAD_PARTS,) + patches.shape, jnp.bfloat16),
            shape(slotted + (depth,), jnp.float32),
            shape(slotted + (ada_width,), jnp.float32),
            shape((ROW_PARTS, 2 * SLOT_ROWS, time_columns.shape[1]), jnp.int32),
        ),
        in_specs=[VMEM_SPEC] * 7,
        out_specs=[ANY_SPEC] * 2 + [VMEM_SPEC] * 3,
        scratch_shapes=[pltpu.VMEM((2 * SLOT_ROWS, time_columns.shape[1]), jnp.int32)]
        + [narrow] * 2
        + [wide] * 5
        + [
            DMA((4, 7)),
            DMA((4, 7)),
            DMA((2,)),
            DMA((2,)),
            DMA((3,)),
            DMA((3,)),
            DMA((3, 7)),
            DMA((3, 7)),
            DMA((2,)),
        ],
        compiler_params=pltpu.CompilerParams(
            collective_id=0, has_side_effects=True, vmem_limit_bytes=GRANT
        ),
        name="front",
    )(bucket_ids, class_labels, time_columns, class_columns, w_ada, patches, w_qkv)


class HeadReduce:
    def __init__(self, partial, beside_in, pair, across_in, sends, recvs):
        row, member, sibling, partner, opposite = places()
        self.member = member
        self.partner = partner
        self.partial = partial
        self.beside_in = beside_in
        self.pair = pair
        self.across_in = across_in
        self.first = to_head(
            partial.at[opposite], beside_in.at[1], sends.at[0], recvs.at[0], sibling
        )
        self.second = to_head(
            partial.at[sibling], beside_in.at[0], sends.at[1], recvs.at[1], sibling
        )
        self.across = to_head(pair, across_in, sends.at[2], recvs.at[2], partner)

    def start(self):
        self.first.start()
        self.second.start()

    def send_pair(self):
        self.first.wait_recv()
        self.pair[...] = (
            self.partial[self.partner].astype(jnp.float32)
            + self.beside_in[1].astype(jnp.float32)
        ).astype(jnp.bfloat16)
        self.across.start()

    def settle(self):
        self.second.wait_recv()
        self.across.wait_recv()

    def rows(self, part):
        return (
            self.partial[self.member, part].astype(jnp.float32)
            + self.beside_in[0, part].astype(jnp.float32)
            + self.across_in[part].astype(jnp.float32)
        )

    def finish(self):
        self.first.wait_send()
        self.second.wait_send()
        self.across.wait_send()


class RowReduce:
    def __init__(self, partial, chunk, buffers, total, sends, recvs):
        row = lax.axis_index("rows")
        self.level = row // 2
        self.side = lax.rem(row, 2)
        mate = row + 1 - 2 * self.side
        self.partial = partial
        self.mate_in, self.pair, self.straight_in = buffers
        self.total = total
        size = total.shape[0]
        self.part = pl.ds(chunk * size, size)
        self.beside = to_row(
            partial.at[:, 1 - self.side, self.part], self.mate_in, sends.at[0], recvs.at[0], mate
        )
        self.straight = []
        for step in range(1, 4):
            target = lax.rem(self.level + step, 4)
            self.straight.append(
                to_row(
                    self.pair.at[target],
                    self.straight_in.at[step - 1],
                    sends.at[step],
                    recvs.at[step],
                    target * 2 + self.side,
                )
            )

    def start(self):
        self.beside.start()

    def send_pair(self):
        self.beside.wait_recv()

        def one(level, carry):
            self.pair[level] = (
                self.partial[level, self.side, self.part].astype(jnp.float32)
                + self.mate_in[level].astype(jnp.float32)
            ).astype(jnp.bfloat16)
            return carry

        lax.fori_loop(0, 4, one, 0)
        for copy in self.straight:
            copy.start()

    def finish(self):
        for copy in self.straight:
            copy.wait_recv()
        self.total[...] = (
            self.pair[self.level].astype(jnp.float32)
            + self.straight_in[0].astype(jnp.float32)
            + self.straight_in[1].astype(jnp.float32)
            + self.straight_in[2].astype(jnp.float32)
        )
        self.beside.wait_send()
        for copy in self.straight:
            copy.wait_send()


def row_reduces(jobs, reducing):
    buffers, sends, recvs = reducing[:-2], reducing[-2], reducing[-1]
    return [
        RowReduce(
            partial,
            chunk,
            buffers[3 * place : 3 * place + 3],
            total,
            sends.at[place],
            recvs.at[place],
        )
        for place, (partial, chunk, total) in enumerate(jobs)
    ]


def reduce_scratch(sizes):
    landing = []
    for rows, columns in sizes:
        landing += [
            pltpu.VMEM((4, rows, columns), jnp.bfloat16),
            pltpu.VMEM((4, rows, columns), jnp.bfloat16),
            pltpu.VMEM((3, rows, columns), jnp.bfloat16),
        ]
    return landing + [DMA((len(sizes), 4)), DMA((len(sizes), 4))]


def picked(vectors, part_index, segments, width):
    wide = jnp.concatenate([segments] * (width // segments.shape[1]), axis=1)
    slot_count = vectors.shape[1]
    chosen = vectors[part_index, slot_count - 1 : slot_count]
    for slot in range(slot_count - 2, -1, -1):
        chosen = jnp.where(wide == slot, vectors[part_index, slot : slot + 1], chosen)
    return chosen


def slot_hot(segment_row, start):
    chosen = segment_row[:, pl.ds(pl.multiple_of(start, 128), 128)]
    slots = lax.broadcasted_iota(jnp.int32, (SLOT_ROWS, 128), 0)
    return (jnp.broadcast_to(chosen, slots.shape) == slots).astype(jnp.float32)


def table_hots(ids_all, table_rows):
    slots = ROW_PARTS * SLOT_ROWS
    table_places = lax.axis_index("rows") * table_rows + lax.broadcasted_iota(
        jnp.int32, (slots, table_rows), 1
    )
    return [
        ids_all[:, start : start + SLOT_ROWS].reshape(slots, table_rows) == table_places
        for start in (0, SLOT_ROWS)
    ]


def centre_rows(values):
    centred = values - jnp.mean(values, axis=1, keepdims=True)
    factor = lax.rsqrt(jnp.mean(centred * centred, axis=1, keepdims=True) + EPSILON)
    return centred * factor, factor


def weight_grad(left, right, target):
    blocks, tok_rows, depth = left.shape
    height = blocks * tok_rows
    flat = target.reshape(depth, target.shape[3])
    third = depth // 3

    def some(step, carry):
        columns = pl.ds(pl.multiple_of(step * third, 128), third)
        flat[columns] = contract_rows(
            left[:, :, columns].reshape(height, third),
            right[...].reshape(height, right.shape[2]),
        ).astype(jnp.bfloat16)
        return carry

    lax.fori_loop(0, 3, some, 0)


def core_kernel(
    patches_full,
    qkv_ref,
    out_shard,
    fc1_shard,
    fc2_shard,
    cotangent_ref,
    patches_ref,
    segment_row,
    mods_ref,
    ada_bias,
    bias_ref,
    value_bias,
    segments_ref,
    vectors_ref,
    normed_rows,
    parts,
    totals_out,
    mixed,
    out_w,
    active_rows,
    after_ref,
    after_grad,
    attn_grad,
    slot_sums,
    bias_sums,
    fc2_rest,
    fc1_part,
    fc2_head,
    fc2_neck,
    qkv_bias,
    ffn_rows,
    hidden_rows,
    inner_grad,
    fc2_part,
    inner_bias,
    ffn_bias,
    out_full,
    fc1_full,
    fc2_full,
    active_grad,
    value_columns,
    head_mixed,
    bias,
    group_part,
    beside_in,
    pair_rows,
    across_in,
    attn_out,
    gather_send,
    gather_recv,
    reduce_send,
    reduce_recv,
    out_send,
    out_recv,
    fc1_send,
    fc1_recv,
    fc2_send,
    fc2_recv,
    local_sems,
    *reducing,
):
    row, member, sibling, partner, opposite = places()
    direction = sibling - member
    greet(range(1, ROW_PARTS), (sibling, partner))
    tok_rows, model_width = patches_ref.shape
    blocks = normed_rows.shape[0]
    seq_len = blocks * tok_rows
    width = qkv_ref.shape[1]
    head_local = totals_out.shape[0]
    head_size = width // (3 * head_local)
    scale_factor = 1.0 / math.sqrt(head_size)
    loads = [
        pltpu.make_async_copy(patches_full.at[block], normed_rows.at[block], local_sems.at[block])
        for block in range(blocks)
    ]
    for load in loads:
        load.start()
    gather_out = RowGather(out_shard, out_full, out_send, out_recv, local_sems.at[4], 1)
    gather_fc1 = RowGather(fc1_shard, fc1_full, fc1_send, fc1_recv, local_sems.at[5], 3)
    gather_fc2 = RowGather(fc2_shard, fc2_full, fc2_send, fc2_recv, local_sems.at[6], 3)
    gather_cotangent = HeadGather(
        cotangent_ref, ffn_rows, gather_send.at[2], gather_recv.at[2], local_sems.at[7]
    )
    gather_out.own.start()
    gather_out.start(0)
    gather_fc1.own.start()
    gather_fc2.own.start()
    for chunk in range(3):
        gather_fc1.start(chunk)
    gather_cotangent.start()
    reduce_attn = HeadReduce(
        group_part, beside_in, pair_rows, across_in, reduce_send.at[0], reduce_recv.at[0]
    )
    reduce_hidden = HeadReduce(
        group_part, beside_in, pair_rows, across_in, reduce_send.at[1], reduce_recv.at[1]
    )
    gather_hidden = HeadGather(None, hidden_rows, gather_send.at[0], gather_recv.at[0], None)
    gather_grad = HeadGather(None, attn_grad, gather_send.at[1], gather_recv.at[1], None)
    parts[...] = jnp.zeros_like(parts)
    segments_ref[...] = (
        jnp.broadcast_to(segment_row[...].astype(jnp.float32), (128, seq_len))
        .T.astype(jnp.int32)
    )
    slot_count = vectors_ref.shape[1]
    fine = mods_ref.shape[2] // 3
    for unit in range(3 * ROW_PARTS):
        part_index, within = divmod(unit * fine, model_width)
        span = slice(within, within + fine)
        vectors_ref[part_index, :, span] = mods_ref[
            unit // 3, 0:slot_count, unit % 3 * fine : (unit % 3 + 1) * fine
        ]
    for part_index in range(6):
        vectors_ref[part_index] += ada_bias[part_index : part_index + 1]
    qkv_bias[...] = jnp.zeros_like(qkv_bias)
    for head in range(head_local):
        for place in (0, 2):
            start = (3 * head + place) * head_size
            taken = slice(place // 2 * head_size, (place // 2 + 1) * head_size)
            qkv_bias[:, start : start + head_size] = value_bias[head : head + 1, taken]
    for load in loads:
        load.wait()

    def first_norm(step, carry):
        block = step // 2
        part = pl.ds(pl.multiple_of(lax.rem(step, 2) * 128, 128), 128)
        segments = segments_ref[pl.ds(pl.multiple_of(step * 128, 128), 128)]
        normed, _ = centre_rows(normed_rows[block, part].astype(jnp.float32))
        normed_rows[block, part] = (
            normed * (1.0 + picked(vectors_ref, 1, segments, model_width))
            + picked(vectors_ref, 0, segments, model_width)
        ).astype(jnp.bfloat16)
        return carry

    lax.fori_loop(0, 2 * blocks, first_norm, 0)
    gather_out.hop(0, 0)
    gather_fc1.hop(0, 0)
    gather_fc1.hop(1, 0)
    gather_fc2.start(0)

    def project_in(block, carry):
        rows = pl.ds(pl.multiple_of(block * tok_rows, tok_rows), tok_rows)
        active_grad[0, :, 0:width] = (
            jnp.dot(normed_rows[block], qkv_ref[...], preferred_element_type=jnp.float32)
            + qkv_bias[...]
        )
        for part in range(3 * head_local):
            parts[part, rows, 0:head_size] = active_grad[
                0, :, part * head_size : (part + 1) * head_size
            ].astype(jnp.bfloat16)
        return carry

    lax.fori_loop(0, blocks, project_in, 0)
    gather_out.hop(0, 1)
    gather_fc1.hop(2, 0)
    gather_fc1.hop(0, 1)
    gather_fc2.start(1)

    def turn(head, carry):
        value_columns[head] = parts[3 * head + 2].astype(jnp.float32).T.astype(jnp.bfloat16)
        return carry

    lax.fori_loop(0, head_local, turn, 0)

    def attend(block):
        rows = pl.ds(pl.multiple_of(block * tok_rows, tok_rows), tok_rows)
        keys = jnp.concatenate([segments_ref[...]] * (tok_rows // 128), axis=1)
        same = keys == jnp.broadcast_to(segment_row[:, rows], keys.shape)
        bias[...] = jnp.where(same, 0.0, MASKED)

        def one_head(head, carry):
            scores = (
                times_transposed(parts[3 * head + 1], parts[3 * head, rows]) * scale_factor
                + bias[...]
            )
            peak = jnp.max(scores, axis=0, keepdims=True)
            raised = jnp.exp(scores - peak)
            total = jnp.sum(raised, axis=0, keepdims=True)
            totals_out[head, block] = peak + jnp.log(total)
            head_mixed[head] = jnp.dot(
                value_columns[head],
                (raised * (1.0 / total)).astype(jnp.bfloat16),
                preferred_element_type=jnp.float32,
            ).T
            return carry

        lax.fori_loop(0, head_local, one_head, 0)
        for head in range(head_local):
            active_grad[1, :, head * head_size : (head + 1) * head_size] = head_mixed[
                head, :, 0:head_size
            ]
        mixed[block] = active_grad[1, :, 0 : head_local * head_size].astype(jnp.bfloat16)

    def project(block):
        group_part[block] = times_transposed(mixed[block], out_w[...]).astype(jnp.bfloat16)

    attend(opposite)
    gather_out.hop(0, 2)
    gather_fc1.hop(1, 1)
    gather_fc2.hop(0, 0)
    gather_fc2.start(2)
    attend(partner)
    gather_fc1.hop(2, 1)
    gather_fc1.hop(0, 2)
    gather_out.finish()
    out_w[...] = out_full[...].reshape(out_w.shape)
    project(opposite)
    reduce_attn.first.start()
    project(partner)
    reduce_attn.send_pair()
    gather_fc2.hop(1, 0)
    attend(sibling)
    gather_fc1.hop(1, 2)
    gather_fc2.hop(0, 1)
    gather_fc2.hop(2, 0)
    attend(member)
    gather_fc1.hop(2, 2)
    gather_fc2.hop(1, 1)
    project(sibling)
    reduce_attn.second.start()
    project(member)
    gather_cotangent.wait_sibling()
    gather_cotangent.wait_partner()
    gather_cotangent.wait_opposite()
    gather_cotangent.finish()

    def scale_cotangent(step, carry):
        block = step // 2
        part = pl.ds(pl.multiple_of(lax.rem(step, 2) * 128, 128), 128)
        segments = segments_ref[pl.ds(pl.multiple_of(step * 128, 128), 128)]
        grad = (
            picked(vectors_ref, 5, segments, model_width)
            * ffn_rows[block, part].astype(jnp.float32)
        ).astype(jnp.bfloat16)
        ffn_rows[block, part] = grad
        ffn_bias[...] += jnp.sum(grad.astype(jnp.float32).reshape(16, 8, model_width), axis=0)
        return carry

    ffn_bias[...] = jnp.zeros_like(ffn_bias)
    lax.fori_loop(0, 2 * blocks, scale_cotangent, 0)
    gather_fc2.hop(0, 2)
    gather_fc2.hop(2, 1)
    reduce_attn.settle()

    def second_norm(block, carry):
        part = pl.ds(pl.multiple_of(block * 128, 128), 128)
        segments = segments_ref[
            pl.ds(pl.multiple_of(member * tok_rows + block * 128, 128), 128)
        ]
        out = reduce_attn.rows(part) + bias_ref[0:1]
        after = patches_ref[part].astype(jnp.float32) + (
            picked(vectors_ref, 2, segments, model_width) * out
        )
        attn_out[part] = out
        after_ref[part] = after
        normed, _ = centre_rows(after)
        hidden_rows[member, part] = (
            normed * (1.0 + picked(vectors_ref, 4, segments, model_width))
            + picked(vectors_ref, 3, segments, model_width)
        ).astype(jnp.bfloat16)
        return carry

    lax.fori_loop(0, tok_rows // 128, second_norm, 0)
    gather_hidden.start()
    reduce_attn.finish()
    gather_fc2.hop(1, 2)
    gather_fc2.hop(2, 2)
    gather_fc1.finish()
    hidden_width = active_rows.shape[2]
    fc1 = fc1_full.reshape(model_width, hidden_width)
    fc2 = fc2_full.reshape(model_width, hidden_width)

    inner_bias[...] = jnp.zeros_like(inner_bias)

    def feed(block, carry):
        inner = jnp.dot(
            hidden_rows[block], fc1[...], preferred_element_type=jnp.float32
        ) + bias_ref[1:2]
        square = inner * inner
        bent = jnp.tanh(TANH_COEFF * (inner + 0.044715 * square * inner))
        half = 0.5 * (1.0 + bent)
        active_rows[block] = (inner * half).astype(jnp.bfloat16)
        active_grad[block] = half + 0.5 * inner * (1.0 - bent * bent) * (
            TANH_COEFF * (1.0 + 3.0 * 0.044715 * square)
        )
        return carry

    def through_fc2(block, carry):
        grad = (
            jnp.dot(ffn_rows[block], fc2[...], preferred_element_type=jnp.float32)
            * active_grad[block]
        ).astype(jnp.bfloat16)
        inner_grad[block] = grad
        inner_bias[...] += jnp.sum(
            grad.astype(jnp.float32).reshape(tok_rows // 8, 8, hidden_width), axis=0
        )
        return carry

    def return_fc1(block, carry):
        group_part[block] = times_transposed(inner_grad[block], fc1[...]).astype(jnp.bfloat16)
        return carry

    gather_hidden.wait_sibling()
    lax.fori_loop(0, 2, lambda step, carry: feed(member + step * direction, carry), 0)
    gather_hidden.wait_partner()
    gather_hidden.wait_opposite()
    lax.fori_loop(0, 2, lambda step, carry: feed(opposite - step * direction, carry), 0)
    gather_fc2.finish()

    def turn_back(block, carry):
        through_fc2(block, carry)
        return return_fc1(block, carry)

    lax.fori_loop(0, 2, lambda step, carry: turn_back(opposite - step * direction, carry), 0)
    reduce_hidden.first.start()
    reduce_hidden.send_pair()
    lax.fori_loop(0, 2, lambda step, carry: turn_back(sibling - step * direction, carry), 0)
    reduce_hidden.second.start()

    def forward_fc2(block, carry):
        active_rows[block] = times_transposed(active_rows[block], fc2[...]).astype(jnp.bfloat16)
        return carry

    weight_grad(ffn_rows, active_rows, fc2_part)
    third = fc2_rest.shape[2]
    fc2_rest[...] = fc2_part[:, :, 2 * third : 3 * third]
    reduces = row_reduces(((fc2_part, 0, fc2_head), (fc2_part, 1, fc2_neck)), reducing)
    for unit in reduces:
        unit.start()
    lax.fori_loop(0, HEAD_PARTS, forward_fc2, 0)
    slot_sums[...] = jnp.zeros_like(slot_sums)
    reduce_hidden.settle()

    def second_back(block, carry):
        part = pl.ds(pl.multiple_of(block * 128, 128), 128)
        segments = segments_ref[
            pl.ds(pl.multiple_of(member * tok_rows + block * 128, 128), 128)
        ]
        grad = reduce_hidden.rows(part)
        normed, factor = centre_rows(after_ref[part])
        weighted = grad * (1.0 + picked(vectors_ref, 4, segments, model_width))
        total = cotangent_ref[part].astype(jnp.float32) + factor * (
            weighted
            - jnp.mean(weighted, axis=1, keepdims=True)
            - normed * jnp.mean(weighted * normed, axis=1, keepdims=True)
        )
        after_grad[part] = total
        attn_grad[member, part] = (
            picked(vectors_ref, 2, segments, model_width) * total
        ).astype(jnp.bfloat16)
        hot = slot_hot(segment_row, member * tok_rows + block * 128)
        for index, term in enumerate((total * attn_out[part], grad, grad * normed)):
            slot_sums[index] += jnp.dot(
                hot, term, precision=HIGH, preferred_element_type=jnp.float32
            )
        return carry

    lax.fori_loop(0, tok_rows // 128, second_back, 0)
    gather_grad.start()
    weight_grad(hidden_rows, inner_grad, fc1_part)
    reduces[0].send_pair()
    bias_sums[...] = jnp.zeros_like(bias_sums)
    bias_sums[0:1] = jnp.sum(inner_bias[...], axis=0, keepdims=True)
    bias_sums[1:2] = jnp.sum(ffn_bias[...], axis=0, keepdims=True)
    gather_grad.wait_sibling()
    gather_grad.wait_partner()
    gather_grad.wait_opposite()
    reduces[1].send_pair()
    for unit in reduces:
        unit.finish()
    gather_hidden.finish()
    gather_grad.finish()
    reduce_hidden.finish()


def core(slot_count, head_size, *args):
    shape = jax.ShapeDtypeStruct
    patches_full, w_qkv, out_shard, fc1_shard = args[:4]
    blocks, tok_rows, model_width = patches_full.shape
    seq_len = blocks * tok_rows
    out_width = out_shard.shape[1]
    width_part, hidden_width = fc1_shard.shape
    third = width_part // 3
    head_local = out_width // head_size
    low = jnp.bfloat16
    full = jnp.float32
    rows_low = shape((blocks, tok_rows, model_width), low)
    own = shape((tok_rows, model_width), full)
    own_low = pltpu.VMEM((tok_rows, model_width), low)
    group_low = pltpu.VMEM((blocks, tok_rows, model_width), low)
    hidden_low = pltpu.VMEM((blocks, tok_rows, hidden_width), low)
    part_low = (4, 2, width_part, hidden_width)
    return pl.pallas_call(
        core_kernel,
        out_shape=[
            shape((seq_len, 128), jnp.int32),
            shape((6, slot_count, model_width), full),
            rows_low,
            shape((3 * head_local, seq_len, HEAD_LANES), low),
            shape((head_local, blocks, 1, tok_rows), full),
            shape((blocks, tok_rows, out_width), low),
            shape((model_width, out_width), low),
            rows_low,
            own,
            own,
            rows_low,
            shape((3, SLOT_ROWS, model_width), full),
            shape((8, hidden_width), full),
            shape((4, 2, third, hidden_width), low),
            shape(part_low, low),
            shape((third, hidden_width), full),
            shape((third, hidden_width), full),
        ],
        in_specs=[ANY_SPEC] + [VMEM_SPEC] * 11,
        out_specs=[VMEM_SPEC] * 17,
        scratch_shapes=[
            pltpu.VMEM((1, args[1].shape[1]), full),
            group_low,
            group_low,
            hidden_low,
            pltpu.VMEM(part_low, low),
            pltpu.VMEM((8, hidden_width), full),
            pltpu.VMEM((8, model_width), full),
            pltpu.VMEM((ROW_PARTS,) + out_shard.shape, low),
            pltpu.VMEM((ROW_PARTS,) + fc1_shard.shape, low),
            pltpu.VMEM((ROW_PARTS,) + fc1_shard.shape, low),
            pltpu.VMEM((blocks, tok_rows, hidden_width), full),
            pltpu.VMEM((head_local, HEAD_LANES, seq_len), low),
            pltpu.VMEM((head_local, tok_rows, HEAD_LANES), full),
            pltpu.VMEM((seq_len, tok_rows), full),
            group_low,
            pltpu.VMEM((2, tok_rows, model_width), low),
            own_low,
            own_low,
            pltpu.VMEM((tok_rows, model_width), full),
            DMA((3, 3)),
            DMA((3, 3)),
            DMA((2, 3)),
            DMA((2, 3)),
            DMA((1, 7)),
            DMA((1, 7)),
            DMA((3, 7)),
            DMA((3, 7)),
            DMA((3, 7)),
            DMA((3, 7)),
            DMA((8,)),
        ]
        + reduce_scratch([(third, hidden_width)] * 2),
        compiler_params=pltpu.CompilerParams(
            collective_id=2, has_side_effects=True, vmem_limit_bytes=67_000_000
        ),
        name="core",
    )(*args)


HEAD_LANES = 128


def rear_kernel(
    parts,
    grad_ref,
    out_ref,
    totals_ref,
    segment_row,
    segments_ref,
    fc2_part,
    fc1_part,
    hidden_rows,
    qkv_ref,
    mixed_ref,
    bias_ref,
    patches_ref,
    after_ref,
    vectors_ref,
    sums_ref,
    condition_ref,
    ids_all,
    ada_ref,
    ffn_ref,
    block_ref,
    cotangent_ref,
    bias_rows,
    fc2_head,
    fc2_neck,
    block_out,
    patches_grad,
    time_grad,
    class_grad,
    ada_grad,
    ada_bias,
    fc2_grad,
    fc1_grad,
    qkv_grad,
    out_grad,
    bias_sum,
    mixed_grad,
    key_columns,
    grad_keys,
    grad_values,
    bias,
    packed,
    packed_grad,
    hidden_part,
    qkv_part,
    out_part,
    bias_own,
    beside_in,
    pair_rows,
    across_in,
    ffn_beside,
    ffn_pair,
    ffn_across,
    slot_sums,
    mods_own,
    mods_sibling,
    mods_pair,
    mods_partner,
    mods_low,
    mods_cols,
    bias_all,
    silu_part,
    silu_in,
    silu_all,
    small_send,
    small_recv,
    pair_send,
    pair_recv,
    head_send,
    head_recv,
    *reducing,
):
    row, member, sibling, partner, opposite = places()
    greet(range(1, ROW_PARTS), (sibling, partner))
    others = [(step, lax.rem(row + step, ROW_PARTS)) for step in range(1, ROW_PARTS)]

    def spread(stage, source_of, target):
        copies = []
        for step, other in others:
            copy = to_row(
                source_of(other),
                target.at[row],
                small_send.at[stage, step - 1],
                small_recv.at[stage, step - 1],
                other,
            )
            copy.start()
            copies.append(copy)
        return copies

    def settle(copies):
        for copy in copies:
            copy.wait()

    third = fc2_head.shape[0]
    fc2_grad[0:third] = fc2_head[...]
    fc2_grad[third : 2 * third] = fc2_neck[...]
    units = row_reduces(
        [(fc2_part, 0, fc2_grad.at[pl.ds(2 * third, third)])]
        + [(fc1_part, chunk, fc1_grad.at[pl.ds(chunk * third, third)]) for chunk in range(3)]
        + [(out_part, 0, out_grad)]
        + [(qkv_part, chunk, qkv_grad.at[pl.ds(chunk * third, third)]) for chunk in range(3)],
        reducing,
    )
    reduce_rows = HeadReduce(
        hidden_part, beside_in, pair_rows, across_in, head_send.at[0], head_recv.at[0]
    )
    reduce_ffn = HeadReduce(
        ffn_ref, ffn_beside, ffn_pair, ffn_across, head_send.at[1], head_recv.at[1]
    )
    for unit in units[:3]:
        unit.start()
    reduce_ffn.start()
    reduce_ffn.send_pair()
    blocks, tok_rows, model_width = grad_ref.shape
    width = qkv_ref.shape[1]
    head_local = totals_ref.shape[0]
    head_size = width // (3 * head_local)
    scale_factor = 1.0 / math.sqrt(head_size)
    seq_len = blocks * tok_rows
    mixed_grad[...] = jnp.zeros_like(mixed_grad)
    bias_own[...] = jnp.zeros_like(bias_own)

    def unpack(block, carry):
        rows = pl.ds(pl.multiple_of(block * tok_rows, tok_rows), tok_rows)
        packed[:, 0 : head_local * head_size] = jnp.dot(
            grad_ref[block], out_ref[...], preferred_element_type=jnp.float32
        )
        for head in range(head_local):
            mixed_grad[head, rows, 0:head_size] = packed[
                :, head * head_size : (head + 1) * head_size
            ].astype(jnp.bfloat16)
        bias_own[0] += jnp.sum(
            grad_ref[block].astype(jnp.float32).reshape(tok_rows // 8, 8, model_width), axis=0
        )
        return carry

    lax.fori_loop(0, blocks, unpack, 0)

    def turn(head, carry):
        key_columns[head] = parts[3 * head + 1].astype(jnp.float32).T.astype(jnp.bfloat16)
        return carry

    lax.fori_loop(0, head_local, turn, 0)
    grad_keys[...] = jnp.zeros_like(grad_keys)
    grad_values[...] = jnp.zeros_like(grad_values)
    weight_grad(grad_ref, mixed_ref, out_part)

    for block in range(blocks):
        rows = pl.ds(block * tok_rows, tok_rows)
        keys = jnp.concatenate([segments_ref[...]] * (tok_rows // 128), axis=1)
        same = keys == jnp.broadcast_to(segment_row[:, rows], keys.shape)
        bias[...] = jnp.where(same, 0.0, MASKED)

        def one_head(head, carry):
            query = parts[3 * head, rows]
            grad = mixed_grad[head, rows]
            scores = times_transposed(parts[3 * head + 1], query) * scale_factor + bias[...]
            probs = jnp.exp(scores - totals_ref[head, block])
            grad_probs = times_transposed(parts[3 * head + 2], grad)
            inner = jnp.sum(probs * grad_probs, axis=0, keepdims=True)
            grad_scores = (probs * (grad_probs - inner)).astype(jnp.bfloat16)
            grad_values[head] += jnp.dot(
                probs.astype(jnp.bfloat16), grad, preferred_element_type=jnp.float32
            )
            grad_keys[head] += jnp.dot(grad_scores, query, preferred_element_type=jnp.float32)
            lanes = pl.ds(pl.multiple_of(head * HEAD_LANES, HEAD_LANES), HEAD_LANES)
            hidden_part[block, :, lanes] = (
                jnp.dot(key_columns[head], grad_scores, preferred_element_type=jnp.float32).T
                * scale_factor
            ).astype(jnp.bfloat16)
            return carry

        lax.fori_loop(0, head_local, one_head, 0)
        units[block].send_pair()
        if block < 2:
            units[block + 3].start()

    def pack(block, carry):
        rows = pl.ds(pl.multiple_of(block * tok_rows, tok_rows), tok_rows)
        for head in range(head_local):
            lane = head * HEAD_LANES
            terms = (
                hidden_part[block, :, lane : lane + head_size].astype(jnp.float32),
                grad_keys[head, rows, 0:head_size] * scale_factor,
                grad_values[head, rows, 0:head_size],
            )
            for place, term in enumerate(terms):
                start = (3 * head + place) * head_size
                packed[:, start : start + head_size] = term
        low = packed[...].astype(jnp.bfloat16)
        packed_grad[block] = low
        bias_own[1, :, 0:width] += jnp.sum(
            low.astype(jnp.float32).reshape(tok_rows // 8, 8, width), axis=0
        )
        return carry

    lax.fori_loop(0, blocks, pack, 0)
    direction = sibling - member

    def project_back(block):
        hidden_part[block] = times_transposed(packed_grad[block], qkv_ref[...]).astype(
            jnp.bfloat16
        )

    def far(step, carry):
        project_back(opposite - step * direction)
        return carry

    def near(step, carry):
        project_back(sibling - step * direction)
        return carry

    lax.fori_loop(0, 2, far, 0)
    reduce_rows.first.start()
    reduce_rows.send_pair()
    lax.fori_loop(0, 2, near, 0)
    reduce_rows.second.start()
    weight_grad(hidden_rows, packed_grad, qkv_part)
    for unit in units[5:]:
        unit.start()
    bias_own[2] = jnp.zeros_like(bias_own[2])
    bias_own[2] = bias_ref[...]
    bias_own[2, 2:3] = jnp.sum(bias_own[0], axis=0, keepdims=True)
    bias_own[2, 3:4] = jnp.sum(bias_own[1], axis=0, keepdims=True)
    bias_copies = spread(1, lambda other: bias_own.at[2], bias_all)
    bias_all[row] = bias_own[2]
    units[4].send_pair()
    slot_sums[...] = jnp.zeros_like(slot_sums)
    reduce_ffn.settle()

    def rows_out(block, carry):
        part = pl.ds(pl.multiple_of(block * 128, 128), 128)
        ffn = reduce_ffn.rows(part) + bias_rows[2:3]
        place = pl.multiple_of(member * tok_rows + block * 128, 128)
        gate = picked(vectors_ref, 5, segments_ref[pl.ds(place, 128)], model_width)
        block_out[part] = (block_ref[part] + gate * ffn).astype(jnp.bfloat16)
        slot_sums[2] += jnp.dot(
            slot_hot(segment_row, place),
            cotangent_ref[part].astype(jnp.float32) * ffn,
            precision=HIGH,
            preferred_element_type=jnp.float32,
        )
        return carry

    lax.fori_loop(0, tok_rows // 128, rows_out, 0)
    units[0].finish()
    units[1].finish()
    units[5].send_pair()
    reduce_rows.settle()

    def rows_back(block, carry):
        part = pl.ds(pl.multiple_of(block * 128, 128), 128)
        grad = reduce_rows.rows(part)
        normed, factor = centre_rows(patches_ref[part].astype(jnp.float32))
        place = pl.multiple_of(member * tok_rows + block * 128, 128)
        weighted = grad * (
            1.0 + picked(vectors_ref, 1, segments_ref[pl.ds(place, 128)], model_width)
        )
        patches_grad[part] = after_ref[part] + factor * (
            weighted
            - jnp.mean(weighted, axis=1, keepdims=True)
            - normed * jnp.mean(weighted * normed, axis=1, keepdims=True)
        )
        hot = slot_hot(segment_row, place)
        slot_sums[0] += jnp.dot(hot, grad, precision=HIGH, preferred_element_type=jnp.float32)
        slot_sums[1] += jnp.dot(
            hot, grad * normed, precision=HIGH, preferred_element_type=jnp.float32
        )
        return carry

    lax.fori_loop(0, tok_rows // 128, rows_back, 0)
    ada_width = ada_ref.shape[1]
    fine = ada_width // 3
    for unit in range(3 * ROW_PARTS):
        part_index, within = divmod(unit * fine, model_width)
        span = slice(within, within + fine)
        if part_index < 2:
            source = slot_sums[part_index, :, span]
        elif part_index == 5:
            source = slot_sums[2, :, span]
        else:
            source = sums_ref[part_index - 2, :, span]
        mods_own[unit // 3, :, unit % 3 * fine : (unit % 3 + 1) * fine] = source
    beside = to_head(mods_own, mods_sibling, pair_send.at[0], pair_recv.at[0], sibling)
    beside.start()
    units[6].send_pair()
    beside.wait()
    mods_pair[...] = (mods_own[...] + mods_sibling[...]).astype(jnp.bfloat16)
    across = to_head(mods_pair, mods_partner, pair_send.at[1], pair_recv.at[1], partner)
    across.start()
    units[2].finish()
    units[3].finish()
    settle(bias_copies)
    bias_sum[...] = jnp.sum(bias_all[...], axis=0)
    across.wait()
    mods_low[...] = (
        mods_pair[...].astype(jnp.float32) + mods_partner[...].astype(jnp.float32)
    ).astype(jnp.bfloat16)
    copies = spread(0, lambda other: mods_low.at[other], mods_cols)
    mods_cols[row] = mods_low[row]
    units[7].send_pair()
    units[4].finish()
    settle(copies)
    slots = ROW_PARTS * SLOT_ROWS
    cols = mods_cols[...].astype(jnp.float32).reshape(slots, ada_width)
    low = cols.astype(jnp.bfloat16)
    condition = condition_ref[...].reshape(slots, condition_ref.shape[2])
    bent = 1.0 / (1.0 + jnp.exp(-condition))
    silu_part[...] = times_transposed(low, ada_ref[...]).reshape(silu_part.shape)
    copies = spread(2, lambda other: silu_part.at[other], silu_in)
    silu_in[row] = silu_part[row]
    ada_grad[...] = contract_rows((condition * bent).astype(jnp.bfloat16), low)
    ada_bias[...] = jnp.broadcast_to(jnp.sum(cols, axis=0, keepdims=True), ada_bias.shape)
    settle(copies)
    summed = jnp.sum(silu_in[...], axis=0)
    silu_all[row] = summed
    silu_part[row] = summed
    copies = spread(3, lambda other: silu_part.at[row], silu_all)
    units[5].finish()
    units[6].finish()
    units[7].finish()
    settle(copies)
    grad_condition = silu_all[...].reshape(slots, silu_all.shape[2]) * (
        bent * (1.0 + condition * (1.0 - bent))
    )
    for target, hot in zip((time_grad, class_grad), table_hots(ids_all, time_grad.shape[1])):
        target[...] = contract_rows_exact(grad_condition, hot.astype(jnp.float32))
    reduce_rows.finish()
    reduce_ffn.finish()


def rear(*args):
    shape = jax.ShapeDtypeStruct
    grads, w_out, totals, grad_w_fc2, w_qkv, biases, ids_all, w_ada = (
        args[place] for place in (1, 2, 3, 6, 9, 11, 17, 18)
    )
    blocks, tok_rows, model_width = grads.shape
    width = w_qkv.shape[1]
    head_local = totals.shape[0]
    seq_len = blocks * tok_rows
    third, hidden_width = grad_w_fc2.shape[2:]
    width_part = 3 * third
    out_width = w_out.shape[1]
    depth, ada_width = w_ada.shape
    table_rows = ids_all.shape[2]
    low = jnp.bfloat16
    full = jnp.float32
    heads_wide = pltpu.VMEM((head_local, seq_len, HEAD_LANES), full)
    slotted = (ROW_PARTS, SLOT_ROWS)
    wide = pltpu.VMEM(slotted + (ada_width,), full)
    wide_low = pltpu.VMEM(slotted + (ada_width,), low)
    narrow = pltpu.VMEM(slotted + (depth,), full)
    sizes = (
        [(third, hidden_width)] * 4 + [(width_part, out_width)] + [(third, width)] * 3
    )
    return pl.pallas_call(
        rear_kernel,
        out_shape=[
            shape((tok_rows, model_width), low),
            shape((tok_rows, model_width), full),
            shape((depth, table_rows), full),
            shape((depth, table_rows), full),
            shape((depth, ada_width), full),
            shape((SLOT_ROWS, ada_width), full),
            shape((width_part, hidden_width), full),
            shape((width_part, hidden_width), full),
            shape((width_part, width), full),
            shape((width_part, out_width), full),
            shape(biases.shape, full),
        ],
        in_specs=[VMEM_SPEC] * 25,
        out_specs=[VMEM_SPEC] * 11,
        scratch_shapes=[
            pltpu.VMEM((head_local, seq_len, HEAD_LANES), low),
            pltpu.VMEM((head_local, HEAD_LANES, seq_len), low),
            heads_wide,
            heads_wide,
            pltpu.VMEM((seq_len, tok_rows), full),
            pltpu.VMEM((tok_rows, width), full),
            pltpu.VMEM((blocks, tok_rows, width), low),
            pltpu.VMEM((blocks, tok_rows, model_width), low),
            pltpu.VMEM((4, 2, width_part, width), low),
            pltpu.VMEM((4, 2, width_part, out_width), low),
            pltpu.VMEM((3,) + biases.shape, full),
        ]
        + [
            pltpu.VMEM((2, tok_rows, model_width), low),
            pltpu.VMEM((tok_rows, model_width), low),
            pltpu.VMEM((tok_rows, model_width), low),
        ]
        * 2
        + [pltpu.VMEM((3, SLOT_ROWS, model_width), full)]
        + [wide] * 2
        + [wide_low] * 4
        + [pltpu.VMEM((ROW_PARTS,) + biases.shape, full)]
        + [narrow] * 3
        + [
            DMA((4, 7)),
            DMA((4, 7)),
            DMA((2,)),
            DMA((2,)),
            DMA((2, 3)),
            DMA((2, 3)),
        ]
        + reduce_scratch(sizes),
        compiler_params=pltpu.CompilerParams(
            collective_id=1, has_side_effects=True, vmem_limit_bytes=67_000_000
        ),
        name="rear",
    )(*args)


def shards_linked(
    patches,
    time_table,
    class_table,
    w_ada,
    b_ada,
    w_qkv,
    b_qv,
    w_out,
    b_out,
    w_fc1,
    b_fc1,
    w_fc2,
    b_fc2,
    image_lengths,
    segment_ids,
    bucket_ids,
    class_labels,
    cotangent,
):
    model_width = patches.shape[1]
    slot_count = image_lengths.shape[1]
    head_local = b_qv.shape[0]
    head_size = b_qv.shape[1] // 2
    qkv_full, patches_full, condition, mods, ids_all = front(
        bucket_ids, class_labels, time_table.T, class_table.T, w_ada, patches, w_qkv
    )
    qkv_cols = qkv_full.reshape(model_width, w_qkv.shape[1])
    biases = jnp.stack([b_out, b_fc1, b_fc2]).astype(jnp.float32)
    (
        segments,
        vectors,
        rows_one,
        parts,
        totals,
        mixed_rows,
        out_cols,
        ffn_part,
        after_attn,
        grad_after,
        attn_rows_grad,
        sums,
        bias_sums,
        grad_w_fc2,
        grad_w_fc1,
        fc2_head,
        fc2_neck,
    ) = core(
        slot_count,
        head_size,
        patches_full,
        qkv_cols,
        w_out,
        w_fc1,
        w_fc2,
        cotangent,
        patches,
        segment_ids,
        mods,
        b_ada.astype(jnp.float32).reshape(6, model_width),
        biases,
        b_qv.astype(jnp.float32),
    )
    (
        block_out,
        grad_patches,
        grad_time,
        grad_class,
        grad_w_ada,
        grad_b_ada,
        grad_w_fc2,
        grad_w_fc1,
        grad_w_qkv,
        grad_w_out,
        bias_all,
    ) = rear(
        parts,
        attn_rows_grad,
        out_cols,
        totals,
        segment_ids,
        segments,
        grad_w_fc2,
        grad_w_fc1,
        rows_one,
        qkv_cols,
        mixed_rows,
        bias_sums,
        patches,
        grad_after,
        vectors,
        sums,
        condition,
        ids_all,
        w_ada,
        ffn_part,
        after_attn,
        cotangent,
        biases,
        fc2_head,
        fc2_neck,
    )
    grad_time = grad_time.T
    grad_class = grad_class.T
    grad_b_ada = grad_b_ada[0]
    bias_rows = model_width // lax.axis_size("rows")
    row_start = lax.axis_index("rows") * bias_rows
    grad_b_fc1 = bias_all[0]
    grad_b_fc2 = lax.dynamic_slice_in_dim(bias_all[1], row_start, bias_rows)
    grad_b_out = lax.dynamic_slice_in_dim(bias_all[2], row_start, bias_rows)
    bias_terms = bias_all[3, : head_local * 3 * head_size].reshape(head_local, 3, head_size)
    grad_b_qv = jnp.concatenate([bias_terms[:, 0], bias_terms[:, 2]], axis=1)
    return (
        block_out,
        grad_patches,
        grad_time,
        grad_class,
        grad_w_ada,
        grad_b_ada,
        grad_w_qkv,
        grad_b_qv,
        grad_w_out,
        grad_b_out,
        grad_w_fc1,
        grad_b_fc1,
        grad_w_fc2,
        grad_b_fc2,
    )


def solution(mesh):
    placed = (
        P(("rows", "heads"), None),
        P("rows", "heads"),
        P("rows", "heads"),
        P("heads", "rows"),
        P(),
        P("rows", "heads"),
        P("heads", None),
        P("rows", "heads"),
        P(),
        P("rows", "heads"),
        P("heads"),
        P("rows", "heads"),
        P(),
        P("rows", None),
        P("rows", None),
        P("rows", None),
        P("rows", None),
        P(("rows", "heads"), None),
    )
    linked = mesh.shape["rows"] == ROW_PARTS and mesh.shape["heads"] == HEAD_PARTS
    return jax.shard_map(
        shards_linked if linked else shards_plain,
        mesh=mesh,
        in_specs=placed,
        out_specs=(
            P(("rows", "heads"), None),
            P(("rows", "heads"), None),
            P("rows", "heads"),
            P("rows", "heads"),
            P("heads", "rows"),
            P("rows"),
            P("rows", "heads"),
            P("heads", None),
            P("rows", "heads"),
            P("rows"),
            P("rows", "heads"),
            P("heads"),
            P("rows", "heads"),
            P("rows"),
        ),
        check_vma=False,
    )
```

```python
import functools
import math

import jax
import jax.numpy as jnp
from jax import lax
from jax.experimental import pallas as pl
from jax.experimental.pallas import tpu as pltpu
from jax.sharding import PartitionSpec as P

EPSILON = 1e-06
MASKED = -1e30
HIGH = lax.Precision.HIGHEST
TANH_COEFF = 0.7978845608028654
BLOCK_LIMIT = 512


def layer_norm(values):
    average = jnp.mean(values, axis=-1, keepdims=True)
    centred = values - average
    variance = jnp.mean(centred * centred, axis=-1, keepdims=True)
    return centred * lax.rsqrt(variance + EPSILON)


def gelu_tanh(values):
    return (
        0.5 * values * (1.0 + jnp.tanh(TANH_COEFF * (values + 0.044715 * values * values * values)))
    )


def silu_plain(values):
    return values / (1.0 + jnp.exp(-values))


def modulate(values, shift_term, scale_term):
    return layer_norm(values) * (1.0 + scale_term) + shift_term


def contract_rows(left_matrix, right_matrix):
    return lax.dot_general(
        left_matrix, right_matrix, (((0,), (0,)), ((), ())), preferred_element_type=jnp.float32
    )


def contract_rows_exact(left_matrix, right_matrix):
    return lax.dot_general(
        left_matrix,
        right_matrix,
        (((0,), (0,)), ((), ())),
        precision=HIGH,
        preferred_element_type=jnp.float32,
    )


def times_transposed(left_matrix, right_matrix):
    return lax.dot_general(
        left_matrix, right_matrix, (((1,), (1,)), ((), ())), preferred_element_type=jnp.float32
    )


def gather_weights(w_qkv, w_out, w_fc1, w_fc2):
    return (
        lax.all_gather(w_qkv, "rows", axis=0, tiled=True),
        lax.all_gather(w_out, "rows", axis=0, tiled=True),
        lax.all_gather(w_fc1, "rows", axis=0, tiled=True),
        lax.all_gather(w_fc2, "rows", axis=0, tiled=True),
    )


def shards_plain(
    patches,
    time_table,
    class_table,
    w_ada,
    b_ada,
    w_qkv,
    b_qv,
    w_out,
    b_out,
    w_fc1,
    b_fc1,
    w_fc2,
    b_fc2,
    image_lengths,
    segment_ids,
    bucket_ids,
    class_labels,
    cotangent,
):
    head_parts = lax.axis_size("heads")
    member = lax.axis_index("heads")
    tok_rows = patches.shape[0]
    model_width = patches.shape[1]
    seq_count = segment_ids.shape[0]
    seq_len = segment_ids.shape[1]
    slot_count = image_lengths.shape[1]
    image_count = seq_count * slot_count
    group_rows = tok_rows * head_parts
    head_local = b_qv.shape[0]
    head_size = b_qv.shape[1] // 2
    block_rows = min(BLOCK_LIMIT, seq_len)
    scale_factor = 1.0 / math.sqrt(head_size)
    row_parts = lax.axis_size("rows")
    table_rows = time_table.shape[0]
    ada_width = w_ada.shape[1]
    qkv_cols, out_cols, fc1_cols, fc2_cols = gather_weights(w_qkv, w_out, w_fc1, w_fc2)
    ids_all = lax.all_gather(
        jnp.concatenate([bucket_ids, class_labels], axis=1), "rows", axis=0, tiled=True
    )
    every_slot = row_parts * image_count
    table_places = lax.axis_index("rows") * table_rows + jnp.arange(table_rows, dtype=jnp.int32)
    bucket_hot = (
        ids_all[:, :slot_count].reshape(every_slot)[:, None] == table_places[None, :]
    ).astype(jnp.bfloat16)
    label_hot = (
        ids_all[:, slot_count:].reshape(every_slot)[:, None] == table_places[None, :]
    ).astype(jnp.bfloat16)
    condition = lax.psum(
        jnp.dot(bucket_hot, time_table, preferred_element_type=jnp.float32)
        + jnp.dot(label_hot, class_table, preferred_element_type=jnp.float32),
        "rows",
    )
    silu_value, silu_pull = jax.vjp(silu_plain, condition)
    silu_low = silu_value.astype(jnp.bfloat16)
    mods_part = jnp.dot(silu_low, w_ada, preferred_element_type=jnp.float32)
    mods_cols = lax.psum(mods_part, "heads").reshape(row_parts, image_count, ada_width)
    mods_own = lax.all_to_all(mods_cols, "rows", split_axis=0, concat_axis=0, tiled=True)
    mods_all = mods_own.transpose(1, 0, 2).reshape(
        image_count, row_parts * ada_width
    ) + b_ada.astype(jnp.float32)
    positions = member * tok_rows + jnp.arange(tok_rows, dtype=jnp.int32)
    own_segments = lax.dynamic_slice_in_dim(
        segment_ids.reshape(seq_count * seq_len), member * tok_rows, tok_rows
    )
    token_image = positions // seq_len * slot_count + own_segments
    token_hot = (token_image[:, None] == jnp.arange(image_count, dtype=jnp.int32)[None, :]).astype(
        jnp.float32
    )
    token_mods = [
        jnp.dot(
            token_hot,
            mods_all[:, part_index * model_width : (part_index + 1) * model_width],
            precision=HIGH,
        )
        for part_index in range(6)
    ]
    shift_attn, scale_attn, gate_attn, shift_mlp, scale_mlp, gate_mlp = token_mods
    inputs = patches.astype(jnp.float32)
    first_value, first_pull = jax.vjp(modulate, inputs, shift_attn, scale_attn)
    hidden_one = first_value.astype(jnp.bfloat16)
    rows_one = lax.all_gather(hidden_one, "heads", axis=0, tiled=True)
    zero_bias = jnp.zeros((head_local, head_size), b_qv.dtype)
    qkv_bias = (
        jnp.concatenate([b_qv[:, :head_size], zero_bias, b_qv[:, head_size:]], axis=1)
        .reshape(head_local * 3 * head_size)
        .astype(jnp.float32)
    )
    projected = (jnp.dot(rows_one, qkv_cols, preferred_element_type=jnp.float32) + qkv_bias).astype(
        jnp.bfloat16
    )
    seq_qkv = projected.reshape(seq_count, seq_len, head_local, 3, head_size)
    slot_ends = jnp.cumsum(image_lengths, axis=1)
    places = jnp.arange(seq_len, dtype=jnp.int32)
    image_of = jnp.sum((places[None, :, None] >= slot_ends[:, None, :]).astype(jnp.int32), axis=2)

    def block_scores(query_rows, key_rows, image_rows, image_cols):
        scores = (
            jnp.einsum("qhd,khd->hqk", query_rows, key_rows, preferred_element_type=jnp.float32)
            * scale_factor
        )
        return jnp.where((image_rows[:, None] == image_cols[None, :])[None], scores, MASKED)

    def attend_forward(pieces):
        seq_block, seq_image = pieces
        key_rows = seq_block[:, :, 1]
        value_rows = seq_block[:, :, 2]
        outputs = []
        totals = []
        for row_start in range(0, seq_len, block_rows):
            stop_row = row_start + block_rows
            query_rows = seq_block[row_start:stop_row, :, 0]
            scores = block_scores(query_rows, key_rows, seq_image[row_start:stop_row], seq_image)
            row_peak = jnp.max(scores, axis=2, keepdims=True)
            raised = jnp.exp(scores - row_peak)
            row_total = jnp.sum(raised, axis=2, keepdims=True)
            soft_low = (raised / row_total).astype(jnp.bfloat16)
            outputs.append(
                jnp.einsum(
                    "hqk,khd->qhd", soft_low, value_rows, preferred_element_type=jnp.float32
                ).astype(jnp.bfloat16)
            )
            totals.append((row_peak + jnp.log(row_total))[:, :, 0])
        return (jnp.concatenate(outputs, axis=0), jnp.concatenate(totals, axis=1))

    mixed, log_totals = lax.map(attend_forward, (seq_qkv, image_of))
    mixed_rows = mixed.reshape(group_rows, head_local * head_size)
    attn_out = lax.psum_scatter(
        times_transposed(
            lax.slice_in_dim(mixed_rows, 0, tok_rows * lax.axis_size("heads"), axis=0), out_cols
        ).astype(jnp.bfloat16),
        "heads",
        scatter_dimension=0,
        tiled=True,
    ).astype(jnp.float32) + b_out.astype(jnp.float32)
    after_attn = inputs + gate_attn * attn_out
    second_value, second_pull = jax.vjp(modulate, after_attn, shift_mlp, scale_mlp)
    hidden_two = second_value.astype(jnp.bfloat16)
    rows_two = lax.all_gather(hidden_two, "heads", axis=0, tiled=True)
    inner = jnp.dot(rows_two, fc1_cols, preferred_element_type=jnp.float32) + b_fc1.astype(
        jnp.float32
    )
    gelu_value, gelu_pull = jax.vjp(gelu_tanh, inner)
    active = gelu_value.astype(jnp.bfloat16)
    ffn_out = lax.psum_scatter(
        times_transposed(
            lax.slice_in_dim(active, 0, tok_rows * lax.axis_size("heads"), axis=0), fc2_cols
        ).astype(jnp.bfloat16),
        "heads",
        scatter_dimension=0,
        tiled=True,
    ).astype(jnp.float32) + b_fc2.astype(jnp.float32)
    block_out = (after_attn + gate_mlp * ffn_out).astype(jnp.bfloat16)
    upstream = cotangent.astype(jnp.float32)
    grad_ffn = (gate_mlp * upstream).astype(jnp.bfloat16)
    ffn_rows = lax.all_gather(grad_ffn, "heads", axis=0, tiled=True)
    grad_w_fc2 = contract_rows(ffn_rows, active)
    grad_b_fc2 = jnp.sum(ffn_rows, axis=0, dtype=jnp.float32)
    grad_active = jnp.dot(ffn_rows, fc2_cols, preferred_element_type=jnp.float32)
    grad_inner = gelu_pull(grad_active)[0].astype(jnp.bfloat16)
    grad_w_fc1 = contract_rows(rows_two, grad_inner)
    grad_b_fc1 = jnp.sum(grad_inner, axis=0, dtype=jnp.float32)
    grad_hidden_two = lax.psum_scatter(
        times_transposed(
            lax.slice_in_dim(grad_inner, 0, tok_rows * lax.axis_size("heads"), axis=0), fc1_cols
        ).astype(jnp.bfloat16),
        "heads",
        scatter_dimension=0,
        tiled=True,
    ).astype(jnp.float32)
    grad_after, grad_shift_mlp, grad_scale_mlp = second_pull(grad_hidden_two)
    grad_after = grad_after + upstream
    grad_gate_mlp = upstream * ffn_out
    grad_gate_attn = grad_after * attn_out
    grad_attn = (gate_attn * grad_after).astype(jnp.bfloat16)
    attn_rows_grad = lax.all_gather(grad_attn, "heads", axis=0, tiled=True)
    grad_w_out = contract_rows(attn_rows_grad, mixed_rows)
    grad_b_out = jnp.sum(attn_rows_grad, axis=0, dtype=jnp.float32)
    grad_mixed = jnp.dot(attn_rows_grad, out_cols, preferred_element_type=jnp.float32).astype(
        jnp.bfloat16
    )
    grad_seq = grad_mixed.reshape(seq_count, seq_len, head_local, head_size)

    def attend_backward(pieces):
        seq_block, seq_image, seq_grad, seq_totals = pieces
        key_rows = seq_block[:, :, 1]
        value_rows = seq_block[:, :, 2]
        grad_keys = jnp.zeros(key_rows.shape, jnp.float32)
        grad_values = jnp.zeros(value_rows.shape, jnp.float32)
        grad_queries = []
        for row_start in range(0, seq_len, block_rows):
            stop_row = row_start + block_rows
            query_rows = seq_block[row_start:stop_row, :, 0]
            grad_rows = seq_grad[row_start:stop_row]
            scores = block_scores(query_rows, key_rows, seq_image[row_start:stop_row], seq_image)
            soft_probs = jnp.exp(scores - seq_totals[:, row_start:stop_row, None])
            grad_probs = jnp.einsum(
                "qhd,khd->hqk", grad_rows, value_rows, preferred_element_type=jnp.float32
            )
            inner_sum = jnp.sum(soft_probs * grad_probs, axis=2, keepdims=True)
            grad_scores = (soft_probs * (grad_probs - inner_sum)).astype(jnp.bfloat16)
            grad_queries.append(
                jnp.einsum(
                    "hqk,khd->qhd", grad_scores, key_rows, preferred_element_type=jnp.float32
                )
                * scale_factor
            )
            grad_keys = (
                grad_keys
                + jnp.einsum(
                    "hqk,qhd->khd", grad_scores, query_rows, preferred_element_type=jnp.float32
                )
                * scale_factor
            )
            grad_values = grad_values + jnp.einsum(
                "hqk,qhd->khd",
                soft_probs.astype(jnp.bfloat16),
                grad_rows,
                preferred_element_type=jnp.float32,
            )
        stacked = jnp.stack([jnp.concatenate(grad_queries, axis=0), grad_keys, grad_values], axis=2)
        return stacked.astype(jnp.bfloat16)

    grad_qkv = lax.map(attend_backward, (seq_qkv, image_of, grad_seq, log_totals)).reshape(
        group_rows, head_local * 3 * head_size
    )
    grad_w_qkv = contract_rows(rows_one, grad_qkv)
    bias_terms = jnp.sum(grad_qkv, axis=0, dtype=jnp.float32).reshape(head_local, 3, head_size)
    grad_b_qv = jnp.concatenate([bias_terms[:, 0], bias_terms[:, 2]], axis=1)
    grad_hidden_one = lax.psum_scatter(
        times_transposed(
            lax.slice_in_dim(grad_qkv, 0, tok_rows * lax.axis_size("heads"), axis=0), qkv_cols
        ).astype(jnp.bfloat16),
        "heads",
        scatter_dimension=0,
        tiled=True,
    ).astype(jnp.float32)
    grad_inputs, grad_shift_attn, grad_scale_attn = first_pull(grad_hidden_one)
    grad_patches = grad_inputs + grad_after
    token_grads = (
        grad_shift_attn,
        grad_scale_attn,
        grad_gate_attn,
        grad_shift_mlp,
        grad_scale_mlp,
        grad_gate_mlp,
    )
    mods_grad_part = jnp.concatenate(
        [contract_rows_exact(token_hot, grad_term) for grad_term in token_grads], axis=1
    )
    grad_mods = lax.psum(mods_grad_part.astype(jnp.bfloat16), "heads")
    grad_cols = lax.all_to_all(
        grad_mods.reshape(image_count, row_parts, ada_width).transpose(1, 0, 2),
        "rows",
        split_axis=0,
        concat_axis=0,
        tiled=True,
    ).reshape(every_slot, ada_width)
    grad_w_ada = contract_rows(silu_low, grad_cols)
    grad_b_ada = jnp.sum(grad_cols, axis=0, dtype=jnp.float32)
    grad_silu = lax.psum(times_transposed(grad_cols, w_ada), "rows")
    grad_condition = silu_pull(grad_silu)[0]
    grad_time = contract_rows_exact(bucket_hot.astype(jnp.float32), grad_condition)
    grad_class = contract_rows_exact(label_hot.astype(jnp.float32), grad_condition)

    def row_reduced(partial):
        return lax.psum_scatter(
            partial.astype(jnp.bfloat16), "rows", scatter_dimension=0, tiled=True
        ).astype(jnp.float32)

    grad_w_qkv, grad_w_out, grad_w_fc1, grad_w_fc2 = (
        row_reduced(grad_w_qkv),
        row_reduced(grad_w_out),
        row_reduced(grad_w_fc1),
        row_reduced(grad_w_fc2),
    )
    bias_sizes = (grad_b_qv.size, grad_b_fc1.size, grad_b_out.size, grad_b_fc2.size)
    bias_all = lax.psum(
        jnp.concatenate([grad_b_qv.reshape(-1), grad_b_fc1, grad_b_out, grad_b_fc2]), "rows"
    )
    edges = [sum(bias_sizes[:step]) for step in range(5)]
    bias_rows = model_width // row_parts
    row_start = lax.axis_index("rows") * bias_rows
    grad_b_qv = bias_all[edges[0] : edges[1]].reshape(grad_b_qv.shape)
    grad_b_fc1 = bias_all[edges[1] : edges[2]]
    grad_b_out = lax.dynamic_slice_in_dim(bias_all[edges[2] : edges[3]], row_start, bias_rows)
    grad_b_fc2 = lax.dynamic_slice_in_dim(bias_all[edges[3] : edges[4]], row_start, bias_rows)
    return (
        block_out,
        grad_patches,
        grad_time,
        grad_class,
        grad_w_ada,
        grad_b_ada,
        grad_w_qkv,
        grad_b_qv,
        grad_w_out,
        grad_b_out,
        grad_w_fc1,
        grad_b_fc1,
        grad_w_fc2,
        grad_b_fc2,
    )


MESH = pl.DeviceIdType.MESH
ROW_PARTS = 8
HEAD_PARTS = 4
SLOT_ROWS = 8
VMEM_SPEC = pl.BlockSpec(memory_space=pltpu.VMEM)
ANY_SPEC = pl.BlockSpec(memory_space=pl.ANY)
DMA = pltpu.SemaphoreType.DMA
GRANT = 60 * 1024 * 1024


def places():
    row = lax.axis_index("rows")
    member = lax.axis_index("heads")
    sibling = member + 1 - 2 * lax.rem(member, 2)
    partner = lax.rem(member + 2, HEAD_PARTS)
    opposite = lax.rem(sibling + 2, HEAD_PARTS)
    return row, member, sibling, partner, opposite


def greet(row_steps, head_members):
    barrier = pltpu.get_barrier_semaphore()
    row = lax.axis_index("rows")
    for step in row_steps:
        pl.semaphore_signal(
            barrier,
            inc=1,
            device_id={"rows": lax.rem(row + step, ROW_PARTS)},
            device_id_type=MESH,
        )
    for other in head_members:
        pl.semaphore_signal(barrier, inc=1, device_id={"heads": other}, device_id_type=MESH)
    pl.semaphore_wait(barrier, len(row_steps) + len(head_members))


def to_row(source, target, send, recv, row):
    return pltpu.make_async_remote_copy(
        src_ref=source,
        dst_ref=target,
        send_sem=send,
        recv_sem=recv,
        device_id={"rows": row},
        device_id_type=MESH,
    )


def to_head(source, target, send, recv, member):
    return pltpu.make_async_remote_copy(
        src_ref=source,
        dst_ref=target,
        send_sem=send,
        recv_sem=recv,
        device_id={"heads": member},
        device_id_type=MESH,
    )


class RowGather:
    def __init__(self, shard, full, sends, recvs, local_sem, chunks):
        self.row = lax.axis_index("rows")
        self.level = self.row // 2
        self.side = lax.rem(self.row, 2)
        self.mate = self.row + 1 - 2 * self.side
        above = lax.rem(self.level + 1, 4) * 2 + self.side
        size = shard.shape[0] // chunks
        self.own = pltpu.make_async_copy(shard, full.at[self.row], local_sem)
        self.straight = []
        self.across = []
        for chunk in range(chunks):
            part = pl.ds(chunk * size, size)
            straight = []
            across = []
            for step in range(4):
                origin = lax.rem(self.level + 4 - step, 4) * 2 + self.side
                source = shard.at[part] if step == 0 else full.at[origin, part]
                target = full.at[origin, part]
                across.append(
                    to_row(
                        source,
                        target,
                        sends.at[chunk, 3 + step],
                        recvs.at[chunk, 3 + step],
                        self.mate,
                    )
                )
                if step < 3:
                    straight.append(
                        to_row(
                            source, target, sends.at[chunk, step], recvs.at[chunk, step], above
                        )
                    )
            self.straight.append(straight)
            self.across.append(across)

    def start(self, chunk):
        self.straight[chunk][0].start()
        self.across[chunk][0].start()

    def hop(self, chunk, step):
        self.straight[chunk][step].wait_recv()
        if step < 2:
            self.straight[chunk][step + 1].start()
        self.across[chunk][step + 1].start()

    def finish(self):
        self.own.wait()
        for straight, across in zip(self.straight, self.across):
            for copy in straight:
                copy.wait_send()
            for copy in across:
                copy.wait()


class HeadGather:
    def __init__(self, block, full, sends, recvs, local_sem):
        row, member, sibling, partner, opposite = places()
        self.own = None
        if block is None:
            block = full.at[member]
        else:
            self.own = pltpu.make_async_copy(block, full.at[member], local_sem)
        self.beside = to_head(block, full.at[member], sends.at[0], recvs.at[0], sibling)
        self.across = to_head(block, full.at[member], sends.at[1], recvs.at[1], partner)
        self.onward = to_head(
            full.at[partner], full.at[partner], sends.at[2], recvs.at[2], sibling
        )

    def start(self):
        self.across.start()
        self.beside.start()
        if self.own is not None:
            self.own.start()

    def wait_sibling(self):
        self.beside.wait_recv()

    def wait_partner(self):
        self.across.wait_recv()
        self.onward.start()

    def wait_opposite(self):
        self.onward.wait_recv()

    def finish(self):
        if self.own is not None:
            self.own.wait()
        self.beside.wait_send()
        self.across.wait_send()
        self.onward.wait_send()


def front_kernel(
    bucket_ref,
    label_ref,
    time_ref,
    class_ref,
    ada_ref,
    patches_ref,
    qkv_ref,
    qkv_full,
    patches_full,
    cond_all,
    mods_ref,
    ids_all,
    ids_own,
    cond_part,
    cond_in,
    mods_part,
    mods_in,
    mods_sibling,
    mods_pair,
    mods_partner,
    small_send,
    small_recv,
    pair_send,
    pair_recv,
    head_send,
    head_recv,
    qkv_send,
    qkv_recv,
    local_sems,
):
    row, member, sibling, partner, opposite = places()
    greet(range(1, ROW_PARTS), (sibling, partner))
    others = [(step, lax.rem(row + step, ROW_PARTS)) for step in range(1, ROW_PARTS)]

    def spread(stage, source_of, target):
        copies = []
        for step, other in others:
            copy = to_row(
                source_of(other),
                target.at[row],
                small_send.at[stage, step - 1],
                small_recv.at[stage, step - 1],
                other,
            )
            copy.start()
            copies.append(copy)
        return copies

    def settle(copies):
        for copy in copies:
            copy.wait()

    table_rows = time_ref.shape[1]
    slots = ROW_PARTS * SLOT_ROWS
    ids_own[...] = jnp.full_like(ids_own, -1)
    for start, chosen in ((0, bucket_ref), (SLOT_ROWS, label_ref)):
        for slot in range(chosen.shape[1]):
            ids_own[start + slot : start + slot + 1] = jnp.broadcast_to(
                chosen[0:1, slot : slot + 1], (1, table_rows)
            )
    ids_copies = spread(0, lambda other: ids_own, ids_all)
    gather_qkv = RowGather(qkv_ref, qkv_full, qkv_send, qkv_recv, local_sems.at[0], 3)
    gather_patches = HeadGather(patches_ref, patches_full, head_send, head_recv, local_sems.at[1])
    gather_patches.start()
    gather_qkv.own.start()
    gather_qkv.start(0)
    ids_all[row] = ids_own[...]
    settle(ids_copies)
    bucket_hot, label_hot = (hot.astype(jnp.bfloat16) for hot in table_hots(ids_all, table_rows))
    found = times_transposed(bucket_hot, time_ref[...]) + times_transposed(
        label_hot, class_ref[...]
    )
    cond_part[...] = found.reshape(cond_part.shape)
    copies = spread(1, lambda other: cond_part.at[other], cond_in)
    gather_qkv.start(1)
    cond_in[row] = cond_part[row]
    gather_qkv.hop(0, 0)
    settle(copies)
    condition = jnp.sum(cond_in[...], axis=0)
    cond_all[row] = condition
    cond_part[row] = condition
    copies = spread(2, lambda other: cond_part.at[row], cond_all)
    gather_qkv.start(2)
    gather_qkv.hop(1, 0)
    gather_qkv.hop(0, 1)
    settle(copies)
    every = cond_all[...].reshape(slots, cond_all.shape[2])
    silu_low = (every / (1.0 + jnp.exp(-every))).astype(jnp.bfloat16)
    mods_part[...] = jnp.dot(
        silu_low, ada_ref[...], preferred_element_type=jnp.float32
    ).reshape(mods_part.shape)
    copies = spread(3, lambda other: mods_part.at[other], mods_in)
    mods_in[row] = mods_part[row]
    gather_qkv.hop(2, 0)
    gather_qkv.hop(1, 1)
    gather_qkv.hop(0, 2)
    settle(copies)
    beside = to_head(mods_in, mods_sibling, pair_send.at[0], pair_recv.at[0], sibling)
    beside.start()
    gather_patches.wait_sibling()
    beside.wait()
    mods_pair[...] = mods_in[...] + mods_sibling[...]
    across = to_head(mods_pair, mods_partner, pair_send.at[1], pair_recv.at[1], partner)
    across.start()
    gather_patches.wait_partner()
    gather_qkv.hop(2, 1)
    gather_qkv.hop(1, 2)
    across.wait()
    mods_ref[...] = mods_pair[...] + mods_partner[...]
    gather_qkv.hop(2, 2)
    gather_patches.wait_opposite()
    gather_patches.finish()
    gather_qkv.finish()


def front(bucket_ids, class_labels, time_columns, class_columns, w_ada, patches, w_qkv):
    depth, ada_width = w_ada.shape
    shape = jax.ShapeDtypeStruct
    slotted = (ROW_PARTS, SLOT_ROWS)
    wide = pltpu.VMEM(slotted + (ada_width,), jnp.float32)
    narrow = pltpu.VMEM(slotted + (depth,), jnp.float32)
    return pl.pallas_call(
        front_kernel,
        out_shape=(
            shape((ROW_PARTS,) + w_qkv.shape, jnp.bfloat16),
            shape((HEAD_PARTS,) + patches.shape, jnp.bfloat16),
            shape(slotted + (depth,), jnp.float32),
            shape(slotted + (ada_width,), jnp.float32),
            shape((ROW_PARTS, 2 * SLOT_ROWS, time_columns.shape[1]), jnp.int32),
        ),
        in_specs=[VMEM_SPEC] * 7,
        out_specs=[ANY_SPEC] * 2 + [VMEM_SPEC] * 3,
        scratch_shapes=[pltpu.VMEM((2 * SLOT_ROWS, time_columns.shape[1]), jnp.int32)]
        + [narrow] * 2
        + [wide] * 5
        + [
            DMA((4, 7)),
            DMA((4, 7)),
            DMA((2,)),
            DMA((2,)),
            DMA((3,)),
            DMA((3,)),
            DMA((3, 7)),
            DMA((3, 7)),
            DMA((2,)),
        ],
        compiler_params=pltpu.CompilerParams(
            collective_id=0, has_side_effects=True, vmem_limit_bytes=GRANT
        ),
        name="front",
    )(bucket_ids, class_labels, time_columns, class_columns, w_ada, patches, w_qkv)


class HeadReduce:
    def __init__(self, partial, beside_in, pair, across_in, sends, recvs):
        row, member, sibling, partner, opposite = places()
        self.member = member
        self.partner = partner
        self.partial = partial
        self.beside_in = beside_in
        self.pair = pair
        self.across_in = across_in
        self.first = to_head(
            partial.at[opposite], beside_in.at[1], sends.at[0], recvs.at[0], sibling
        )
        self.second = to_head(
            partial.at[sibling], beside_in.at[0], sends.at[1], recvs.at[1], sibling
        )
        self.across = to_head(pair, across_in, sends.at[2], recvs.at[2], partner)

    def start(self):
        self.first.start()
        self.second.start()

    def send_pair(self):
        self.first.wait_recv()
        self.pair[...] = (
            self.partial[self.partner].astype(jnp.float32)
            + self.beside_in[1].astype(jnp.float32)
        ).astype(jnp.bfloat16)
        self.across.start()

    def settle(self):
        self.second.wait_recv()
        self.across.wait_recv()

    def rows(self, part):
        return (
            self.partial[self.member, part].astype(jnp.float32)
            + self.beside_in[0, part].astype(jnp.float32)
            + self.across_in[part].astype(jnp.float32)
        )

    def finish(self):
        self.first.wait_send()
        self.second.wait_send()
        self.across.wait_send()


class RowReduce:
    def __init__(self, partial, chunk, buffers, total, sends, recvs):
        row = lax.axis_index("rows")
        self.level = row // 2
        self.side = lax.rem(row, 2)
        mate = row + 1 - 2 * self.side
        self.partial = partial
        self.mate_in, self.pair, self.straight_in = buffers
        self.total = total
        size = total.shape[0]
        self.part = pl.ds(chunk * size, size)
        self.beside = to_row(
            partial.at[:, 1 - self.side, self.part], self.mate_in, sends.at[0], recvs.at[0], mate
        )
        self.straight = []
        for step in range(1, 4):
            target = lax.rem(self.level + step, 4)
            self.straight.append(
                to_row(
                    self.pair.at[target],
                    self.straight_in.at[step - 1],
                    sends.at[step],
                    recvs.at[step],
                    target * 2 + self.side,
                )
            )

    def start(self):
        self.beside.start()

    def send_pair(self):
        self.beside.wait_recv()

        def one(level, carry):
            self.pair[level] = (
                self.partial[level, self.side, self.part].astype(jnp.float32)
                + self.mate_in[level].astype(jnp.float32)
            ).astype(jnp.bfloat16)
            return carry

        lax.fori_loop(0, 4, one, 0)
        for copy in self.straight:
            copy.start()

    def finish(self):
        for copy in self.straight:
            copy.wait_recv()
        self.total[...] = (
            self.pair[self.level].astype(jnp.float32)
            + self.straight_in[0].astype(jnp.float32)
            + self.straight_in[1].astype(jnp.float32)
            + self.straight_in[2].astype(jnp.float32)
        )
        self.beside.wait_send()
        for copy in self.straight:
            copy.wait_send()


def row_reduces(jobs, reducing):
    buffers, sends, recvs = reducing[:-2], reducing[-2], reducing[-1]
    return [
        RowReduce(
            partial,
            chunk,
            buffers[3 * place : 3 * place + 3],
            total,
            sends.at[place],
            recvs.at[place],
        )
        for place, (partial, chunk, total) in enumerate(jobs)
    ]


def reduce_scratch(sizes):
    landing = []
    for rows, columns in sizes:
        landing += [
            pltpu.VMEM((4, rows, columns), jnp.bfloat16),
            pltpu.VMEM((4, rows, columns), jnp.bfloat16),
            pltpu.VMEM((3, rows, columns), jnp.bfloat16),
        ]
    return landing + [DMA((len(sizes), 4)), DMA((len(sizes), 4))]


def picked(vectors, part_index, segments, width):
    wide = jnp.concatenate([segments] * (width // segments.shape[1]), axis=1)
    slot_count = vectors.shape[1]
    chosen = vectors[part_index, slot_count - 1 : slot_count]
    for slot in range(slot_count - 2, -1, -1):
        chosen = jnp.where(wide == slot, vectors[part_index, slot : slot + 1], chosen)
    return chosen


def slot_hot(segment_row, start):
    chosen = segment_row[:, pl.ds(pl.multiple_of(start, 128), 128)]
    slots = lax.broadcasted_iota(jnp.int32, (SLOT_ROWS, 128), 0)
    return (jnp.broadcast_to(chosen, slots.shape) == slots).astype(jnp.float32)


def table_hots(ids_all, table_rows):
    slots = ROW_PARTS * SLOT_ROWS
    table_places = lax.axis_index("rows") * table_rows + lax.broadcasted_iota(
        jnp.int32, (slots, table_rows), 1
    )
    return [
        ids_all[:, start : start + SLOT_ROWS].reshape(slots, table_rows) == table_places
        for start in (0, SLOT_ROWS)
    ]


def centre_rows(values):
    centred = values - jnp.mean(values, axis=1, keepdims=True)
    factor = lax.rsqrt(jnp.mean(centred * centred, axis=1, keepdims=True) + EPSILON)
    return centred * factor, factor


def weight_grad(left, right, target):
    blocks, tok_rows, depth = left.shape
    height = blocks * tok_rows
    flat = target.reshape(depth, target.shape[3])
    third = depth // 3

    def some(step, carry):
        columns = pl.ds(pl.multiple_of(step * third, 128), third)
        flat[columns] = contract_rows(
            left[:, :, columns].reshape(height, third),
            right[...].reshape(height, right.shape[2]),
        ).astype(jnp.bfloat16)
        return carry

    lax.fori_loop(0, 3, some, 0)


def core_kernel(
    patches_full,
    qkv_ref,
    out_shard,
    fc1_shard,
    fc2_shard,
    cotangent_ref,
    patches_ref,
    segment_row,
    mods_ref,
    bias_ref,
    value_bias,
    segments_ref,
    vectors_ref,
    normed_rows,
    parts,
    totals_out,
    mixed,
    out_w,
    active_rows,
    after_ref,
    after_grad,
    attn_grad,
    slot_sums,
    bias_sums,
    fc2_rest,
    fc1_part,
    fc2_head,
    fc2_neck,
    qkv_bias,
    head_bias,
    ffn_rows,
    hidden_rows,
    inner_grad,
    fc2_part,
    inner_bias,
    ffn_bias,
    out_full,
    fc1_full,
    fc2_full,
    active_grad,
    value_columns,
    head_mixed,
    bias,
    group_part,
    beside_in,
    pair_rows,
    across_in,
    attn_out,
    gather_send,
    gather_recv,
    reduce_send,
    reduce_recv,
    out_send,
    out_recv,
    fc1_send,
    fc1_recv,
    fc2_send,
    fc2_recv,
    local_sems,
    *reducing,
):
    row, member, sibling, partner, opposite = places()
    direction = sibling - member
    greet(range(1, ROW_PARTS), (sibling, partner))
    tok_rows, model_width = patches_ref.shape
    blocks = normed_rows.shape[0]
    seq_len = blocks * tok_rows
    width = qkv_ref.shape[1]
    head_local = totals_out.shape[0]
    head_size = width // (3 * head_local)
    scale_factor = 1.0 / math.sqrt(head_size)
    loads = [
        pltpu.make_async_copy(patches_full.at[block], normed_rows.at[block], local_sems.at[block])
        for block in range(blocks)
    ]
    for load in loads:
        load.start()
    gather_out = RowGather(out_shard, out_full, out_send, out_recv, local_sems.at[4], 1)
    gather_fc1 = RowGather(fc1_shard, fc1_full, fc1_send, fc1_recv, local_sems.at[5], 3)
    gather_fc2 = RowGather(fc2_shard, fc2_full, fc2_send, fc2_recv, local_sems.at[6], 3)
    gather_cotangent = HeadGather(
        cotangent_ref, ffn_rows, gather_send.at[2], gather_recv.at[2], local_sems.at[7]
    )
    gather_out.own.start()
    gather_out.start(0)
    gather_fc1.own.start()
    gather_fc2.own.start()
    for chunk in range(3):
        gather_fc1.start(chunk)
    gather_cotangent.start()
    reduce_attn = HeadReduce(
        group_part, beside_in, pair_rows, across_in, reduce_send.at[0], reduce_recv.at[0]
    )
    reduce_hidden = HeadReduce(
        group_part, beside_in, pair_rows, across_in, reduce_send.at[1], reduce_recv.at[1]
    )
    gather_hidden = HeadGather(None, hidden_rows, gather_send.at[0], gather_recv.at[0], None)
    gather_grad = HeadGather(None, attn_grad, gather_send.at[1], gather_recv.at[1], None)
    parts[...] = jnp.zeros_like(parts)
    segments_ref[...] = (
        jnp.broadcast_to(segment_row[...].astype(jnp.float32), (128, seq_len))
        .T.astype(jnp.int32)
    )
    slot_count = vectors_ref.shape[1]
    fine = mods_ref.shape[2] // 3
    for unit in range(3 * ROW_PARTS):
        part_index, within = divmod(unit * fine, model_width)
        span = slice(within, within + fine)
        vectors_ref[part_index, :, span] = mods_ref[
            unit // 3, 0:slot_count, unit % 3 * fine : (unit % 3 + 1) * fine
        ]
    for part_index in range(6):
        vectors_ref[part_index] += bias_ref[part_index : part_index + 1]
    qkv_bias[...] = jnp.zeros_like(qkv_bias)
    head_bias[...] = value_bias[...].astype(jnp.float32)
    for head in range(head_local):
        for place in (0, 2):
            start = (3 * head + place) * head_size
            taken = slice(place // 2 * head_size, (place // 2 + 1) * head_size)
            qkv_bias[:, start : start + head_size] = head_bias[head : head + 1, taken]
    for load in loads:
        load.wait()

    def first_norm(step, carry):
        block = step // 2
        part = pl.ds(pl.multiple_of(lax.rem(step, 2) * 128, 128), 128)
        segments = segments_ref[pl.ds(pl.multiple_of(step * 128, 128), 128)]
        normed, _ = centre_rows(normed_rows[block, part].astype(jnp.float32))
        normed_rows[block, part] = (
            normed * (1.0 + picked(vectors_ref, 1, segments, model_width))
            + picked(vectors_ref, 0, segments, model_width)
        ).astype(jnp.bfloat16)
        return carry

    lax.fori_loop(0, 2 * blocks, first_norm, 0)
    gather_out.hop(0, 0)
    gather_fc1.hop(0, 0)
    gather_fc1.hop(1, 0)
    gather_fc2.start(0)

    def project_in(block, carry):
        rows = pl.ds(pl.multiple_of(block * tok_rows, tok_rows), tok_rows)
        active_grad[0, :, 0:width] = (
            jnp.dot(normed_rows[block], qkv_ref[...], preferred_element_type=jnp.float32)
            + qkv_bias[...]
        )
        for part in range(3 * head_local):
            parts[part, rows, 0:head_size] = active_grad[
                0, :, part * head_size : (part + 1) * head_size
            ].astype(jnp.bfloat16)
        return carry

    lax.fori_loop(0, blocks, project_in, 0)
    gather_out.hop(0, 1)
    gather_fc1.hop(2, 0)
    gather_fc1.hop(0, 1)
    gather_fc2.start(1)

    def turn(head, carry):
        value_columns[head] = parts[3 * head + 2].astype(jnp.float32).T.astype(jnp.bfloat16)
        return carry

    lax.fori_loop(0, head_local, turn, 0)

    def attend(block):
        rows = pl.ds(pl.multiple_of(block * tok_rows, tok_rows), tok_rows)
        keys = jnp.concatenate([segments_ref[...]] * (tok_rows // 128), axis=1)
        same = keys == jnp.broadcast_to(segment_row[:, rows], keys.shape)
        bias[...] = jnp.where(same, 0.0, MASKED)

        def one_head(head, carry):
            scores = (
                times_transposed(parts[3 * head + 1], parts[3 * head, rows]) * scale_factor
                + bias[...]
            )
            peak = jnp.max(scores, axis=0, keepdims=True)
            raised = jnp.exp(scores - peak)
            total = jnp.sum(raised, axis=0, keepdims=True)
            totals_out[head, block] = peak + jnp.log(total)
            head_mixed[head] = jnp.dot(
                value_columns[head],
                (raised * (1.0 / total)).astype(jnp.bfloat16),
                preferred_element_type=jnp.float32,
            ).T
            return carry

        lax.fori_loop(0, head_local, one_head, 0)
        for head in range(head_local):
            active_grad[1, :, head * head_size : (head + 1) * head_size] = head_mixed[
                head, :, 0:head_size
            ]
        mixed[block] = active_grad[1, :, 0 : head_local * head_size].astype(jnp.bfloat16)

    def project(block):
        group_part[block] = times_transposed(mixed[block], out_w[...]).astype(jnp.bfloat16)

    attend(opposite)
    gather_out.hop(0, 2)
    gather_fc1.hop(1, 1)
    gather_fc2.hop(0, 0)
    gather_fc2.start(2)
    attend(partner)
    gather_fc1.hop(2, 1)
    gather_fc1.hop(0, 2)
    gather_out.finish()
    out_w[...] = out_full[...].reshape(out_w.shape)
    project(opposite)
    reduce_attn.first.start()
    project(partner)
    reduce_attn.send_pair()
    gather_fc2.hop(1, 0)
    attend(sibling)
    gather_fc1.hop(1, 2)
    gather_fc2.hop(0, 1)
    gather_fc2.hop(2, 0)
    attend(member)
    gather_fc1.hop(2, 2)
    gather_fc2.hop(1, 1)
    project(sibling)
    reduce_attn.second.start()
    project(member)
    gather_cotangent.wait_sibling()
    gather_cotangent.wait_partner()
    gather_cotangent.wait_opposite()
    gather_cotangent.finish()

    def scale_cotangent(step, carry):
        block = step // 2
        part = pl.ds(pl.multiple_of(lax.rem(step, 2) * 128, 128), 128)
        segments = segments_ref[pl.ds(pl.multiple_of(step * 128, 128), 128)]
        grad = (
            picked(vectors_ref, 5, segments, model_width)
            * ffn_rows[block, part].astype(jnp.float32)
        ).astype(jnp.bfloat16)
        ffn_rows[block, part] = grad
        ffn_bias[...] += jnp.sum(grad.astype(jnp.float32).reshape(16, 8, model_width), axis=0)
        return carry

    ffn_bias[...] = jnp.zeros_like(ffn_bias)
    lax.fori_loop(0, 2 * blocks, scale_cotangent, 0)
    gather_fc2.hop(0, 2)
    gather_fc2.hop(2, 1)
    reduce_attn.settle()

    def second_norm(block, carry):
        part = pl.ds(pl.multiple_of(block * 128, 128), 128)
        segments = segments_ref[
            pl.ds(pl.multiple_of(member * tok_rows + block * 128, 128), 128)
        ]
        out = reduce_attn.rows(part) + bias_ref[6:7]
        after = patches_ref[part].astype(jnp.float32) + (
            picked(vectors_ref, 2, segments, model_width) * out
        )
        attn_out[part] = out
        after_ref[part] = after
        normed, _ = centre_rows(after)
        hidden_rows[member, part] = (
            normed * (1.0 + picked(vectors_ref, 4, segments, model_width))
            + picked(vectors_ref, 3, segments, model_width)
        ).astype(jnp.bfloat16)
        return carry

    lax.fori_loop(0, tok_rows // 128, second_norm, 0)
    gather_hidden.start()
    reduce_attn.finish()
    gather_fc2.hop(1, 2)
    gather_fc2.hop(2, 2)
    gather_fc1.finish()
    hidden_width = active_rows.shape[2]
    fc1 = fc1_full.reshape(model_width, hidden_width)
    fc2 = fc2_full.reshape(model_width, hidden_width)

    inner_bias[...] = jnp.zeros_like(inner_bias)

    def feed(block, carry):
        inner = jnp.dot(
            hidden_rows[block], fc1[...], preferred_element_type=jnp.float32
        ) + bias_ref[7:8]
        square = inner * inner
        bent = jnp.tanh(TANH_COEFF * (inner + 0.044715 * square * inner))
        half = 0.5 * (1.0 + bent)
        active_rows[block] = (inner * half).astype(jnp.bfloat16)
        active_grad[block] = half + 0.5 * inner * (1.0 - bent * bent) * (
            TANH_COEFF * (1.0 + 3.0 * 0.044715 * square)
        )
        return carry

    def through_fc2(block, carry):
        grad = (
            jnp.dot(ffn_rows[block], fc2[...], preferred_element_type=jnp.float32)
            * active_grad[block]
        ).astype(jnp.bfloat16)
        inner_grad[block] = grad
        inner_bias[...] += jnp.sum(
            grad.astype(jnp.float32).reshape(tok_rows // 8, 8, hidden_width), axis=0
        )
        return carry

    def return_fc1(block, carry):
        group_part[block] = times_transposed(inner_grad[block], fc1[...]).astype(jnp.bfloat16)
        return carry

    gather_hidden.wait_sibling()
    lax.fori_loop(0, 2, lambda step, carry: feed(member + step * direction, carry), 0)
    gather_hidden.wait_partner()
    gather_hidden.wait_opposite()
    lax.fori_loop(0, 2, lambda step, carry: feed(opposite - step * direction, carry), 0)
    gather_fc2.finish()

    def turn_back(block, carry):
        through_fc2(block, carry)
        return return_fc1(block, carry)

    lax.fori_loop(0, 2, lambda step, carry: turn_back(opposite - step * direction, carry), 0)
    reduce_hidden.first.start()
    reduce_hidden.send_pair()
    lax.fori_loop(0, 2, lambda step, carry: turn_back(sibling - step * direction, carry), 0)
    reduce_hidden.second.start()

    def forward_fc2(block, carry):
        active_rows[block] = times_transposed(active_rows[block], fc2[...]).astype(jnp.bfloat16)
        return carry

    weight_grad(ffn_rows, active_rows, fc2_part)
    third = fc2_rest.shape[2]
    fc2_rest[...] = fc2_part[:, :, 2 * third : 3 * third]
    reduces = row_reduces(((fc2_part, 0, fc2_head), (fc2_part, 1, fc2_neck)), reducing)
    for unit in reduces:
        unit.start()
    lax.fori_loop(0, HEAD_PARTS, forward_fc2, 0)
    slot_sums[...] = jnp.zeros_like(slot_sums)
    reduce_hidden.settle()

    def second_back(block, carry):
        part = pl.ds(pl.multiple_of(block * 128, 128), 128)
        segments = segments_ref[
            pl.ds(pl.multiple_of(member * tok_rows + block * 128, 128), 128)
        ]
        grad = reduce_hidden.rows(part)
        normed, factor = centre_rows(after_ref[part])
        weighted = grad * (1.0 + picked(vectors_ref, 4, segments, model_width))
        total = cotangent_ref[part].astype(jnp.float32) + factor * (
            weighted
            - jnp.mean(weighted, axis=1, keepdims=True)
            - normed * jnp.mean(weighted * normed, axis=1, keepdims=True)
        )
        after_grad[part] = total
        attn_grad[member, part] = (
            picked(vectors_ref, 2, segments, model_width) * total
        ).astype(jnp.bfloat16)
        hot = slot_hot(segment_row, member * tok_rows + block * 128)
        for index, term in enumerate((total * attn_out[part], grad, grad * normed)):
            slot_sums[index] += jnp.dot(
                hot, term, precision=HIGH, preferred_element_type=jnp.float32
            )
        return carry

    lax.fori_loop(0, tok_rows // 128, second_back, 0)
    gather_grad.start()
    weight_grad(hidden_rows, inner_grad, fc1_part)
    reduces[0].send_pair()
    bias_sums[...] = jnp.zeros_like(bias_sums)
    bias_sums[0:1] = jnp.sum(inner_bias[...], axis=0, keepdims=True)
    bias_sums[1:2] = jnp.sum(ffn_bias[...], axis=0, keepdims=True)
    gather_grad.wait_sibling()
    gather_grad.wait_partner()
    gather_grad.wait_opposite()
    reduces[1].send_pair()
    for unit in reduces:
        unit.finish()
    gather_hidden.finish()
    gather_grad.finish()
    reduce_hidden.finish()


def core(slot_count, head_size, *args):
    shape = jax.ShapeDtypeStruct
    patches_full, w_qkv, out_shard, fc1_shard = args[:4]
    blocks, tok_rows, model_width = patches_full.shape
    seq_len = blocks * tok_rows
    out_width = out_shard.shape[1]
    width_part, hidden_width = fc1_shard.shape
    third = width_part // 3
    head_local = out_width // head_size
    low = jnp.bfloat16
    full = jnp.float32
    rows_low = shape((blocks, tok_rows, model_width), low)
    own = shape((tok_rows, model_width), full)
    own_low = pltpu.VMEM((tok_rows, model_width), low)
    group_low = pltpu.VMEM((blocks, tok_rows, model_width), low)
    hidden_low = pltpu.VMEM((blocks, tok_rows, hidden_width), low)
    part_low = (4, 2, width_part, hidden_width)
    return pl.pallas_call(
        core_kernel,
        out_shape=[
            shape((seq_len, 128), jnp.int32),
            shape((6, slot_count, model_width), full),
            rows_low,
            shape((3 * head_local, seq_len, HEAD_LANES), low),
            shape((head_local, blocks, 1, tok_rows), full),
            shape((blocks, tok_rows, out_width), low),
            shape((model_width, out_width), low),
            rows_low,
            own,
            own,
            rows_low,
            shape((3, SLOT_ROWS, model_width), full),
            shape((8, hidden_width), full),
            shape((4, 2, third, hidden_width), low),
            shape(part_low, low),
            shape((third, hidden_width), full),
            shape((third, hidden_width), full),
        ],
        in_specs=[ANY_SPEC] + [VMEM_SPEC] * 10,
        out_specs=[VMEM_SPEC] * 17,
        scratch_shapes=[
            pltpu.VMEM((1, args[1].shape[1]), full),
            pltpu.VMEM(args[-1].shape, full),
            group_low,
            group_low,
            hidden_low,
            pltpu.VMEM(part_low, low),
            pltpu.VMEM((8, hidden_width), full),
            pltpu.VMEM((8, model_width), full),
            pltpu.VMEM((ROW_PARTS,) + out_shard.shape, low),
            pltpu.VMEM((ROW_PARTS,) + fc1_shard.shape, low),
            pltpu.VMEM((ROW_PARTS,) + fc1_shard.shape, low),
            pltpu.VMEM((blocks, tok_rows, hidden_width), full),
            pltpu.VMEM((head_local, HEAD_LANES, seq_len), low),
            pltpu.VMEM((head_local, tok_rows, HEAD_LANES), full),
            pltpu.VMEM((seq_len, tok_rows), full),
            group_low,
            pltpu.VMEM((2, tok_rows, model_width), low),
            own_low,
            own_low,
            pltpu.VMEM((tok_rows, model_width), full),
            DMA((3, 3)),
            DMA((3, 3)),
            DMA((2, 3)),
            DMA((2, 3)),
            DMA((1, 7)),
            DMA((1, 7)),
            DMA((3, 7)),
            DMA((3, 7)),
            DMA((3, 7)),
            DMA((3, 7)),
            DMA((8,)),
        ]
        + reduce_scratch([(third, hidden_width)] * 2),
        compiler_params=pltpu.CompilerParams(
            collective_id=2, has_side_effects=True, vmem_limit_bytes=67_000_000
        ),
        name="core",
    )(*args)


HEAD_LANES = 128


def rear_kernel(
    parts,
    grad_ref,
    out_ref,
    totals_ref,
    segment_row,
    segments_ref,
    fc2_part,
    fc1_part,
    hidden_rows,
    qkv_ref,
    mixed_ref,
    bias_ref,
    patches_ref,
    after_ref,
    vectors_ref,
    sums_ref,
    condition_ref,
    ids_all,
    ada_ref,
    ffn_ref,
    block_ref,
    cotangent_ref,
    bias_rows,
    fc2_head,
    fc2_neck,
    block_out,
    patches_grad,
    time_grad,
    class_grad,
    ada_grad,
    ada_bias,
    fc2_grad,
    fc1_grad,
    qkv_grad,
    out_grad,
    bias_sum,
    mixed_grad,
    key_columns,
    grad_keys,
    grad_values,
    bias,
    packed,
    packed_grad,
    hidden_part,
    qkv_part,
    out_part,
    bias_own,
    beside_in,
    pair_rows,
    across_in,
    ffn_beside,
    ffn_pair,
    ffn_across,
    slot_sums,
    mods_own,
    mods_sibling,
    mods_pair,
    mods_partner,
    mods_low,
    mods_cols,
    bias_all,
    silu_part,
    silu_in,
    silu_all,
    small_send,
    small_recv,
    pair_send,
    pair_recv,
    head_send,
    head_recv,
    *reducing,
):
    row, member, sibling, partner, opposite = places()
    greet(range(1, ROW_PARTS), (sibling, partner))
    others = [(step, lax.rem(row + step, ROW_PARTS)) for step in range(1, ROW_PARTS)]

    def spread(stage, source_of, target):
        copies = []
        for step, other in others:
            copy = to_row(
                source_of(other),
                target.at[row],
                small_send.at[stage, step - 1],
                small_recv.at[stage, step - 1],
                other,
            )
            copy.start()
            copies.append(copy)
        return copies

    def settle(copies):
        for copy in copies:
            copy.wait()

    third = fc2_head.shape[0]
    fc2_grad[0:third] = fc2_head[...]
    fc2_grad[third : 2 * third] = fc2_neck[...]
    units = row_reduces(
        [(fc2_part, 0, fc2_grad.at[pl.ds(2 * third, third)])]
        + [(fc1_part, chunk, fc1_grad.at[pl.ds(chunk * third, third)]) for chunk in range(3)]
        + [(out_part, 0, out_grad)]
        + [(qkv_part, chunk, qkv_grad.at[pl.ds(chunk * third, third)]) for chunk in range(3)],
        reducing,
    )
    reduce_rows = HeadReduce(
        hidden_part, beside_in, pair_rows, across_in, head_send.at[0], head_recv.at[0]
    )
    reduce_ffn = HeadReduce(
        ffn_ref, ffn_beside, ffn_pair, ffn_across, head_send.at[1], head_recv.at[1]
    )
    for unit in units[:3]:
        unit.start()
    reduce_ffn.start()
    reduce_ffn.send_pair()
    blocks, tok_rows, model_width = grad_ref.shape
    width = qkv_ref.shape[1]
    head_local = totals_ref.shape[0]
    head_size = width // (3 * head_local)
    scale_factor = 1.0 / math.sqrt(head_size)
    seq_len = blocks * tok_rows
    mixed_grad[...] = jnp.zeros_like(mixed_grad)
    bias_own[...] = jnp.zeros_like(bias_own)

    def unpack(block, carry):
        rows = pl.ds(pl.multiple_of(block * tok_rows, tok_rows), tok_rows)
        packed[:, 0 : head_local * head_size] = jnp.dot(
            grad_ref[block], out_ref[...], preferred_element_type=jnp.float32
        )
        for head in range(head_local):
            mixed_grad[head, rows, 0:head_size] = packed[
                :, head * head_size : (head + 1) * head_size
            ].astype(jnp.bfloat16)
        bias_own[0] += jnp.sum(
            grad_ref[block].astype(jnp.float32).reshape(tok_rows // 8, 8, model_width), axis=0
        )
        return carry

    lax.fori_loop(0, blocks, unpack, 0)

    def turn(head, carry):
        key_columns[head] = parts[3 * head + 1].astype(jnp.float32).T.astype(jnp.bfloat16)
        return carry

    lax.fori_loop(0, head_local, turn, 0)
    grad_keys[...] = jnp.zeros_like(grad_keys)
    grad_values[...] = jnp.zeros_like(grad_values)
    weight_grad(grad_ref, mixed_ref, out_part)

    for block in range(blocks):
        rows = pl.ds(block * tok_rows, tok_rows)
        keys = jnp.concatenate([segments_ref[...]] * (tok_rows // 128), axis=1)
        same = keys == jnp.broadcast_to(segment_row[:, rows], keys.shape)
        bias[...] = jnp.where(same, 0.0, MASKED)

        def one_head(head, carry):
            query = parts[3 * head, rows]
            grad = mixed_grad[head, rows]
            scores = times_transposed(parts[3 * head + 1], query) * scale_factor + bias[...]
            probs = jnp.exp(scores - totals_ref[head, block])
            grad_probs = times_transposed(parts[3 * head + 2], grad)
            inner = jnp.sum(probs * grad_probs, axis=0, keepdims=True)
            grad_scores = (probs * (grad_probs - inner)).astype(jnp.bfloat16)
            grad_values[head] += jnp.dot(
                probs.astype(jnp.bfloat16), grad, preferred_element_type=jnp.float32
            )
            grad_keys[head] += jnp.dot(grad_scores, query, preferred_element_type=jnp.float32)
            lanes = pl.ds(pl.multiple_of(head * HEAD_LANES, HEAD_LANES), HEAD_LANES)
            hidden_part[block, :, lanes] = (
                jnp.dot(key_columns[head], grad_scores, preferred_element_type=jnp.float32).T
                * scale_factor
            ).astype(jnp.bfloat16)
            return carry

        lax.fori_loop(0, head_local, one_head, 0)
        units[block].send_pair()
        if block < 2:
            units[block + 3].start()

    def pack(block, carry):
        rows = pl.ds(pl.multiple_of(block * tok_rows, tok_rows), tok_rows)
        for head in range(head_local):
            lane = head * HEAD_LANES
            terms = (
                hidden_part[block, :, lane : lane + head_size].astype(jnp.float32),
                grad_keys[head, rows, 0:head_size] * scale_factor,
                grad_values[head, rows, 0:head_size],
            )
            for place, term in enumerate(terms):
                start = (3 * head + place) * head_size
                packed[:, start : start + head_size] = term
        low = packed[...].astype(jnp.bfloat16)
        packed_grad[block] = low
        bias_own[1, :, 0:width] += jnp.sum(
            low.astype(jnp.float32).reshape(tok_rows // 8, 8, width), axis=0
        )
        return carry

    lax.fori_loop(0, blocks, pack, 0)
    direction = sibling - member

    def project_back(block):
        hidden_part[block] = times_transposed(packed_grad[block], qkv_ref[...]).astype(
            jnp.bfloat16
        )

    def far(step, carry):
        project_back(opposite - step * direction)
        return carry

    def near(step, carry):
        project_back(sibling - step * direction)
        return carry

    lax.fori_loop(0, 2, far, 0)
    reduce_rows.first.start()
    reduce_rows.send_pair()
    lax.fori_loop(0, 2, near, 0)
    reduce_rows.second.start()
    weight_grad(hidden_rows, packed_grad, qkv_part)
    for unit in units[5:]:
        unit.start()
    bias_own[2] = jnp.zeros_like(bias_own[2])
    bias_own[2] = bias_ref[...]
    bias_own[2, 2:3] = jnp.sum(bias_own[0], axis=0, keepdims=True)
    bias_own[2, 3:4] = jnp.sum(bias_own[1], axis=0, keepdims=True)
    bias_copies = spread(1, lambda other: bias_own.at[2], bias_all)
    bias_all[row] = bias_own[2]
    units[4].send_pair()
    slot_sums[...] = jnp.zeros_like(slot_sums)
    reduce_ffn.settle()

    def rows_out(block, carry):
        part = pl.ds(pl.multiple_of(block * 128, 128), 128)
        ffn = reduce_ffn.rows(part) + bias_rows[8:9]
        place = pl.multiple_of(member * tok_rows + block * 128, 128)
        gate = picked(vectors_ref, 5, segments_ref[pl.ds(place, 128)], model_width)
        block_out[part] = (block_ref[part] + gate * ffn).astype(jnp.bfloat16)
        slot_sums[2] += jnp.dot(
            slot_hot(segment_row, place),
            cotangent_ref[part].astype(jnp.float32) * ffn,
            precision=HIGH,
            preferred_element_type=jnp.float32,
        )
        return carry

    lax.fori_loop(0, tok_rows // 128, rows_out, 0)
    units[0].finish()
    units[1].finish()
    units[5].send_pair()
    reduce_rows.settle()

    def rows_back(block, carry):
        part = pl.ds(pl.multiple_of(block * 128, 128), 128)
        grad = reduce_rows.rows(part)
        normed, factor = centre_rows(patches_ref[part].astype(jnp.float32))
        place = pl.multiple_of(member * tok_rows + block * 128, 128)
        weighted = grad * (
            1.0 + picked(vectors_ref, 1, segments_ref[pl.ds(place, 128)], model_width)
        )
        patches_grad[part] = after_ref[part] + factor * (
            weighted
            - jnp.mean(weighted, axis=1, keepdims=True)
            - normed * jnp.mean(weighted * normed, axis=1, keepdims=True)
        )
        hot = slot_hot(segment_row, place)
        slot_sums[0] += jnp.dot(hot, grad, precision=HIGH, preferred_element_type=jnp.float32)
        slot_sums[1] += jnp.dot(
            hot, grad * normed, precision=HIGH, preferred_element_type=jnp.float32
        )
        return carry

    lax.fori_loop(0, tok_rows // 128, rows_back, 0)
    ada_width = ada_ref.shape[1]
    fine = ada_width // 3
    for unit in range(3 * ROW_PARTS):
        part_index, within = divmod(unit * fine, model_width)
        span = slice(within, within + fine)
        if part_index < 2:
            source = slot_sums[part_index, :, span]
        elif part_index == 5:
            source = slot_sums[2, :, span]
        else:
            source = sums_ref[part_index - 2, :, span]
        mods_own[unit // 3, :, unit % 3 * fine : (unit % 3 + 1) * fine] = source
    beside = to_head(mods_own, mods_sibling, pair_send.at[0], pair_recv.at[0], sibling)
    beside.start()
    units[6].send_pair()
    beside.wait()
    mods_pair[...] = (mods_own[...] + mods_sibling[...]).astype(jnp.bfloat16)
    across = to_head(mods_pair, mods_partner, pair_send.at[1], pair_recv.at[1], partner)
    across.start()
    units[2].finish()
    units[3].finish()
    settle(bias_copies)
    bias_sum[...] = jnp.sum(bias_all[...], axis=0)
    across.wait()
    mods_low[...] = (
        mods_pair[...].astype(jnp.float32) + mods_partner[...].astype(jnp.float32)
    ).astype(jnp.bfloat16)
    copies = spread(0, lambda other: mods_low.at[other], mods_cols)
    mods_cols[row] = mods_low[row]
    units[7].send_pair()
    units[4].finish()
    settle(copies)
    slots = ROW_PARTS * SLOT_ROWS
    cols = mods_cols[...].astype(jnp.float32).reshape(slots, ada_width)
    low = cols.astype(jnp.bfloat16)
    condition = condition_ref[...].reshape(slots, condition_ref.shape[2])
    bent = 1.0 / (1.0 + jnp.exp(-condition))
    silu_part[...] = times_transposed(low, ada_ref[...]).reshape(silu_part.shape)
    copies = spread(2, lambda other: silu_part.at[other], silu_in)
    silu_in[row] = silu_part[row]
    ada_grad[...] = contract_rows((condition * bent).astype(jnp.bfloat16), low)
    ada_bias[...] = jnp.broadcast_to(jnp.sum(cols, axis=0, keepdims=True), ada_bias.shape)
    settle(copies)
    summed = jnp.sum(silu_in[...], axis=0)
    silu_all[row] = summed
    silu_part[row] = summed
    copies = spread(3, lambda other: silu_part.at[row], silu_all)
    units[5].finish()
    units[6].finish()
    units[7].finish()
    settle(copies)
    grad_condition = silu_all[...].reshape(slots, silu_all.shape[2]) * (
        bent * (1.0 + condition * (1.0 - bent))
    )
    for target, hot in zip((time_grad, class_grad), table_hots(ids_all, time_grad.shape[1])):
        target[...] = contract_rows_exact(grad_condition, hot.astype(jnp.float32))
    reduce_rows.finish()
    reduce_ffn.finish()


def rear(*args):
    shape = jax.ShapeDtypeStruct
    grads, w_out, totals, grad_w_fc2, w_qkv, biases, ids_all, w_ada = (
        args[place] for place in (1, 2, 3, 6, 9, 11, 17, 18)
    )
    blocks, tok_rows, model_width = grads.shape
    width = w_qkv.shape[1]
    head_local = totals.shape[0]
    seq_len = blocks * tok_rows
    third, hidden_width = grad_w_fc2.shape[2:]
    width_part = 3 * third
    out_width = w_out.shape[1]
    depth, ada_width = w_ada.shape
    table_rows = ids_all.shape[2]
    low = jnp.bfloat16
    full = jnp.float32
    heads_wide = pltpu.VMEM((head_local, seq_len, HEAD_LANES), full)
    slotted = (ROW_PARTS, SLOT_ROWS)
    wide = pltpu.VMEM(slotted + (ada_width,), full)
    wide_low = pltpu.VMEM(slotted + (ada_width,), low)
    narrow = pltpu.VMEM(slotted + (depth,), full)
    sizes = (
        [(third, hidden_width)] * 4 + [(width_part, out_width)] + [(third, width)] * 3
    )
    return pl.pallas_call(
        rear_kernel,
        out_shape=[
            shape((tok_rows, model_width), low),
            shape((tok_rows, model_width), full),
            shape((depth, table_rows), full),
            shape((depth, table_rows), full),
            shape((depth, ada_width), full),
            shape((SLOT_ROWS, ada_width), full),
            shape((width_part, hidden_width), full),
            shape((width_part, hidden_width), full),
            shape((width_part, width), full),
            shape((width_part, out_width), full),
            shape(biases.shape, full),
        ],
        in_specs=[VMEM_SPEC] * 25,
        out_specs=[VMEM_SPEC] * 11,
        scratch_shapes=[
            pltpu.VMEM((head_local, seq_len, HEAD_LANES), low),
            pltpu.VMEM((head_local, HEAD_LANES, seq_len), low),
            heads_wide,
            heads_wide,
            pltpu.VMEM((seq_len, tok_rows), full),
            pltpu.VMEM((tok_rows, width), full),
            pltpu.VMEM((blocks, tok_rows, width), low),
            pltpu.VMEM((blocks, tok_rows, model_width), low),
            pltpu.VMEM((4, 2, width_part, width), low),
            pltpu.VMEM((4, 2, width_part, out_width), low),
            pltpu.VMEM((3,) + biases.shape, full),
        ]
        + [
            pltpu.VMEM((2, tok_rows, model_width), low),
            pltpu.VMEM((tok_rows, model_width), low),
            pltpu.VMEM((tok_rows, model_width), low),
        ]
        * 2
        + [pltpu.VMEM((3, SLOT_ROWS, model_width), full)]
        + [wide] * 2
        + [wide_low] * 4
        + [pltpu.VMEM((ROW_PARTS,) + biases.shape, full)]
        + [narrow] * 3
        + [
            DMA((4, 7)),
            DMA((4, 7)),
            DMA((2,)),
            DMA((2,)),
            DMA((2, 3)),
            DMA((2, 3)),
        ]
        + reduce_scratch(sizes),
        compiler_params=pltpu.CompilerParams(
            collective_id=1, has_side_effects=True, vmem_limit_bytes=67_000_000
        ),
        name="rear",
    )(*args)


def shards_linked(
    patches,
    time_table,
    class_table,
    w_ada,
    b_ada,
    w_qkv,
    b_qv,
    w_out,
    b_out,
    w_fc1,
    b_fc1,
    w_fc2,
    b_fc2,
    image_lengths,
    segment_ids,
    bucket_ids,
    class_labels,
    cotangent,
):
    model_width = patches.shape[1]
    slot_count = image_lengths.shape[1]
    head_local = b_qv.shape[0]
    head_size = b_qv.shape[1] // 2
    qkv_full, patches_full, condition, mods, ids_all = front(
        bucket_ids, class_labels, time_table.T, class_table.T, w_ada, patches, w_qkv
    )
    qkv_cols = qkv_full.reshape(model_width, w_qkv.shape[1])
    biases = (
        jnp.concatenate([b_ada, b_out, b_fc1, b_fc2]).astype(jnp.float32).reshape(9, model_width)
    )
    (
        segments,
        vectors,
        rows_one,
        parts,
        totals,
        mixed_rows,
        out_cols,
        ffn_part,
        after_attn,
        grad_after,
        attn_rows_grad,
        sums,
        bias_sums,
        grad_w_fc2,
        grad_w_fc1,
        fc2_head,
        fc2_neck,
    ) = core(
        slot_count,
        head_size,
        patches_full,
        qkv_cols,
        w_out,
        w_fc1,
        w_fc2,
        cotangent,
        patches,
        segment_ids,
        mods,
        biases,
        b_qv,
    )
    (
        block_out,
        grad_patches,
        grad_time,
        grad_class,
        grad_w_ada,
        grad_b_ada,
        grad_w_fc2,
        grad_w_fc1,
        grad_w_qkv,
        grad_w_out,
        bias_all,
    ) = rear(
        parts,
        attn_rows_grad,
        out_cols,
        totals,
        segment_ids,
        segments,
        grad_w_fc2,
        grad_w_fc1,
        rows_one,
        qkv_cols,
        mixed_rows,
        bias_sums,
        patches,
        grad_after,
        vectors,
        sums,
        condition,
        ids_all,
        w_ada,
        ffn_part,
        after_attn,
        cotangent,
        biases,
        fc2_head,
        fc2_neck,
    )
    grad_time = grad_time.T
    grad_class = grad_class.T
    grad_b_ada = grad_b_ada[0]
    bias_rows = model_width // lax.axis_size("rows")
    row_start = lax.axis_index("rows") * bias_rows
    grad_b_fc1 = bias_all[0]
    grad_b_fc2 = lax.dynamic_slice_in_dim(bias_all[1], row_start, bias_rows)
    grad_b_out = lax.dynamic_slice_in_dim(bias_all[2], row_start, bias_rows)
    bias_terms = bias_all[3, : head_local * 3 * head_size].reshape(head_local, 3, head_size)
    grad_b_qv = jnp.concatenate([bias_terms[:, 0], bias_terms[:, 2]], axis=1)
    return (
        block_out,
        grad_patches,
        grad_time,
        grad_class,
        grad_w_ada,
        grad_b_ada,
        grad_w_qkv,
        grad_b_qv,
        grad_w_out,
        grad_b_out,
        grad_w_fc1,
        grad_b_fc1,
        grad_w_fc2,
        grad_b_fc2,
    )


def solution(mesh):
    placed = (
        P(("rows", "heads"), None),
        P("rows", "heads"),
        P("rows", "heads"),
        P("heads", "rows"),
        P(),
        P("rows", "heads"),
        P("heads", None),
        P("rows", "heads"),
        P(),
        P("rows", "heads"),
        P("heads"),
        P("rows", "heads"),
        P(),
        P("rows", None),
        P("rows", None),
        P("rows", None),
        P("rows", None),
        P(("rows", "heads"), None),
    )
    linked = mesh.shape["rows"] == ROW_PARTS and mesh.shape["heads"] == HEAD_PARTS
    return jax.shard_map(
        shards_linked if linked else shards_plain,
        mesh=mesh,
        in_specs=placed,
        out_specs=(
            P(("rows", "heads"), None),
            P(("rows", "heads"), None),
            P("rows", "heads"),
            P("rows", "heads"),
            P("heads", "rows"),
            P("rows"),
            P("rows", "heads"),
            P("heads", None),
            P("rows", "heads"),
            P("rows"),
            P("rows", "heads"),
            P("heads"),
            P("rows", "heads"),
            P("rows"),
        ),
        check_vma=False,
    )
```

```python
import functools
import math

import jax
import jax.numpy as jnp
from jax import lax
from jax.experimental import pallas as pl
from jax.experimental.pallas import tpu as pltpu
from jax.sharding import PartitionSpec as P

EPSILON = 1e-06
MASKED = -1e30
HIGH = lax.Precision.HIGHEST
TANH_COEFF = 0.7978845608028654
BLOCK_LIMIT = 512


def layer_norm(values):
    average = jnp.mean(values, axis=-1, keepdims=True)
    centred = values - average
    variance = jnp.mean(centred * centred, axis=-1, keepdims=True)
    return centred * lax.rsqrt(variance + EPSILON)


def gelu_tanh(values):
    return (
        0.5 * values * (1.0 + jnp.tanh(TANH_COEFF * (values + 0.044715 * values * values * values)))
    )


def silu_plain(values):
    return values / (1.0 + jnp.exp(-values))


def modulate(values, shift_term, scale_term):
    return layer_norm(values) * (1.0 + scale_term) + shift_term


def contract_rows(left_matrix, right_matrix):
    return lax.dot_general(
        left_matrix, right_matrix, (((0,), (0,)), ((), ())), preferred_element_type=jnp.float32
    )


def contract_rows_exact(left_matrix, right_matrix):
    return lax.dot_general(
        left_matrix,
        right_matrix,
        (((0,), (0,)), ((), ())),
        precision=HIGH,
        preferred_element_type=jnp.float32,
    )


def times_transposed(left_matrix, right_matrix):
    return lax.dot_general(
        left_matrix, right_matrix, (((1,), (1,)), ((), ())), preferred_element_type=jnp.float32
    )


def gather_weights(w_qkv, w_out, w_fc1, w_fc2):
    return (
        lax.all_gather(w_qkv, "rows", axis=0, tiled=True),
        lax.all_gather(w_out, "rows", axis=0, tiled=True),
        lax.all_gather(w_fc1, "rows", axis=0, tiled=True),
        lax.all_gather(w_fc2, "rows", axis=0, tiled=True),
    )


def shards_plain(
    patches,
    time_table,
    class_table,
    w_ada,
    b_ada,
    w_qkv,
    b_qv,
    w_out,
    b_out,
    w_fc1,
    b_fc1,
    w_fc2,
    b_fc2,
    image_lengths,
    segment_ids,
    bucket_ids,
    class_labels,
    cotangent,
):
    head_parts = lax.axis_size("heads")
    member = lax.axis_index("heads")
    tok_rows = patches.shape[0]
    model_width = patches.shape[1]
    seq_count = segment_ids.shape[0]
    seq_len = segment_ids.shape[1]
    slot_count = image_lengths.shape[1]
    image_count = seq_count * slot_count
    group_rows = tok_rows * head_parts
    head_local = b_qv.shape[0]
    head_size = b_qv.shape[1] // 2
    block_rows = min(BLOCK_LIMIT, seq_len)
    scale_factor = 1.0 / math.sqrt(head_size)
    row_parts = lax.axis_size("rows")
    table_rows = time_table.shape[0]
    ada_width = w_ada.shape[1]
    qkv_cols, out_cols, fc1_cols, fc2_cols = gather_weights(w_qkv, w_out, w_fc1, w_fc2)
    ids_all = lax.all_gather(
        jnp.concatenate([bucket_ids, class_labels], axis=1), "rows", axis=0, tiled=True
    )
    every_slot = row_parts * image_count
    table_places = lax.axis_index("rows") * table_rows + jnp.arange(table_rows, dtype=jnp.int32)
    bucket_hot = (
        ids_all[:, :slot_count].reshape(every_slot)[:, None] == table_places[None, :]
    ).astype(jnp.bfloat16)
    label_hot = (
        ids_all[:, slot_count:].reshape(every_slot)[:, None] == table_places[None, :]
    ).astype(jnp.bfloat16)
    condition = lax.psum(
        jnp.dot(bucket_hot, time_table, preferred_element_type=jnp.float32)
        + jnp.dot(label_hot, class_table, preferred_element_type=jnp.float32),
        "rows",
    )
    silu_value, silu_pull = jax.vjp(silu_plain, condition)
    silu_low = silu_value.astype(jnp.bfloat16)
    mods_part = jnp.dot(silu_low, w_ada, preferred_element_type=jnp.float32)
    mods_cols = lax.psum(mods_part, "heads").reshape(row_parts, image_count, ada_width)
    mods_own = lax.all_to_all(mods_cols, "rows", split_axis=0, concat_axis=0, tiled=True)
    mods_all = mods_own.transpose(1, 0, 2).reshape(
        image_count, row_parts * ada_width
    ) + b_ada.astype(jnp.float32)
    positions = member * tok_rows + jnp.arange(tok_rows, dtype=jnp.int32)
    own_segments = lax.dynamic_slice_in_dim(
        segment_ids.reshape(seq_count * seq_len), member * tok_rows, tok_rows
    )
    token_image = positions // seq_len * slot_count + own_segments
    token_hot = (token_image[:, None] == jnp.arange(image_count, dtype=jnp.int32)[None, :]).astype(
        jnp.float32
    )
    token_mods = [
        jnp.dot(
            token_hot,
            mods_all[:, part_index * model_width : (part_index + 1) * model_width],
            precision=HIGH,
        )
        for part_index in range(6)
    ]
    shift_attn, scale_attn, gate_attn, shift_mlp, scale_mlp, gate_mlp = token_mods
    inputs = patches.astype(jnp.float32)
    first_value, first_pull = jax.vjp(modulate, inputs, shift_attn, scale_attn)
    hidden_one = first_value.astype(jnp.bfloat16)
    rows_one = lax.all_gather(hidden_one, "heads", axis=0, tiled=True)
    zero_bias = jnp.zeros((head_local, head_size), b_qv.dtype)
    qkv_bias = (
        jnp.concatenate([b_qv[:, :head_size], zero_bias, b_qv[:, head_size:]], axis=1)
        .reshape(head_local * 3 * head_size)
        .astype(jnp.float32)
    )
    projected = (jnp.dot(rows_one, qkv_cols, preferred_element_type=jnp.float32) + qkv_bias).astype(
        jnp.bfloat16
    )
    seq_qkv = projected.reshape(seq_count, seq_len, head_local, 3, head_size)
    slot_ends = jnp.cumsum(image_lengths, axis=1)
    places = jnp.arange(seq_len, dtype=jnp.int32)
    image_of = jnp.sum((places[None, :, None] >= slot_ends[:, None, :]).astype(jnp.int32), axis=2)

    def block_scores(query_rows, key_rows, image_rows, image_cols):
        scores = (
            jnp.einsum("qhd,khd->hqk", query_rows, key_rows, preferred_element_type=jnp.float32)
            * scale_factor
        )
        return jnp.where((image_rows[:, None] == image_cols[None, :])[None], scores, MASKED)

    def attend_forward(pieces):
        seq_block, seq_image = pieces
        key_rows = seq_block[:, :, 1]
        value_rows = seq_block[:, :, 2]
        outputs = []
        totals = []
        for row_start in range(0, seq_len, block_rows):
            stop_row = row_start + block_rows
            query_rows = seq_block[row_start:stop_row, :, 0]
            scores = block_scores(query_rows, key_rows, seq_image[row_start:stop_row], seq_image)
            row_peak = jnp.max(scores, axis=2, keepdims=True)
            raised = jnp.exp(scores - row_peak)
            row_total = jnp.sum(raised, axis=2, keepdims=True)
            soft_low = (raised / row_total).astype(jnp.bfloat16)
            outputs.append(
                jnp.einsum(
                    "hqk,khd->qhd", soft_low, value_rows, preferred_element_type=jnp.float32
                ).astype(jnp.bfloat16)
            )
            totals.append((row_peak + jnp.log(row_total))[:, :, 0])
        return (jnp.concatenate(outputs, axis=0), jnp.concatenate(totals, axis=1))

    mixed, log_totals = lax.map(attend_forward, (seq_qkv, image_of))
    mixed_rows = mixed.reshape(group_rows, head_local * head_size)
    attn_out = lax.psum_scatter(
        times_transposed(
            lax.slice_in_dim(mixed_rows, 0, tok_rows * lax.axis_size("heads"), axis=0), out_cols
        ).astype(jnp.bfloat16),
        "heads",
        scatter_dimension=0,
        tiled=True,
    ).astype(jnp.float32) + b_out.astype(jnp.float32)
    after_attn = inputs + gate_attn * attn_out
    second_value, second_pull = jax.vjp(modulate, after_attn, shift_mlp, scale_mlp)
    hidden_two = second_value.astype(jnp.bfloat16)
    rows_two = lax.all_gather(hidden_two, "heads", axis=0, tiled=True)
    inner = jnp.dot(rows_two, fc1_cols, preferred_element_type=jnp.float32) + b_fc1.astype(
        jnp.float32
    )
    gelu_value, gelu_pull = jax.vjp(gelu_tanh, inner)
    active = gelu_value.astype(jnp.bfloat16)
    ffn_out = lax.psum_scatter(
        times_transposed(
            lax.slice_in_dim(active, 0, tok_rows * lax.axis_size("heads"), axis=0), fc2_cols
        ).astype(jnp.bfloat16),
        "heads",
        scatter_dimension=0,
        tiled=True,
    ).astype(jnp.float32) + b_fc2.astype(jnp.float32)
    block_out = (after_attn + gate_mlp * ffn_out).astype(jnp.bfloat16)
    upstream = cotangent.astype(jnp.float32)
    grad_ffn = (gate_mlp * upstream).astype(jnp.bfloat16)
    ffn_rows = lax.all_gather(grad_ffn, "heads", axis=0, tiled=True)
    grad_w_fc2 = contract_rows(ffn_rows, active)
    grad_b_fc2 = jnp.sum(ffn_rows, axis=0, dtype=jnp.float32)
    grad_active = jnp.dot(ffn_rows, fc2_cols, preferred_element_type=jnp.float32)
    grad_inner = gelu_pull(grad_active)[0].astype(jnp.bfloat16)
    grad_w_fc1 = contract_rows(rows_two, grad_inner)
    grad_b_fc1 = jnp.sum(grad_inner, axis=0, dtype=jnp.float32)
    grad_hidden_two = lax.psum_scatter(
        times_transposed(
            lax.slice_in_dim(grad_inner, 0, tok_rows * lax.axis_size("heads"), axis=0), fc1_cols
        ).astype(jnp.bfloat16),
        "heads",
        scatter_dimension=0,
        tiled=True,
    ).astype(jnp.float32)
    grad_after, grad_shift_mlp, grad_scale_mlp = second_pull(grad_hidden_two)
    grad_after = grad_after + upstream
    grad_gate_mlp = upstream * ffn_out
    grad_gate_attn = grad_after * attn_out
    grad_attn = (gate_attn * grad_after).astype(jnp.bfloat16)
    attn_rows_grad = lax.all_gather(grad_attn, "heads", axis=0, tiled=True)
    grad_w_out = contract_rows(attn_rows_grad, mixed_rows)
    grad_b_out = jnp.sum(attn_rows_grad, axis=0, dtype=jnp.float32)
    grad_mixed = jnp.dot(attn_rows_grad, out_cols, preferred_element_type=jnp.float32).astype(
        jnp.bfloat16
    )
    grad_seq = grad_mixed.reshape(seq_count, seq_len, head_local, head_size)

    def attend_backward(pieces):
        seq_block, seq_image, seq_grad, seq_totals = pieces
        key_rows = seq_block[:, :, 1]
        value_rows = seq_block[:, :, 2]
        grad_keys = jnp.zeros(key_rows.shape, jnp.float32)
        grad_values = jnp.zeros(value_rows.shape, jnp.float32)
        grad_queries = []
        for row_start in range(0, seq_len, block_rows):
            stop_row = row_start + block_rows
            query_rows = seq_block[row_start:stop_row, :, 0]
            grad_rows = seq_grad[row_start:stop_row]
            scores = block_scores(query_rows, key_rows, seq_image[row_start:stop_row], seq_image)
            soft_probs = jnp.exp(scores - seq_totals[:, row_start:stop_row, None])
            grad_probs = jnp.einsum(
                "qhd,khd->hqk", grad_rows, value_rows, preferred_element_type=jnp.float32
            )
            inner_sum = jnp.sum(soft_probs * grad_probs, axis=2, keepdims=True)
            grad_scores = (soft_probs * (grad_probs - inner_sum)).astype(jnp.bfloat16)
            grad_queries.append(
                jnp.einsum(
                    "hqk,khd->qhd", grad_scores, key_rows, preferred_element_type=jnp.float32
                )
                * scale_factor
            )
            grad_keys = (
                grad_keys
                + jnp.einsum(
                    "hqk,qhd->khd", grad_scores, query_rows, preferred_element_type=jnp.float32
                )
                * scale_factor
            )
            grad_values = grad_values + jnp.einsum(
                "hqk,qhd->khd",
                soft_probs.astype(jnp.bfloat16),
                grad_rows,
                preferred_element_type=jnp.float32,
            )
        stacked = jnp.stack([jnp.concatenate(grad_queries, axis=0), grad_keys, grad_values], axis=2)
        return stacked.astype(jnp.bfloat16)

    grad_qkv = lax.map(attend_backward, (seq_qkv, image_of, grad_seq, log_totals)).reshape(
        group_rows, head_local * 3 * head_size
    )
    grad_w_qkv = contract_rows(rows_one, grad_qkv)
    bias_terms = jnp.sum(grad_qkv, axis=0, dtype=jnp.float32).reshape(head_local, 3, head_size)
    grad_b_qv = jnp.concatenate([bias_terms[:, 0], bias_terms[:, 2]], axis=1)
    grad_hidden_one = lax.psum_scatter(
        times_transposed(
            lax.slice_in_dim(grad_qkv, 0, tok_rows * lax.axis_size("heads"), axis=0), qkv_cols
        ).astype(jnp.bfloat16),
        "heads",
        scatter_dimension=0,
        tiled=True,
    ).astype(jnp.float32)
    grad_inputs, grad_shift_attn, grad_scale_attn = first_pull(grad_hidden_one)
    grad_patches = grad_inputs + grad_after
    token_grads = (
        grad_shift_attn,
        grad_scale_attn,
        grad_gate_attn,
        grad_shift_mlp,
        grad_scale_mlp,
        grad_gate_mlp,
    )
    mods_grad_part = jnp.concatenate(
        [contract_rows_exact(token_hot, grad_term) for grad_term in token_grads], axis=1
    )
    grad_mods = lax.psum(mods_grad_part.astype(jnp.bfloat16), "heads")
    grad_cols = lax.all_to_all(
        grad_mods.reshape(image_count, row_parts, ada_width).transpose(1, 0, 2),
        "rows",
        split_axis=0,
        concat_axis=0,
        tiled=True,
    ).reshape(every_slot, ada_width)
    grad_w_ada = contract_rows(silu_low, grad_cols)
    grad_b_ada = jnp.sum(grad_cols, axis=0, dtype=jnp.float32)
    grad_silu = lax.psum(times_transposed(grad_cols, w_ada), "rows")
    grad_condition = silu_pull(grad_silu)[0]
    grad_time = contract_rows_exact(bucket_hot.astype(jnp.float32), grad_condition)
    grad_class = contract_rows_exact(label_hot.astype(jnp.float32), grad_condition)

    def row_reduced(partial):
        return lax.psum_scatter(
            partial.astype(jnp.bfloat16), "rows", scatter_dimension=0, tiled=True
        ).astype(jnp.float32)

    grad_w_qkv, grad_w_out, grad_w_fc1, grad_w_fc2 = (
        row_reduced(grad_w_qkv),
        row_reduced(grad_w_out),
        row_reduced(grad_w_fc1),
        row_reduced(grad_w_fc2),
    )
    bias_sizes = (grad_b_qv.size, grad_b_fc1.size, grad_b_out.size, grad_b_fc2.size)
    bias_all = lax.psum(
        jnp.concatenate([grad_b_qv.reshape(-1), grad_b_fc1, grad_b_out, grad_b_fc2]), "rows"
    )
    edges = [sum(bias_sizes[:step]) for step in range(5)]
    bias_rows = model_width // row_parts
    row_start = lax.axis_index("rows") * bias_rows
    grad_b_qv = bias_all[edges[0] : edges[1]].reshape(grad_b_qv.shape)
    grad_b_fc1 = bias_all[edges[1] : edges[2]]
    grad_b_out = lax.dynamic_slice_in_dim(bias_all[edges[2] : edges[3]], row_start, bias_rows)
    grad_b_fc2 = lax.dynamic_slice_in_dim(bias_all[edges[3] : edges[4]], row_start, bias_rows)
    return (
        block_out,
        grad_patches,
        grad_time,
        grad_class,
        grad_w_ada,
        grad_b_ada,
        grad_w_qkv,
        grad_b_qv,
        grad_w_out,
        grad_b_out,
        grad_w_fc1,
        grad_b_fc1,
        grad_w_fc2,
        grad_b_fc2,
    )


MESH = pl.DeviceIdType.MESH
ROW_PARTS = 8
HEAD_PARTS = 4
SLOT_ROWS = 8
VMEM_SPEC = pl.BlockSpec(memory_space=pltpu.VMEM)
ANY_SPEC = pl.BlockSpec(memory_space=pl.ANY)
DMA = pltpu.SemaphoreType.DMA
GRANT = 60 * 1024 * 1024


def places():
    row = lax.axis_index("rows")
    member = lax.axis_index("heads")
    sibling = member + 1 - 2 * lax.rem(member, 2)
    partner = lax.rem(member + 2, HEAD_PARTS)
    opposite = lax.rem(sibling + 2, HEAD_PARTS)
    return row, member, sibling, partner, opposite


def greet(row_steps, head_members):
    barrier = pltpu.get_barrier_semaphore()
    row = lax.axis_index("rows")
    for step in row_steps:
        pl.semaphore_signal(
            barrier,
            inc=1,
            device_id={"rows": lax.rem(row + step, ROW_PARTS)},
            device_id_type=MESH,
        )
    for other in head_members:
        pl.semaphore_signal(barrier, inc=1, device_id={"heads": other}, device_id_type=MESH)
    pl.semaphore_wait(barrier, len(row_steps) + len(head_members))


def to_row(source, target, send, recv, row):
    return pltpu.make_async_remote_copy(
        src_ref=source,
        dst_ref=target,
        send_sem=send,
        recv_sem=recv,
        device_id={"rows": row},
        device_id_type=MESH,
    )


def to_head(source, target, send, recv, member):
    return pltpu.make_async_remote_copy(
        src_ref=source,
        dst_ref=target,
        send_sem=send,
        recv_sem=recv,
        device_id={"heads": member},
        device_id_type=MESH,
    )


class RowGather:
    def __init__(self, shard, full, sends, recvs, local_sem, chunks):
        self.row = lax.axis_index("rows")
        self.level = self.row // 2
        self.side = lax.rem(self.row, 2)
        self.mate = self.row + 1 - 2 * self.side
        above = lax.rem(self.level + 1, 4) * 2 + self.side
        size = shard.shape[0] // chunks
        self.own = pltpu.make_async_copy(shard, full.at[self.row], local_sem)
        self.straight = []
        self.across = []
        for chunk in range(chunks):
            part = pl.ds(chunk * size, size)
            straight = []
            across = []
            for step in range(4):
                origin = lax.rem(self.level + 4 - step, 4) * 2 + self.side
                source = shard.at[part] if step == 0 else full.at[origin, part]
                target = full.at[origin, part]
                across.append(
                    to_row(
                        source,
                        target,
                        sends.at[chunk, 3 + step],
                        recvs.at[chunk, 3 + step],
                        self.mate,
                    )
                )
                if step < 3:
                    straight.append(
                        to_row(
                            source, target, sends.at[chunk, step], recvs.at[chunk, step], above
                        )
                    )
            self.straight.append(straight)
            self.across.append(across)

    def start(self, chunk):
        self.straight[chunk][0].start()
        self.across[chunk][0].start()

    def hop(self, chunk, step):
        self.straight[chunk][step].wait_recv()
        if step < 2:
            self.straight[chunk][step + 1].start()
        self.across[chunk][step + 1].start()

    def finish(self):
        self.own.wait()
        for straight, across in zip(self.straight, self.across):
            for copy in straight:
                copy.wait_send()
            for copy in across:
                copy.wait()


class HeadGather:
    def __init__(self, block, full, sends, recvs, local_sem):
        row, member, sibling, partner, opposite = places()
        self.own = None
        if block is None:
            block = full.at[member]
        else:
            self.own = pltpu.make_async_copy(block, full.at[member], local_sem)
        self.beside = to_head(block, full.at[member], sends.at[0], recvs.at[0], sibling)
        self.across = to_head(block, full.at[member], sends.at[1], recvs.at[1], partner)
        self.onward = to_head(
            full.at[partner], full.at[partner], sends.at[2], recvs.at[2], sibling
        )

    def start(self):
        self.across.start()
        self.beside.start()
        if self.own is not None:
            self.own.start()

    def wait_sibling(self):
        self.beside.wait_recv()

    def wait_partner(self):
        self.across.wait_recv()
        self.onward.start()

    def wait_opposite(self):
        self.onward.wait_recv()

    def finish(self):
        if self.own is not None:
            self.own.wait()
        self.beside.wait_send()
        self.across.wait_send()
        self.onward.wait_send()


def front_kernel(
    bucket_ref,
    label_ref,
    time_ref,
    class_ref,
    ada_ref,
    patches_ref,
    qkv_ref,
    qkv_full,
    patches_full,
    cond_all,
    mods_ref,
    ids_all,
    ids_own,
    cond_part,
    cond_in,
    mods_part,
    mods_in,
    mods_sibling,
    mods_pair,
    mods_partner,
    small_send,
    small_recv,
    pair_send,
    pair_recv,
    head_send,
    head_recv,
    qkv_send,
    qkv_recv,
    local_sems,
):
    row, member, sibling, partner, opposite = places()
    greet(range(1, ROW_PARTS), (sibling, partner))
    others = [(step, lax.rem(row + step, ROW_PARTS)) for step in range(1, ROW_PARTS)]

    def spread(stage, source_of, target):
        copies = []
        for step, other in others:
            copy = to_row(
                source_of(other),
                target.at[row],
                small_send.at[stage, step - 1],
                small_recv.at[stage, step - 1],
                other,
            )
            copy.start()
            copies.append(copy)
        return copies

    def settle(copies):
        for copy in copies:
            copy.wait()

    table_rows = time_ref.shape[1]
    slots = ROW_PARTS * SLOT_ROWS
    ids_own[...] = jnp.full_like(ids_own, -1)
    for start, chosen in ((0, bucket_ref), (SLOT_ROWS, label_ref)):
        for slot in range(chosen.shape[1]):
            ids_own[start + slot : start + slot + 1] = jnp.broadcast_to(
                chosen[0:1, slot : slot + 1], (1, table_rows)
            )
    ids_copies = spread(0, lambda other: ids_own, ids_all)
    gather_qkv = RowGather(qkv_ref, qkv_full, qkv_send, qkv_recv, local_sems.at[0], 3)
    gather_patches = HeadGather(patches_ref, patches_full, head_send, head_recv, local_sems.at[1])
    gather_patches.start()
    gather_qkv.own.start()
    gather_qkv.start(0)
    ids_all[row] = ids_own[...]
    settle(ids_copies)
    bucket_hot, label_hot = (hot.astype(jnp.bfloat16) for hot in table_hots(ids_all, table_rows))
    found = times_transposed(bucket_hot, time_ref[...]) + times_transposed(
        label_hot, class_ref[...]
    )
    cond_part[...] = found.reshape(cond_part.shape)
    copies = spread(1, lambda other: cond_part.at[other], cond_in)
    gather_qkv.start(1)
    cond_in[row] = cond_part[row]
    gather_qkv.hop(0, 0)
    settle(copies)
    condition = jnp.sum(cond_in[...], axis=0)
    cond_all[row] = condition
    cond_part[row] = condition
    copies = spread(2, lambda other: cond_part.at[row], cond_all)
    gather_qkv.start(2)
    gather_qkv.hop(1, 0)
    gather_qkv.hop(0, 1)
    settle(copies)
    every = cond_all[...].reshape(slots, cond_all.shape[2])
    silu_low = (every / (1.0 + jnp.exp(-every))).astype(jnp.bfloat16)
    mods_part[...] = jnp.dot(
        silu_low, ada_ref[...], preferred_element_type=jnp.float32
    ).reshape(mods_part.shape)
    copies = spread(3, lambda other: mods_part.at[other], mods_in)
    mods_in[row] = mods_part[row]
    gather_qkv.hop(2, 0)
    gather_qkv.hop(1, 1)
    gather_qkv.hop(0, 2)
    settle(copies)
    beside = to_head(mods_in, mods_sibling, pair_send.at[0], pair_recv.at[0], sibling)
    beside.start()
    gather_patches.wait_sibling()
    beside.wait()
    mods_pair[...] = mods_in[...] + mods_sibling[...]
    across = to_head(mods_pair, mods_partner, pair_send.at[1], pair_recv.at[1], partner)
    across.start()
    gather_patches.wait_partner()
    gather_qkv.hop(2, 1)
    gather_qkv.hop(1, 2)
    across.wait()
    mods_ref[...] = mods_pair[...] + mods_partner[...]
    gather_qkv.hop(2, 2)
    gather_patches.wait_opposite()
    gather_patches.finish()
    gather_qkv.finish()


def front(bucket_ids, class_labels, time_columns, class_columns, w_ada, patches, w_qkv):
    depth, ada_width = w_ada.shape
    shape = jax.ShapeDtypeStruct
    slotted = (ROW_PARTS, SLOT_ROWS)
    wide = pltpu.VMEM(slotted + (ada_width,), jnp.float32)
    narrow = pltpu.VMEM(slotted + (depth,), jnp.float32)
    return pl.pallas_call(
        front_kernel,
        out_shape=(
            shape((ROW_PARTS,) + w_qkv.shape, jnp.bfloat16),
            shape((HEAD_PARTS,) + patches.shape, jnp.bfloat16),
            shape(slotted + (depth,), jnp.float32),
            shape(slotted + (ada_width,), jnp.float32),
            shape((ROW_PARTS, 2 * SLOT_ROWS, time_columns.shape[1]), jnp.int32),
        ),
        in_specs=[VMEM_SPEC] * 7,
        out_specs=[ANY_SPEC] * 2 + [VMEM_SPEC] * 3,
        scratch_shapes=[pltpu.VMEM((2 * SLOT_ROWS, time_columns.shape[1]), jnp.int32)]
        + [narrow] * 2
        + [wide] * 5
        + [
            DMA((4, 7)),
            DMA((4, 7)),
            DMA((2,)),
            DMA((2,)),
            DMA((3,)),
            DMA((3,)),
            DMA((3, 7)),
            DMA((3, 7)),
            DMA((2,)),
        ],
        compiler_params=pltpu.CompilerParams(
            collective_id=0, has_side_effects=True, vmem_limit_bytes=GRANT
        ),
        name="front",
    )(bucket_ids, class_labels, time_columns, class_columns, w_ada, patches, w_qkv)


class HeadReduce:
    def __init__(self, partial, beside_in, pair, across_in, sends, recvs):
        row, member, sibling, partner, opposite = places()
        self.member = member
        self.partner = partner
        self.partial = partial
        self.beside_in = beside_in
        self.pair = pair
        self.across_in = across_in
        self.first = to_head(
            partial.at[opposite], beside_in.at[1], sends.at[0], recvs.at[0], sibling
        )
        self.second = to_head(
            partial.at[sibling], beside_in.at[0], sends.at[1], recvs.at[1], sibling
        )
        self.across = to_head(pair, across_in, sends.at[2], recvs.at[2], partner)

    def start(self):
        self.first.start()
        self.second.start()

    def send_pair(self):
        self.first.wait_recv()
        self.pair[...] = (
            self.partial[self.partner].astype(jnp.float32)
            + self.beside_in[1].astype(jnp.float32)
        ).astype(jnp.bfloat16)
        self.across.start()

    def settle(self):
        self.second.wait_recv()
        self.across.wait_recv()

    def rows(self, part):
        return (
            self.partial[self.member, part].astype(jnp.float32)
            + self.beside_in[0, part].astype(jnp.float32)
            + self.across_in[part].astype(jnp.float32)
        )

    def finish(self):
        self.first.wait_send()
        self.second.wait_send()
        self.across.wait_send()


class RowReduce:
    def __init__(self, partial, chunk, buffers, total, sends, recvs):
        row = lax.axis_index("rows")
        self.level = row // 2
        self.side = lax.rem(row, 2)
        mate = row + 1 - 2 * self.side
        self.partial = partial
        self.mate_in, self.pair, self.straight_in = buffers
        self.total = total
        size = total.shape[0]
        self.part = pl.ds(chunk * size, size)
        self.beside = to_row(
            partial.at[:, 1 - self.side, self.part], self.mate_in, sends.at[0], recvs.at[0], mate
        )
        self.straight = []
        above = lax.rem(self.level + 1, 4) * 2 + self.side
        for step in range(3):
            self.straight.append(
                to_row(
                    self.pair.at[lax.rem(self.level + 3 - step, 4)],
                    self.straight_in.at[step],
                    sends.at[1 + step],
                    recvs.at[1 + step],
                    above,
                )
            )

    def start(self):
        self.beside.start()

    def send_pair(self):
        self.beside.wait_recv()

        def one(level, carry):
            self.pair[level] = (
                self.partial[level, self.side, self.part].astype(jnp.float32)
                + self.mate_in[level].astype(jnp.float32)
            ).astype(jnp.bfloat16)
            return carry

        lax.fori_loop(0, 4, one, 0)
        self.straight[0].start()

    def hop(self, step):
        self.straight[step].wait_recv()
        block = lax.rem(self.level + 2 - step, 4)
        self.pair[block] = (
            self.pair[block].astype(jnp.float32) + self.straight_in[step].astype(jnp.float32)
        ).astype(jnp.bfloat16)
        self.straight[step + 1].start()

    def finish(self):
        self.straight[2].wait_recv()
        self.total[...] = self.pair[self.level].astype(jnp.float32) + self.straight_in[2].astype(
            jnp.float32
        )
        self.beside.wait_send()
        for copy in self.straight:
            copy.wait_send()


def row_reduces(jobs, reducing):
    buffers, sends, recvs = reducing[:-2], reducing[-2], reducing[-1]
    return [
        RowReduce(
            partial,
            chunk,
            buffers[3 * place : 3 * place + 3],
            total,
            sends.at[place],
            recvs.at[place],
        )
        for place, (partial, chunk, total) in enumerate(jobs)
    ]


def reduce_scratch(sizes):
    landing = []
    for rows, columns in sizes:
        landing += [
            pltpu.VMEM((4, rows, columns), jnp.bfloat16),
            pltpu.VMEM((4, rows, columns), jnp.bfloat16),
            pltpu.VMEM((3, rows, columns), jnp.bfloat16),
        ]
    return landing + [DMA((len(sizes), 4)), DMA((len(sizes), 4))]


def picked(vectors, part_index, segments, width):
    wide = jnp.concatenate([segments] * (width // segments.shape[1]), axis=1)
    slot_count = vectors.shape[1]
    chosen = vectors[part_index, slot_count - 1 : slot_count]
    for slot in range(slot_count - 2, -1, -1):
        chosen = jnp.where(wide == slot, vectors[part_index, slot : slot + 1], chosen)
    return chosen


def slot_hot(segment_row, start):
    chosen = segment_row[:, pl.ds(pl.multiple_of(start, 128), 128)]
    slots = lax.broadcasted_iota(jnp.int32, (SLOT_ROWS, 128), 0)
    return (jnp.broadcast_to(chosen, slots.shape) == slots).astype(jnp.float32)


def table_hots(ids_all, table_rows):
    slots = ROW_PARTS * SLOT_ROWS
    table_places = lax.axis_index("rows") * table_rows + lax.broadcasted_iota(
        jnp.int32, (slots, table_rows), 1
    )
    return [
        ids_all[:, start : start + SLOT_ROWS].reshape(slots, table_rows) == table_places
        for start in (0, SLOT_ROWS)
    ]


def centre_rows(values):
    centred = values - jnp.mean(values, axis=1, keepdims=True)
    factor = lax.rsqrt(jnp.mean(centred * centred, axis=1, keepdims=True) + EPSILON)
    return centred * factor, factor


def weight_grad(left, right, target):
    blocks, tok_rows, depth = left.shape
    height = blocks * tok_rows
    flat = target.reshape(depth, target.shape[3])
    third = depth // 3

    def some(step, carry):
        columns = pl.ds(pl.multiple_of(step * third, 128), third)
        flat[columns] = contract_rows(
            left[:, :, columns].reshape(height, third),
            right[...].reshape(height, right.shape[2]),
        ).astype(jnp.bfloat16)
        return carry

    lax.fori_loop(0, 3, some, 0)


def core_kernel(
    patches_full,
    qkv_ref,
    out_shard,
    fc1_shard,
    fc2_shard,
    cotangent_ref,
    patches_ref,
    segment_row,
    mods_ref,
    bias_ref,
    value_bias,
    segments_ref,
    vectors_ref,
    normed_rows,
    parts,
    totals_out,
    mixed,
    out_w,
    active_rows,
    after_ref,
    after_grad,
    attn_grad,
    slot_sums,
    bias_sums,
    fc2_rest,
    fc1_part,
    fc2_head,
    fc2_neck,
    qkv_bias,
    head_bias,
    ffn_rows,
    hidden_rows,
    inner_grad,
    fc2_part,
    inner_bias,
    ffn_bias,
    out_full,
    fc1_full,
    fc2_full,
    active_grad,
    value_columns,
    head_mixed,
    bias,
    group_part,
    beside_in,
    pair_rows,
    across_in,
    attn_out,
    gather_send,
    gather_recv,
    reduce_send,
    reduce_recv,
    out_send,
    out_recv,
    fc1_send,
    fc1_recv,
    fc2_send,
    fc2_recv,
    local_sems,
    *reducing,
):
    row, member, sibling, partner, opposite = places()
    direction = sibling - member
    greet(range(1, ROW_PARTS), (sibling, partner))
    tok_rows, model_width = patches_ref.shape
    blocks = normed_rows.shape[0]
    seq_len = blocks * tok_rows
    width = qkv_ref.shape[1]
    head_local = totals_out.shape[0]
    head_size = width // (3 * head_local)
    scale_factor = 1.0 / math.sqrt(head_size)
    loads = [
        pltpu.make_async_copy(patches_full.at[block], normed_rows.at[block], local_sems.at[block])
        for block in range(blocks)
    ]
    for load in loads:
        load.start()
    gather_out = RowGather(out_shard, out_full, out_send, out_recv, local_sems.at[4], 1)
    gather_fc1 = RowGather(fc1_shard, fc1_full, fc1_send, fc1_recv, local_sems.at[5], 3)
    gather_fc2 = RowGather(fc2_shard, fc2_full, fc2_send, fc2_recv, local_sems.at[6], 3)
    gather_cotangent = HeadGather(
        cotangent_ref, ffn_rows, gather_send.at[2], gather_recv.at[2], local_sems.at[7]
    )
    gather_out.own.start()
    gather_out.start(0)
    gather_fc1.own.start()
    gather_fc2.own.start()
    for chunk in range(3):
        gather_fc1.start(chunk)
    gather_cotangent.start()
    reduce_attn = HeadReduce(
        group_part, beside_in, pair_rows, across_in, reduce_send.at[0], reduce_recv.at[0]
    )
    reduce_hidden = HeadReduce(
        group_part, beside_in, pair_rows, across_in, reduce_send.at[1], reduce_recv.at[1]
    )
    gather_hidden = HeadGather(None, hidden_rows, gather_send.at[0], gather_recv.at[0], None)
    gather_grad = HeadGather(None, attn_grad, gather_send.at[1], gather_recv.at[1], None)
    parts[...] = jnp.zeros_like(parts)
    segments_ref[...] = (
        jnp.broadcast_to(segment_row[...].astype(jnp.float32), (128, seq_len))
        .T.astype(jnp.int32)
    )
    slot_count = vectors_ref.shape[1]
    fine = mods_ref.shape[2] // 3
    for unit in range(3 * ROW_PARTS):
        part_index, within = divmod(unit * fine, model_width)
        span = slice(within, within + fine)
        vectors_ref[part_index, :, span] = mods_ref[
            unit // 3, 0:slot_count, unit % 3 * fine : (unit % 3 + 1) * fine
        ]
    for part_index in range(6):
        vectors_ref[part_index] += bias_ref[part_index : part_index + 1]
    qkv_bias[...] = jnp.zeros_like(qkv_bias)
    head_bias[...] = value_bias[...].astype(jnp.float32)
    for head in range(head_local):
        for place in (0, 2):
            start = (3 * head + place) * head_size
            taken = slice(place // 2 * head_size, (place // 2 + 1) * head_size)
            qkv_bias[:, start : start + head_size] = head_bias[head : head + 1, taken]
    for load in loads:
        load.wait()

    def first_norm(step, carry):
        block = step // 2
        part = pl.ds(pl.multiple_of(lax.rem(step, 2) * 128, 128), 128)
        segments = segments_ref[pl.ds(pl.multiple_of(step * 128, 128), 128)]
        normed, _ = centre_rows(normed_rows[block, part].astype(jnp.float32))
        normed_rows[block, part] = (
            normed * (1.0 + picked(vectors_ref, 1, segments, model_width))
            + picked(vectors_ref, 0, segments, model_width)
        ).astype(jnp.bfloat16)
        return carry

    lax.fori_loop(0, 2 * blocks, first_norm, 0)
    gather_out.hop(0, 0)
    gather_fc1.hop(0, 0)
    gather_fc1.hop(1, 0)
    gather_fc2.start(0)

    def project_in(block, carry):
        rows = pl.ds(pl.multiple_of(block * tok_rows, tok_rows), tok_rows)
        active_grad[0, :, 0:width] = (
            jnp.dot(normed_rows[block], qkv_ref[...], preferred_element_type=jnp.float32)
            + qkv_bias[...]
        )
        for part in range(3 * head_local):
            parts[part, rows, 0:head_size] = active_grad[
                0, :, part * head_size : (part + 1) * head_size
            ].astype(jnp.bfloat16)
        return carry

    lax.fori_loop(0, blocks, project_in, 0)
    gather_out.hop(0, 1)
    gather_fc1.hop(2, 0)
    gather_fc1.hop(0, 1)
    gather_fc2.start(1)

    def turn(head, carry):
        value_columns[head] = parts[3 * head + 2].astype(jnp.float32).T.astype(jnp.bfloat16)
        return carry

    lax.fori_loop(0, head_local, turn, 0)

    def attend(block):
        rows = pl.ds(pl.multiple_of(block * tok_rows, tok_rows), tok_rows)
        keys = jnp.concatenate([segments_ref[...]] * (tok_rows // 128), axis=1)
        same = keys == jnp.broadcast_to(segment_row[:, rows], keys.shape)
        bias[...] = jnp.where(same, 0.0, MASKED)

        def one_head(head, carry):
            scores = (
                times_transposed(parts[3 * head + 1], parts[3 * head, rows]) * scale_factor
                + bias[...]
            )
            peak = jnp.max(scores, axis=0, keepdims=True)
            raised = jnp.exp(scores - peak)
            total = jnp.sum(raised, axis=0, keepdims=True)
            totals_out[head, block] = peak + jnp.log(total)
            head_mixed[head] = jnp.dot(
                value_columns[head],
                (raised * (1.0 / total)).astype(jnp.bfloat16),
                preferred_element_type=jnp.float32,
            ).T
            return carry

        lax.fori_loop(0, head_local, one_head, 0)
        for head in range(head_local):
            active_grad[1, :, head * head_size : (head + 1) * head_size] = head_mixed[
                head, :, 0:head_size
            ]
        mixed[block] = active_grad[1, :, 0 : head_local * head_size].astype(jnp.bfloat16)

    def project(block):
        group_part[block] = times_transposed(mixed[block], out_w[...]).astype(jnp.bfloat16)

    attend(opposite)
    gather_out.hop(0, 2)
    gather_fc1.hop(1, 1)
    gather_fc2.hop(0, 0)
    gather_fc2.start(2)
    attend(partner)
    gather_fc1.hop(2, 1)
    gather_fc1.hop(0, 2)
    gather_out.finish()
    out_w[...] = out_full[...].reshape(out_w.shape)
    project(opposite)
    reduce_attn.first.start()
    project(partner)
    reduce_attn.send_pair()
    gather_fc2.hop(1, 0)
    attend(sibling)
    gather_fc1.hop(1, 2)
    gather_fc2.hop(0, 1)
    gather_fc2.hop(2, 0)
    attend(member)
    gather_fc1.hop(2, 2)
    gather_fc2.hop(1, 1)
    project(sibling)
    reduce_attn.second.start()
    project(member)
    gather_cotangent.wait_sibling()
    gather_cotangent.wait_partner()
    gather_cotangent.wait_opposite()
    gather_cotangent.finish()

    def scale_cotangent(step, carry):
        block = step // 2
        part = pl.ds(pl.multiple_of(lax.rem(step, 2) * 128, 128), 128)
        segments = segments_ref[pl.ds(pl.multiple_of(step * 128, 128), 128)]
        grad = (
            picked(vectors_ref, 5, segments, model_width)
            * ffn_rows[block, part].astype(jnp.float32)
        ).astype(jnp.bfloat16)
        ffn_rows[block, part] = grad
        ffn_bias[...] += jnp.sum(grad.astype(jnp.float32).reshape(16, 8, model_width), axis=0)
        return carry

    ffn_bias[...] = jnp.zeros_like(ffn_bias)
    lax.fori_loop(0, 2 * blocks, scale_cotangent, 0)
    gather_fc2.hop(0, 2)
    gather_fc2.hop(2, 1)
    reduce_attn.settle()

    def second_norm(block, carry):
        part = pl.ds(pl.multiple_of(block * 128, 128), 128)
        segments = segments_ref[
            pl.ds(pl.multiple_of(member * tok_rows + block * 128, 128), 128)
        ]
        out = reduce_attn.rows(part) + bias_ref[6:7]
        after = patches_ref[part].astype(jnp.float32) + (
            picked(vectors_ref, 2, segments, model_width) * out
        )
        attn_out[part] = out
        after_ref[part] = after
        normed, _ = centre_rows(after)
        hidden_rows[member, part] = (
            normed * (1.0 + picked(vectors_ref, 4, segments, model_width))
            + picked(vectors_ref, 3, segments, model_width)
        ).astype(jnp.bfloat16)
        return carry

    lax.fori_loop(0, tok_rows // 128, second_norm, 0)
    gather_hidden.start()
    reduce_attn.finish()
    gather_fc2.hop(1, 2)
    gather_fc2.hop(2, 2)
    gather_fc1.finish()
    hidden_width = active_rows.shape[2]
    fc1 = fc1_full.reshape(model_width, hidden_width)
    fc2 = fc2_full.reshape(model_width, hidden_width)

    inner_bias[...] = jnp.zeros_like(inner_bias)

    def feed(block, carry):
        inner = jnp.dot(
            hidden_rows[block], fc1[...], preferred_element_type=jnp.float32
        ) + bias_ref[7:8]
        square = inner * inner
        bent = jnp.tanh(TANH_COEFF * (inner + 0.044715 * square * inner))
        half = 0.5 * (1.0 + bent)
        active_rows[block] = (inner * half).astype(jnp.bfloat16)
        active_grad[block] = half + 0.5 * inner * (1.0 - bent * bent) * (
            TANH_COEFF * (1.0 + 3.0 * 0.044715 * square)
        )
        return carry

    def through_fc2(block, carry):
        grad = (
            jnp.dot(ffn_rows[block], fc2[...], preferred_element_type=jnp.float32)
            * active_grad[block]
        ).astype(jnp.bfloat16)
        inner_grad[block] = grad
        inner_bias[...] += jnp.sum(
            grad.astype(jnp.float32).reshape(tok_rows // 8, 8, hidden_width), axis=0
        )
        return carry

    def return_fc1(block, carry):
        group_part[block] = times_transposed(inner_grad[block], fc1[...]).astype(jnp.bfloat16)
        return carry

    gather_hidden.wait_sibling()
    lax.fori_loop(0, 2, lambda step, carry: feed(member + step * direction, carry), 0)
    gather_hidden.wait_partner()
    gather_hidden.wait_opposite()
    lax.fori_loop(0, 2, lambda step, carry: feed(opposite - step * direction, carry), 0)
    gather_fc2.finish()

    def turn_back(block, carry):
        through_fc2(block, carry)
        return return_fc1(block, carry)

    lax.fori_loop(0, 2, lambda step, carry: turn_back(opposite - step * direction, carry), 0)
    reduce_hidden.first.start()
    reduce_hidden.send_pair()
    lax.fori_loop(0, 2, lambda step, carry: turn_back(sibling - step * direction, carry), 0)
    reduce_hidden.second.start()

    def forward_fc2(block, carry):
        active_rows[block] = times_transposed(active_rows[block], fc2[...]).astype(jnp.bfloat16)
        return carry

    weight_grad(ffn_rows, active_rows, fc2_part)
    third = fc2_rest.shape[2]
    fc2_rest[...] = fc2_part[:, :, 2 * third : 3 * third]
    reduces = row_reduces(((fc2_part, 0, fc2_head), (fc2_part, 1, fc2_neck)), reducing)
    for unit in reduces:
        unit.start()
    lax.fori_loop(0, HEAD_PARTS, forward_fc2, 0)
    slot_sums[...] = jnp.zeros_like(slot_sums)
    reduce_hidden.settle()

    def second_back(block, carry):
        part = pl.ds(pl.multiple_of(block * 128, 128), 128)
        segments = segments_ref[
            pl.ds(pl.multiple_of(member * tok_rows + block * 128, 128), 128)
        ]
        grad = reduce_hidden.rows(part)
        normed, factor = centre_rows(after_ref[part])
        weighted = grad * (1.0 + picked(vectors_ref, 4, segments, model_width))
        total = cotangent_ref[part].astype(jnp.float32) + factor * (
            weighted
            - jnp.mean(weighted, axis=1, keepdims=True)
            - normed * jnp.mean(weighted * normed, axis=1, keepdims=True)
        )
        after_grad[part] = total
        attn_grad[member, part] = (
            picked(vectors_ref, 2, segments, model_width) * total
        ).astype(jnp.bfloat16)
        hot = slot_hot(segment_row, member * tok_rows + block * 128)
        for index, term in enumerate((total * attn_out[part], grad, grad * normed)):
            slot_sums[index] += jnp.dot(
                hot, term, precision=HIGH, preferred_element_type=jnp.float32
            )
        return carry

    lax.fori_loop(0, tok_rows // 128, second_back, 0)
    gather_grad.start()
    weight_grad(hidden_rows, inner_grad, fc1_part)
    reduces[0].send_pair()
    bias_sums[...] = jnp.zeros_like(bias_sums)
    bias_sums[0:1] = jnp.sum(inner_bias[...], axis=0, keepdims=True)
    bias_sums[1:2] = jnp.sum(ffn_bias[...], axis=0, keepdims=True)
    gather_grad.wait_sibling()
    reduces[0].hop(0)
    reduces[0].hop(1)
    reduces[1].send_pair()
    gather_grad.wait_partner()
    gather_grad.wait_opposite()
    reduces[1].hop(0)
    reduces[1].hop(1)
    for unit in reduces:
        unit.finish()
    gather_hidden.finish()
    gather_grad.finish()
    reduce_hidden.finish()


def core(slot_count, head_size, *args):
    shape = jax.ShapeDtypeStruct
    patches_full, w_qkv, out_shard, fc1_shard = args[:4]
    blocks, tok_rows, model_width = patches_full.shape
    seq_len = blocks * tok_rows
    out_width = out_shard.shape[1]
    width_part, hidden_width = fc1_shard.shape
    third = width_part // 3
    head_local = out_width // head_size
    low = jnp.bfloat16
    full = jnp.float32
    rows_low = shape((blocks, tok_rows, model_width), low)
    own = shape((tok_rows, model_width), full)
    own_low = pltpu.VMEM((tok_rows, model_width), low)
    group_low = pltpu.VMEM((blocks, tok_rows, model_width), low)
    hidden_low = pltpu.VMEM((blocks, tok_rows, hidden_width), low)
    part_low = (4, 2, width_part, hidden_width)
    return pl.pallas_call(
        core_kernel,
        out_shape=[
            shape((seq_len, 128), jnp.int32),
            shape((6, slot_count, model_width), full),
            rows_low,
            shape((3 * head_local, seq_len, HEAD_LANES), low),
            shape((head_local, blocks, 1, tok_rows), full),
            shape((blocks, tok_rows, out_width), low),
            shape((model_width, out_width), low),
            rows_low,
            own,
            own,
            rows_low,
            shape((3, SLOT_ROWS, model_width), full),
            shape((8, hidden_width), full),
            shape((4, 2, third, hidden_width), low),
            shape(part_low, low),
            shape((third, hidden_width), full),
            shape((third, hidden_width), full),
        ],
        in_specs=[ANY_SPEC] + [VMEM_SPEC] * 10,
        out_specs=[VMEM_SPEC] * 17,
        scratch_shapes=[
            pltpu.VMEM((1, args[1].shape[1]), full),
            pltpu.VMEM(args[-1].shape, full),
            group_low,
            group_low,
            hidden_low,
            pltpu.VMEM(part_low, low),
            pltpu.VMEM((8, hidden_width), full),
            pltpu.VMEM((8, model_width), full),
            pltpu.VMEM((ROW_PARTS,) + out_shard.shape, low),
            pltpu.VMEM((ROW_PARTS,) + fc1_shard.shape, low),
            pltpu.VMEM((ROW_PARTS,) + fc1_shard.shape, low),
            pltpu.VMEM((blocks, tok_rows, hidden_width), full),
            pltpu.VMEM((head_local, HEAD_LANES, seq_len), low),
            pltpu.VMEM((head_local, tok_rows, HEAD_LANES), full),
            pltpu.VMEM((seq_len, tok_rows), full),
            group_low,
            pltpu.VMEM((2, tok_rows, model_width), low),
            own_low,
            own_low,
            pltpu.VMEM((tok_rows, model_width), full),
            DMA((3, 3)),
            DMA((3, 3)),
            DMA((2, 3)),
            DMA((2, 3)),
            DMA((1, 7)),
            DMA((1, 7)),
            DMA((3, 7)),
            DMA((3, 7)),
            DMA((3, 7)),
            DMA((3, 7)),
            DMA((8,)),
        ]
        + reduce_scratch([(third, hidden_width)] * 2),
        compiler_params=pltpu.CompilerParams(
            collective_id=2, has_side_effects=True, vmem_limit_bytes=67_000_000
        ),
        name="core",
    )(*args)


HEAD_LANES = 128


def rear_kernel(
    parts,
    grad_ref,
    out_ref,
    totals_ref,
    segment_row,
    segments_ref,
    fc2_part,
    fc1_part,
    hidden_rows,
    qkv_ref,
    mixed_ref,
    bias_ref,
    patches_ref,
    after_ref,
    vectors_ref,
    sums_ref,
    condition_ref,
    ids_all,
    ada_ref,
    ffn_ref,
    block_ref,
    cotangent_ref,
    bias_rows,
    fc2_head,
    fc2_neck,
    block_out,
    patches_grad,
    time_grad,
    class_grad,
    ada_grad,
    ada_bias,
    fc2_grad,
    fc1_grad,
    qkv_grad,
    out_grad,
    bias_sum,
    mixed_grad,
    key_columns,
    grad_keys,
    grad_values,
    bias,
    packed,
    packed_grad,
    hidden_part,
    qkv_part,
    out_part,
    bias_own,
    beside_in,
    pair_rows,
    across_in,
    ffn_beside,
    ffn_pair,
    ffn_across,
    slot_sums,
    mods_own,
    mods_sibling,
    mods_pair,
    mods_partner,
    mods_low,
    mods_cols,
    bias_all,
    silu_part,
    silu_in,
    silu_all,
    small_send,
    small_recv,
    pair_send,
    pair_recv,
    head_send,
    head_recv,
    *reducing,
):
    row, member, sibling, partner, opposite = places()
    greet(range(1, ROW_PARTS), (sibling, partner))
    others = [(step, lax.rem(row + step, ROW_PARTS)) for step in range(1, ROW_PARTS)]

    def spread(stage, source_of, target):
        copies = []
        for step, other in others:
            copy = to_row(
                source_of(other),
                target.at[row],
                small_send.at[stage, step - 1],
                small_recv.at[stage, step - 1],
                other,
            )
            copy.start()
            copies.append(copy)
        return copies

    def settle(copies):
        for copy in copies:
            copy.wait()

    third = fc2_head.shape[0]
    fc2_grad[0:third] = fc2_head[...]
    fc2_grad[third : 2 * third] = fc2_neck[...]
    units = row_reduces(
        [(fc2_part, 0, fc2_grad.at[pl.ds(2 * third, third)])]
        + [(fc1_part, chunk, fc1_grad.at[pl.ds(chunk * third, third)]) for chunk in range(3)]
        + [(out_part, 0, out_grad)]
        + [(qkv_part, chunk, qkv_grad.at[pl.ds(chunk * third, third)]) for chunk in range(3)],
        reducing,
    )
    reduce_rows = HeadReduce(
        hidden_part, beside_in, pair_rows, across_in, head_send.at[0], head_recv.at[0]
    )
    reduce_ffn = HeadReduce(
        ffn_ref, ffn_beside, ffn_pair, ffn_across, head_send.at[1], head_recv.at[1]
    )
    for unit in units[:3]:
        unit.start()
    reduce_ffn.start()
    reduce_ffn.send_pair()
    blocks, tok_rows, model_width = grad_ref.shape
    width = qkv_ref.shape[1]
    head_local = totals_ref.shape[0]
    head_size = width // (3 * head_local)
    scale_factor = 1.0 / math.sqrt(head_size)
    seq_len = blocks * tok_rows
    mixed_grad[...] = jnp.zeros_like(mixed_grad)
    bias_own[...] = jnp.zeros_like(bias_own)

    def unpack(block, carry):
        rows = pl.ds(pl.multiple_of(block * tok_rows, tok_rows), tok_rows)
        packed[:, 0 : head_local * head_size] = jnp.dot(
            grad_ref[block], out_ref[...], preferred_element_type=jnp.float32
        )
        for head in range(head_local):
            mixed_grad[head, rows, 0:head_size] = packed[
                :, head * head_size : (head + 1) * head_size
            ].astype(jnp.bfloat16)
        bias_own[0] += jnp.sum(
            grad_ref[block].astype(jnp.float32).reshape(tok_rows // 8, 8, model_width), axis=0
        )
        return carry

    lax.fori_loop(0, blocks, unpack, 0)

    def turn(head, carry):
        key_columns[head] = parts[3 * head + 1].astype(jnp.float32).T.astype(jnp.bfloat16)
        return carry

    lax.fori_loop(0, head_local, turn, 0)
    grad_keys[...] = jnp.zeros_like(grad_keys)
    grad_values[...] = jnp.zeros_like(grad_values)
    weight_grad(grad_ref, mixed_ref, out_part)

    for block in range(blocks):
        rows = pl.ds(block * tok_rows, tok_rows)
        keys = jnp.concatenate([segments_ref[...]] * (tok_rows // 128), axis=1)
        same = keys == jnp.broadcast_to(segment_row[:, rows], keys.shape)
        bias[...] = jnp.where(same, 0.0, MASKED)

        def one_head(head, carry):
            query = parts[3 * head, rows]
            grad = mixed_grad[head, rows]
            scores = times_transposed(parts[3 * head + 1], query) * scale_factor + bias[...]
            probs = jnp.exp(scores - totals_ref[head, block])
            grad_probs = times_transposed(parts[3 * head + 2], grad)
            inner = jnp.sum(probs * grad_probs, axis=0, keepdims=True)
            grad_scores = (probs * (grad_probs - inner)).astype(jnp.bfloat16)
            grad_values[head] += jnp.dot(
                probs.astype(jnp.bfloat16), grad, preferred_element_type=jnp.float32
            )
            grad_keys[head] += jnp.dot(grad_scores, query, preferred_element_type=jnp.float32)
            lanes = pl.ds(pl.multiple_of(head * HEAD_LANES, HEAD_LANES), HEAD_LANES)
            hidden_part[block, :, lanes] = (
                jnp.dot(key_columns[head], grad_scores, preferred_element_type=jnp.float32).T
                * scale_factor
            ).astype(jnp.bfloat16)
            return carry

        lax.fori_loop(0, head_local, one_head, 0)
        units[block].send_pair()
        if block < 2:
            units[block + 3].start()
        if block > 0:
            units[block - 1].hop(0)
        if block > 1:
            units[block - 2].hop(1)

    def pack(block, carry):
        rows = pl.ds(pl.multiple_of(block * tok_rows, tok_rows), tok_rows)
        for head in range(head_local):
            lane = head * HEAD_LANES
            terms = (
                hidden_part[block, :, lane : lane + head_size].astype(jnp.float32),
                grad_keys[head, rows, 0:head_size] * scale_factor,
                grad_values[head, rows, 0:head_size],
            )
            for place, term in enumerate(terms):
                start = (3 * head + place) * head_size
                packed[:, start : start + head_size] = term
        low = packed[...].astype(jnp.bfloat16)
        packed_grad[block] = low
        bias_own[1, :, 0:width] += jnp.sum(
            low.astype(jnp.float32).reshape(tok_rows // 8, 8, width), axis=0
        )
        return carry

    lax.fori_loop(0, blocks, pack, 0)
    units[3].hop(0)
    units[2].hop(1)
    direction = sibling - member

    def project_back(block):
        hidden_part[block] = times_transposed(packed_grad[block], qkv_ref[...]).astype(
            jnp.bfloat16
        )

    def far(step, carry):
        project_back(opposite - step * direction)
        return carry

    def near(step, carry):
        project_back(sibling - step * direction)
        return carry

    lax.fori_loop(0, 2, far, 0)
    reduce_rows.first.start()
    reduce_rows.send_pair()
    lax.fori_loop(0, 2, near, 0)
    reduce_rows.second.start()
    weight_grad(hidden_rows, packed_grad, qkv_part)
    for unit in units[5:]:
        unit.start()
    bias_own[2] = jnp.zeros_like(bias_own[2])
    bias_own[2] = bias_ref[...]
    bias_own[2, 2:3] = jnp.sum(bias_own[0], axis=0, keepdims=True)
    bias_own[2, 3:4] = jnp.sum(bias_own[1], axis=0, keepdims=True)
    bias_copies = spread(1, lambda other: bias_own.at[2], bias_all)
    bias_all[row] = bias_own[2]
    units[4].send_pair()
    units[3].hop(1)
    slot_sums[...] = jnp.zeros_like(slot_sums)
    reduce_ffn.settle()

    def rows_out(block, carry):
        part = pl.ds(pl.multiple_of(block * 128, 128), 128)
        ffn = reduce_ffn.rows(part) + bias_rows[8:9]
        place = pl.multiple_of(member * tok_rows + block * 128, 128)
        gate = picked(vectors_ref, 5, segments_ref[pl.ds(place, 128)], model_width)
        block_out[part] = (block_ref[part] + gate * ffn).astype(jnp.bfloat16)
        slot_sums[2] += jnp.dot(
            slot_hot(segment_row, place),
            cotangent_ref[part].astype(jnp.float32) * ffn,
            precision=HIGH,
            preferred_element_type=jnp.float32,
        )
        return carry

    lax.fori_loop(0, tok_rows // 128, rows_out, 0)
    units[0].finish()
    units[1].finish()
    units[4].hop(0)
    units[5].send_pair()
    reduce_rows.settle()

    def rows_back(block, carry):
        part = pl.ds(pl.multiple_of(block * 128, 128), 128)
        grad = reduce_rows.rows(part)
        normed, factor = centre_rows(patches_ref[part].astype(jnp.float32))
        place = pl.multiple_of(member * tok_rows + block * 128, 128)
        weighted = grad * (
            1.0 + picked(vectors_ref, 1, segments_ref[pl.ds(place, 128)], model_width)
        )
        patches_grad[part] = after_ref[part] + factor * (
            weighted
            - jnp.mean(weighted, axis=1, keepdims=True)
            - normed * jnp.mean(weighted * normed, axis=1, keepdims=True)
        )
        hot = slot_hot(segment_row, place)
        slot_sums[0] += jnp.dot(hot, grad, precision=HIGH, preferred_element_type=jnp.float32)
        slot_sums[1] += jnp.dot(
            hot, grad * normed, precision=HIGH, preferred_element_type=jnp.float32
        )
        return carry

    lax.fori_loop(0, tok_rows // 128, rows_back, 0)
    ada_width = ada_ref.shape[1]
    fine = ada_width // 3
    for unit in range(3 * ROW_PARTS):
        part_index, within = divmod(unit * fine, model_width)
        span = slice(within, within + fine)
        if part_index < 2:
            source = slot_sums[part_index, :, span]
        elif part_index == 5:
            source = slot_sums[2, :, span]
        else:
            source = sums_ref[part_index - 2, :, span]
        mods_own[unit // 3, :, unit % 3 * fine : (unit % 3 + 1) * fine] = source
    beside = to_head(mods_own, mods_sibling, pair_send.at[0], pair_recv.at[0], sibling)
    beside.start()
    units[5].hop(0)
    units[4].hop(1)
    units[6].send_pair()
    beside.wait()
    mods_pair[...] = (mods_own[...] + mods_sibling[...]).astype(jnp.bfloat16)
    across = to_head(mods_pair, mods_partner, pair_send.at[1], pair_recv.at[1], partner)
    across.start()
    units[2].finish()
    units[3].finish()
    units[5].hop(1)
    settle(bias_copies)
    bias_sum[...] = jnp.sum(bias_all[...], axis=0)
    across.wait()
    mods_low[...] = (
        mods_pair[...].astype(jnp.float32) + mods_partner[...].astype(jnp.float32)
    ).astype(jnp.bfloat16)
    copies = spread(0, lambda other: mods_low.at[other], mods_cols)
    mods_cols[row] = mods_low[row]
    units[6].hop(0)
    units[7].send_pair()
    units[4].finish()
    settle(copies)
    slots = ROW_PARTS * SLOT_ROWS
    cols = mods_cols[...].astype(jnp.float32).reshape(slots, ada_width)
    low = cols.astype(jnp.bfloat16)
    condition = condition_ref[...].reshape(slots, condition_ref.shape[2])
    bent = 1.0 / (1.0 + jnp.exp(-condition))
    silu_part[...] = times_transposed(low, ada_ref[...]).reshape(silu_part.shape)
    copies = spread(2, lambda other: silu_part.at[other], silu_in)
    silu_in[row] = silu_part[row]
    ada_grad[...] = contract_rows((condition * bent).astype(jnp.bfloat16), low)
    units[7].hop(0)
    units[6].hop(1)
    ada_bias[...] = jnp.broadcast_to(jnp.sum(cols, axis=0, keepdims=True), ada_bias.shape)
    settle(copies)
    summed = jnp.sum(silu_in[...], axis=0)
    silu_all[row] = summed
    silu_part[row] = summed
    copies = spread(3, lambda other: silu_part.at[row], silu_all)
    units[7].hop(1)
    units[5].finish()
    units[6].finish()
    units[7].finish()
    settle(copies)
    grad_condition = silu_all[...].reshape(slots, silu_all.shape[2]) * (
        bent * (1.0 + condition * (1.0 - bent))
    )
    for target, hot in zip((time_grad, class_grad), table_hots(ids_all, time_grad.shape[1])):
        target[...] = contract_rows_exact(grad_condition, hot.astype(jnp.float32))
    reduce_rows.finish()
    reduce_ffn.finish()


def rear(*args):
    shape = jax.ShapeDtypeStruct
    grads, w_out, totals, grad_w_fc2, w_qkv, biases, ids_all, w_ada = (
        args[place] for place in (1, 2, 3, 6, 9, 11, 17, 18)
    )
    blocks, tok_rows, model_width = grads.shape
    width = w_qkv.shape[1]
    head_local = totals.shape[0]
    seq_len = blocks * tok_rows
    third, hidden_width = grad_w_fc2.shape[2:]
    width_part = 3 * third
    out_width = w_out.shape[1]
    depth, ada_width = w_ada.shape
    table_rows = ids_all.shape[2]
    low = jnp.bfloat16
    full = jnp.float32
    heads_wide = pltpu.VMEM((head_local, seq_len, HEAD_LANES), full)
    slotted = (ROW_PARTS, SLOT_ROWS)
    wide = pltpu.VMEM(slotted + (ada_width,), full)
    wide_low = pltpu.VMEM(slotted + (ada_width,), low)
    narrow = pltpu.VMEM(slotted + (depth,), full)
    sizes = (
        [(third, hidden_width)] * 4 + [(width_part, out_width)] + [(third, width)] * 3
    )
    return pl.pallas_call(
        rear_kernel,
        out_shape=[
            shape((tok_rows, model_width), low),
            shape((tok_rows, model_width), full),
            shape((depth, table_rows), full),
            shape((depth, table_rows), full),
            shape((depth, ada_width), full),
            shape((SLOT_ROWS, ada_width), full),
            shape((width_part, hidden_width), full),
            shape((width_part, hidden_width), full),
            shape((width_part, width), full),
            shape((width_part, out_width), full),
            shape(biases.shape, full),
        ],
        in_specs=[VMEM_SPEC] * 25,
        out_specs=[VMEM_SPEC] * 11,
        scratch_shapes=[
            pltpu.VMEM((head_local, seq_len, HEAD_LANES), low),
            pltpu.VMEM((head_local, HEAD_LANES, seq_len), low),
            heads_wide,
            heads_wide,
            pltpu.VMEM((seq_len, tok_rows), full),
            pltpu.VMEM((tok_rows, width), full),
            pltpu.VMEM((blocks, tok_rows, width), low),
            pltpu.VMEM((blocks, tok_rows, model_width), low),
            pltpu.VMEM((4, 2, width_part, width), low),
            pltpu.VMEM((4, 2, width_part, out_width), low),
            pltpu.VMEM((3,) + biases.shape, full),
        ]
        + [
            pltpu.VMEM((2, tok_rows, model_width), low),
            pltpu.VMEM((tok_rows, model_width), low),
            pltpu.VMEM((tok_rows, model_width), low),
        ]
        * 2
        + [pltpu.VMEM((3, SLOT_ROWS, model_width), full)]
        + [wide] * 2
        + [wide_low] * 4
        + [pltpu.VMEM((ROW_PARTS,) + biases.shape, full)]
        + [narrow] * 3
        + [
            DMA((4, 7)),
            DMA((4, 7)),
            DMA((2,)),
            DMA((2,)),
            DMA((2, 3)),
            DMA((2, 3)),
        ]
        + reduce_scratch(sizes),
        compiler_params=pltpu.CompilerParams(
            collective_id=1, has_side_effects=True, vmem_limit_bytes=67_000_000
        ),
        name="rear",
    )(*args)


def shards_linked(
    patches,
    time_table,
    class_table,
    w_ada,
    b_ada,
    w_qkv,
    b_qv,
    w_out,
    b_out,
    w_fc1,
    b_fc1,
    w_fc2,
    b_fc2,
    image_lengths,
    segment_ids,
    bucket_ids,
    class_labels,
    cotangent,
):
    model_width = patches.shape[1]
    slot_count = image_lengths.shape[1]
    head_local = b_qv.shape[0]
    head_size = b_qv.shape[1] // 2
    qkv_full, patches_full, condition, mods, ids_all = front(
        bucket_ids, class_labels, time_table.T, class_table.T, w_ada, patches, w_qkv
    )
    qkv_cols = qkv_full.reshape(model_width, w_qkv.shape[1])
    biases = (
        jnp.concatenate([b_ada, b_out, b_fc1, b_fc2]).astype(jnp.float32).reshape(9, model_width)
    )
    (
        segments,
        vectors,
        rows_one,
        parts,
        totals,
        mixed_rows,
        out_cols,
        ffn_part,
        after_attn,
        grad_after,
        attn_rows_grad,
        sums,
        bias_sums,
        grad_w_fc2,
        grad_w_fc1,
        fc2_head,
        fc2_neck,
    ) = core(
        slot_count,
        head_size,
        patches_full,
        qkv_cols,
        w_out,
        w_fc1,
        w_fc2,
        cotangent,
        patches,
        segment_ids,
        mods,
        biases,
        b_qv,
    )
    (
        block_out,
        grad_patches,
        grad_time,
        grad_class,
        grad_w_ada,
        grad_b_ada,
        grad_w_fc2,
        grad_w_fc1,
        grad_w_qkv,
        grad_w_out,
        bias_all,
    ) = rear(
        parts,
        attn_rows_grad,
        out_cols,
        totals,
        segment_ids,
        segments,
        grad_w_fc2,
        grad_w_fc1,
        rows_one,
        qkv_cols,
        mixed_rows,
        bias_sums,
        patches,
        grad_after,
        vectors,
        sums,
        condition,
        ids_all,
        w_ada,
        ffn_part,
        after_attn,
        cotangent,
        biases,
        fc2_head,
        fc2_neck,
    )
    grad_time = grad_time.T
    grad_class = grad_class.T
    grad_b_ada = grad_b_ada[0]
    bias_rows = model_width // lax.axis_size("rows")
    row_start = lax.axis_index("rows") * bias_rows
    grad_b_fc1 = bias_all[0]
    bias_own = lax.dynamic_slice(bias_all, (1, row_start), (2, bias_rows))
    grad_b_fc2 = bias_own[0]
    grad_b_out = bias_own[1]
    bias_terms = bias_all[3, : head_local * 3 * head_size].reshape(head_local, 3, head_size)
    grad_b_qv = jnp.concatenate([bias_terms[:, 0], bias_terms[:, 2]], axis=1)
    return (
        block_out,
        grad_patches,
        grad_time,
        grad_class,
        grad_w_ada,
        grad_b_ada,
        grad_w_qkv,
        grad_b_qv,
        grad_w_out,
        grad_b_out,
        grad_w_fc1,
        grad_b_fc1,
        grad_w_fc2,
        grad_b_fc2,
    )


def solution(mesh):
    placed = (
        P(("rows", "heads"), None),
        P("rows", "heads"),
        P("rows", "heads"),
        P("heads", "rows"),
        P(),
        P("rows", "heads"),
        P("heads", None),
        P("rows", "heads"),
        P(),
        P("rows", "heads"),
        P("heads"),
        P("rows", "heads"),
        P(),
        P("rows", None),
        P("rows", None),
        P("rows", None),
        P("rows", None),
        P(("rows", "heads"), None),
    )
    linked = mesh.shape["rows"] == ROW_PARTS and mesh.shape["heads"] == HEAD_PARTS
    return jax.shard_map(
        shards_linked if linked else shards_plain,
        mesh=mesh,
        in_specs=placed,
        out_specs=(
            P(("rows", "heads"), None),
            P(("rows", "heads"), None),
            P("rows", "heads"),
            P("rows", "heads"),
            P("heads", "rows"),
            P("rows"),
            P("rows", "heads"),
            P("heads", None),
            P("rows", "heads"),
            P("rows"),
            P("rows", "heads"),
            P("heads"),
            P("rows", "heads"),
            P("rows"),
        ),
        check_vma=False,
    )
```
